32 devices in a mesh: section: 2 (over core), fsdp: 4 (over y, x), ctx: 4 (over z).
Axes of the slice: x: 2, y: 2, z: 4, core: 2. Of those that a mesh axis runs over, the one named last changes fastest.
Arguments:
- inputs: bfloat16 [2, 4, 1024, 1088], P(None, 'fsdp', 'ctx'), may hold values from -6 to 6
- segments: int32 [2, 4, 1024], P(None, 'fsdp'), may hold values from 0 to 3, never falling along the last dimension, each value on 1 to 512 neighbouring positions
- cotangent: bfloat16 [2, 4, 1024, 1088], P(None, 'fsdp', 'ctx'), may hold values from -6 to 6
- qkv_weight: bfloat16 [2, 1088, 3264], P('section', 'fsdp'), may hold values from -0.1875 to 0.1875
- out_weight: bfloat16 [2, 1088, 1088], P('section', 'fsdp'), may hold values from -0.75 to 0.75
- up_weight: bfloat16 [2, 1088, 4352], P('section', 'fsdp'), may hold values from -0.1875 to 0.1875
- down_weight: bfloat16 [2, 4352, 1088], P('section', 'fsdp'), may hold values from -0.09375 to 0.09375
- norm_gains: bfloat16 [2, 2, 1088], P('section', None, 'fsdp'), may hold values from 0.5 to 1.5
- biases: bfloat16 [2, 6, 1088], P('section', None, 'fsdp'), may hold values from -3 to 3
- ff_bias: bfloat16 [2, 4352], P('section', 'fsdp'), may hold values from -3 to 3
Outputs:
- section_out: bfloat16 [2, 2, 4, 1024, 1088], P('section', None, 'fsdp', 'ctx')
- input_grad: float32 [2, 2, 4, 1024, 1088], P('section', None, 'fsdp', 'ctx')
- qkv_grad: float32 [2, 1088, 3264], P('section', 'fsdp')
- out_grad: float32 [2, 1088, 1088], P('section', 'fsdp')
- up_grad: float32 [2, 1088, 4352], P('section', 'fsdp')
- down_grad: float32 [2, 4352, 1088], P('section', 'fsdp')
- gain_grad: float32 [2, 2, 1088], P('section', None, 'fsdp')
- bias_grad: float32 [2, 6, 1088], P('section', None, 'fsdp')
- ff_bias_grad: float32 [2, 4352], P('section', 'fsdp')
The draws below stay inside these ranges and needn't reach their ends.
Inputs may be any that keep to these rules, and one draw needn't show every extreme that they name: `segments`: along each sequence the segment numbers never fall, every number appears, and one document covers exactly 512 positions, none more.
All inputs are finite; a program needn't handle non-finite values.
Results may differ from the reference program's by a relative error of at most 0.018.
Values may be sent and summed in bfloat16 or wider, within the bound.
A program may use at most 320 MiB of HBM per device.

```python
import math
import jax
import jax.numpy as jnp
import numpy as np
from jax import lax

D = 1088
HEADS = 17
HD = 64
FF = 4352
LEN = 1024
MICRO = 2
SEQS = 4


def level_of(rng, dims, pieces, least, top_value):
    def one(dim, blocks):
        heights = jax.random.uniform(jax.random.fold_in(jax.random.fold_in(rng, 6), dim), (blocks,), jnp.float32, least / len(pieces), top_value / len(pieces))
        return jnp.repeat(jnp.exp(heights), dims[dim] // blocks).reshape((-1,) + (1,) * (len(dims) - dim - 1))

    loudness = one(*pieces[0])
    for cut in pieces[1:]:
        loudness = loudness * one(*cut)
    return loudness


def length_profile(number_of, total, limit, slope):
    loads = [(1 << 20) // math.isqrt(rank ** slope) + 1 for rank in range(2, number_of + 1)]
    rest, counts = total - limit - (number_of - 1), [1] * (number_of - 1)
    while rest > 0:
        candidates = [i for i in range(number_of - 1) if counts[i] < limit]
        pool, left = sum([loads[i] for i in candidates]), rest
        for i in candidates:
            extra = min(limit - counts[i], max(1, left * loads[i] // pool), rest)
            counts[i] = counts[i] + extra
            rest = rest - extra
    return np.array([limit] + counts)


def uneven(rng, count, total, bound, skew):
    if count == 2:
        one = jax.random.randint(rng, (), max(1, total - bound), min(bound, total - 1) + 1)
        return jnp.stack([one, total - one])
    lengths = jnp.asarray(length_profile(count, total, bound, skew), jnp.int32)
    pairs = (count - 1) // 2
    source_of, sink = lengths[1:1 + 2 * pairs:2], lengths[2:2 + 2 * pairs:2]
    slack = jnp.minimum(source_of - 1, bound - sink)
    moved = jax.random.randint(jax.random.fold_in(rng, 1), (pairs,), 0, 1 << 20) % (slack + 1)
    lengths = lengths.at[1:1 + 2 * pairs:2].set(source_of - moved).at[2:2 + 2 * pairs:2].set(sink + moved)
    return lengths[jax.random.permutation(jax.random.fold_in(rng, 2), count)]


def scatter_about(rng, shape, width, reach, pieces=(), kind=jnp.bfloat16):
    result = width * jax.random.normal(rng, shape, jnp.float32)
    if pieces:
        result = result * level_of(rng, shape, pieces, -0.22, 0.18)
    return jnp.clip(result, -reach, reach).astype(kind)


def setup_inputs(seed: int = 0) -> dict:
    arg_keys = jax.random.split(jax.random.key(seed), 11)
    return {
        "inputs": scatter_about(arg_keys[0], (MICRO, SEQS, LEN, D), 1.0, 6.0, ((1, 4), (2, 4))),
        "segments": jax.vmap(lambda own: jnp.searchsorted(jnp.cumsum(uneven(own, 4, LEN, LEN // 2, 2)), jnp.arange(LEN), side="right"))(jax.random.split(arg_keys[1], MICRO * SEQS)).reshape((MICRO, SEQS, LEN)).astype(jnp.int32),
        "cotangent": scatter_about(arg_keys[2], (MICRO, SEQS, LEN, D), 1.0, 6.0, ((1, 4), (2, 4))),
        "qkv_weight": scatter_about(arg_keys[3], (2, D, 3 * D), D ** -0.5, 0.1875, ((0, 2), (1, 4))),
        "out_weight": scatter_about(arg_keys[4], (2, D, D), (D // 16) ** -0.5, 0.75, ((0, 2), (1, 4))),
        "up_weight": scatter_about(arg_keys[5], (2, D, FF), D ** -0.5, 0.1875, ((0, 2), (1, 4))),
        "down_weight": scatter_about(arg_keys[6], (2, FF, D), FF ** -0.5, 0.09375, ((0, 2), (1, 4))),
        "norm_gains": jnp.clip(1.0 + 0.1 * jax.random.normal(arg_keys[7], (2, 2, D), jnp.float32), 0.5, 1.5).astype(jnp.bfloat16),
        "biases": scatter_about(arg_keys[8], (2, 6, D), 0.5, 3.0, ((0, 2), (2, 4))),
        "ff_bias": scatter_about(arg_keys[9], (2, FF), 0.5, 3.0, ((0, 2), (1, 4))),
    }


@jax.custom_vjp
def low(v):
    return lax.optimization_barrier(v.astype(jnp.bfloat16)).astype(jnp.float32)

@jax.custom_vjp
def low_back(v):
    return v

def low_keep(v):
    return (low(v), None)

def low_pass(kept, grad):
    return (grad,)

def back_keep(v):
    return (v, None)

def back_low(kept, grad):
    return (low(grad),)
low.defvjp(low_keep, low_pass)
low_back.defvjp(back_keep, back_low)

def normalize(values, gain_row, shift_row):
    center = lax.optimization_barrier(jnp.mean(values, axis=-1, keepdims=True))
    offset = values - center
    spread = lax.optimization_barrier(jnp.mean(offset * offset, axis=-1, keepdims=True))
    return offset * lax.rsqrt(spread + 1e-05) * gain_row + shift_row

def product(left_op, right_op):
    return jnp.dot(left_op, right_op, precision=lax.Precision.HIGHEST, preferred_element_type=jnp.float32)

def block_layer(layer_in, allowed, weights):
    qkv_w, out_w, up_w, down_w, gain_rows, bias_rows, hidden_bias = weights
    normed = low(normalize(layer_in, gain_rows[0], bias_rows[0]))
    qkv_out = product(normed, qkv_w)
    query_rows = low_back(low(qkv_out[:, :D] + bias_rows[1])).reshape(LEN, HEADS, HD)
    key_rows = low_back(low(qkv_out[:, D:2 * D])).reshape(LEN, HEADS, HD)
    value_rows = low_back(low(qkv_out[:, 2 * D:] + bias_rows[2])).reshape(LEN, HEADS, HD)
    raw_scores = jnp.einsum('qhd,khd->hqk', query_rows, key_rows, precision=lax.Precision.HIGHEST)
    scores = low_back(raw_scores * (1.0 / math.sqrt(HD)))
    sum_exp = lax.optimization_barrier(jnp.sum(jnp.where(allowed, jnp.exp(scores), 0.0), axis=-1, keepdims=True))
    weights_p = low(jnp.where(allowed, jnp.exp(scores - jnp.log(sum_exp)), 0.0))
    attended = jnp.einsum('hqk,khd->qhd', weights_p, value_rows, precision=lax.Precision.HIGHEST)
    attended = low_back(low(attended.reshape(LEN, D)))
    residual = layer_in + low_back(product(attended, out_w)) + bias_rows[3]
    second = low(normalize(residual, gain_rows[1], bias_rows[4]))
    hidden = low_back(product(second, up_w)) + hidden_bias
    active = low(jax.nn.gelu(hidden, approximate=False))
    return residual + low_back(product(active, down_w)) + bias_rows[5]

def reference(inputs, segments, cotangent, qkv_weight, out_weight, up_weight, down_weight, norm_gains, biases, ff_bias):
    params = tuple((weight.astype(jnp.float32) for weight in (qkv_weight, out_weight, up_weight, down_weight, norm_gains, biases, ff_bias)))
    seq_count = MICRO * SEQS
    flat_in = inputs.astype(jnp.float32).reshape(seq_count, LEN, D)
    flat_seg = segments.reshape(seq_count, LEN)
    flat_cot = cotangent.astype(jnp.float32).reshape(seq_count, LEN, D)
    positions = jnp.arange(LEN, dtype=jnp.int32)
    causal = positions[None, :] <= positions[:, None]

    def forward(layer_params, first_in, mid_zero):

        def one_sequence(entry):
            seq_in, seq_seg, seq_zero = entry
            allowed = (causal & (seq_seg[:, None] == seq_seg[None, :]))[None]
            first_params = tuple((weight[0] for weight in layer_params))
            second_params = tuple((weight[1] for weight in layer_params))
            first_out = block_layer(seq_in, allowed, first_params)
            sent_rows = low_back(low(first_out)) + seq_zero
            return (sent_rows, block_layer(sent_rows, allowed, second_params))
        return lax.map(jax.checkpoint(one_sequence), (first_in, flat_seg, mid_zero))
    mid_zero = jnp.zeros_like(flat_in)
    (sent_all, final_all), pullback = jax.vjp(forward, params, flat_in, mid_zero)
    param_grads, first_grad, mid_grad = pullback((jnp.zeros_like(sent_all), flat_cot))
    grad_qkv, grad_out, grad_up, grad_down, grad_gain, grad_bias, grad_ffb = param_grads
    shape_out = (2, MICRO, SEQS, LEN, D)
    section_out = jnp.stack([sent_all, final_all]).reshape(shape_out).astype(jnp.bfloat16)
    input_grad = jnp.stack([first_grad, mid_grad]).reshape(shape_out)
    return (section_out, input_grad, grad_qkv, grad_out, grad_up, grad_down, grad_gain, grad_bias, grad_ffb)
```

```python
import math

import jax
import jax.numpy as jnp
from jax import lax
from jax.experimental import pallas as pl
from jax.experimental.pallas import tpu as pltpu
from jax.sharding import PartitionSpec as P

D = 1088
HEADS = 17
HD = 64
F32 = jnp.float32
BF = jnp.bfloat16
SCALE = 1.0 / math.sqrt(HD)
EXT = 3328
MESH = pl.DeviceIdType.MESH
SWAP = [(0, 1), (1, 0)]


def mm(a, b):
    return jnp.dot(a, b, preferred_element_type=F32)


def mm_nt(a, b):
    return lax.dot_general(a, b, (((1,), (1,)), ((), ())), preferred_element_type=F32)


def mm_tn(a, b):
    return lax.dot_general(a, b, (((0,), (0,)), ((), ())), preferred_element_type=F32)


def norm_parts(values):
    center = jnp.mean(values, axis=-1, keepdims=True)
    offset = values - center
    spread = jnp.mean(offset * offset, axis=-1, keepdims=True)
    inv = lax.rsqrt(spread + 1e-05)
    return offset * inv, inv


def norm_back(grad, gain, unit, inv):
    dn = grad * gain
    return inv * (
        dn
        - jnp.mean(dn, axis=-1, keepdims=True)
        - unit * jnp.mean(dn * unit, axis=-1, keepdims=True)
    )


def phi_parts(z):
    cdf = 0.5 * (1.0 + lax.erf(z * (1.0 / math.sqrt(2.0))))
    pdf = jnp.exp(-0.5 * z * z) * (1.0 / math.sqrt(2.0 * math.pi))
    return cdf, pdf


def plane_neighbours():
    f = lax.axis_index("fsdp")
    x = lax.rem(f, 2)
    y = f // 2
    return y * 2 + (1 - x), (1 - y) * 2 + x


def plane_barrier(xn, yn):
    barrier = pltpu.get_barrier_semaphore()
    for nb in (xn, yn):
        pl.semaphore_signal(barrier, inc=1, device_id={"fsdp": nb}, device_id_type=MESH)
    pl.semaphore_wait(barrier, 2)


def remote(src, dst, send, recv, nb):
    return pltpu.make_async_remote_copy(
        src_ref=src, dst_ref=dst, send_sem=send, recv_sem=recv,
        device_id={"fsdp": nb}, device_id_type=MESH,
    )


def gather_kernel(b_ref, out_ref, send, recv):
    xn, yn = plane_neighbours()
    half = b_ref.shape[0] // 2
    plane_barrier(xn, yn)
    to_x = remote(b_ref, out_ref.at[1], send.at[0], recv.at[0], xn)
    to_y = remote(b_ref, out_ref.at[2], send.at[1], recv.at[1], yn)
    to_x.start()
    to_y.start()
    out_ref[0] = b_ref[...]
    to_x.wait_recv()
    low = remote(
        out_ref.at[1, pl.ds(half, half)], out_ref.at[3, pl.ds(half, half)],
        send.at[3], recv.at[3], yn,
    )
    low.start()
    to_y.wait_recv()
    top = remote(
        out_ref.at[2, pl.ds(0, half)], out_ref.at[3, pl.ds(0, half)],
        send.at[2], recv.at[2], xn,
    )
    top.start()
    to_x.wait_send()
    to_y.wait_send()
    low.wait()
    top.wait()


def scatter_kernel(p_ref, out_ref, x1, y1, x2, y2, sum_x, sum_y, send, recv):
    xn, yn = plane_neighbours()
    half = p_ref.shape[1] // 2
    top = pl.ds(0, half)
    low = pl.ds(half, half)
    plane_barrier(xn, yn)
    first_x = remote(p_ref.at[3, top], x1, send.at[0], recv.at[0], xn)
    first_y = remote(p_ref.at[3, low], y1, send.at[1], recv.at[1], yn)
    own_x = remote(p_ref.at[1, top], x2.at[top], send.at[2], recv.at[2], xn)
    own_y = remote(p_ref.at[2, low], y2.at[low], send.at[3], recv.at[3], yn)
    for copy in (first_x, first_y, own_x, own_y):
        copy.start()
    first_x.wait_recv()
    sum_y[...] = (p_ref[2, top, :].astype(F32) + x1[...].astype(F32)).astype(BF)
    rest_y = remote(sum_y, y2.at[top], send.at[5], recv.at[5], yn)
    rest_y.start()
    first_y.wait_recv()
    sum_x[...] = (p_ref[1, low, :].astype(F32) + y1[...].astype(F32)).astype(BF)
    rest_x = remote(sum_x, x2.at[low], send.at[4], recv.at[4], xn)
    rest_x.start()
    own_x.wait_recv()
    own_y.wait_recv()
    rest_y.wait_recv()
    out_ref[top, :] = (
        p_ref[0, top, :].astype(F32) + x2[top, :].astype(F32) + y2[top, :].astype(F32)
    )
    rest_x.wait_recv()
    out_ref[low, :] = (
        p_ref[0, low, :].astype(F32) + x2[low, :].astype(F32) + y2[low, :].astype(F32)
    )
    for copy in (first_x, first_y, own_x, own_y, rest_x, rest_y):
        copy.wait_send()


VSPEC = pl.BlockSpec(memory_space=pltpu.VMEM)


def plane_gather(value):
    if lax.axis_size("fsdp") != 4:
        return lax.all_gather(value, "fsdp", axis=0, tiled=True)
    rows, width = value.shape
    out = pl.pallas_call(
        gather_kernel,
        out_shape=jax.ShapeDtypeStruct((4, rows, width), value.dtype),
        in_specs=[VSPEC],
        out_specs=VSPEC,
        scratch_shapes=[pltpu.SemaphoreType.DMA((4,)), pltpu.SemaphoreType.DMA((4,))],
        compiler_params=pltpu.CompilerParams(collective_id=1, has_side_effects=True),
        name="plane_gather",
    )(value)
    return out.reshape(4 * rows, width)


def plane_scatter(value, rows):
    if lax.axis_size("fsdp") != 4:
        return lax.psum_scatter(value, "fsdp", scatter_dimension=0, tiled=True).astype(F32)
    width = value.shape[-1]
    half = rows // 2
    return pl.pallas_call(
        scatter_kernel,
        out_shape=jax.ShapeDtypeStruct((rows, width), F32),
        in_specs=[VSPEC],
        out_specs=VSPEC,
        scratch_shapes=[
            pltpu.VMEM((half, width), BF),
            pltpu.VMEM((half, width), BF),
            pltpu.VMEM((rows, width), BF),
            pltpu.VMEM((rows, width), BF),
            pltpu.VMEM((half, width), BF),
            pltpu.VMEM((half, width), BF),
            pltpu.SemaphoreType.DMA((6,)),
            pltpu.SemaphoreType.DMA((6,)),
        ],
        compiler_params=pltpu.CompilerParams(collective_id=2, has_side_effects=True),
        name="plane_scatter",
    )(value.reshape(4, rows, width))


def shift(value, steps):
    count = lax.axis_size("ctx")
    pairs = [(i, i + steps) for i in range(count) if 0 <= i + steps < count]
    return lax.ppermute(value, "ctx", pairs)


def with_halo(own, chunks):
    parts = [own]
    for _ in range(chunks):
        parts.append(shift(parts[-1], 1))
    return jnp.concatenate(parts[::-1], axis=0)


def return_halo(halo, chunks, rows):
    carried = None
    for far in range(chunks):
        mine = halo[far * rows : (far + 1) * rows]
        carried = mine if carried is None else mine + carried
        carried = shift(carried.astype(BF), -1).astype(F32)
    return carried


def pick(s, first, second):
    return jnp.where(s == 0, first, second)


def on_chip(value):
    return lax.ppermute(value, "section", SWAP)


def both_layers(own, s):
    other = on_chip(own)
    return pick(s, own, other), pick(s, other, own)


def half_rows(own, s):
    half = own.shape[0] // 2
    halves = own.reshape(2, half, own.shape[1])
    keep = lax.dynamic_index_in_dim(halves, s, 0, keepdims=False)
    give = lax.dynamic_index_in_dim(halves, 1 - s, 0, keepdims=False)
    recv = on_chip(give)
    return pick(s, keep, recv), pick(s, recv, keep)


def heads(values):
    return values.reshape(values.shape[0], HEADS, HD)


def attention(q, k, v, allowed):
    scores = jnp.einsum("qhd,khd->hqk", heads(q), heads(k), preferred_element_type=F32) * SCALE
    total = jnp.sum(jnp.where(allowed, jnp.exp(scores), 0.0), axis=-1, keepdims=True)
    logs = jnp.log(total)
    prob = jnp.where(allowed, jnp.exp(scores - logs), 0.0).astype(BF)
    out = jnp.einsum("hqk,khd->qhd", prob, heads(v), preferred_element_type=F32)
    return out.reshape(q.shape[0], D).astype(BF), logs


def attention_back(q, k, v, logs, d_out, allowed):
    qh, kh, vh, gh = heads(q), heads(k), heads(v), heads(d_out)
    scores = jnp.einsum("qhd,khd->hqk", qh, kh, preferred_element_type=F32) * SCALE
    prob = jnp.where(allowed, jnp.exp(scores - logs), 0.0)
    d_prob = jnp.einsum("qhd,khd->hqk", gh, vh, preferred_element_type=F32)
    row = jnp.sum(prob * d_prob, axis=-1, keepdims=True)
    d_score = (prob * (d_prob - row)).astype(BF)
    dq = jnp.einsum("hqk,khd->qhd", d_score, kh, preferred_element_type=F32) * SCALE
    dk = jnp.einsum("hqk,qhd->khd", d_score, qh, preferred_element_type=F32) * SCALE
    dv = jnp.einsum("hqk,qhd->khd", prob.astype(BF), gh, preferred_element_type=F32)
    return (
        dq.reshape(q.shape[0], D).astype(BF),
        dk.reshape(k.shape[0], D).astype(BF),
        dv.reshape(k.shape[0], D).astype(BF),
    )


def on_device(
    inputs, segments, cotangent, qkv_weight, out_weight, up_weight, down_weight,
    norm_gains, biases, ff_bias,
):
    rows = inputs.shape[2]
    length = segments.shape[2]
    chunks = min((length // 2 - 1 + rows - 1) // rows, lax.axis_size("ctx") - 1)
    reach = chunks * rows
    s = lax.axis_index("section")
    f = lax.axis_index("fsdp")
    nf = lax.axis_size("fsdp")
    shard = D // nf
    ff_here = ff_bias.shape[1]
    per_row = ff_here // shard
    pair = ("fsdp", "section")

    own_in = lax.dynamic_index_in_dim(inputs, s, 0, keepdims=False)[0]
    own_cot = lax.dynamic_index_in_dim(cotangent, s, 0, keepdims=False)[0]
    seg = lax.dynamic_index_in_dim(segments, s, 0, keepdims=False)[0]
    start = lax.axis_index("ctx") * rows
    key_seg = lax.dynamic_slice_in_dim(
        jnp.pad(seg, (reach, 0), constant_values=-1), start, reach + rows, 0
    )
    allowed = (key_seg[reach:, None] == key_seg[None, :]) & (
        jnp.arange(reach + rows, dtype=jnp.int32)[None, :] - reach
        <= jnp.arange(rows, dtype=jnp.int32)[:, None]
    )

    small = jnp.concatenate(
        [norm_gains[0].T, biases[0].T, ff_bias[0].reshape(shard, per_row)], axis=1
    )
    qkv_own = jnp.concatenate(
        [qkv_weight[0], small, jnp.zeros((shard, EXT - 3 * D - 8 - per_row), BF)], axis=1
    )
    qkv_halves = half_rows(qkv_own, s)
    out_halves = half_rows(out_weight[0], s)
    up_own = lax.all_to_all(
        up_weight[0].reshape(shard, nf, ff_here), "fsdp", split_axis=1, concat_axis=0, tiled=True
    ).reshape(D, ff_here)
    up_w = both_layers(up_own, s)
    down_w = both_layers(down_weight[0], s)

    qkv_w, out_w, gains, shifts, ffb = [], [], [], [], []
    for layer in range(2):
        full = lax.all_gather(qkv_halves[layer], pair, axis=0, tiled=True)
        qkv_w.append(full)
        out_w.append(lax.all_gather(out_halves[layer], pair, axis=0, tiled=True))
        vectors = full[:, 3 * D : 3 * D + 8].T.astype(F32)
        gains.append(vectors[:2])
        shifts.append(vectors[2:])
        hidden = full[:, 3 * D + 8 : 3 * D + 8 + per_row].reshape(-1).astype(F32)
        ffb.append(lax.dynamic_slice_in_dim(hidden, f * ff_here, ff_here, 0))

    kept = []
    current = own_in
    produced = []
    for layer in range(2):
        gain, shift_rows = gains[layer], shifts[layer]
        wide = with_halo(current, chunks).astype(F32)
        n1, inv1 = norm_parts(wide)
        normed = (n1 * gain[0] + shift_rows[0]).astype(BF)
        q = (mm(normed[reach:], qkv_w[layer][:, :D]) + shift_rows[1]).astype(BF)
        k = mm(normed, qkv_w[layer][:, D : 2 * D]).astype(BF)
        v = (mm(normed, qkv_w[layer][:, 2 * D : 3 * D]) + shift_rows[2]).astype(BF)
        att, logs = attention(q, k, v, allowed)
        resid = current.astype(F32) + mm(att, out_w[layer]) + shift_rows[3]
        n2, inv2 = norm_parts(resid)
        second = (n2 * gain[1] + shift_rows[4]).astype(BF)
        second_all = plane_gather(second)
        z = mm(second_all, up_w[layer]) + ffb[layer]
        cdf, _ = phi_parts(z)
        active = (z * cdf).astype(BF)
        partial = mm(active, down_w[layer]).astype(BF)
        out = resid + plane_scatter(partial, rows) + shift_rows[5]
        low = out.astype(BF)
        produced.append(low)
        kept.append((wide, normed, q, k, v, att, logs, resid, second_all, z, active))
        current = low

    upstream = own_cot.astype(F32)
    derived = [None, None]
    totals = [None, None]
    for layer in (1, 0):
        wide, normed, q, k, v, att, logs, resid, second_all, z, active = kept[layer]
        gain = gains[layer]
        up_b = upstream.astype(BF)
        up_all = plane_gather(up_b)
        cdf, pdf = phi_parts(z)
        dz = mm_nt(up_all, down_w[layer]) * (cdf + z * pdf)
        dz_b = dz.astype(BF)
        d_second = plane_scatter(mm_nt(dz_b, up_w[layer]).astype(BF), rows)
        down_g = mm_tn(active, up_all)
        up_g = mm_tn(second_all, dz_b)
        ffb_g = jnp.sum(dz, axis=0)
        n2, inv2 = norm_parts(resid)
        d_resid = upstream + norm_back(d_second, gain[1], n2, inv2)
        c = d_resid.astype(BF)
        d_att = mm_nt(c, out_w[layer]).astype(BF)
        out_g = mm_tn(att, c)
        dq, dk, dv = attention_back(q, k, v, logs, d_att, allowed)
        w = qkv_w[layer]
        da_wide = mm_nt(dk, w[:, D : 2 * D]) + mm_nt(dv, w[:, 2 * D : 3 * D])
        da_own = da_wide[reach:] + mm_nt(dq, w[:, :D])
        da_halo = da_wide[:reach]
        n1, inv1 = norm_parts(wide)
        da = da_own + return_halo(da_halo, chunks, rows)
        d_in = d_resid + norm_back(da, gain[0], n1[reach:], inv1[reach:])
        derived[layer] = d_in
        upstream_next = d_in.astype(BF).astype(F32)
        vectors = jnp.stack(
            [
                jnp.sum(da_halo * n1[:reach], axis=0) + jnp.sum(da_own * n1[reach:], axis=0),
                jnp.sum(d_second * n2, axis=0),
                jnp.sum(da_halo, axis=0) + jnp.sum(da_own, axis=0),
                jnp.sum(dq.astype(F32), axis=0),
                jnp.sum(dv.astype(F32), axis=0),
                jnp.sum(d_resid, axis=0),
                jnp.sum(d_second, axis=0),
                jnp.sum(upstream, axis=0),
            ]
        )
        ffb_block = lax.dynamic_update_slice(
            jnp.zeros((D, per_row), BF),
            ffb_g.reshape(shard, per_row).astype(BF),
            (f * shard, 0),
        )
        qkv_g = jnp.concatenate(
            [
                mm_tn(normed[reach:], dq).astype(BF),
                mm_tn(normed, dk).astype(BF),
                mm_tn(normed, dv).astype(BF),
                vectors.T.astype(BF),
                ffb_block,
                jnp.zeros((D, EXT - 3 * D - 8 - per_row), BF),
            ],
            axis=1,
        )
        qkv_g = lax.psum_scatter(qkv_g, pair, scatter_dimension=0, tiled=True)
        out_g = lax.psum_scatter(out_g.astype(BF), pair, scatter_dimension=0, tiled=True)
        down_pair = down_g.astype(BF).reshape(2, ff_here // 2, D)
        up_pair = up_g.astype(BF).reshape(nf, 2, shard // 2, ff_here)
        give = (
            lax.dynamic_index_in_dim(down_pair, 1 - s, 0, keepdims=False),
            lax.dynamic_index_in_dim(up_pair, 1 - s, 1, keepdims=False),
        )
        keep = (
            lax.dynamic_index_in_dim(down_pair, s, 0, keepdims=False),
            lax.dynamic_index_in_dim(up_pair, s, 1, keepdims=False),
        )
        down_g, up_g = (
            (a.astype(F32) + on_chip(b).astype(F32)).astype(BF) for a, b in zip(keep, give)
        )
        up_g = lax.all_to_all(up_g, "fsdp", split_axis=0, concat_axis=0, tiled=True)
        totals[layer] = lax.psum((qkv_g, out_g, down_g, up_g), "ctx")
        upstream = upstream_next

    def settle(zero, one):
        mine = pick(s, zero, one)
        other = on_chip(pick(s, one, zero))
        return pick(s, mine, other).astype(F32), pick(s, other, mine).astype(F32)

    qkv_t, out_t, down_t, up_t = (settle(a, b) for a, b in zip(*totals))
    qkv_full = jnp.concatenate(qkv_t, axis=0)
    grad_up = jnp.concatenate(up_t, axis=1).transpose(1, 0, 2).reshape(shard, nf * ff_here)
    vectors = qkv_full[:, 3 * D : 3 * D + 8].T
    return (
        gather_micro(jnp.stack(produced), s),
        gather_micro(jnp.stack(derived), s),
        qkv_full[None, :, : 3 * D],
        jnp.concatenate(out_t, axis=0)[None],
        grad_up[None],
        jnp.concatenate(down_t, axis=0)[None],
        vectors[None, :2],
        vectors[None, 2:],
        qkv_full[:, 3 * D + 8 : 3 * D + 8 + per_row].reshape(1, ff_here),
    )


def gather_micro(layers, s):
    mine = lax.dynamic_index_in_dim(layers, s, 0, keepdims=False)
    other = on_chip(lax.dynamic_index_in_dim(layers, 1 - s, 0, keepdims=False))
    return jnp.stack([pick(s, mine, other), pick(s, other, mine)])[None, :, None]


def solution(mesh):
    return jax.shard_map(
        on_device,
        mesh=mesh,
        in_specs=(
            P(None, "fsdp", "ctx", None),
            P(None, "fsdp", None),
            P(None, "fsdp", "ctx", None),
            P("section", "fsdp", None),
            P("section", "fsdp", None),
            P("section", "fsdp", None),
            P("section", "fsdp", None),
            P("section", None, "fsdp"),
            P("section", None, "fsdp"),
            P("section", "fsdp"),
        ),
        out_specs=(
            P("section", None, "fsdp", "ctx", None),
            P("section", None, "fsdp", "ctx", None),
            P("section", "fsdp", None),
            P("section", "fsdp", None),
            P("section", "fsdp", None),
            P("section", "fsdp", None),
            P("section", None, "fsdp"),
            P("section", None, "fsdp"),
            P("section", "fsdp"),
        ),
        check_vma=False,
    )
```

```python
import math

import jax
import jax.numpy as jnp
from jax import lax
from jax.experimental import pallas as pl
from jax.experimental.pallas import tpu as pltpu
from jax.sharding import PartitionSpec as P

D = 1088
HEADS = 17
HD = 64
F32 = jnp.float32
BF = jnp.bfloat16
SCALE = 1.0 / math.sqrt(HD)
WIDE = 1152
EXT = 3328
MESH = pl.DeviceIdType.MESH
SWAP = [(0, 1), (1, 0)]


def mm(a, b):
    return jnp.dot(a, b, preferred_element_type=F32)


def mm_nt(a, b):
    return lax.dot_general(a, b, (((1,), (1,)), ((), ())), preferred_element_type=F32)


def mm_tn(a, b):
    return lax.dot_general(a, b, (((0,), (0,)), ((), ())), preferred_element_type=F32)


def norm_parts(values):
    center = jnp.mean(values, axis=-1, keepdims=True)
    offset = values - center
    spread = jnp.mean(offset * offset, axis=-1, keepdims=True)
    inv = lax.rsqrt(spread + 1e-05)
    return offset * inv, inv


def norm_back(grad, gain, unit, inv):
    dn = grad * gain
    return inv * (
        dn
        - jnp.mean(dn, axis=-1, keepdims=True)
        - unit * jnp.mean(dn * unit, axis=-1, keepdims=True)
    )


def phi_parts(z):
    cdf = 0.5 * (1.0 + lax.erf(z * (1.0 / math.sqrt(2.0))))
    pdf = jnp.exp(-0.5 * z * z) * (1.0 / math.sqrt(2.0 * math.pi))
    return cdf, pdf


def plane_neighbours():
    f = lax.axis_index("fsdp")
    x = lax.rem(f, 2)
    y = f // 2
    return y * 2 + (1 - x), (1 - y) * 2 + x


def plane_barrier(xn, yn):
    barrier = pltpu.get_barrier_semaphore()
    for nb in (xn, yn):
        pl.semaphore_signal(barrier, inc=1, device_id={"fsdp": nb}, device_id_type=MESH)
    pl.semaphore_wait(barrier, 2)


def remote(src, dst, send, recv, nb):
    return pltpu.make_async_remote_copy(
        src_ref=src, dst_ref=dst, send_sem=send, recv_sem=recv,
        device_id={"fsdp": nb}, device_id_type=MESH,
    )


def gather_kernel(b_ref, out_ref, send, recv):
    xn, yn = plane_neighbours()
    half = b_ref.shape[0] // 2
    plane_barrier(xn, yn)
    to_x = remote(b_ref, out_ref.at[1], send.at[0], recv.at[0], xn)
    to_y = remote(b_ref, out_ref.at[2], send.at[1], recv.at[1], yn)
    to_x.start()
    to_y.start()
    out_ref[0] = b_ref[...]
    to_x.wait_recv()
    low = remote(
        out_ref.at[1, pl.ds(half, half)], out_ref.at[3, pl.ds(half, half)],
        send.at[3], recv.at[3], yn,
    )
    low.start()
    to_y.wait_recv()
    top = remote(
        out_ref.at[2, pl.ds(0, half)], out_ref.at[3, pl.ds(0, half)],
        send.at[2], recv.at[2], xn,
    )
    top.start()
    to_x.wait_send()
    to_y.wait_send()
    low.wait()
    top.wait()


def scatter_kernel(p_ref, out_ref, x1, y1, x2, y2, sum_x, sum_y, send, recv):
    xn, yn = plane_neighbours()
    half = p_ref.shape[1] // 2
    top = pl.ds(0, half)
    low = pl.ds(half, half)
    plane_barrier(xn, yn)
    first_x = remote(p_ref.at[3, top], x1, send.at[0], recv.at[0], xn)
    first_y = remote(p_ref.at[3, low], y1, send.at[1], recv.at[1], yn)
    own_x = remote(p_ref.at[1, top], x2.at[top], send.at[2], recv.at[2], xn)
    own_y = remote(p_ref.at[2, low], y2.at[low], send.at[3], recv.at[3], yn)
    for copy in (first_x, first_y, own_x, own_y):
        copy.start()
    first_x.wait_recv()
    sum_y[...] = (p_ref[2, top, :].astype(F32) + x1[...].astype(F32)).astype(BF)
    rest_y = remote(sum_y, y2.at[top], send.at[5], recv.at[5], yn)
    rest_y.start()
    first_y.wait_recv()
    sum_x[...] = (p_ref[1, low, :].astype(F32) + y1[...].astype(F32)).astype(BF)
    rest_x = remote(sum_x, x2.at[low], send.at[4], recv.at[4], xn)
    rest_x.start()
    own_x.wait_recv()
    own_y.wait_recv()
    rest_y.wait_recv()
    out_ref[top, :] = (
        p_ref[0, top, :].astype(F32) + x2[top, :].astype(F32) + y2[top, :].astype(F32)
    )
    rest_x.wait_recv()
    out_ref[low, :] = (
        p_ref[0, low, :].astype(F32) + x2[low, :].astype(F32) + y2[low, :].astype(F32)
    )
    for copy in (first_x, first_y, own_x, own_y, rest_x, rest_y):
        copy.wait_send()


def z_partners():
    z = lax.axis_index("ctx")
    return z + 1 - 2 * lax.rem(z, 2), 3 - z, (z == 1) | (z == 2)


def add_rows(dst, one, two, rows, step):
    @pl.loop(0, rows // step)
    def _(i):
        at = pl.ds(pl.multiple_of(i * step, 16), step)
        dst[at, :] = (one[at, :].astype(F32) + two[at, :].astype(F32)).astype(dst.dtype)


def reduce_kernel(
    aq, ak, av, ao, down, up, a_out, m_out,
    a_own, a_in, x1, y1, x2, y2, sx, sy, a_t, a_za, a_zb, a_fin,
    m_own, m_in, m_za, m_zb, m_fin,
    load, core_s, core_r, p_send, p_recv, z_send, z_recv, fin_s, fin_r,
):
    s = lax.axis_index("section")
    f = lax.axis_index("fsdp")
    xn, yn = plane_neighbours()
    dn = 3 - f
    side, across, inner = z_partners()
    shard = a_t.shape[1]
    cut = x1.shape[2]
    wide = a_t.shape[2]
    left = pl.ds(0, cut)
    right = pl.ds(cut, wide - cut)

    def to(src, dst, send, recv, **where):
        return pltpu.make_async_remote_copy(
            src_ref=src, dst_ref=dst, send_sem=send, recv_sem=recv,
            device_id=where, device_id_type=MESH,
        )

    barrier = pltpu.get_barrier_semaphore()
    partners = ({"section": 1 - s}, {"fsdp": xn}, {"fsdp": yn}, {"ctx": side}, {"ctx": across})
    for where in partners:
        pl.semaphore_signal(barrier, inc=1, device_id=where, device_id_type=MESH)
    pl.semaphore_wait(barrier, 5)

    def rows_of(half, k):
        return pl.ds(pl.multiple_of(half * 2 * shard + k * shard, 16), shard)

    def m_src(i):
        return (down, up)[i // 2], i % 2

    def m_copies(i):
        ref, k = m_src(i)
        return (
            to(ref.at[rows_of(1 - s, k)], m_in.at[i], core_s.at[i], core_r.at[i], section=1 - s),
            pltpu.make_async_copy(ref.at[rows_of(s, k)], m_own.at[i], load.at[i]),
        )

    def a_copies(j, give, keep):
        return (
            to(give, a_in.at[j], core_s.at[4 + j], core_r.at[4 + j], section=1 - s),
            pltpu.make_async_copy(keep, a_own.at[j], load.at[4 + j]),
        )

    def start_a(j):
        for half in range(2):

            @pl.when(s == half)
            def _(half=half):
                pieces = (aq, ak, av, ao)
                for copy in a_copies(j, pieces[2 - 2 * half + j], pieces[2 * half + j]):
                    copy.start()

    for i in range(4):
        for copy in m_copies(i):
            copy.start()
        if i == 0:
            start_a(0)
            start_a(1)

    def z_step(own, za, zb, fin, k):
        return (
            to(own, za, z_send.at[3 * k], z_recv.at[3 * k], ctx=side),
            to(za, zb, z_send.at[3 * k + 1], z_recv.at[3 * k + 1], ctx=across),
            to(fin, fin, z_send.at[3 * k + 2], z_recv.at[3 * k + 2], ctx=side),
        )

    def m_z(i):
        return z_step(m_own.at[i], m_za.at[i], m_zb.at[i], m_fin.at[i], i)

    def a_z(j):
        return z_step(a_t.at[j], a_za.at[j], a_zb.at[j], a_fin.at[j], 4 + j)

    def z_first(copies):
        @pl.when(jnp.logical_not(inner))
        def _():
            copies[0].start()

    def z_second(copies, own, za):
        @pl.when(inner)
        def _():
            copies[0].wait_recv()
            add_rows(za, own, za, shard, shard // 2 if shard % 32 == 0 else shard)
            copies[1].start()

    def z_third(copies, za, zb, fin):
        @pl.when(inner)
        def _():
            copies[1].wait_recv()
            add_rows(fin, za, zb, shard, shard // 2 if shard % 32 == 0 else shard)
            copies[2].start()

    def z_last(copies):
        @pl.when(jnp.logical_not(inner))
        def _():
            copies[2].wait_recv()

    def m_one(i):
        far, near = m_copies(i)
        far.wait_recv()
        near.wait()
        add_rows(m_own.at[i], m_own.at[i], m_in.at[i], shard, shard)
        z_first(m_z(i))

    def blk(owner):
        return pl.ds(pl.multiple_of(owner * shard, 16), shard)

    def plane(j):
        own = a_own.at[j]
        return (
            to(own.at[blk(dn), left], x1.at[j], p_send.at[j, 0], p_recv.at[j, 0], fsdp=xn),
            to(own.at[blk(dn), right], y1.at[j], p_send.at[j, 1], p_recv.at[j, 1], fsdp=yn),
            to(own.at[blk(xn), left], x2.at[j, :, left], p_send.at[j, 2], p_recv.at[j, 2], fsdp=xn),
            to(own.at[blk(yn), right], y2.at[j, :, right], p_send.at[j, 3], p_recv.at[j, 3], fsdp=yn),
            to(sx.at[j], x2.at[j, :, right], p_send.at[j, 4], p_recv.at[j, 4], fsdp=xn),
            to(sy.at[j], y2.at[j, :, left], p_send.at[j, 5], p_recv.at[j, 5], fsdp=yn),
        )

    def a_one(j):
        far, near = a_copies(j, aq, aq)
        far.wait_recv()
        near.wait()
        add_rows(a_own.at[j], a_own.at[j], a_in.at[j], 4 * shard, shard)
        for copy in plane(j)[:4]:
            copy.start()

    def a_two(j):
        copies = plane(j)
        copies[0].wait_recv()
        add_rows(sy.at[j], a_own.at[j, blk(yn), left], x1.at[j], shard, shard)
        copies[5].start()
        copies[1].wait_recv()
        add_rows(sx.at[j], a_own.at[j, blk(xn), right], y1.at[j], shard, shard)
        copies[4].start()

    def a_three(j):
        copies = plane(j)
        for copy in copies[2:]:
            copy.wait_recv()
        a_t[j] = (
            a_own[j, blk(f), :].astype(F32) + x2[j].astype(F32) + y2[j].astype(F32)
        ).astype(BF)
        z_first(a_z(j))

    def m_two(i):
        z_second(m_z(i), m_own.at[i], m_za.at[i])

    def m_three(i):
        z_third(m_z(i), m_za.at[i], m_zb.at[i], m_fin.at[i])

    def fin_copy(i):
        if i < 4:
            k = i % 2
            return to(
                m_fin.at[i], m_out.at[i // 2, rows_of(s, k)], fin_s.at[i], fin_r.at[i], section=1 - s
            )
        return to(
            a_fin.at[i - 4], a_out.at[s, i - 4], fin_s.at[i], fin_r.at[i], section=1 - s
        )

    def m_four(i):
        z_last(m_z(i))
        fin_copy(i).start()
        m_out[i // 2, rows_of(s, i % 2), :] = m_fin[i]

    def a_four(j):
        z_last(a_z(j))
        fin_copy(4 + j).start()
        a_out[s, j] = a_fin[j]

    m_one(0)
    a_one(0)
    m_one(1)
    a_one(1)
    m_one(2)
    m_one(3)
    m_two(0)
    a_two(0)
    m_two(1)
    m_three(0)
    a_two(1)
    a_three(0)
    m_two(2)
    m_three(1)
    m_four(0)
    a_three(1)
    m_two(3)
    m_three(2)
    m_four(1)
    z_second(a_z(0), a_t.at[0], a_za.at[0])
    m_three(3)
    m_four(2)
    z_second(a_z(1), a_t.at[1], a_za.at[1])
    z_third(a_z(0), a_za.at[0], a_zb.at[0], a_fin.at[0])
    m_four(3)
    z_third(a_z(1), a_za.at[1], a_zb.at[1], a_fin.at[1])
    a_four(0)
    a_four(1)

    for i in range(6):
        fin_copy(i).wait()
    for i in range(4):
        m_copies(i)[0].wait_send()
    for j in range(2):
        a_copies(j, aq, aq)[0].wait_send()
        for copy in plane(j):
            copy.wait_send()
    for copies in [m_z(i) for i in range(4)] + [a_z(j) for j in range(2)]:

        @pl.when(inner)
        def _(copies=copies):
            copies[1].wait_send()
            copies[2].wait_send()

        @pl.when(jnp.logical_not(inner))
        def _(copies=copies):
            copies[0].wait_send()


def reduce_layer(pieces, down, up):
    shard = D // 4
    cut = 640
    dma = pltpu.SemaphoreType.DMA
    any_spec = pl.BlockSpec(memory_space=pl.ANY)

    def buf(*shape):
        return pltpu.VMEM(shape, BF)

    return pl.pallas_call(
        reduce_kernel,
        out_shape=(
            jax.ShapeDtypeStruct((2, 2, shard, WIDE), BF),
            jax.ShapeDtypeStruct((2, D, D), BF),
        ),
        in_specs=[any_spec] * 6,
        out_specs=(VSPEC, VSPEC),
        scratch_shapes=[
            buf(2, D, WIDE), buf(2, D, WIDE),
            buf(2, shard, cut), buf(2, shard, WIDE - cut),
            buf(2, shard, WIDE), buf(2, shard, WIDE),
            buf(2, shard, WIDE - cut), buf(2, shard, cut),
            buf(2, shard, WIDE), buf(2, shard, WIDE), buf(2, shard, WIDE), buf(2, shard, WIDE),
            buf(4, shard, D), buf(4, shard, D), buf(4, shard, D), buf(4, shard, D), buf(4, shard, D),
            dma((6,)), dma((6,)), dma((6,)), dma((2, 6)), dma((2, 6)),
            dma((18,)), dma((18,)), dma((6,)), dma((6,)),
        ],
        compiler_params=pltpu.CompilerParams(
            collective_id=3, has_side_effects=True, vmem_limit_bytes=60 * 1024 * 1024
        ),
        name="reduce_layer",
    )(*pieces, down, up)


def reduce_plain(pieces, down, up):
    s = lax.axis_index("section")
    half = down.shape[0] // 2
    both = jnp.stack([down, up]).reshape(2, 2, half, D)
    keep = lax.dynamic_index_in_dim(both, s, 1, keepdims=False)
    give = lax.dynamic_index_in_dim(both, 1 - s, 1, keepdims=False)
    m = (keep.astype(F32) + on_chip(give).astype(F32)).astype(BF)
    m = lax.psum(m, "ctx")
    pair = ("fsdp", "section")
    a = [lax.psum_scatter(p, pair, scatter_dimension=0, tiled=True) for p in pieces]
    a, m = lax.optimization_barrier((a, m))
    a = lax.psum(jnp.stack(a), "ctx")
    a_far, m_far = on_chip(a), on_chip(m)
    a = jnp.concatenate([pick(s, a, a_far), pick(s, a_far, a)], axis=1)
    m = jnp.concatenate([pick(s, m, m_far), pick(s, m_far, m)], axis=1)
    return a.reshape(2, 2, a.shape[1], WIDE), m


VSPEC = pl.BlockSpec(memory_space=pltpu.VMEM)


def plane_gather(value):
    if lax.axis_size("fsdp") != 4:
        return lax.all_gather(value, "fsdp", axis=0, tiled=True)
    rows, width = value.shape
    out = pl.pallas_call(
        gather_kernel,
        out_shape=jax.ShapeDtypeStruct((4, rows, width), value.dtype),
        in_specs=[VSPEC],
        out_specs=VSPEC,
        scratch_shapes=[pltpu.SemaphoreType.DMA((4,)), pltpu.SemaphoreType.DMA((4,))],
        compiler_params=pltpu.CompilerParams(collective_id=1, has_side_effects=True),
        name="plane_gather",
    )(value)
    return out.reshape(4 * rows, width)


def plane_scatter(value, rows):
    if lax.axis_size("fsdp") != 4:
        return lax.psum_scatter(value, "fsdp", scatter_dimension=0, tiled=True).astype(F32)
    width = value.shape[-1]
    half = rows // 2
    return pl.pallas_call(
        scatter_kernel,
        out_shape=jax.ShapeDtypeStruct((rows, width), F32),
        in_specs=[VSPEC],
        out_specs=VSPEC,
        scratch_shapes=[
            pltpu.VMEM((half, width), BF),
            pltpu.VMEM((half, width), BF),
            pltpu.VMEM((rows, width), BF),
            pltpu.VMEM((rows, width), BF),
            pltpu.VMEM((half, width), BF),
            pltpu.VMEM((half, width), BF),
            pltpu.SemaphoreType.DMA((6,)),
            pltpu.SemaphoreType.DMA((6,)),
        ],
        compiler_params=pltpu.CompilerParams(collective_id=2, has_side_effects=True),
        name="plane_scatter",
    )(value.reshape(4, rows, width))


def shift(value, steps):
    count = lax.axis_size("ctx")
    pairs = [(i, i + steps) for i in range(count) if 0 <= i + steps < count]
    return lax.ppermute(value, "ctx", pairs)


def with_halo(own, chunks):
    parts = [own]
    for _ in range(chunks):
        parts.append(shift(parts[-1], 1))
    return jnp.concatenate(parts[::-1], axis=0)


def return_halo(halo, chunks, rows):
    carried = None
    for far in range(chunks):
        mine = halo[far * rows : (far + 1) * rows]
        carried = mine if carried is None else mine + carried
        carried = shift(carried.astype(BF), -1).astype(F32)
    return carried


def pick(s, first, second):
    return jnp.where(s == 0, first, second)


def on_chip(value):
    return lax.ppermute(value, "section", SWAP)


def both_layers(own, s):
    other = on_chip(own)
    return pick(s, own, other), pick(s, other, own)


def half_rows(own, s):
    half = own.shape[0] // 2
    halves = own.reshape(2, half, own.shape[1])
    keep = lax.dynamic_index_in_dim(halves, s, 0, keepdims=False)
    give = lax.dynamic_index_in_dim(halves, 1 - s, 0, keepdims=False)
    recv = on_chip(give)
    return pick(s, keep, recv), pick(s, recv, keep)


def widen(values):
    return jnp.pad(values, ((0, 0), (0, WIDE - D)))


def heads(values):
    return values.reshape(values.shape[0], HEADS, HD)


def attention(q, k, v, allowed):
    scores = jnp.einsum("qhd,khd->hqk", heads(q), heads(k), preferred_element_type=F32) * SCALE
    total = jnp.sum(jnp.where(allowed, jnp.exp(scores), 0.0), axis=-1, keepdims=True)
    logs = jnp.log(total)
    prob = jnp.where(allowed, jnp.exp(scores - logs), 0.0).astype(BF)
    out = jnp.einsum("hqk,khd->qhd", prob, heads(v), preferred_element_type=F32)
    return out.reshape(q.shape[0], D).astype(BF), logs


def attention_back(q, k, v, logs, d_out, allowed):
    qh, kh, vh, gh = heads(q), heads(k), heads(v), heads(d_out)
    scores = jnp.einsum("qhd,khd->hqk", qh, kh, preferred_element_type=F32) * SCALE
    prob = jnp.where(allowed, jnp.exp(scores - logs), 0.0)
    d_prob = jnp.einsum("qhd,khd->hqk", gh, vh, preferred_element_type=F32)
    row = jnp.sum(prob * d_prob, axis=-1, keepdims=True)
    d_score = (prob * (d_prob - row)).astype(BF)
    dq = jnp.einsum("hqk,khd->qhd", d_score, kh, preferred_element_type=F32) * SCALE
    dk = jnp.einsum("hqk,qhd->khd", d_score, qh, preferred_element_type=F32) * SCALE
    dv = jnp.einsum("hqk,qhd->khd", prob.astype(BF), gh, preferred_element_type=F32)
    return (
        dq.reshape(q.shape[0], D).astype(BF),
        dk.reshape(k.shape[0], D).astype(BF),
        dv.reshape(k.shape[0], D).astype(BF),
    )


def on_device(
    inputs, segments, cotangent, qkv_weight, out_weight, up_weight, down_weight,
    norm_gains, biases, ff_bias,
):
    rows = inputs.shape[2]
    length = segments.shape[2]
    chunks = min((length // 2 - 1 + rows - 1) // rows, lax.axis_size("ctx") - 1)
    reach = chunks * rows
    s = lax.axis_index("section")
    f = lax.axis_index("fsdp")
    nf = lax.axis_size("fsdp")
    shard = D // nf
    ff_here = ff_bias.shape[1]
    per_row = ff_here // shard
    pair = ("fsdp", "section")

    own_in = lax.dynamic_index_in_dim(inputs, s, 0, keepdims=False)[0]
    own_cot = lax.dynamic_index_in_dim(cotangent, s, 0, keepdims=False)[0]
    seg = lax.dynamic_index_in_dim(segments, s, 0, keepdims=False)[0]
    start = lax.axis_index("ctx") * rows
    key_seg = lax.dynamic_slice_in_dim(
        jnp.pad(seg, (reach, 0), constant_values=-1), start, reach + rows, 0
    )
    allowed = (key_seg[reach:, None] == key_seg[None, :]) & (
        jnp.arange(reach + rows, dtype=jnp.int32)[None, :] - reach
        <= jnp.arange(rows, dtype=jnp.int32)[:, None]
    )

    small = jnp.concatenate(
        [norm_gains[0].T, biases[0].T, ff_bias[0].reshape(shard, per_row)], axis=1
    )
    qkv_own = jnp.concatenate(
        [qkv_weight[0], small, jnp.zeros((shard, EXT - 3 * D - 8 - per_row), BF)], axis=1
    )
    qkv_halves = half_rows(qkv_own, s)
    out_halves = half_rows(out_weight[0], s)
    up_own = lax.all_to_all(
        up_weight[0].reshape(shard, nf, ff_here), "fsdp", split_axis=1, concat_axis=0, tiled=True
    ).reshape(D, ff_here)
    up_w = both_layers(up_own, s)
    down_w = both_layers(down_weight[0], s)

    qkv_w, out_w, gains, shifts, ffb = [], [], [], [], []
    for layer in range(2):
        full = lax.all_gather(qkv_halves[layer], pair, axis=0, tiled=True)
        qkv_w.append(full)
        out_w.append(lax.all_gather(out_halves[layer], pair, axis=0, tiled=True))
        vectors = full[:, 3 * D : 3 * D + 8].T.astype(F32)
        gains.append(vectors[:2])
        shifts.append(vectors[2:])
        hidden = full[:, 3 * D + 8 : 3 * D + 8 + per_row].reshape(-1).astype(F32)
        ffb.append(lax.dynamic_slice_in_dim(hidden, f * ff_here, ff_here, 0))

    kept = []
    current = own_in
    produced = []
    for layer in range(2):
        gain, shift_rows = gains[layer], shifts[layer]
        wide = with_halo(current, chunks).astype(F32)
        n1, inv1 = norm_parts(wide)
        normed = (n1 * gain[0] + shift_rows[0]).astype(BF)
        q = (mm(normed[reach:], qkv_w[layer][:, :D]) + shift_rows[1]).astype(BF)
        k = mm(normed, qkv_w[layer][:, D : 2 * D]).astype(BF)
        v = (mm(normed, qkv_w[layer][:, 2 * D : 3 * D]) + shift_rows[2]).astype(BF)
        att, logs = attention(q, k, v, allowed)
        resid = current.astype(F32) + mm(att, out_w[layer]) + shift_rows[3]
        n2, inv2 = norm_parts(resid)
        second = (n2 * gain[1] + shift_rows[4]).astype(BF)
        second_all = plane_gather(second)
        z = mm(second_all, up_w[layer]) + ffb[layer]
        cdf, _ = phi_parts(z)
        active = (z * cdf).astype(BF)
        partial = mm(active, down_w[layer]).astype(BF)
        out = resid + plane_scatter(partial, rows) + shift_rows[5]
        low = out.astype(BF)
        produced.append(low)
        kept.append((wide, normed, q, k, v, att, logs, resid, second_all, z, active))
        current = low

    upstream = own_cot.astype(F32)
    derived = [None, None]
    totals = [None, None]
    for layer in (1, 0):
        wide, normed, q, k, v, att, logs, resid, second_all, z, active = kept[layer]
        gain = gains[layer]
        up_b = upstream.astype(BF)
        up_all = plane_gather(up_b)
        cdf, pdf = phi_parts(z)
        dz = mm_nt(up_all, down_w[layer]) * (cdf + z * pdf)
        dz_b = dz.astype(BF)
        d_second = plane_scatter(mm_nt(dz_b, up_w[layer]).astype(BF), rows)
        down_g = mm_tn(active, up_all)
        up_g = mm_tn(second_all, dz_b)
        ffb_g = jnp.sum(dz, axis=0)
        n2, inv2 = norm_parts(resid)
        d_resid = upstream + norm_back(d_second, gain[1], n2, inv2)
        c = d_resid.astype(BF)
        d_att = mm_nt(c, out_w[layer]).astype(BF)
        dq, dk, dv = attention_back(q, k, v, logs, d_att, allowed)
        w = qkv_w[layer]
        da_wide = mm_nt(dk, w[:, D : 2 * D]) + mm_nt(dv, w[:, 2 * D : 3 * D])
        da_own = da_wide[reach:] + mm_nt(dq, w[:, :D])
        da_halo = da_wide[:reach]
        n1, inv1 = norm_parts(wide)
        da = da_own + return_halo(da_halo, chunks, rows)
        d_in = d_resid + norm_back(da, gain[0], n1[reach:], inv1[reach:])
        derived[layer] = d_in
        upstream_next = d_in.astype(BF).astype(F32)
        vectors = jnp.stack(
            [
                jnp.sum(da_halo * n1[:reach], axis=0) + jnp.sum(da_own * n1[reach:], axis=0),
                jnp.sum(d_second * n2, axis=0),
                jnp.sum(da_halo, axis=0) + jnp.sum(da_own, axis=0),
                jnp.sum(dq.astype(F32), axis=0),
                jnp.sum(dv.astype(F32), axis=0),
                jnp.sum(d_resid, axis=0),
                jnp.sum(d_second, axis=0),
                jnp.sum(upstream, axis=0),
            ]
        )
        ffb_block = lax.dynamic_update_slice(
            jnp.zeros((D, per_row), F32), ffb_g.reshape(shard, per_row), (f * shard, 0)
        )
        extra = jnp.pad(
            jnp.concatenate([vectors.T, ffb_block], axis=1),
            ((0, 0), (D, WIDE - D - 8 - per_row)),
        )
        pieces = (
            mm_tn(normed[reach:], widen(dq)).astype(BF),
            mm_tn(normed, widen(dk)).astype(BF),
            mm_tn(normed, widen(dv)).astype(BF),
            (mm_tn(att, widen(c)) + extra).astype(BF),
        )
        up_g = lax.all_to_all(
            up_g.astype(BF).reshape(nf, shard, ff_here), "fsdp",
            split_axis=0, concat_axis=0, tiled=True,
        ).reshape(nf * shard, ff_here)
        if nf != 4 or lax.axis_size("ctx") != 4 or layer == 1:
            if ff_here != D:
                up_g = up_g.reshape(ff_here, D)
            totals[layer] = reduce_plain(pieces, down_g.astype(BF), up_g)
        else:
            totals[layer] = reduce_layer(pieces, down_g.astype(BF), up_g)
        upstream = upstream_next

    a_tot = pick(s, totals[0][0], totals[1][0]).astype(F32)
    m_tot = pick(s, totals[0][1], totals[1][1]).astype(F32)
    a_tot = a_tot.reshape(4, shard, WIDE)
    grad_up = m_tot[1].reshape(nf, shard, ff_here).transpose(1, 0, 2).reshape(shard, nf * ff_here)
    vectors = a_tot[3, :, D : D + 8].T
    return (
        gather_micro(jnp.stack(produced), s),
        gather_micro(jnp.stack(derived), s),
        jnp.concatenate([a_tot[i, :, :D] for i in range(3)], axis=1)[None],
        a_tot[3, None, :, :D],
        grad_up[None],
        m_tot[0][None],
        vectors[None, :2],
        vectors[None, 2:],
        a_tot[3, :, D + 8 : D + 8 + per_row].reshape(1, ff_here),
    )


def gather_micro(layers, s):
    mine = lax.dynamic_index_in_dim(layers, s, 0, keepdims=False)
    other = on_chip(lax.dynamic_index_in_dim(layers, 1 - s, 0, keepdims=False))
    return jnp.stack([pick(s, mine, other), pick(s, other, mine)])[None, :, None]


def solution(mesh):
    return jax.shard_map(
        on_device,
        mesh=mesh,
        in_specs=(
            P(None, "fsdp", "ctx", None),
            P(None, "fsdp", None),
            P(None, "fsdp", "ctx", None),
            P("section", "fsdp", None),
            P("section", "fsdp", None),
            P("section", "fsdp", None),
            P("section", "fsdp", None),
            P("section", None, "fsdp"),
            P("section", None, "fsdp"),
            P("section", "fsdp"),
        ),
        out_specs=(
            P("section", None, "fsdp", "ctx", None),
            P("section", None, "fsdp", "ctx", None),
            P("section", "fsdp", None),
            P("section", "fsdp", None),
            P("section", "fsdp", None),
            P("section", "fsdp", None),
            P("section", None, "fsdp"),
            P("section", None, "fsdp"),
            P("section", "fsdp"),
        ),
        check_vma=False,
    )
```

```python
import functools
import math

import jax
import jax.numpy as jnp
from jax import lax
from jax.experimental import pallas as pl
from jax.experimental.pallas import tpu as pltpu
from jax.sharding import PartitionSpec as P

D = 1088
HD = 64
F32 = jnp.float32
BF = jnp.bfloat16
SCALE = 1.0 / math.sqrt(HD)
WIDE = 1152
MESH = pl.DeviceIdType.MESH
SWAP = [(0, 1), (1, 0)]


def mm(a, b):
    return jnp.dot(a, b, preferred_element_type=F32)


def mm_nt(a, b):
    return lax.dot_general(a, b, (((1,), (1,)), ((), ())), preferred_element_type=F32)


def mm_tn(a, b):
    return lax.dot_general(a, b, (((0,), (0,)), ((), ())), preferred_element_type=F32)


def norm_parts(values):
    center = jnp.mean(values, axis=-1, keepdims=True)
    offset = values - center
    spread = jnp.mean(offset * offset, axis=-1, keepdims=True)
    inv = lax.rsqrt(spread + 1e-05)
    return offset * inv, inv


def norm_back(grad, gain, unit, inv):
    dn = grad * gain
    return inv * (
        dn
        - jnp.mean(dn, axis=-1, keepdims=True)
        - unit * jnp.mean(dn * unit, axis=-1, keepdims=True)
    )


def phi_parts(z):
    cdf = 0.5 * (1.0 + lax.erf(z * (1.0 / math.sqrt(2.0))))
    pdf = jnp.exp(-0.5 * z * z) * (1.0 / math.sqrt(2.0 * math.pi))
    return cdf, pdf


def plane_neighbours():
    f = lax.axis_index("fsdp")
    x = lax.rem(f, 2)
    y = f // 2
    return y * 2 + (1 - x), (1 - y) * 2 + x


def plane_barrier(xn, yn):
    barrier = pltpu.get_barrier_semaphore()
    for nb in (xn, yn):
        pl.semaphore_signal(barrier, inc=1, device_id={"fsdp": nb}, device_id_type=MESH)
    pl.semaphore_wait(barrier, 2)


def remote(src, dst, send, recv, nb):
    return pltpu.make_async_remote_copy(
        src_ref=src, dst_ref=dst, send_sem=send, recv_sem=recv,
        device_id={"fsdp": nb}, device_id_type=MESH,
    )


def exchange_rows(own_ref, all_ref, parts, compute, total_ref, bufs, send, recv):
    x1, y1, x2, y2, sum_x, sum_y = bufs
    xn, yn = plane_neighbours()
    half = own_ref.shape[0] // 2
    top, low = pl.ds(0, half), pl.ds(half, half)
    plane_barrier(xn, yn)

    to_x = remote(own_ref, all_ref.at[1], send.at[0], recv.at[0], xn)
    to_y = remote(own_ref, all_ref.at[2], send.at[1], recv.at[1], yn)
    far_x = remote(all_ref.at[2, top], all_ref.at[3, top], send.at[2], recv.at[2], xn)
    far_y = remote(all_ref.at[1, low], all_ref.at[3, low], send.at[3], recv.at[3], yn)
    first_x = remote(parts.at[3, top], x1, send.at[4], recv.at[4], xn)
    first_y = remote(parts.at[3, low], y1, send.at[5], recv.at[5], yn)
    own_x = remote(parts.at[1, top], x2.at[top], send.at[6], recv.at[6], xn)
    own_y = remote(parts.at[2, low], y2.at[low], send.at[7], recv.at[7], yn)
    rest_x = remote(sum_x, x2.at[low], send.at[8], recv.at[8], xn)
    rest_y = remote(sum_y, y2.at[top], send.at[9], recv.at[9], yn)

    to_x.start()
    to_y.start()
    all_ref[0] = own_ref[...]
    compute(0)
    to_x.wait_recv()
    far_y.start()
    to_y.wait_recv()
    far_x.start()
    compute(1)
    own_x.start()
    far_x.wait_recv()
    far_y.wait_recv()
    compute(3)
    first_x.start()
    first_y.start()
    compute(2)
    own_y.start()
    first_x.wait_recv()
    sum_y[...] = (parts[2, top, :].astype(F32) + x1[...].astype(F32)).astype(BF)
    rest_y.start()
    first_y.wait_recv()
    sum_x[...] = (parts[1, low, :].astype(F32) + y1[...].astype(F32)).astype(BF)
    rest_x.start()
    own_x.wait_recv()
    rest_y.wait_recv()
    total_ref[top, :] = (
        parts[0, top, :].astype(F32) + x2[top, :].astype(F32) + y2[top, :].astype(F32)
    )
    own_y.wait_recv()
    rest_x.wait_recv()
    total_ref[low, :] = (
        parts[0, low, :].astype(F32) + x2[low, :].astype(F32) + y2[low, :].astype(F32)
    )
    for copy in (to_x, to_y, far_x, far_y, first_x, first_y, own_x, own_y, rest_x, rest_y):
        copy.wait_send()


def forward_kernel(
    own, up, down, bias, total, all_ref, active, slope, parts, x1, y1, x2, y2, sx, sy, send, recv
):
    def compute(r):
        z = mm(all_ref[r], up[...]) + bias[...]
        cdf, pdf = phi_parts(z)
        active[r] = (z * cdf).astype(BF)
        slope[r] = cdf + z * pdf
        parts[r] = mm(active[r], down[...]).astype(BF)

    exchange_rows(own, all_ref, parts, compute, total, (x1, y1, x2, y2, sx, sy), send, recv)


def backward_kernel(
    own, up, down, slope, total, all_ref, dz_all, bias_g, parts, x1, y1, x2, y2, sx, sy, send, recv
):
    bias_g[...] = jnp.zeros_like(bias_g)

    def compute(r):
        dz = mm_nt(all_ref[r], down[...]) * slope[r]
        bias_g[...] += jnp.sum(dz, axis=0, keepdims=True)
        dz_all[r] = dz.astype(BF)
        parts[r] = mm_nt(dz_all[r], up[...]).astype(BF)

    exchange_rows(own, all_ref, parts, compute, total, (x1, y1, x2, y2, sx, sy), send, recv)


VSPEC = pl.BlockSpec(memory_space=pltpu.VMEM)


def lasting(micros):
    return pl.CostEstimate(flops=0, transcendentals=0, bytes_accessed=int(micros * 3.5e6))


def plane_call(kernel, ident, outs, rows, *operands):
    half = rows // 2
    return pl.pallas_call(
        kernel,
        out_shape=outs,
        in_specs=[VSPEC] * len(operands),
        out_specs=(VSPEC,) * len(outs),
        scratch_shapes=[
            pltpu.VMEM((4, rows, D), BF),
            pltpu.VMEM((half, D), BF),
            pltpu.VMEM((half, D), BF),
            pltpu.VMEM((rows, D), BF),
            pltpu.VMEM((rows, D), BF),
            pltpu.VMEM((half, D), BF),
            pltpu.VMEM((half, D), BF),
            pltpu.SemaphoreType.DMA((10,)),
            pltpu.SemaphoreType.DMA((10,)),
        ],
        compiler_params=pltpu.CompilerParams(
            collective_id=ident, has_side_effects=True, vmem_limit_bytes=40 * 1024 * 1024
        ),
        cost_estimate=lasting(40),
    )(*operands)


def mlp_forward(own, up, down, bias):
    rows = own.shape[0]
    if lax.axis_size("fsdp") != 4:
        every = lax.all_gather(own, "fsdp", axis=0, tiled=True)
        z = mm(every, up) + bias
        cdf, pdf = phi_parts(z)
        active = (z * cdf).astype(BF)
        part = mm(active, down).astype(BF)
        total = lax.psum_scatter(part, "fsdp", scatter_dimension=0, tiled=True).astype(F32)
        return total, every, active, cdf + z * pdf
    shape = (4, rows, D)
    return plane_call(
        forward_kernel, 1,
        (
            jax.ShapeDtypeStruct((rows, D), F32),
            jax.ShapeDtypeStruct(shape, BF),
            jax.ShapeDtypeStruct(shape, BF),
            jax.ShapeDtypeStruct(shape, F32),
        ),
        rows, own, up, down, bias,
    )


def mlp_backward(own, up, down, slope):
    rows = own.shape[0]
    if lax.axis_size("fsdp") != 4:
        every = lax.all_gather(own, "fsdp", axis=0, tiled=True)
        dz = mm_nt(every, down) * slope
        dz_b = dz.astype(BF)
        part = mm_nt(dz_b, up).astype(BF)
        total = lax.psum_scatter(part, "fsdp", scatter_dimension=0, tiled=True).astype(F32)
        return total, every, dz_b, jnp.sum(dz, axis=0, keepdims=True)
    shape = (4, rows, D)
    return plane_call(
        backward_kernel, 2,
        (
            jax.ShapeDtypeStruct((rows, D), F32),
            jax.ShapeDtypeStruct(shape, BF),
            jax.ShapeDtypeStruct(shape, BF),
            jax.ShapeDtypeStruct((1, D), F32),
        ),
        rows, own, up, down, slope,
    )


def weights_kernel(
    own, rows_in, full, rows_out, load, core_s, core_r, p_send, p_recv, f_send, f_recv, z_send, z_recv
):
    s = lax.axis_index("section")
    f = lax.axis_index("fsdp")
    xn, yn = plane_neighbours()
    dn = 3 - f
    shard, wide = own.shape[1], own.shape[2]
    cut = 640
    left = pl.ds(0, cut)
    right = pl.ds(cut, wide - cut)

    def to(src, dst, send, recv, **where):
        return pltpu.make_async_remote_copy(
            src_ref=src, dst_ref=dst, send_sem=send, recv_sem=recv,
            device_id=where, device_id_type=MESH,
        )

    barrier = pltpu.get_barrier_semaphore()
    z = lax.axis_index("ctx")
    above = {"ctx": lax.rem(z + 1, 4)}
    below = {"ctx": lax.rem(z + 3, 4)}
    for where in ({"section": 1 - s}, {"fsdp": xn}, {"fsdp": yn}, above, below):
        pl.semaphore_signal(barrier, inc=1, device_id=where, device_id_type=MESH)
    pl.semaphore_wait(barrier, 5)
    rows = rows_in.shape[0]
    near_rows, far_rows = pl.ds(rows, rows), pl.ds(0, rows)
    step_one = to(rows_in, rows_out.at[near_rows], z_send.at[0], z_recv.at[0], **above)
    step_two = to(
        rows_out.at[near_rows], rows_out.at[far_rows], z_send.at[1], z_recv.at[1], **above
    )

    @pl.when(z < 3)
    def _():
        step_one.start()

    rows_out[pl.ds(2 * rows, rows), :] = rows_in[...]

    @pl.when(z == 0)
    def _():
        rows_out[near_rows, :] = jnp.zeros(rows_in.shape, BF)

    @pl.when(z < 2)
    def _():
        rows_out[far_rows, :] = jnp.zeros(rows_in.shape, BF)

    def blk(owner):
        return pl.ds(pl.multiple_of(owner * shard, 16), shard)

    def give(p):
        return to(own.at[p], full.at[p, blk(f)], core_s.at[p], core_r.at[p], section=1)

    def keep(p):
        return pltpu.make_async_copy(own.at[p], full.at[p, blk(f)], load.at[p])

    @pl.when(s == 0)
    def _():
        for p in (2, 3, 0, 1):
            give(p).start()
        for p in range(4):
            keep(p).start()
        keep(0).wait()
        keep(1).wait()

    @pl.when(s == 1)
    def _():
        give(2).wait_recv()
        give(3).wait_recv()

    def same(piece, rows, send, recv, cols=slice(None), **where):
        ref = full.at[piece, rows, cols]
        return to(ref, ref, send, recv, **where)

    def hops(k):
        p = 2 * s + k
        return (
            same(p, blk(f), p_send.at[k, 0], p_recv.at[k, 0], fsdp=xn),
            same(p, blk(f), p_send.at[k, 1], p_recv.at[k, 1], fsdp=yn),
            same(p, blk(yn), p_send.at[k, 2], p_recv.at[k, 2], left, fsdp=xn),
            same(p, blk(xn), p_send.at[k, 3], p_recv.at[k, 3], right, fsdp=yn),
        )

    def here(k):
        p = 2 * s + k
        return [
            same(p, blk(owner), f_send.at[k, i], f_recv.at[k, i], section=1 - s)
            for i, owner in enumerate((xn, yn, dn))
        ]

    for k in range(2):
        copies = hops(k)
        copies[0].start()
        copies[1].start()
    for k in range(2):
        copies, across = hops(k), here(k)
        copies[0].wait_recv()
        copies[3].start()
        across[0].start()
        copies[1].wait_recv()
        copies[2].start()
        across[1].start()

    @pl.when(z > 0)
    def _():
        step_one.wait_recv()

    @pl.when((z == 1) | (z == 2))
    def _():
        step_two.start()

    for k in range(2):
        copies, across = hops(k), here(k)
        copies[2].wait_recv()
        copies[3].wait_recv()
        across[2].start()
    for k in range(2):
        for copy in here(k):
            copy.wait()
        for copy in hops(k):
            copy.wait_send()

    @pl.when(s == 0)
    def _():
        for p in range(4):
            give(p).wait_send()
        keep(2).wait()
        keep(3).wait()

    @pl.when(s == 1)
    def _():
        give(0).wait_recv()
        give(1).wait_recv()

    @pl.when(z < 3)
    def _():
        step_one.wait_send()

    @pl.when((z == 1) | (z == 2))
    def _():
        step_two.wait_send()

    @pl.when(z > 1)
    def _():
        step_two.wait_recv()


def first_weights(own, rows_in):
    dma = pltpu.SemaphoreType.DMA
    return pl.pallas_call(
        weights_kernel,
        out_shape=(
            jax.ShapeDtypeStruct((4, D, WIDE), BF),
            jax.ShapeDtypeStruct((3 * rows_in.shape[0], D), BF),
        ),
        in_specs=[pl.BlockSpec(memory_space=pl.ANY), VSPEC],
        out_specs=(VSPEC, VSPEC),
        scratch_shapes=[
            dma((4,)), dma((4,)), dma((4,)), dma((2, 4)), dma((2, 4)), dma((2, 3)), dma((2, 3)),
            dma((2,)), dma((2,)),
        ],
        compiler_params=pltpu.CompilerParams(
            collective_id=4, has_side_effects=True, vmem_limit_bytes=16 * 1024 * 1024
        ),
        cost_estimate=lasting(50),
        name="first_weights",
    )(own, rows_in)


def z_partners():
    z = lax.axis_index("ctx")
    return z + 1 - 2 * lax.rem(z, 2), 3 - z, (z == 1) | (z == 2)


def add_rows(dst, one, two, rows, step):
    @pl.loop(0, rows // step)
    def _(i):
        at = pl.ds(pl.multiple_of(i * step, 16), step)
        dst[at, :] = (one[at, :].astype(F32) + two[at, :].astype(F32)).astype(dst.dtype)


CUTS = ((0, 640, 384), (640, 512, 256))


def reduce_kernel(
    q0, k0, v0, o0, q1, k1, v1, o1, mlp, halo,
    qkv_out, out_out, down_out, up_out, rows_out,
    own_in, held, up_own, up_far, sent, caught,
    x1a, y1a, x2a, y2a, sxa, sya, ta, zaa, zba,
    x1b, y1b, x2b, y2b, sxb, syb, tb, zab, zbb,
    load, core_s, core_r, p_send, p_recv, z_send, z_recv, h_send, h_recv,
):
    s = lax.axis_index("section")
    f = lax.axis_index("fsdp")
    xn, yn = plane_neighbours()
    dn = 3 - f
    side, across, inner = z_partners()
    pieces = ((q0, k0, v0, o0), (q1, k1, v1, o1))
    sets = (
        (x1a, y1a, x2a, y2a, sxa, sya, ta, zaa, zba),
        (x1b, y1b, x2b, y2b, sxb, syb, tb, zab, zbb),
    )
    shard = out_out.shape[0]
    rows = rows_out.shape[0]
    z = lax.axis_index("ctx")
    above, below = {"ctx": lax.rem(z + 1, 4)}, {"ctx": lax.rem(z + 3, 4)}

    def to(src, dst, send, recv, **where):
        return pltpu.make_async_remote_copy(
            src_ref=src, dst_ref=dst, send_sem=send, recv_sem=recv,
            device_id=where, device_id_type=MESH,
        )

    barrier = pltpu.get_barrier_semaphore()
    partners = ({"section": 1 - s}, {"fsdp": xn}, {"fsdp": yn}, above, below)
    for where in partners:
        pl.semaphore_signal(barrier, inc=1, device_id=where, device_id_type=MESH)
    pl.semaphore_wait(barrier, 5)

    def blk(owner):
        return pl.ds(pl.multiple_of(owner * shard, 16), shard)

    def by_core(act):
        for core in range(2):
            pl.when(s == core)(functools.partial(act, core))

    def far(j, src):
        return to(src, held.at[j], core_s.at[j], core_r.at[j], section=1 - s)

    def near(j, src):
        return pltpu.make_async_copy(src, own_in.at[j % 2], load.at[j])

    def bufs(c):
        return tuple(ref.at[c // 2] for ref in sets[c % 2])

    def plane(c):
        x1, y1, x2, y2, sx, sy = bufs(c)[:6]
        own = held.at[c // 2]
        at, width, cut = CUTS[c % 2]
        left, right = pl.ds(at, cut), pl.ds(at + cut, width - cut)
        to_left, to_right = pl.ds(0, cut), pl.ds(cut, width - cut)
        sems = [(p_send.at[c, i], p_recv.at[c, i]) for i in range(6)]
        return (
            to(own.at[blk(dn), left], x1, *sems[0], fsdp=xn),
            to(own.at[blk(dn), right], y1, *sems[1], fsdp=yn),
            to(own.at[blk(xn), left], x2.at[:, to_left], *sems[2], fsdp=xn),
            to(own.at[blk(yn), right], y2.at[:, to_right], *sems[3], fsdp=yn),
            to(sx, x2.at[:, to_right], *sems[4], fsdp=xn),
            to(sy, y2.at[:, to_left], *sems[5], fsdp=yn),
        )

    def along(c):
        t, za, zb = bufs(c)[6:]
        sems = [(z_send.at[c, i], z_recv.at[c, i]) for i in range(3)]
        return (
            to(t, za, *sems[0], ctx=side),
            to(za, zb, *sems[1], ctx=across),
            to(zb, zb, *sems[2], ctx=side),
        )

    def join(j):
        far(j, q0).wait_recv()
        near(j, q0).wait()
        add_rows(held.at[j], own_in.at[j % 2], held.at[j], 4 * shard, shard)
        for c in (2 * j, 2 * j + 1):
            for copy in plane(c)[:4]:
                copy.start()
        if j < 2:
            by_core(lambda core: near(j + 2, pieces[core][j + 2]).start())

    def second(c):
        copies = plane(c)
        x1, y1, _, _, sx, sy = bufs(c)[:6]
        at, width, cut = CUTS[c % 2]
        own = held.at[c // 2]
        copies[0].wait_recv()
        add_rows(sy, own.at[blk(yn), pl.ds(at, cut)], x1, shard, shard)
        copies[5].start()
        copies[1].wait_recv()
        add_rows(sx, own.at[blk(xn), pl.ds(at + cut, width - cut)], y1, shard, shard)
        copies[4].start()

    def third(c):
        copies = plane(c)
        _, _, x2, y2, _, _, t, _, _ = bufs(c)
        at, width, _ = CUTS[c % 2]
        for copy in copies[2:]:
            copy.wait_recv()
        t[...] = (
            held[c // 2, blk(f), pl.ds(at, width)].astype(F32)
            + x2[...].astype(F32)
            + y2[...].astype(F32)
        ).astype(BF)

        @pl.when(jnp.logical_not(inner))
        def _():
            along(c)[0].start()

    def inward(c):
        @pl.when(inner)
        def _():
            t, za, _ = bufs(c)[6:]
            copies = along(c)
            copies[0].wait_recv()
            add_rows(za, t, za, shard, shard)
            copies[1].start()

    def crossed(c):
        @pl.when(inner)
        def _():
            _, za, zb = bufs(c)[6:]
            copies = along(c)
            copies[1].wait_recv()
            add_rows(zb, za, zb, shard, shard)
            copies[2].start()

    def last(c):
        at, width, _ = CUTS[c % 2]
        j = c // 2

        @pl.when(jnp.logical_not(inner))
        def _():
            along(c)[2].wait_recv()

        if j < 3:
            width = min(width, D - at)
            qkv_out[:, pl.ds(j * D + at, width)] = bufs(c)[8][:, pl.ds(0, width)]
        else:
            out_out[:, pl.ds(at, width)] = bufs(c)[8][...]

    half = down_out.shape[0] // 2
    mine = pl.ds(pl.multiple_of(s * half, 16), half)
    down_far = to(mlp.at[0], down_out.at[mine], core_s.at[4], core_r.at[4], section=1 - s)
    down_near = pltpu.make_async_copy(mlp.at[0], down_out.at[mine], load.at[4])
    far_up = to(mlp.at[1], up_far, core_s.at[5], core_r.at[5], section=1 - s)
    near_up = pltpu.make_async_copy(mlp.at[1], up_own, load.at[5])

    def lay_up():
        far_up.wait_recv()
        near_up.wait()

        @pl.when(s == 1)
        def _():
            for k in range(2):
                up_out[:, pl.ds(k * D, D)] = up_far[pl.ds(k * shard, shard), :]
                up_out[:, pl.ds((2 + k) * D, D)] = up_own[pl.ds(k * shard, shard), :]

    back_one = to(halo.at[pl.ds(0, rows)], caught.at[0], h_send.at[0], h_recv.at[0], **below)
    back_two = to(sent, caught.at[1], h_send.at[1], h_recv.at[1], **below)

    def back():
        @pl.when(z < 3)
        def _():
            back_one.wait_recv()

        @pl.when(z == 3)
        def _():
            caught[0] = jnp.zeros_like(caught[0])

        @pl.when(z > 0)
        def _():
            add_rows(sent, halo.at[pl.ds(rows, rows)], caught.at[0], rows, rows)
            back_two.start()

    def back_end():
        @pl.when(z < 3)
        def _():
            back_two.wait_recv()
            rows_out[...] = caught[1]

        @pl.when(z == 3)
        def _():
            rows_out[...] = jnp.zeros_like(rows_out)

    @pl.when(z > 0)
    def _():
        back_one.start()

    for j in range(4):
        by_core(lambda core: far(j, pieces[1 - core][j]).start())
        if j < 2:
            by_core(lambda core: near(j, pieces[core][j]).start())
    for copy in (down_far, down_near, far_up, near_up):
        copy.start()

    join(0)
    for c in range(12):
        if c in (1, 3, 5):
            join((c + 1) // 2)
        if c < 8:
            second(c)
        if 1 <= c <= 8:
            third(c - 1)
        if 2 <= c <= 9:
            inward(c - 2)
        if 3 <= c <= 10:
            crossed(c - 3)
        if c >= 4:
            last(c - 4)
        if c == 2:
            back()
        if c == 4:
            lay_up()
        if c == 6:
            back_end()

    down_near.wait()
    down_far.wait()
    far_up.wait_send()

    @pl.when(z > 0)
    def _():
        back_one.wait_send()
        back_two.wait_send()

    for j in range(4):
        far(j, q0).wait_send()
    for c in range(8):
        for copy in plane(c):
            copy.wait_send()

    @pl.when(inner)
    def _():
        for c in range(8):
            for copy in along(c)[1:]:
                copy.wait_send()

    @pl.when(jnp.logical_not(inner))
    def _():
        for c in range(8):
            along(c)[0].wait_send()


def reduce_both(zero, one, mlp, halo):
    shard = D // 4
    rows = halo.shape[0] // 2
    dma = pltpu.SemaphoreType.DMA
    any_spec = pl.BlockSpec(memory_space=pl.ANY)

    def buf(*shape):
        return pltpu.VMEM(shape, BF)

    def part(_, width, cut):
        wide = buf(4, shard, width)
        return [
            buf(4, shard, cut), buf(4, shard, width - cut), wide, wide,
            buf(4, shard, width - cut), buf(4, shard, cut), wide, wide, wide,
        ]

    return pl.pallas_call(
        reduce_kernel,
        out_shape=tuple(
            jax.ShapeDtypeStruct(shape, BF)
            for shape in ((shard, 3 * D), (shard, WIDE), (D, D), (shard, 4 * D), (rows, D))
        ),
        in_specs=[any_spec] * 9 + [VSPEC],
        out_specs=(VSPEC,) * 5,
        scratch_shapes=[
            buf(2, D, WIDE), buf(4, D, WIDE), buf(D // 2, D), buf(D // 2, D), buf(rows, D),
            buf(2, rows, D), *part(*CUTS[0]), *part(*CUTS[1]),
            dma((6,)), dma((6,)), dma((6,)), dma((8, 6)), dma((8, 6)), dma((8, 3)), dma((8, 3)),
            dma((2,)), dma((2,)),
        ],
        compiler_params=pltpu.CompilerParams(
            collective_id=3, has_side_effects=True, vmem_limit_bytes=58 * 1024 * 1024
        ),
        cost_estimate=lasting(120),
        name="reduce_both",
    )(*zero, *one, mlp, halo)


def halves_pair(down, up):
    s = lax.axis_index("section")
    both = jnp.stack([down, up])
    both = both.reshape(2, 2, both.shape[1] // 2, D)
    keep = lax.dynamic_index_in_dim(both, s, 1, keepdims=False)
    give = lax.dynamic_index_in_dim(both, 1 - s, 1, keepdims=False)
    return (keep.astype(F32) + on_chip(give).astype(F32)).astype(BF)


def halves_settle(zero, one):
    s = lax.axis_index("section")
    mine, far = pick(s, zero, one), on_chip(pick(s, one, zero))
    return jnp.concatenate([pick(s, mine, far), pick(s, far, mine)], axis=1).astype(F32)


def reduce_plain(pieces):
    s = lax.axis_index("section")
    pair = ("fsdp", "section")
    a = jnp.stack([lax.psum_scatter(p, pair, scatter_dimension=0, tiled=True) for p in pieces])
    a = lax.psum(a, "ctx")
    far = on_chip(a)
    return jnp.concatenate([pick(s, a, far), pick(s, far, a)], axis=1)


def shift(value, steps):
    count = lax.axis_size("ctx")
    pairs = [(i, i + steps) for i in range(count) if 0 <= i + steps < count]
    return lax.ppermute(value, "ctx", pairs)


def with_halo(own, chunks):
    parts = [own]
    for _ in range(chunks):
        parts.append(shift(parts[-1], 1))
    return jnp.concatenate(parts[::-1], axis=0)


def return_halo(halo, chunks, rows):
    carried = None
    for far in range(chunks):
        mine = halo[far * rows : (far + 1) * rows]
        carried = mine if carried is None else mine + carried
        carried = shift(carried.astype(BF), -1).astype(F32)
    return carried


def pick(s, first, second):
    return jnp.where(s == 0, first, second)


def on_chip(value):
    return lax.ppermute(value, "section", SWAP)


def both_layers(own, s):
    other = on_chip(own)
    return pick(s, own, other), pick(s, other, own)


def flat(values):
    return values.reshape(-1, values.shape[-1])


def widen(values):
    return jnp.pad(values, ((0, 0), (0, WIDE - D)))


def attend_kernel(q_ref, k_ref, v_ref, bias_ref, out_ref):
    lanes = lax.broadcasted_iota(jnp.int32, q_ref.shape, 1)
    q = q_ref[...] * jnp.asarray(SCALE, BF)
    outs = []
    for low in (True, False):
        mine = (lanes < HD) if low else (lanes >= HD)
        one = jnp.where(mine, q, jnp.zeros_like(q))
        weight = jnp.exp(mm_nt(one, k_ref[...]) + bias_ref[...])
        prob = weight * (1.0 / jnp.sum(weight, axis=-1, keepdims=True))
        outs.append(mm(prob.astype(BF), v_ref[...]))
    out_ref[...] = jnp.where(lanes < HD, outs[0], outs[1]).astype(BF)


def attend(q, k, v, bias):
    rows, keys = q.shape[0], k.shape[0]
    return pl.pallas_call(
        attend_kernel,
        out_shape=jax.ShapeDtypeStruct((rows, D), BF),
        grid=(WIDE // 128,),
        in_specs=[
            pl.BlockSpec((rows, 128), lambda i: (0, i)),
            pl.BlockSpec((keys, 128), lambda i: (0, i)),
            pl.BlockSpec((keys, 128), lambda i: (0, i)),
            pl.BlockSpec((rows, keys), lambda i: (0, 0)),
        ],
        out_specs=pl.BlockSpec((rows, 128), lambda i: (0, i)),
        compiler_params=pltpu.CompilerParams(vmem_limit_bytes=24 * 1024 * 1024),
        cost_estimate=lasting(12),
        name="attend",
    )(q, k, v, bias)


def attend_back_kernel(q_ref, k_ref, v_ref, g_ref, bias_ref, dq_ref, dk_ref, dv_ref):
    lanes = lax.broadcasted_iota(jnp.int32, q_ref.shape, 1)
    q = q_ref[...] * jnp.asarray(SCALE, BF)
    dqs, dk, dv = [], 0.0, 0.0
    for low in (True, False):
        mine = (lanes < HD) if low else (lanes >= HD)
        one = jnp.where(mine, q, jnp.zeros_like(q))
        grad = jnp.where(mine, g_ref[...], jnp.zeros_like(q))
        weight = jnp.exp(mm_nt(k_ref[...], one) + bias_ref[...])
        prob = weight * (1.0 / jnp.sum(weight, axis=0, keepdims=True))
        d_prob = mm_nt(v_ref[...], grad)
        row = jnp.sum(prob * d_prob, axis=0, keepdims=True)
        d_score = (prob * (d_prob - row)).astype(BF)
        dqs.append(mm_tn(d_score, k_ref[...]))
        dk = dk + mm(d_score, one)
        dv = dv + mm(prob.astype(BF), grad)
    dq_ref[...] = (jnp.where(lanes < HD, dqs[0], dqs[1]) * SCALE).astype(BF)
    dk_ref[...] = dk.astype(BF)
    dv_ref[...] = dv.astype(BF)


def attend_back(q, k, v, grad, bias):
    rows, keys = q.shape[0], k.shape[0]
    few = pl.BlockSpec((rows, 128), lambda i: (0, i))
    many = pl.BlockSpec((keys, 128), lambda i: (0, i))
    return pl.pallas_call(
        attend_back_kernel,
        out_shape=(
            jax.ShapeDtypeStruct((rows, WIDE), BF),
            jax.ShapeDtypeStruct((keys, WIDE), BF),
            jax.ShapeDtypeStruct((keys, WIDE), BF),
        ),
        grid=(WIDE // 128,),
        in_specs=[few, many, many, few, pl.BlockSpec((keys, rows), lambda i: (0, 0))],
        out_specs=(few, many, many),
        compiler_params=pltpu.CompilerParams(vmem_limit_bytes=24 * 1024 * 1024),
        cost_estimate=lasting(22),
        name="attend_back",
    )(q, k, v, grad, bias)


def on_device(
    inputs, segments, cotangent, qkv_weight, out_weight, up_weight, down_weight,
    norm_gains, biases, ff_bias,
):
    rows = inputs.shape[2]
    length = segments.shape[2]
    chunks = min((length // 2 - 1 + rows - 1) // rows, lax.axis_size("ctx") - 1)
    reach = chunks * rows
    s = lax.axis_index("section")
    f = lax.axis_index("fsdp")
    nf = lax.axis_size("fsdp")
    shard = D // nf
    ff_here = ff_bias.shape[1]
    per_row = ff_here // shard
    pair = ("fsdp", "section")
    fits = nf == 4 and lax.axis_size("ctx") == 4 and chunks == 2

    own_in = lax.dynamic_index_in_dim(inputs, s, 0, keepdims=False)[0]
    own_cot = lax.dynamic_index_in_dim(cotangent, s, 0, keepdims=False)[0]
    seg = lax.dynamic_index_in_dim(segments, s, 0, keepdims=False)[0]
    start = lax.axis_index("ctx") * rows
    key_seg = lax.dynamic_slice_in_dim(
        jnp.pad(seg, (reach, 0), constant_values=-1), start, reach + rows, 0
    )
    allowed = (key_seg[reach:, None] == key_seg[None, :]) & (
        jnp.arange(reach + rows, dtype=jnp.int32)[None, :] - reach
        <= jnp.arange(rows, dtype=jnp.int32)[:, None]
    )

    bias = jnp.where(allowed, 0.0, -1e30).astype(F32)
    bias_t = bias.T

    small = jnp.concatenate(
        [norm_gains[0].T, biases[0].T, ff_bias[0].reshape(shard, per_row)], axis=1
    )
    packed = jnp.stack(
        [
            widen(qkv_weight[0][:, :D]),
            widen(qkv_weight[0][:, D : 2 * D]),
            widen(qkv_weight[0][:, 2 * D :]),
            jnp.concatenate(
                [out_weight[0], small, jnp.zeros((shard, WIDE - D - 8 - per_row), BF)], axis=1
            ),
        ]
    )
    if fits:
        zero, wide_in = first_weights(packed, own_in)
        packed, up_shard, down_shard, zero = lax.optimization_barrier(
            (packed, up_weight[0], down_weight[0], zero)
        )
    else:
        up_shard, down_shard = up_weight[0], down_weight[0]
        wide_in = with_halo(own_in, chunks)
    half = shard // 2
    halves = packed.reshape(4, 2, half, WIDE)
    keep = lax.dynamic_index_in_dim(halves, s, 1, keepdims=False)
    give = lax.dynamic_index_in_dim(halves, 1 - s, 1, keepdims=False)

    def gathered(part):
        rows_first = part.transpose(1, 0, 2).reshape(half, 4 * WIDE)
        every = lax.all_gather(rows_first, pair, axis=0, tiled=True)
        return [every[:, i * WIDE : (i + 1) * WIDE] for i in range(4)]

    recv = on_chip(give)
    one = gathered(pick(s, recv, keep))
    zero = [zero[i] for i in range(4)] if fits else gathered(pick(s, keep, recv))
    up_own = lax.all_to_all(
        up_shard.reshape(shard, nf, ff_here), "fsdp", split_axis=1, concat_axis=0, tiled=True
    ).reshape(D, ff_here)
    up_w = both_layers(up_own, s)
    down_w = both_layers(down_shard, s)

    weights = (zero, one)
    gains, shifts, ffb = [], [], []
    for layer in range(2):
        beside = weights[layer][3]
        vectors = beside[:, D : D + 8].T.astype(F32)
        gains.append(vectors[:2])
        shifts.append(vectors[2:])
        hidden = beside[:, D + 8 : D + 8 + per_row].reshape(-1).astype(F32)
        ffb.append(lax.dynamic_slice_in_dim(hidden, f * ff_here, ff_here, 0))

    kept = []
    current = own_in
    produced = []
    for layer in range(2):
        gain, shift_rows = gains[layer], shifts[layer]
        wide = (with_halo(current, chunks) if layer else wide_in).astype(F32)
        n1, inv1 = norm_parts(wide)
        normed = (n1 * gain[0] + shift_rows[0]).astype(BF)
        wq, wk, wv, wo = weights[layer]
        q = (mm(normed[reach:], wq) + widen(shift_rows[1:2])).astype(BF)
        k = mm(normed, wk).astype(BF)
        v = (mm(normed, wv) + widen(shift_rows[2:3])).astype(BF)
        att = attend(q, k, v, bias)
        resid = current.astype(F32) + mm(att, wo[:, :D]) + shift_rows[3]
        n2, inv2 = norm_parts(resid)
        second = (n2 * gain[1] + shift_rows[4]).astype(BF)
        total, second_all, active, slope = mlp_forward(
            second, up_w[layer], down_w[layer], ffb[layer][None]
        )
        out = resid + total + shift_rows[5]
        low = out.astype(BF)
        produced.append(low)
        kept.append((wide, normed, q, k, v, att, resid, second_all, slope, active))
        current = low

    upstream = own_cot.astype(F32)
    derived = [None, None]
    parts = [None, None]
    mlp_sums = [None, None]
    for layer in (1, 0):
        wide, normed, q, k, v, att, resid, second_all, slope, active = kept[layer]
        gain = gains[layer]
        up_b = upstream.astype(BF)
        d_second, up_all, dz_b, ffb_g = mlp_backward(up_b, up_w[layer], down_w[layer], slope)
        down_g = mm_tn(flat(active), flat(up_all))
        up_g = mm_tn(flat(second_all), flat(dz_b))
        n2, inv2 = norm_parts(resid)
        d_resid = upstream + norm_back(d_second, gain[1], n2, inv2)
        c = d_resid.astype(BF)
        wq, wk, wv, wo = weights[layer]
        d_att = widen(mm_nt(c, wo[:, :D]).astype(BF))
        dq, dk, dv = attend_back(q, k, v, d_att, bias_t)
        da_wide = mm_nt(dk, wk) + mm_nt(dv, wv)
        da_own = da_wide[reach:] + mm_nt(dq, wq)
        da_halo = da_wide[:reach]
        n1, inv1 = norm_parts(wide)
        if layer == 1 or not fits:
            da = da_own + return_halo(da_halo, chunks, rows)
            derived[layer] = d_resid + norm_back(da, gain[0], n1[reach:], inv1[reach:])
            upstream_next = derived[layer].astype(BF).astype(F32)
        vectors = jnp.stack(
            [
                jnp.sum(da_halo * n1[:reach], axis=0) + jnp.sum(da_own * n1[reach:], axis=0),
                jnp.sum(d_second * n2, axis=0),
                jnp.sum(da_halo, axis=0) + jnp.sum(da_own, axis=0),
                jnp.sum(dq.astype(F32), axis=0)[:D],
                jnp.sum(dv.astype(F32), axis=0)[:D],
                jnp.sum(d_resid, axis=0),
                jnp.sum(d_second, axis=0),
                jnp.sum(upstream, axis=0),
            ]
        )
        ffb_block = lax.dynamic_update_slice(
            jnp.zeros((D, per_row), F32), ffb_g.reshape(shard, per_row), (f * shard, 0)
        )
        extra = jnp.pad(
            jnp.concatenate([vectors.T, ffb_block], axis=1),
            ((0, 0), (D, WIDE - D - 8 - per_row)),
        )
        pieces = (
            mm_tn(normed[reach:], dq).astype(BF),
            mm_tn(normed, dk).astype(BF),
            mm_tn(normed, dv).astype(BF),
            (mm_tn(att, widen(c)) + extra).astype(BF),
        )
        parts[layer] = pieces
        up_g = lax.all_to_all(
            up_g.astype(BF).reshape(nf, shard, ff_here), "fsdp",
            split_axis=0, concat_axis=0, tiled=True,
        ).reshape(nf * shard * ff_here // D, D)
        down_g = down_g.astype(BF)
        if layer == 0:
            down_g, up_g, _ = lax.optimization_barrier((down_g, up_g, dq))
        halves = halves_pair(down_g, up_g)
        if layer == 1:
            _, upstream_next = lax.optimization_barrier((halves, upstream_next))
        else:
            halves, mlp_sums[1] = lax.optimization_barrier((halves, mlp_sums[1]))
        mlp_sums[layer] = lax.psum(halves, "ctx")
        if layer == 1:
            upstream = upstream_next

    if fits:
        qkv_g, out_g, down_one, up_one, late = reduce_both(
            parts[0], parts[1], mlp_sums[1], da_halo.astype(BF)
        )
        da = da_own + late.astype(F32)
        derived[0] = d_resid + norm_back(da, gain[0], n1[reach:], inv1[reach:])
        far = lax.ppermute(mlp_sums[0], "section", [(1, 0)])
        down_zero, up_zero = split_up(jnp.concatenate([mlp_sums[0], far], axis=1), nf, shard)
        grad_down = pick(s, down_zero, down_one).astype(F32)
        grad_up = pick(s, up_zero, up_one).astype(F32)
        qkv_g, out_g = qkv_g.astype(F32), out_g.astype(F32)
    else:
        a_tot = pick(s, reduce_plain(parts[0]), reduce_plain(parts[1])).astype(F32)
        qkv_g = jnp.concatenate([a_tot[i, :, :D] for i in range(3)], axis=1)
        out_g = a_tot[3]
        grad_down, grad_up = split_up(halves_settle(*mlp_sums), nf, shard)
    vectors = out_g[:, D : D + 8].T
    return (
        both_micros(produced, s),
        both_micros(derived, s),
        qkv_g[None],
        out_g[None, :, :D],
        grad_up[None],
        grad_down[None],
        vectors[None, :2],
        vectors[None, 2:],
        out_g[:, D + 8 : D + 8 + per_row].reshape(1, ff_here),
    )


def split_up(both, nf, shard):
    up = both[1].reshape(nf, shard, -1)
    return both[0], up.transpose(1, 0, 2).reshape(shard, -1)


def both_micros(layers, s):
    to_zero = lax.ppermute(layers[0], "section", [(1, 0)])
    to_one = lax.ppermute(layers[1], "section", [(0, 1)])
    out = jnp.stack([pick(s, layers[0], to_one), pick(s, to_zero, layers[1])])
    return out[None, :, None]


def solution(mesh):
    return jax.shard_map(
        on_device,
        mesh=mesh,
        in_specs=(
            P(None, "fsdp", "ctx", None),
            P(None, "fsdp", None),
            P(None, "fsdp", "ctx", None),
            P("section", "fsdp", None),
            P("section", "fsdp", None),
            P("section", "fsdp", None),
            P("section", "fsdp", None),
            P("section", None, "fsdp"),
            P("section", None, "fsdp"),
            P("section", "fsdp"),
        ),
        out_specs=(
            P("section", None, "fsdp", "ctx", None),
            P("section", None, "fsdp", "ctx", None),
            P("section", "fsdp", None),
            P("section", "fsdp", None),
            P("section", "fsdp", None),
            P("section", "fsdp", None),
            P("section", None, "fsdp"),
            P("section", None, "fsdp"),
            P("section", "fsdp"),
        ),
        check_vma=False,
    )
```

```python
import functools
import math

import jax
import jax.numpy as jnp
from jax import lax
from jax.experimental import pallas as pl
from jax.experimental.pallas import tpu as pltpu
from jax.sharding import PartitionSpec as P

D = 1088
HD = 64
F32 = jnp.float32
BF = jnp.bfloat16
SCALE = 1.0 / math.sqrt(HD)
WIDE = 1152
MESH = pl.DeviceIdType.MESH
SWAP = [(0, 1), (1, 0)]


def mm(a, b):
    return jnp.dot(a, b, preferred_element_type=F32)


def mm_nt(a, b):
    return lax.dot_general(a, b, (((1,), (1,)), ((), ())), preferred_element_type=F32)


def mm_tn(a, b):
    return lax.dot_general(a, b, (((0,), (0,)), ((), ())), preferred_element_type=F32)


def norm_parts(values):
    center = jnp.mean(values, axis=-1, keepdims=True)
    offset = values - center
    spread = jnp.mean(offset * offset, axis=-1, keepdims=True)
    inv = lax.rsqrt(spread + 1e-05)
    return offset * inv, inv


def norm_back(grad, gain, unit, inv):
    dn = grad * gain
    return inv * (
        dn
        - jnp.mean(dn, axis=-1, keepdims=True)
        - unit * jnp.mean(dn * unit, axis=-1, keepdims=True)
    )


def phi_parts(z):
    cdf = 0.5 * (1.0 + lax.erf(z * (1.0 / math.sqrt(2.0))))
    pdf = jnp.exp(-0.5 * z * z) * (1.0 / math.sqrt(2.0 * math.pi))
    return cdf, pdf


def plane_neighbours():
    f = lax.axis_index("fsdp")
    x = lax.rem(f, 2)
    y = f // 2
    return y * 2 + (1 - x), (1 - y) * 2 + x


def plane_barrier(xn, yn):
    barrier = pltpu.get_barrier_semaphore()
    for nb in (xn, yn):
        pl.semaphore_signal(barrier, inc=1, device_id={"fsdp": nb}, device_id_type=MESH)
    pl.semaphore_wait(barrier, 2)


def remote(src, dst, send, recv, nb):
    return pltpu.make_async_remote_copy(
        src_ref=src, dst_ref=dst, send_sem=send, recv_sem=recv,
        device_id={"fsdp": nb}, device_id_type=MESH,
    )


def exchange_rows(own_ref, all_ref, parts, compute, finish, bufs, send, recv):
    x1, y1, x2, y2, sum_x, sum_y = bufs
    xn, yn = plane_neighbours()
    half = own_ref.shape[0] // 2
    top, low = pl.ds(0, half), pl.ds(half, half)
    plane_barrier(xn, yn)

    to_x = remote(own_ref, all_ref.at[1], send.at[0], recv.at[0], xn)
    to_y = remote(own_ref, all_ref.at[2], send.at[1], recv.at[1], yn)
    far_x = remote(all_ref.at[2, top], all_ref.at[3, top], send.at[2], recv.at[2], xn)
    far_y = remote(all_ref.at[1, low], all_ref.at[3, low], send.at[3], recv.at[3], yn)
    first_x = remote(parts.at[3, top], x1, send.at[4], recv.at[4], xn)
    first_y = remote(parts.at[3, low], y1, send.at[5], recv.at[5], yn)
    own_x = remote(parts.at[1, top], x2.at[top], send.at[6], recv.at[6], xn)
    own_y = remote(parts.at[2, low], y2.at[low], send.at[7], recv.at[7], yn)
    rest_x = remote(sum_x, x2.at[low], send.at[8], recv.at[8], xn)
    rest_y = remote(sum_y, y2.at[top], send.at[9], recv.at[9], yn)

    to_x.start()
    to_y.start()
    all_ref[0] = own_ref[...]
    compute(0)
    to_x.wait_recv()
    far_y.start()
    to_y.wait_recv()
    far_x.start()
    compute(1)
    own_x.start()
    far_x.wait_recv()
    far_y.wait_recv()
    compute(3)
    first_x.start()
    first_y.start()
    compute(2)
    own_y.start()
    first_x.wait_recv()
    sum_y[...] = (parts[2, top, :].astype(F32) + x1[...].astype(F32)).astype(BF)
    rest_y.start()
    first_y.wait_recv()
    sum_x[...] = (parts[1, low, :].astype(F32) + y1[...].astype(F32)).astype(BF)
    rest_x.start()
    own_x.wait_recv()
    rest_y.wait_recv()
    finish(top, parts[0, top, :].astype(F32) + x2[top, :].astype(F32) + y2[top, :].astype(F32))
    own_y.wait_recv()
    rest_x.wait_recv()
    finish(low, parts[0, low, :].astype(F32) + x2[low, :].astype(F32) + y2[low, :].astype(F32))
    for copy in (to_x, to_y, far_x, far_y, first_x, first_y, own_x, own_y, rest_x, rest_y):
        copy.wait_send()


def forward_kernel(
    own, up, down, bias, resid, par, out, all_ref, active, slope,
    parts, x1, y1, x2, y2, sx, sy, send, recv,
):
    def finish(at, value):
        out[at, :] = (resid[at, :] + value + par[7:8, :]).astype(BF)

    def compute(r):
        z = mm(all_ref[r], up[...]) + bias[...]
        cdf, pdf = phi_parts(z)
        active[r] = (z * cdf).astype(BF)
        slope[r] = cdf + z * pdf
        parts[r] = mm(active[r], down[...]).astype(BF)

    exchange_rows(own, all_ref, parts, compute, finish, (x1, y1, x2, y2, sx, sy), send, recv)


def backward_kernel(
    own, up, down, slope, total, all_ref, dz_all, bias_g, parts, x1, y1, x2, y2, sx, sy, send, recv
):
    bias_g[...] = jnp.zeros_like(bias_g)

    def finish(at, value):
        total[at, :] = value

    def compute(r):
        dz = mm_nt(all_ref[r], down[...]) * slope[r]
        bias_g[...] += jnp.sum(dz, axis=0, keepdims=True)
        dz_all[r] = dz.astype(BF)
        parts[r] = mm_nt(dz_all[r], up[...]).astype(BF)

    exchange_rows(own, all_ref, parts, compute, finish, (x1, y1, x2, y2, sx, sy), send, recv)


VSPEC = pl.BlockSpec(memory_space=pltpu.VMEM)


def lasting(micros):
    return pl.CostEstimate(flops=0, transcendentals=0, bytes_accessed=int(micros * 3.5e6))


def plane_call(kernel, ident, outs, rows, *operands):
    half = rows // 2
    return pl.pallas_call(
        kernel,
        out_shape=outs,
        in_specs=[VSPEC] * len(operands),
        out_specs=(VSPEC,) * len(outs),
        scratch_shapes=[
            pltpu.VMEM((4, rows, D), BF),
            pltpu.VMEM((half, D), BF),
            pltpu.VMEM((half, D), BF),
            pltpu.VMEM((rows, D), BF),
            pltpu.VMEM((rows, D), BF),
            pltpu.VMEM((half, D), BF),
            pltpu.VMEM((half, D), BF),
            pltpu.SemaphoreType.DMA((10,)),
            pltpu.SemaphoreType.DMA((10,)),
        ],
        compiler_params=pltpu.CompilerParams(
            collective_id=ident, has_side_effects=True, vmem_limit_bytes=40 * 1024 * 1024
        ),
        cost_estimate=lasting(40),
    )(*operands)


def mlp_forward(own, up, down, bias, resid, par):
    rows = own.shape[0]
    if lax.axis_size("fsdp") != 4:
        every = lax.all_gather(own, "fsdp", axis=0, tiled=True)
        z = mm(every, up) + bias
        cdf, pdf = phi_parts(z)
        active = (z * cdf).astype(BF)
        part = mm(active, down).astype(BF)
        total = lax.psum_scatter(part, "fsdp", scatter_dimension=0, tiled=True).astype(F32)
        out = (resid + total + par[7]).astype(BF)
        return out, every, active, cdf + z * pdf
    shape = (4, rows, D)
    return plane_call(
        forward_kernel, 1,
        (
            jax.ShapeDtypeStruct((rows, D), BF),
            jax.ShapeDtypeStruct(shape, BF),
            jax.ShapeDtypeStruct(shape, BF),
            jax.ShapeDtypeStruct(shape, F32),
        ),
        rows, own, up, down, bias, resid, par,
    )


def mlp_backward(own, up, down, slope):
    rows = own.shape[0]
    if lax.axis_size("fsdp") != 4:
        every = lax.all_gather(own, "fsdp", axis=0, tiled=True)
        dz = mm_nt(every, down) * slope
        dz_b = dz.astype(BF)
        part = mm_nt(dz_b, up).astype(BF)
        total = lax.psum_scatter(part, "fsdp", scatter_dimension=0, tiled=True).astype(F32)
        return total, every, dz_b, jnp.sum(dz, axis=0, keepdims=True)
    shape = (4, rows, D)
    return plane_call(
        backward_kernel, 2,
        (
            jax.ShapeDtypeStruct((rows, D), F32),
            jax.ShapeDtypeStruct(shape, BF),
            jax.ShapeDtypeStruct(shape, BF),
            jax.ShapeDtypeStruct((1, D), F32),
        ),
        rows, own, up, down, slope,
    )


def weights_kernel(
    own, rows_in, full, rows_out, load, core_s, core_r, p_send, p_recv, f_send, f_recv, z_send, z_recv
):
    s = lax.axis_index("section")
    f = lax.axis_index("fsdp")
    xn, yn = plane_neighbours()
    dn = 3 - f
    shard, wide = own.shape[1], own.shape[2]
    cut = 640
    left = pl.ds(0, cut)
    right = pl.ds(cut, wide - cut)

    def to(src, dst, send, recv, **where):
        return pltpu.make_async_remote_copy(
            src_ref=src, dst_ref=dst, send_sem=send, recv_sem=recv,
            device_id=where, device_id_type=MESH,
        )

    barrier = pltpu.get_barrier_semaphore()
    z = lax.axis_index("ctx")
    above = {"ctx": lax.rem(z + 1, 4)}
    below = {"ctx": lax.rem(z + 3, 4)}
    for where in ({"section": 1 - s}, {"fsdp": xn}, {"fsdp": yn}, above, below):
        pl.semaphore_signal(barrier, inc=1, device_id=where, device_id_type=MESH)
    pl.semaphore_wait(barrier, 5)
    rows = rows_in.shape[0]
    near_rows, far_rows = pl.ds(rows, rows), pl.ds(0, rows)
    step_one = to(rows_in, rows_out.at[near_rows], z_send.at[0], z_recv.at[0], **above)
    step_two = to(
        rows_out.at[near_rows], rows_out.at[far_rows], z_send.at[1], z_recv.at[1], **above
    )

    @pl.when(z < 3)
    def _():
        step_one.start()

    rows_out[pl.ds(2 * rows, rows), :] = rows_in[...]

    @pl.when(z == 0)
    def _():
        rows_out[near_rows, :] = jnp.zeros(rows_in.shape, BF)

    @pl.when(z < 2)
    def _():
        rows_out[far_rows, :] = jnp.zeros(rows_in.shape, BF)

    def blk(owner):
        return pl.ds(pl.multiple_of(owner * shard, 16), shard)

    def give(p):
        return to(own.at[p], full.at[p, blk(f)], core_s.at[p], core_r.at[p], section=1)

    def keep(p):
        return pltpu.make_async_copy(own.at[p], full.at[p, blk(f)], load.at[p])

    @pl.when(s == 0)
    def _():
        for p in (2, 3, 0, 1):
            give(p).start()
        for p in range(4):
            keep(p).start()
        keep(0).wait()
        keep(1).wait()

    @pl.when(s == 1)
    def _():
        give(2).wait_recv()
        give(3).wait_recv()

    def same(piece, rows, send, recv, cols=slice(None), **where):
        ref = full.at[piece, rows, cols]
        return to(ref, ref, send, recv, **where)

    def hops(k):
        p = 2 * s + k
        return (
            same(p, blk(f), p_send.at[k, 0], p_recv.at[k, 0], fsdp=xn),
            same(p, blk(f), p_send.at[k, 1], p_recv.at[k, 1], fsdp=yn),
            same(p, blk(yn), p_send.at[k, 2], p_recv.at[k, 2], left, fsdp=xn),
            same(p, blk(xn), p_send.at[k, 3], p_recv.at[k, 3], right, fsdp=yn),
        )

    def here(k):
        p = 2 * s + k
        return [
            same(p, blk(owner), f_send.at[k, i], f_recv.at[k, i], section=1 - s)
            for i, owner in enumerate((xn, yn, dn))
        ]

    for k in range(2):
        copies = hops(k)
        copies[0].start()
        copies[1].start()
    for k in range(2):
        copies, across = hops(k), here(k)
        copies[0].wait_recv()
        copies[3].start()
        across[0].start()
        copies[1].wait_recv()
        copies[2].start()
        across[1].start()

    @pl.when(z > 0)
    def _():
        step_one.wait_recv()

    @pl.when((z == 1) | (z == 2))
    def _():
        step_two.start()

    for k in range(2):
        copies, across = hops(k), here(k)
        copies[2].wait_recv()
        copies[3].wait_recv()
        across[2].start()
    for k in range(2):
        for copy in here(k):
            copy.wait()
        for copy in hops(k):
            copy.wait_send()

    @pl.when(s == 0)
    def _():
        for p in range(4):
            give(p).wait_send()
        keep(2).wait()
        keep(3).wait()

    @pl.when(s == 1)
    def _():
        give(0).wait_recv()
        give(1).wait_recv()

    @pl.when(z < 3)
    def _():
        step_one.wait_send()

    @pl.when((z == 1) | (z == 2))
    def _():
        step_two.wait_send()

    @pl.when(z > 1)
    def _():
        step_two.wait_recv()


def first_weights(own, rows_in):
    dma = pltpu.SemaphoreType.DMA
    return pl.pallas_call(
        weights_kernel,
        out_shape=(
            jax.ShapeDtypeStruct((4, D, WIDE), BF),
            jax.ShapeDtypeStruct((3 * rows_in.shape[0], D), BF),
        ),
        in_specs=[pl.BlockSpec(memory_space=pl.ANY), VSPEC],
        out_specs=(VSPEC, VSPEC),
        scratch_shapes=[
            dma((4,)), dma((4,)), dma((4,)), dma((2, 4)), dma((2, 4)), dma((2, 3)), dma((2, 3)),
            dma((2,)), dma((2,)),
        ],
        compiler_params=pltpu.CompilerParams(
            collective_id=4, has_side_effects=True, vmem_limit_bytes=16 * 1024 * 1024
        ),
        cost_estimate=lasting(50),
        name="first_weights",
    )(own, rows_in)


def z_partners():
    z = lax.axis_index("ctx")
    return z + 1 - 2 * lax.rem(z, 2), 3 - z, (z == 1) | (z == 2)


def add_rows(dst, one, two, rows, step):
    @pl.loop(0, rows // step)
    def _(i):
        at = pl.ds(pl.multiple_of(i * step, 16), step)
        dst[at, :] = (one[at, :].astype(F32) + two[at, :].astype(F32)).astype(dst.dtype)


CUTS = ((0, 640, 384), (640, 512, 256))


def reduce_kernel(
    q0, k0, v0, o0, q1, k1, v1, o1, mlp, halo,
    qkv_out, out_out, down_out, up_out, rows_out,
    own_in, held, up_own, up_far, sent, caught,
    x1a, y1a, x2a, y2a, sxa, sya, ta, zaa, zba,
    x1b, y1b, x2b, y2b, sxb, syb, tb, zab, zbb,
    load, core_s, core_r, p_send, p_recv, z_send, z_recv, h_send, h_recv,
):
    s = lax.axis_index("section")
    f = lax.axis_index("fsdp")
    xn, yn = plane_neighbours()
    dn = 3 - f
    side, across, inner = z_partners()
    pieces = ((q0, k0, v0, o0), (q1, k1, v1, o1))
    sets = (
        (x1a, y1a, x2a, y2a, sxa, sya, ta, zaa, zba),
        (x1b, y1b, x2b, y2b, sxb, syb, tb, zab, zbb),
    )
    shard = out_out.shape[0]
    rows = rows_out.shape[0]
    z = lax.axis_index("ctx")
    above, below = {"ctx": lax.rem(z + 1, 4)}, {"ctx": lax.rem(z + 3, 4)}

    def to(src, dst, send, recv, **where):
        return pltpu.make_async_remote_copy(
            src_ref=src, dst_ref=dst, send_sem=send, recv_sem=recv,
            device_id=where, device_id_type=MESH,
        )

    barrier = pltpu.get_barrier_semaphore()
    partners = ({"section": 1 - s}, {"fsdp": xn}, {"fsdp": yn}, above, below)
    for where in partners:
        pl.semaphore_signal(barrier, inc=1, device_id=where, device_id_type=MESH)
    pl.semaphore_wait(barrier, 5)

    def blk(owner):
        return pl.ds(pl.multiple_of(owner * shard, 16), shard)

    def by_core(act):
        for core in range(2):
            pl.when(s == core)(functools.partial(act, core))

    def far(j, src):
        return to(src, held.at[j], core_s.at[j], core_r.at[j], section=1 - s)

    def near(j, src):
        return pltpu.make_async_copy(src, own_in.at[j % 2], load.at[j])

    def bufs(c):
        return tuple(ref.at[c // 2] for ref in sets[c % 2])

    def plane(c):
        x1, y1, x2, y2, sx, sy = bufs(c)[:6]
        own = held.at[c // 2]
        at, width, cut = CUTS[c % 2]
        left, right = pl.ds(at, cut), pl.ds(at + cut, width - cut)
        to_left, to_right = pl.ds(0, cut), pl.ds(cut, width - cut)
        sems = [(p_send.at[c, i], p_recv.at[c, i]) for i in range(6)]
        return (
            to(own.at[blk(dn), left], x1, *sems[0], fsdp=xn),
            to(own.at[blk(dn), right], y1, *sems[1], fsdp=yn),
            to(own.at[blk(xn), left], x2.at[:, to_left], *sems[2], fsdp=xn),
            to(own.at[blk(yn), right], y2.at[:, to_right], *sems[3], fsdp=yn),
            to(sx, x2.at[:, to_right], *sems[4], fsdp=xn),
            to(sy, y2.at[:, to_left], *sems[5], fsdp=yn),
        )

    def along(c):
        t, za, zb = bufs(c)[6:]
        sems = [(z_send.at[c, i], z_recv.at[c, i]) for i in range(3)]
        return (
            to(t, za, *sems[0], ctx=side),
            to(za, zb, *sems[1], ctx=across),
            to(zb, zb, *sems[2], ctx=side),
        )

    def join(j):
        far(j, q0).wait_recv()
        near(j, q0).wait()
        add_rows(held.at[j], own_in.at[j % 2], held.at[j], 4 * shard, shard)
        for c in (2 * j, 2 * j + 1):
            for copy in plane(c)[:4]:
                copy.start()
        if j < 2:
            by_core(lambda core: near(j + 2, pieces[core][j + 2]).start())

    def second(c):
        copies = plane(c)
        x1, y1, _, _, sx, sy = bufs(c)[:6]
        at, width, cut = CUTS[c % 2]
        own = held.at[c // 2]
        copies[0].wait_recv()
        add_rows(sy, own.at[blk(yn), pl.ds(at, cut)], x1, shard, shard)
        copies[5].start()
        copies[1].wait_recv()
        add_rows(sx, own.at[blk(xn), pl.ds(at + cut, width - cut)], y1, shard, shard)
        copies[4].start()

    def third(c):
        copies = plane(c)
        _, _, x2, y2, _, _, t, _, _ = bufs(c)
        at, width, _ = CUTS[c % 2]
        for copy in copies[2:]:
            copy.wait_recv()
        t[...] = (
            held[c // 2, blk(f), pl.ds(at, width)].astype(F32)
            + x2[...].astype(F32)
            + y2[...].astype(F32)
        ).astype(BF)

        @pl.when(jnp.logical_not(inner))
        def _():
            along(c)[0].start()

    def inward(c):
        @pl.when(inner)
        def _():
            t, za, _ = bufs(c)[6:]
            copies = along(c)
            copies[0].wait_recv()
            add_rows(za, t, za, shard, shard)
            copies[1].start()

    def crossed(c):
        @pl.when(inner)
        def _():
            _, za, zb = bufs(c)[6:]
            copies = along(c)
            copies[1].wait_recv()
            add_rows(zb, za, zb, shard, shard)
            copies[2].start()

    def last(c):
        at, width, _ = CUTS[c % 2]
        j = c // 2

        @pl.when(jnp.logical_not(inner))
        def _():
            along(c)[2].wait_recv()

        if j < 3:
            width = min(width, D - at)
            qkv_out[:, pl.ds(j * D + at, width)] = bufs(c)[8][:, pl.ds(0, width)]
        else:
            out_out[:, pl.ds(at, width)] = bufs(c)[8][...]

    half = down_out.shape[0] // 2
    mine = pl.ds(pl.multiple_of(s * half, 16), half)
    down_far = to(mlp.at[0], down_out.at[mine], core_s.at[4], core_r.at[4], section=1 - s)
    down_near = pltpu.make_async_copy(mlp.at[0], down_out.at[mine], load.at[4])
    far_up = to(mlp.at[1], up_far, core_s.at[5], core_r.at[5], section=1 - s)
    near_up = pltpu.make_async_copy(mlp.at[1], up_own, load.at[5])

    def lay_up():
        far_up.wait_recv()
        near_up.wait()

        @pl.when(s == 1)
        def _():
            for k in range(2):
                up_out[:, pl.ds(k * D, D)] = up_far[pl.ds(k * shard, shard), :]
                up_out[:, pl.ds((2 + k) * D, D)] = up_own[pl.ds(k * shard, shard), :]

    back_one = to(halo.at[pl.ds(0, rows)], caught.at[0], h_send.at[0], h_recv.at[0], **below)
    back_two = to(sent, caught.at[1], h_send.at[1], h_recv.at[1], **below)

    def back():
        @pl.when(z < 3)
        def _():
            back_one.wait_recv()

        @pl.when(z == 3)
        def _():
            caught[0] = jnp.zeros_like(caught[0])

        @pl.when(z > 0)
        def _():
            add_rows(sent, halo.at[pl.ds(rows, rows)], caught.at[0], rows, rows)
            back_two.start()

    def back_end():
        @pl.when(z < 3)
        def _():
            back_two.wait_recv()
            rows_out[...] = caught[1]

        @pl.when(z == 3)
        def _():
            rows_out[...] = jnp.zeros_like(rows_out)

    @pl.when(z > 0)
    def _():
        back_one.start()

    for j in range(4):
        by_core(lambda core: far(j, pieces[1 - core][j]).start())
        if j < 2:
            by_core(lambda core: near(j, pieces[core][j]).start())
    for copy in (down_far, down_near, far_up, near_up):
        copy.start()

    join(0)
    for c in range(12):
        if c in (1, 3, 5):
            join((c + 1) // 2)
        if c < 8:
            second(c)
        if 1 <= c <= 8:
            third(c - 1)
        if 2 <= c <= 9:
            inward(c - 2)
        if 3 <= c <= 10:
            crossed(c - 3)
        if c >= 4:
            last(c - 4)
        if c == 2:
            back()
        if c == 4:
            lay_up()
        if c == 6:
            back_end()

    down_near.wait()
    down_far.wait()
    far_up.wait_send()

    @pl.when(z > 0)
    def _():
        back_one.wait_send()
        back_two.wait_send()

    for j in range(4):
        far(j, q0).wait_send()
    for c in range(8):
        for copy in plane(c):
            copy.wait_send()

    @pl.when(inner)
    def _():
        for c in range(8):
            for copy in along(c)[1:]:
                copy.wait_send()

    @pl.when(jnp.logical_not(inner))
    def _():
        for c in range(8):
            along(c)[0].wait_send()


def reduce_both(zero, one, mlp, halo):
    shard = D // 4
    rows = halo.shape[0] // 2
    dma = pltpu.SemaphoreType.DMA
    any_spec = pl.BlockSpec(memory_space=pl.ANY)

    def buf(*shape):
        return pltpu.VMEM(shape, BF)

    def part(_, width, cut):
        wide = buf(4, shard, width)
        return [
            buf(4, shard, cut), buf(4, shard, width - cut), wide, wide,
            buf(4, shard, width - cut), buf(4, shard, cut), wide, wide, wide,
        ]

    return pl.pallas_call(
        reduce_kernel,
        out_shape=tuple(
            jax.ShapeDtypeStruct(shape, BF)
            for shape in ((shard, 3 * D), (shard, WIDE), (D, D), (shard, 4 * D), (rows, D))
        ),
        in_specs=[any_spec] * 9 + [VSPEC],
        out_specs=(VSPEC,) * 5,
        scratch_shapes=[
            buf(2, D, WIDE), buf(4, D, WIDE), buf(D // 2, D), buf(D // 2, D), buf(rows, D),
            buf(2, rows, D), *part(*CUTS[0]), *part(*CUTS[1]),
            dma((6,)), dma((6,)), dma((6,)), dma((8, 6)), dma((8, 6)), dma((8, 3)), dma((8, 3)),
            dma((2,)), dma((2,)),
        ],
        compiler_params=pltpu.CompilerParams(
            collective_id=3, has_side_effects=True, vmem_limit_bytes=58 * 1024 * 1024
        ),
        cost_estimate=lasting(120),
        name="reduce_both",
    )(*zero, *one, mlp, halo)


def halves_pair(down, up):
    s = lax.axis_index("section")
    both = jnp.stack([down, up])
    both = both.reshape(2, 2, both.shape[1] // 2, D)
    keep = lax.dynamic_index_in_dim(both, s, 1, keepdims=False)
    give = lax.dynamic_index_in_dim(both, 1 - s, 1, keepdims=False)
    return (keep.astype(F32) + on_chip(give).astype(F32)).astype(BF)


def halves_settle(zero, one):
    s = lax.axis_index("section")
    mine, far = pick(s, zero, one), on_chip(pick(s, one, zero))
    return jnp.concatenate([pick(s, mine, far), pick(s, far, mine)], axis=1).astype(F32)


def reduce_plain(pieces):
    s = lax.axis_index("section")
    pair = ("fsdp", "section")
    a = jnp.stack([lax.psum_scatter(p, pair, scatter_dimension=0, tiled=True) for p in pieces])
    a = lax.psum(a, "ctx")
    far = on_chip(a)
    return jnp.concatenate([pick(s, a, far), pick(s, far, a)], axis=1)


def shift(value, steps):
    count = lax.axis_size("ctx")
    pairs = [(i, i + steps) for i in range(count) if 0 <= i + steps < count]
    return lax.ppermute(value, "ctx", pairs)


def with_halo(own, chunks):
    parts = [own]
    for _ in range(chunks):
        parts.append(shift(parts[-1], 1))
    return jnp.concatenate(parts[::-1], axis=0)


def return_halo(halo, chunks, rows):
    carried = None
    for far in range(chunks):
        mine = halo[far * rows : (far + 1) * rows]
        carried = mine if carried is None else mine + carried
        carried = shift(carried.astype(BF), -1).astype(F32)
    return carried


def pick(s, first, second):
    return jnp.where(s == 0, first, second)


def on_chip(value):
    return lax.ppermute(value, "section", SWAP)


def both_layers(own, s):
    other = on_chip(own)
    return pick(s, own, other), pick(s, other, own)


def flat(values):
    return values.reshape(-1, values.shape[-1])


def widen(values):
    return jnp.pad(values, ((0, 0), (0, WIDE - D)))


TAIL = 1024


def scores_forward(q, k, v, bias, lanes):
    outs = []
    for low in (True, False):
        one = jnp.where((lanes < HD) if low else (lanes >= HD), q, jnp.zeros_like(q))
        weight = jnp.exp(mm_nt(one, k) + bias)
        prob = weight * (1.0 / jnp.sum(weight, axis=-1, keepdims=True))
        outs.append(mm(prob.astype(BF), v))
    return jnp.where(lanes < HD, outs[0], outs[1]).astype(BF)


def scores_backward(q, k, v, grad, bias_t, lanes):
    dqs, dk, dv = [], 0.0, 0.0
    for low in (True, False):
        mine = (lanes < HD) if low else (lanes >= HD)
        one = jnp.where(mine, q, jnp.zeros_like(q))
        g = jnp.where(mine, grad, jnp.zeros_like(grad))
        weight = jnp.exp(mm_nt(k, one) + bias_t)
        prob = weight * (1.0 / jnp.sum(weight, axis=0, keepdims=True))
        d_prob = mm_nt(v, g)
        row = jnp.sum(prob * d_prob, axis=0, keepdims=True)
        d_score = (prob * (d_prob - row)).astype(BF)
        dqs.append(mm_tn(d_score, k))
        dk = dk + mm(d_score, one)
        dv = dv + mm(prob.astype(BF), g)
    dq = jnp.where(lanes < HD, dqs[0], dqs[1]) * SCALE
    return dq.astype(BF), dk.astype(BF), dv.astype(BF)


def lane_tile(i):
    return pl.ds(pl.multiple_of(i * 128, 128), 128)


def widened(row):
    return jnp.concatenate([row, jnp.zeros((row.shape[0], WIDE - D), row.dtype)], axis=1)


def block_kernel(
    wide, wq, wk, wv, wo, bias, normed, q_ref, k_ref, v_ref, att, resid, second, par, held
):
    rows = resid.shape[0]
    total = wide.shape[0]
    pick_row = (
        lax.broadcasted_iota(jnp.int32, (16, 128), 1)
        == lax.broadcasted_iota(jnp.int32, (16, 128), 0) + (D - TAIL)
    )
    par[...] = mm_nt(pick_row.astype(F32).astype(BF), wo[:, pl.ds(TAIL, 128)])

    @pl.loop(0, total // rows)
    def _(i):
        at = pl.ds(pl.multiple_of(i * rows, 16), rows)
        unit, _ = norm_parts(wide[at, :].astype(F32))
        low = (unit * par[0:1, :] + par[2:3, :]).astype(BF)
        normed[at, :] = low
        k_ref[at, :] = mm(low, wk[...]).astype(BF)
        v_ref[at, :] = (mm(low, wv[...]) + widened(par[4:5, :])).astype(BF)

    own = pl.ds(total - rows, rows)
    q_ref[...] = (mm(normed[own, :], wq[...]) + widened(par[3:4, :])).astype(BF)
    lanes = lax.broadcasted_iota(jnp.int32, (rows, 128), 1)

    @pl.loop(0, WIDE // 128)
    def _(i):
        at = lane_tile(i)
        held[:, at] = scores_forward(
            q_ref[:, at] * jnp.asarray(SCALE, BF), k_ref[:, at], v_ref[:, at], bias[...], lanes
        )

    att[...] = held[:, pl.ds(0, D)]
    res = wide[own, :].astype(F32) + mm(att[...], wo[:, pl.ds(0, D)]) + par[5:6, :]
    resid[...] = res
    unit, _ = norm_parts(res)
    second[...] = (unit * par[1:2, :] + par[6:7, :]).astype(BF)


def weight_specs(weights):
    if weights.ndim == 3:
        return [pl.BlockSpec((None, D, WIDE), lambda i, p=p: (p, 0, 0)) for p in range(4)]
    return [pl.BlockSpec((D, WIDE), lambda i, p=p: (0, p)) for p in range(4)]


def whole(shape):
    return pl.BlockSpec(shape, lambda i: (0,) * len(shape))


def block_forward(wide, weights, bias):
    total, rows = wide.shape[0], bias.shape[0]
    outs = (
        ((total, D), BF), ((rows, WIDE), BF), ((total, WIDE), BF), ((total, WIDE), BF),
        ((rows, D), BF), ((rows, D), F32), ((rows, D), BF), ((16, D), F32),
    )
    return pl.pallas_call(
        block_kernel,
        out_shape=tuple(jax.ShapeDtypeStruct(*out) for out in outs),
        grid=(1,),
        in_specs=[whole(wide.shape), *weight_specs(weights), whole(bias.shape)],
        out_specs=tuple(whole(shape) for shape, _ in outs),
        scratch_shapes=[pltpu.VMEM((rows, WIDE), BF)],
        compiler_params=pltpu.CompilerParams(vmem_limit_bytes=56 * 1024 * 1024),
        cost_estimate=lasting(22),
        name="block_forward",
    )(wide, weights, weights, weights, weights, bias)


def block_back_kernel(
    d_second, up, resid, wide, q_ref, k_ref, v_ref, att, ffb_rows, wq, wk, wv, wo, par, bias_t,
    d_resid, dq_ref, dk_ref, dv_ref, da_own, da_halo, left, right, held, sums,
):
    rows = resid.shape[0]
    total = wide.shape[0]
    own = total - rows

    def total_of(values):
        return jnp.sum(values, axis=0, keepdims=True)

    upstream = up[...].astype(F32)
    unit, inv = norm_parts(resid[...])
    grad = upstream + norm_back(d_second[...], par[1:2, :], unit, inv)
    d_resid[...] = grad
    sums[1:2, :] = total_of(d_second[...] * unit)
    sums[5:6, :] = total_of(grad)
    sums[6:7, :] = total_of(d_second[...])
    sums[7:8, :] = total_of(upstream)
    sums[8:16, :] = ffb_rows[...]
    low = grad.astype(BF)
    right[pl.ds(0, rows), :] = jnp.zeros((rows, WIDE), BF)
    right[pl.ds(0, rows), pl.ds(0, D)] = low
    right[pl.ds(rows, 16), :] = (
        lax.broadcasted_iota(jnp.int32, (16, WIDE), 1)
        == lax.broadcasted_iota(jnp.int32, (16, WIDE), 0) + D
    ).astype(F32).astype(BF)
    held[...] = jnp.zeros((rows, WIDE), BF)
    held[:, pl.ds(0, D)] = mm_nt(low, wo[:, pl.ds(0, D)]).astype(BF)
    lanes = lax.broadcasted_iota(jnp.int32, (rows, 128), 1)

    @pl.loop(0, WIDE // 128)
    def _(i):
        at = lane_tile(i)
        dq_ref[:, at], dk_ref[:, at], dv_ref[:, at] = scores_backward(
            q_ref[:, at] * jnp.asarray(SCALE, BF), k_ref[:, at], v_ref[:, at], held[:, at],
            bias_t[...], lanes,
        )

    sums[3:4, :] = total_of(dq_ref[...].astype(F32))[:, :D]
    sums[4:5, :] = total_of(dv_ref[...].astype(F32))[:, :D]
    sums[0:1, :] = jnp.zeros((1, D), F32)
    sums[2:3, :] = jnp.zeros((1, D), F32)

    def back(at):
        da = mm_nt(dk_ref[at, :], wk[...]) + mm_nt(dv_ref[at, :], wv[...])
        return da

    def count(da, at):
        unit, _ = norm_parts(wide[at, :].astype(F32))
        sums[0:1, :] += total_of(da * unit)
        sums[2:3, :] += total_of(da)

    @pl.loop(0, own // rows)
    def _(i):
        at = pl.ds(pl.multiple_of(i * rows, 16), rows)
        da = back(at)
        da_halo[at, :] = da.astype(BF)
        count(da, at)

    at = pl.ds(own, rows)
    da = back(at) + mm_nt(dq_ref[...], wq[...])
    da_own[...] = da
    count(da, at)
    left[pl.ds(0, rows), :] = att[...]
    left[pl.ds(rows, 16), :] = sums[...].astype(BF)


def block_backward(d_second, up, resid, wide, q, k, v, att, ffb_rows, weights, par, bias_t):
    total, rows = wide.shape[0], resid.shape[0]
    outs = (
        ((rows, D), F32), ((rows, WIDE), BF), ((total, WIDE), BF), ((total, WIDE), BF),
        ((rows, D), F32), ((total - rows, D), BF), ((rows + 16, D), BF), ((rows + 16, WIDE), BF),
    )
    before = (d_second, up, resid, wide, q, k, v, att, ffb_rows)
    return pl.pallas_call(
        block_back_kernel,
        out_shape=tuple(jax.ShapeDtypeStruct(*out) for out in outs),
        grid=(1,),
        in_specs=[
            *(whole(value.shape) for value in before), *weight_specs(weights),
            whole(par.shape), whole(bias_t.shape),
        ],
        out_specs=tuple(whole(shape) for shape, _ in outs),
        scratch_shapes=[pltpu.VMEM((rows, WIDE), BF), pltpu.VMEM((16, D), F32)],
        compiler_params=pltpu.CompilerParams(vmem_limit_bytes=60 * 1024 * 1024),
        cost_estimate=lasting(38),
        name="block_backward",
    )(*before, weights, weights, weights, weights, par, bias_t)


def on_device(
    inputs, segments, cotangent, qkv_weight, out_weight, up_weight, down_weight,
    norm_gains, biases, ff_bias,
):
    rows = inputs.shape[2]
    length = segments.shape[2]
    chunks = min((length // 2 - 1 + rows - 1) // rows, lax.axis_size("ctx") - 1)
    reach = chunks * rows
    s = lax.axis_index("section")
    f = lax.axis_index("fsdp")
    nf = lax.axis_size("fsdp")
    shard = D // nf
    ff_here = ff_bias.shape[1]
    per_row = ff_here // shard
    pair = ("fsdp", "section")
    fits = nf == 4 and lax.axis_size("ctx") == 4 and chunks == 2

    own_in = lax.dynamic_index_in_dim(inputs, s, 0, keepdims=False)[0]
    own_cot = lax.dynamic_index_in_dim(cotangent, s, 0, keepdims=False)[0]
    seg = lax.dynamic_index_in_dim(segments, s, 0, keepdims=False)[0]
    start = lax.axis_index("ctx") * rows
    key_seg = lax.dynamic_slice_in_dim(
        jnp.pad(seg, (reach, 0), constant_values=-1), start, reach + rows, 0
    )
    allowed = (key_seg[reach:, None] == key_seg[None, :]) & (
        jnp.arange(reach + rows, dtype=jnp.int32)[None, :] - reach
        <= jnp.arange(rows, dtype=jnp.int32)[:, None]
    )

    bias = jnp.where(allowed, 0.0, -1e30).astype(F32)
    bias_t = bias.T

    small = jnp.concatenate(
        [norm_gains[0].T, biases[0].T, ff_bias[0].reshape(per_row, shard).T], axis=1
    )
    packed = jnp.stack(
        [
            widen(qkv_weight[0][:, :D]),
            widen(qkv_weight[0][:, D : 2 * D]),
            widen(qkv_weight[0][:, 2 * D :]),
            jnp.concatenate(
                [out_weight[0], small, jnp.zeros((shard, WIDE - D - 8 - per_row), BF)], axis=1
            ),
        ]
    )
    if fits:
        zero, wide_in = first_weights(packed, own_in)
        packed, up_shard, down_shard, zero = lax.optimization_barrier(
            (packed, up_weight[0], down_weight[0], zero)
        )
    else:
        up_shard, down_shard = up_weight[0], down_weight[0]
        wide_in = with_halo(own_in, chunks)
    half = shard // 2
    halves = packed.reshape(4, 2, half, WIDE)
    keep = lax.dynamic_index_in_dim(halves, s, 1, keepdims=False)
    give = lax.dynamic_index_in_dim(halves, 1 - s, 1, keepdims=False)

    def gathered(part):
        rows_first = part.transpose(1, 0, 2).reshape(half, 4 * WIDE)
        return lax.all_gather(rows_first, pair, axis=0, tiled=True)

    recv = on_chip(give)
    one = gathered(pick(s, recv, keep))
    if not fits:
        zero = gathered(pick(s, keep, recv))
    up_own = lax.all_to_all(
        up_shard.reshape(shard, nf, ff_here), "fsdp", split_axis=1, concat_axis=0, tiled=True
    ).reshape(D, ff_here)
    up_w = both_layers(up_own, s)
    down_w = both_layers(down_shard, s)

    weights = (zero, one)

    kept = []
    current = own_in
    produced = []
    for layer in range(2):
        wide = with_halo(current, chunks) if layer else wide_in
        normed, q, k, v, att, resid, second, par = block_forward(wide, weights[layer], bias)
        ffb = lax.dynamic_slice(par, (8, f * shard), (per_row, shard)).reshape(1, ff_here)
        current, second_all, active, slope = mlp_forward(
            second, up_w[layer], down_w[layer], ffb, resid, par
        )
        produced.append(current)
        kept.append((wide, normed, q, k, v, att, resid, second_all, slope, active, par))

    upstream = own_cot
    derived = [None, None]
    parts = [None, None]
    mlp_sums = [None, None]
    for layer in (1, 0):
        wide, normed, q, k, v, att, resid, second_all, slope, active, par = kept[layer]
        d_second, up_all, dz_b, ffb_g = mlp_backward(upstream, up_w[layer], down_w[layer], slope)
        down_g = mm_tn(flat(active), flat(up_all))
        up_g = mm_tn(flat(second_all), flat(dz_b))
        ffb_rows = lax.dynamic_update_slice(
            jnp.zeros((8, D), F32), ffb_g.reshape(per_row, shard), (0, f * shard)
        )
        d_resid, dq, dk, dv, da_own, da_halo, left, right = block_backward(
            d_second, upstream, resid, wide, q, k, v, att, ffb_rows, weights[layer], par, bias_t
        )

        def through_norm(late):
            unit, inv = norm_parts(wide[reach:].astype(F32))
            return d_resid + norm_back(da_own + late, par[0], unit, inv)

        if layer == 1 or not fits:
            derived[layer] = through_norm(return_halo(da_halo, chunks, rows))
            upstream_next = derived[layer].astype(BF)
        pieces = (
            mm_tn(normed[reach:], dq).astype(BF),
            mm_tn(normed, dk).astype(BF),
            mm_tn(normed, dv).astype(BF),
            mm_tn(left, right).astype(BF),
        )
        parts[layer] = pieces
        up_g = lax.all_to_all(
            up_g.astype(BF).reshape(nf, shard, ff_here), "fsdp",
            split_axis=0, concat_axis=0, tiled=True,
        ).reshape(nf * shard * ff_here // D, D)
        down_g = down_g.astype(BF)
        if layer == 0:
            down_g, up_g, _ = lax.optimization_barrier((down_g, up_g, dq))
        halves = halves_pair(down_g, up_g)
        if layer == 1:
            _, upstream_next = lax.optimization_barrier((halves, upstream_next))
        else:
            halves, mlp_sums[1] = lax.optimization_barrier((halves, mlp_sums[1]))
        mlp_sums[layer] = lax.psum(halves, "ctx")
        if layer == 1:
            upstream = upstream_next

    if fits:
        qkv_g, out_g, down_one, up_one, late = reduce_both(
            parts[0], parts[1], mlp_sums[1], da_halo
        )
        derived[0] = through_norm(late.astype(F32))
        far = lax.ppermute(mlp_sums[0], "section", [(1, 0)])
        down_zero, up_zero = split_up(jnp.concatenate([mlp_sums[0], far], axis=1), nf, shard)
        grad_down = pick(s, down_zero, down_one).astype(F32)
        grad_up = pick(s, up_zero, up_one).astype(F32)
        qkv_g, out_g = qkv_g.astype(F32), out_g.astype(F32)
    else:
        a_tot = pick(s, reduce_plain(parts[0]), reduce_plain(parts[1])).astype(F32)
        qkv_g = jnp.concatenate([a_tot[i, :, :D] for i in range(3)], axis=1)
        out_g = a_tot[3]
        grad_down, grad_up = split_up(halves_settle(*mlp_sums), nf, shard)
    vectors = out_g[:, D : D + 8].T
    return (
        both_micros(produced, s),
        both_micros(derived, s),
        qkv_g[None],
        out_g[None, :, :D],
        grad_up[None],
        grad_down[None],
        vectors[None, :2],
        vectors[None, 2:],
        out_g[:, D + 8 : D + 8 + per_row].T.reshape(1, ff_here),
    )


def split_up(both, nf, shard):
    up = both[1].reshape(nf, shard, -1)
    return both[0], up.transpose(1, 0, 2).reshape(shard, -1)


def both_micros(layers, s):
    to_zero = lax.ppermute(layers[0], "section", [(1, 0)])
    to_one = lax.ppermute(layers[1], "section", [(0, 1)])
    out = jnp.stack([pick(s, layers[0], to_one), pick(s, to_zero, layers[1])])
    return out[None, :, None]


def solution(mesh):
    return jax.shard_map(
        on_device,
        mesh=mesh,
        in_specs=(
            P(None, "fsdp", "ctx", None),
            P(None, "fsdp", None),
            P(None, "fsdp", "ctx", None),
            P("section", "fsdp", None),
            P("section", "fsdp", None),
            P("section", "fsdp", None),
            P("section", "fsdp", None),
            P("section", None, "fsdp"),
            P("section", None, "fsdp"),
            P("section", "fsdp"),
        ),
        out_specs=(
            P("section", None, "fsdp", "ctx", None),
            P("section", None, "fsdp", "ctx", None),
            P("section", "fsdp", None),
            P("section", "fsdp", None),
            P("section", "fsdp", None),
            P("section", "fsdp", None),
            P("section", None, "fsdp"),
            P("section", None, "fsdp"),
            P("section", "fsdp"),
        ),
        check_vma=False,
    )
```

```python
import functools
import math

import jax
import jax.numpy as jnp
from jax import lax
from jax.experimental import pallas as pl
from jax.experimental.pallas import tpu as pltpu
from jax.sharding import PartitionSpec as P

D = 1088
HD = 64
F32 = jnp.float32
BF = jnp.bfloat16
SCALE = 1.0 / math.sqrt(HD)
WIDE = 1152
MESH = pl.DeviceIdType.MESH
SWAP = [(0, 1), (1, 0)]


def mm(a, b):
    return jnp.dot(a, b, preferred_element_type=F32)


def mm_nt(a, b):
    return lax.dot_general(a, b, (((1,), (1,)), ((), ())), preferred_element_type=F32)


def mm_tn(a, b):
    return lax.dot_general(a, b, (((0,), (0,)), ((), ())), preferred_element_type=F32)


def norm_parts(values):
    center = jnp.mean(values, axis=-1, keepdims=True)
    offset = values - center
    spread = jnp.mean(offset * offset, axis=-1, keepdims=True)
    inv = lax.rsqrt(spread + 1e-05)
    return offset * inv, inv


def norm_back(grad, gain, unit, inv):
    dn = grad * gain
    return inv * (
        dn
        - jnp.mean(dn, axis=-1, keepdims=True)
        - unit * jnp.mean(dn * unit, axis=-1, keepdims=True)
    )


def phi_parts(z):
    cdf = 0.5 * (1.0 + lax.erf(z * (1.0 / math.sqrt(2.0))))
    pdf = jnp.exp(-0.5 * z * z) * (1.0 / math.sqrt(2.0 * math.pi))
    return cdf, pdf


def plane_neighbours():
    f = lax.axis_index("fsdp")
    x = lax.rem(f, 2)
    y = f // 2
    return y * 2 + (1 - x), (1 - y) * 2 + x


def plane_barrier(xn, yn):
    barrier = pltpu.get_barrier_semaphore()
    for nb in (xn, yn):
        pl.semaphore_signal(barrier, inc=1, device_id={"fsdp": nb}, device_id_type=MESH)
    pl.semaphore_wait(barrier, 2)


def remote(src, dst, send, recv, nb):
    return pltpu.make_async_remote_copy(
        src_ref=src, dst_ref=dst, send_sem=send, recv_sem=recv,
        device_id={"fsdp": nb}, device_id_type=MESH,
    )


def exchange_rows(own_ref, all_ref, parts, compute, finish, bufs, send, recv):
    x1, y1, x2, y2, sum_x, sum_y = bufs
    xn, yn = plane_neighbours()
    half = own_ref.shape[0] // 2
    top, low = pl.ds(0, half), pl.ds(half, half)
    plane_barrier(xn, yn)

    to_x = remote(own_ref, all_ref.at[1], send.at[0], recv.at[0], xn)
    to_y = remote(own_ref, all_ref.at[2], send.at[1], recv.at[1], yn)
    far_x = remote(all_ref.at[2, top], all_ref.at[3, top], send.at[2], recv.at[2], xn)
    far_y = remote(all_ref.at[1, low], all_ref.at[3, low], send.at[3], recv.at[3], yn)
    first_x = remote(parts.at[3, top], x1, send.at[4], recv.at[4], xn)
    first_y = remote(parts.at[3, low], y1, send.at[5], recv.at[5], yn)
    own_x = remote(parts.at[1, top], x2.at[top], send.at[6], recv.at[6], xn)
    own_y = remote(parts.at[2, low], y2.at[low], send.at[7], recv.at[7], yn)
    rest_x = remote(sum_x, x2.at[low], send.at[8], recv.at[8], xn)
    rest_y = remote(sum_y, y2.at[top], send.at[9], recv.at[9], yn)

    to_x.start()
    to_y.start()
    all_ref[0] = own_ref[...]
    compute(0)
    to_x.wait_recv()
    far_y.start()
    to_y.wait_recv()
    far_x.start()
    compute(1)
    own_x.start()
    far_x.wait_recv()
    far_y.wait_recv()
    compute(3)
    first_x.start()
    first_y.start()
    compute(2)
    own_y.start()
    first_x.wait_recv()
    sum_y[...] = (parts[2, top, :].astype(F32) + x1[...].astype(F32)).astype(BF)
    rest_y.start()
    first_y.wait_recv()
    sum_x[...] = (parts[1, low, :].astype(F32) + y1[...].astype(F32)).astype(BF)
    rest_x.start()
    own_x.wait_recv()
    rest_y.wait_recv()
    finish(top, parts[0, top, :].astype(F32) + x2[top, :].astype(F32) + y2[top, :].astype(F32))
    own_y.wait_recv()
    rest_x.wait_recv()
    finish(low, parts[0, low, :].astype(F32) + x2[low, :].astype(F32) + y2[low, :].astype(F32))
    for copy in (to_x, to_y, far_x, far_y, first_x, first_y, own_x, own_y, rest_x, rest_y):
        copy.wait_send()


def forward_kernel(
    own, up, down, bias, resid, par, out, all_ref, active, slope,
    parts, x1, y1, x2, y2, sx, sy, send, recv,
):
    def finish(at, value):
        out[at, :] = (resid[at, :] + value + par[7:8, :]).astype(BF)

    def compute(r):
        z = mm(all_ref[r], up[...]) + bias[...]
        cdf, pdf = phi_parts(z)
        active[r] = (z * cdf).astype(BF)
        slope[r] = cdf + z * pdf
        parts[r] = mm(active[r], down[...]).astype(BF)

    exchange_rows(own, all_ref, parts, compute, finish, (x1, y1, x2, y2, sx, sy), send, recv)


def backward_kernel(
    own, up, down, slope, total, all_ref, dz_all, bias_g, parts, x1, y1, x2, y2, sx, sy, send, recv
):
    bias_g[...] = jnp.zeros_like(bias_g)

    def finish(at, value):
        total[at, :] = value

    def compute(r):
        dz = mm_nt(all_ref[r], down[...]) * slope[r]
        bias_g[...] += jnp.sum(dz, axis=0, keepdims=True)
        dz_all[r] = dz.astype(BF)
        parts[r] = mm_nt(dz_all[r], up[...]).astype(BF)

    exchange_rows(own, all_ref, parts, compute, finish, (x1, y1, x2, y2, sx, sy), send, recv)


VSPEC = pl.BlockSpec(memory_space=pltpu.VMEM)


def lasting(micros):
    return pl.CostEstimate(flops=0, transcendentals=0, bytes_accessed=int(micros * 3.5e6))


def plane_call(kernel, ident, outs, rows, *operands):
    half = rows // 2
    return pl.pallas_call(
        kernel,
        out_shape=outs,
        in_specs=[VSPEC] * len(operands),
        out_specs=(VSPEC,) * len(outs),
        scratch_shapes=[
            pltpu.VMEM((4, rows, D), BF),
            pltpu.VMEM((half, D), BF),
            pltpu.VMEM((half, D), BF),
            pltpu.VMEM((rows, D), BF),
            pltpu.VMEM((rows, D), BF),
            pltpu.VMEM((half, D), BF),
            pltpu.VMEM((half, D), BF),
            pltpu.SemaphoreType.DMA((10,)),
            pltpu.SemaphoreType.DMA((10,)),
        ],
        compiler_params=pltpu.CompilerParams(
            collective_id=ident, has_side_effects=True, vmem_limit_bytes=40 * 1024 * 1024
        ),
        cost_estimate=lasting(40),
    )(*operands)


def mlp_forward(own, up, down, bias, resid, par):
    rows = own.shape[0]
    if lax.axis_size("fsdp") != 4:
        every = lax.all_gather(own, "fsdp", axis=0, tiled=True)
        z = mm(every, up) + bias
        cdf, pdf = phi_parts(z)
        active = (z * cdf).astype(BF)
        part = mm(active, down).astype(BF)
        total = lax.psum_scatter(part, "fsdp", scatter_dimension=0, tiled=True).astype(F32)
        out = (resid + total + par[7]).astype(BF)
        return out, every, active, cdf + z * pdf
    shape = (4, rows, D)
    return plane_call(
        forward_kernel, 1,
        (
            jax.ShapeDtypeStruct((rows, D), BF),
            jax.ShapeDtypeStruct(shape, BF),
            jax.ShapeDtypeStruct(shape, BF),
            jax.ShapeDtypeStruct(shape, F32),
        ),
        rows, own, up, down, bias, resid, par,
    )


def mlp_backward(own, up, down, slope):
    rows = own.shape[0]
    if lax.axis_size("fsdp") != 4:
        every = lax.all_gather(own, "fsdp", axis=0, tiled=True)
        dz = mm_nt(every, down) * slope
        dz_b = dz.astype(BF)
        part = mm_nt(dz_b, up).astype(BF)
        total = lax.psum_scatter(part, "fsdp", scatter_dimension=0, tiled=True).astype(F32)
        return total, every, dz_b, jnp.sum(dz, axis=0, keepdims=True)
    shape = (4, rows, D)
    return plane_call(
        backward_kernel, 2,
        (
            jax.ShapeDtypeStruct((rows, D), F32),
            jax.ShapeDtypeStruct(shape, BF),
            jax.ShapeDtypeStruct(shape, BF),
            jax.ShapeDtypeStruct((1, D), F32),
        ),
        rows, own, up, down, slope,
    )


def weights_kernel(
    own, rows_in, up_in, down_in, full, rows_out, up_out, down_out,
    load, core_s, core_r, p_send, p_recv, f_send, f_recv, z_send, z_recv,
):
    s = lax.axis_index("section")
    f = lax.axis_index("fsdp")
    xn, yn = plane_neighbours()
    dn = 3 - f
    shard, wide = own.shape[1], own.shape[2]
    cut = 640
    left = pl.ds(0, cut)
    right = pl.ds(cut, wide - cut)

    def to(src, dst, send, recv, **where):
        return pltpu.make_async_remote_copy(
            src_ref=src, dst_ref=dst, send_sem=send, recv_sem=recv,
            device_id=where, device_id_type=MESH,
        )

    barrier = pltpu.get_barrier_semaphore()
    z = lax.axis_index("ctx")
    above = {"ctx": lax.rem(z + 1, 4)}
    below = {"ctx": lax.rem(z + 3, 4)}
    for where in ({"section": 1 - s}, {"fsdp": xn}, {"fsdp": yn}, above, below):
        pl.semaphore_signal(barrier, inc=1, device_id=where, device_id_type=MESH)
    pl.semaphore_wait(barrier, 5)
    rows = rows_in.shape[0]
    near_rows, far_rows = pl.ds(rows, rows), pl.ds(0, rows)
    step_one = to(rows_in, rows_out.at[near_rows], z_send.at[0], z_recv.at[0], **above)
    step_two = to(
        rows_out.at[near_rows], rows_out.at[far_rows], z_send.at[1], z_recv.at[1], **above
    )

    @pl.when(z < 3)
    def _():
        step_one.start()

    rows_out[pl.ds(2 * rows, rows), :] = rows_in[...]

    @pl.when(z == 0)
    def _():
        rows_out[near_rows, :] = jnp.zeros(rows_in.shape, BF)

    @pl.when(z < 2)
    def _():
        rows_out[far_rows, :] = jnp.zeros(rows_in.shape, BF)

    def blk(owner):
        return pl.ds(pl.multiple_of(owner * shard, 16), shard)

    def give(p):
        return to(own.at[p], full.at[p, blk(f)], core_s.at[p], core_r.at[p], section=1)

    def keep(p):
        return pltpu.make_async_copy(own.at[p], full.at[p, blk(f)], load.at[p])

    @pl.when(s == 0)
    def _():
        for p in (2, 3, 0, 1):
            give(p).start()
        for p in range(4):
            keep(p).start()
        keep(0).wait()
        keep(1).wait()

    @pl.when(s == 1)
    def _():
        give(2).wait_recv()
        give(3).wait_recv()

    def same(piece, rows, send, recv, cols=slice(None), **where):
        ref = full.at[piece, rows, cols]
        return to(ref, ref, send, recv, **where)

    def hops(k):
        p = 2 * s + k
        return (
            same(p, blk(f), p_send.at[k, 0], p_recv.at[k, 0], fsdp=xn),
            same(p, blk(f), p_send.at[k, 1], p_recv.at[k, 1], fsdp=yn),
            same(p, blk(yn), p_send.at[k, 2], p_recv.at[k, 2], left, fsdp=xn),
            same(p, blk(xn), p_send.at[k, 3], p_recv.at[k, 3], right, fsdp=yn),
        )

    def here(k):
        p = 2 * s + k
        return [
            same(p, blk(owner), f_send.at[k, i], f_recv.at[k, i], section=1 - s)
            for i, owner in enumerate((xn, yn, dn))
        ]

    for k in range(2):
        copies = hops(k)
        copies[0].start()
        copies[1].start()
    down_far = to(down_in, down_out.at[s], core_s.at[4], core_r.at[4], section=1 - s)
    down_near = pltpu.make_async_copy(down_in, down_out.at[s], load.at[4])
    down_far.start()
    down_near.start()
    for j in range(4):
        up_out[j] = up_in[:, pl.ds(j * D, D)]
    for k in range(2):
        copies, across = hops(k), here(k)
        copies[0].wait_recv()
        copies[3].start()
        across[0].start()
        copies[1].wait_recv()
        copies[2].start()
        across[1].start()

    @pl.when(z > 0)
    def _():
        step_one.wait_recv()

    @pl.when((z == 1) | (z == 2))
    def _():
        step_two.start()

    for k in range(2):
        copies, across = hops(k), here(k)
        copies[2].wait_recv()
        copies[3].wait_recv()
        across[2].start()
    for k in range(2):
        for copy in here(k):
            copy.wait()
        for copy in hops(k):
            copy.wait_send()

    @pl.when(s == 0)
    def _():
        for p in range(4):
            give(p).wait_send()
        keep(2).wait()
        keep(3).wait()

    @pl.when(s == 1)
    def _():
        give(0).wait_recv()
        give(1).wait_recv()

    down_near.wait()
    down_far.wait()

    @pl.when(z < 3)
    def _():
        step_one.wait_send()

    @pl.when((z == 1) | (z == 2))
    def _():
        step_two.wait_send()

    @pl.when(z > 1)
    def _():
        step_two.wait_recv()


def first_weights(own, rows_in, up, down):
    dma = pltpu.SemaphoreType.DMA
    return pl.pallas_call(
        weights_kernel,
        out_shape=(
            jax.ShapeDtypeStruct((4, D, WIDE), BF),
            jax.ShapeDtypeStruct((3 * rows_in.shape[0], D), BF),
            jax.ShapeDtypeStruct((4, up.shape[0], D), BF),
            jax.ShapeDtypeStruct((2, D, D), BF),
        ),
        in_specs=[pl.BlockSpec(memory_space=pl.ANY), VSPEC, VSPEC, pl.BlockSpec(memory_space=pl.ANY)],
        out_specs=(VSPEC,) * 4,
        scratch_shapes=[
            dma((5,)), dma((5,)), dma((5,)), dma((2, 4)), dma((2, 4)), dma((2, 3)), dma((2, 3)),
            dma((2,)), dma((2,)),
        ],
        compiler_params=pltpu.CompilerParams(
            collective_id=4, has_side_effects=True, vmem_limit_bytes=32 * 1024 * 1024
        ),
        cost_estimate=lasting(50),
        name="first_weights",
    )(own, rows_in, up, down)


def z_partners():
    z = lax.axis_index("ctx")
    return z + 1 - 2 * lax.rem(z, 2), 3 - z, (z == 1) | (z == 2)


def add_rows(dst, one, two, rows, step):
    @pl.loop(0, rows // step)
    def _(i):
        at = pl.ds(pl.multiple_of(i * step, 16), step)
        dst[at, :] = (one[at, :].astype(F32) + two[at, :].astype(F32)).astype(dst.dtype)


CUTS = ((0, 640, 384), (640, 512, 256))


def reduce_kernel(
    q0, k0, v0, o0, q1, k1, v1, o1, mlp, made0, made1, grad1, halo, d_resid, da_own, wide, par,
    qkv_out, out_out, down_out, up_out, made_out, grad_out,
    own_in, held, up_own, up_far, sent, caught, grad0,
    x1a, y1a, x2a, y2a, sxa, sya, ta, zaa, zba,
    x1b, y1b, x2b, y2b, sxb, syb, tb, zab, zbb,
    load, core_s, core_r, p_send, p_recv, z_send, z_recv, h_send, h_recv, x_send, x_recv,
):
    s = lax.axis_index("section")
    f = lax.axis_index("fsdp")
    xn, yn = plane_neighbours()
    dn = 3 - f
    side, across, inner = z_partners()
    pieces = ((q0, k0, v0, o0), (q1, k1, v1, o1))
    sets = (
        (x1a, y1a, x2a, y2a, sxa, sya, ta, zaa, zba),
        (x1b, y1b, x2b, y2b, sxb, syb, tb, zab, zbb),
    )
    shard = out_out.shape[0]
    rows = da_own.shape[0]
    z = lax.axis_index("ctx")
    above, below = {"ctx": lax.rem(z + 1, 4)}, {"ctx": lax.rem(z + 3, 4)}

    def to(src, dst, send, recv, **where):
        return pltpu.make_async_remote_copy(
            src_ref=src, dst_ref=dst, send_sem=send, recv_sem=recv,
            device_id=where, device_id_type=MESH,
        )

    barrier = pltpu.get_barrier_semaphore()
    partners = ({"section": 1 - s}, {"fsdp": xn}, {"fsdp": yn}, above, below)
    for where in partners:
        pl.semaphore_signal(barrier, inc=1, device_id=where, device_id_type=MESH)
    pl.semaphore_wait(barrier, 5)

    def blk(owner):
        return pl.ds(pl.multiple_of(owner * shard, 16), shard)

    def by_core(act):
        for core in range(2):
            pl.when(s == core)(functools.partial(act, core))

    def far(j, src):
        return to(src, held.at[j], core_s.at[j], core_r.at[j], section=1 - s)

    def near(j, src):
        return pltpu.make_async_copy(src, own_in.at[j % 2], load.at[j])

    def bufs(c):
        return tuple(ref.at[c // 2] for ref in sets[c % 2])

    def plane(c):
        x1, y1, x2, y2, sx, sy = bufs(c)[:6]
        own = held.at[c // 2]
        at, width, cut = CUTS[c % 2]
        left, right = pl.ds(at, cut), pl.ds(at + cut, width - cut)
        to_left, to_right = pl.ds(0, cut), pl.ds(cut, width - cut)
        sems = [(p_send.at[c, i], p_recv.at[c, i]) for i in range(6)]
        return (
            to(own.at[blk(dn), left], x1, *sems[0], fsdp=xn),
            to(own.at[blk(dn), right], y1, *sems[1], fsdp=yn),
            to(own.at[blk(xn), left], x2.at[:, to_left], *sems[2], fsdp=xn),
            to(own.at[blk(yn), right], y2.at[:, to_right], *sems[3], fsdp=yn),
            to(sx, x2.at[:, to_right], *sems[4], fsdp=xn),
            to(sy, y2.at[:, to_left], *sems[5], fsdp=yn),
        )

    def along(c):
        t, za, zb = bufs(c)[6:]
        sems = [(z_send.at[c, i], z_recv.at[c, i]) for i in range(3)]
        return (
            to(t, za, *sems[0], ctx=side),
            to(za, zb, *sems[1], ctx=across),
            to(zb, zb, *sems[2], ctx=side),
        )

    def join(j):
        far(j, q0).wait_recv()
        near(j, q0).wait()
        add_rows(held.at[j], own_in.at[j % 2], held.at[j], 4 * shard, shard)
        for c in (2 * j, 2 * j + 1):
            for copy in plane(c)[:4]:
                copy.start()
        if j < 2:
            by_core(lambda core: near(j + 2, pieces[core][j + 2]).start())

    def second(c):
        copies = plane(c)
        x1, y1, _, _, sx, sy = bufs(c)[:6]
        at, width, cut = CUTS[c % 2]
        own = held.at[c // 2]
        copies[0].wait_recv()
        add_rows(sy, own.at[blk(yn), pl.ds(at, cut)], x1, shard, shard)
        copies[5].start()
        copies[1].wait_recv()
        add_rows(sx, own.at[blk(xn), pl.ds(at + cut, width - cut)], y1, shard, shard)
        copies[4].start()

    def third(c):
        copies = plane(c)
        _, _, x2, y2, _, _, t, _, _ = bufs(c)
        at, width, _ = CUTS[c % 2]
        for copy in copies[2:]:
            copy.wait_recv()
        t[...] = (
            held[c // 2, blk(f), pl.ds(at, width)].astype(F32)
            + x2[...].astype(F32)
            + y2[...].astype(F32)
        ).astype(BF)

        @pl.when(jnp.logical_not(inner))
        def _():
            along(c)[0].start()

    def inward(c):
        @pl.when(inner)
        def _():
            t, za, _ = bufs(c)[6:]
            copies = along(c)
            copies[0].wait_recv()
            add_rows(za, t, za, shard, shard)
            copies[1].start()

    def crossed(c):
        @pl.when(inner)
        def _():
            _, za, zb = bufs(c)[6:]
            copies = along(c)
            copies[1].wait_recv()
            add_rows(zb, za, zb, shard, shard)
            copies[2].start()

    def last(c):
        at, width, _ = CUTS[c % 2]
        j = c // 2

        @pl.when(jnp.logical_not(inner))
        def _():
            along(c)[2].wait_recv()

        if j < 3:
            width = min(width, D - at)
            qkv_out[:, pl.ds(j * D + at, width)] = bufs(c)[8][:, pl.ds(0, width)]
        else:
            out_out[:, pl.ds(at, width)] = bufs(c)[8][...]

    half = down_out.shape[0] // 2
    mine = pl.ds(pl.multiple_of(s * half, 16), half)
    down_far = to(mlp.at[0], down_out.at[mine], core_s.at[4], core_r.at[4], section=1 - s)
    down_near = pltpu.make_async_copy(mlp.at[0], down_out.at[mine], load.at[4])
    far_up = to(mlp.at[1], up_far, core_s.at[5], core_r.at[5], section=1 - s)
    near_up = pltpu.make_async_copy(mlp.at[1], up_own, load.at[5])

    def lay_up():
        far_up.wait_recv()
        near_up.wait()

        @pl.when(s == 1)
        def _():
            for k in range(2):
                up_out[:, pl.ds(k * D, D)] = up_far[pl.ds(k * shard, shard), :]
                up_out[:, pl.ds((2 + k) * D, D)] = up_own[pl.ds(k * shard, shard), :]

    back_one = to(halo.at[pl.ds(0, rows)], caught.at[0], h_send.at[0], h_recv.at[0], **below)
    back_two = to(sent, caught.at[1], h_send.at[1], h_recv.at[1], **below)

    def back():
        @pl.when(z < 3)
        def _():
            back_one.wait_recv()

        @pl.when(z == 3)
        def _():
            caught[0] = jnp.zeros_like(caught[0])

        @pl.when(z > 0)
        def _():
            add_rows(sent, halo.at[pl.ds(rows, rows)], caught.at[0], rows, rows)
            back_two.start()

    made_far = (
        to(made1, made_out.at[0], x_send.at[0], x_recv.at[0], section=1),
        to(made0, made_out.at[1], x_send.at[0], x_recv.at[0], section=0),
    )
    grad_far = (
        to(grad1, grad_out.at[0], x_send.at[1], x_recv.at[1], section=1),
        to(grad0, grad_out.at[1], x_send.at[1], x_recv.at[1], section=0),
    )
    made_near = (
        pltpu.make_async_copy(made0, made_out.at[0], load.at[6]),
        pltpu.make_async_copy(made1, made_out.at[1], load.at[6]),
    )
    grad_near = pltpu.make_async_copy(grad1, grad_out.at[1], load.at[7])

    def back_end():
        @pl.when(z < 3)
        def _():
            back_two.wait_recv()

        @pl.when(z == 3)
        def _():
            caught[1] = jnp.zeros_like(caught[1])

        unit, inv = norm_parts(wide[...].astype(F32))
        da = da_own[...] + caught[1].astype(F32)
        grad0[...] = d_resid[...] + norm_back(da, par[0:1, :], unit, inv)

        @pl.when(s == 0)
        def _():
            grad_out[0] = grad0[...]

        @pl.when(s == 1)
        def _():
            grad_far[1].start()

    @pl.when(s == 0)
    def _():
        made_far[0].start()
        grad_far[0].start()
        made_near[0].start()

    @pl.when(s == 1)
    def _():
        made_far[1].start()
        made_near[1].start()
        grad_near.start()

    @pl.when(z > 0)
    def _():
        back_one.start()

    for j in range(4):
        by_core(lambda core: far(j, pieces[1 - core][j]).start())
        if j < 2:
            by_core(lambda core: near(j, pieces[core][j]).start())
    for copy in (down_far, down_near, far_up, near_up):
        copy.start()

    join(0)
    for c in range(12):
        if c in (1, 3, 5):
            join((c + 1) // 2)
        if c < 8:
            second(c)
        if 1 <= c <= 8:
            third(c - 1)
        if 2 <= c <= 9:
            inward(c - 2)
        if 3 <= c <= 10:
            crossed(c - 3)
        if c >= 4:
            last(c - 4)
        if c == 2:
            back()
        if c == 4:
            lay_up()
        if c == 6:
            back_end()

    down_near.wait()
    down_far.wait()
    far_up.wait_send()

    @pl.when(s == 0)
    def _():
        made_near[0].wait()
        made_far[0].wait_send()
        grad_far[0].wait_send()
        made_far[1].wait_recv()
        grad_far[1].wait_recv()

    @pl.when(s == 1)
    def _():
        made_near[1].wait()
        grad_near.wait()
        made_far[1].wait_send()
        grad_far[1].wait_send()
        made_far[0].wait_recv()
        grad_far[0].wait_recv()

    @pl.when(z > 0)
    def _():
        back_one.wait_send()
        back_two.wait_send()

    for j in range(4):
        far(j, q0).wait_send()
    for c in range(8):
        for copy in plane(c):
            copy.wait_send()

    @pl.when(inner)
    def _():
        for c in range(8):
            for copy in along(c)[1:]:
                copy.wait_send()

    @pl.when(jnp.logical_not(inner))
    def _():
        for c in range(8):
            along(c)[0].wait_send()


def reduce_both(zero, one, mlp, made, grad1, halo, d_resid, da_own, wide, par):
    shard = D // 4
    rows = da_own.shape[0]
    dma = pltpu.SemaphoreType.DMA
    any_spec = pl.BlockSpec(memory_space=pl.ANY)

    def buf(*shape):
        return pltpu.VMEM(shape, BF)

    def part(_, width, cut):
        wide_buf = buf(4, shard, width)
        return [
            buf(4, shard, cut), buf(4, shard, width - cut), wide_buf, wide_buf,
            buf(4, shard, width - cut), buf(4, shard, cut), wide_buf, wide_buf, wide_buf,
        ]

    shapes = ((shard, 3 * D), (shard, WIDE), (D, D), (shard, 4 * D), (2, rows, D))
    return pl.pallas_call(
        reduce_kernel,
        out_shape=(
            *(jax.ShapeDtypeStruct(shape, BF) for shape in shapes),
            jax.ShapeDtypeStruct((2, rows, D), F32),
        ),
        in_specs=[any_spec] * 12 + [VSPEC] * 5,
        out_specs=(VSPEC,) * 6,
        scratch_shapes=[
            buf(2, D, WIDE), buf(4, D, WIDE), buf(D // 2, D), buf(D // 2, D), buf(rows, D),
            buf(2, rows, D), pltpu.VMEM((rows, D), F32), *part(*CUTS[0]), *part(*CUTS[1]),
            dma((8,)), dma((6,)), dma((6,)), dma((8, 6)), dma((8, 6)), dma((8, 3)), dma((8, 3)),
            dma((2,)), dma((2,)), dma((2,)), dma((2,)),
        ],
        compiler_params=pltpu.CompilerParams(
            collective_id=3, has_side_effects=True, vmem_limit_bytes=60 * 1024 * 1024
        ),
        cost_estimate=lasting(120),
        name="reduce_both",
    )(*zero, *one, mlp, *made, grad1, halo, d_resid, da_own, wide, par)


def final_kernel(qkv, out, mine, far, down_one, up_one, qkv_f, out_f, down_f, up_f, small):
    s = lax.axis_index("section")
    half = mine.shape[1]
    shard = qkv.shape[0]
    qkv_f[...] = qkv[...].astype(F32)
    out_f[...] = out[:, pl.ds(0, D)].astype(F32)
    pick_row = (
        lax.broadcasted_iota(jnp.int32, (16, 128), 1)
        == lax.broadcasted_iota(jnp.int32, (16, 128), 0) + (D - TAIL)
    )
    small[...] = mm_nt(pick_row.astype(F32).astype(BF), out[:, pl.ds(TAIL, 128)])

    @pl.when(s == 0)
    def _():
        down_f[pl.ds(0, half), :] = mine[0].astype(F32)
        down_f[pl.ds(half, half), :] = far[0].astype(F32)
        for k in range(2):
            at = pl.ds(k * shard, shard)
            up_f[:, pl.ds(k * D, D)] = mine[1, at, :].astype(F32)
            up_f[:, pl.ds((2 + k) * D, D)] = far[1, at, :].astype(F32)

    @pl.when(s == 1)
    def _():
        down_f[...] = down_one[...].astype(F32)
        up_f[...] = up_one[...].astype(F32)


def final_layouts(qkv, out, mine, far, down_one, up_one):
    shard = qkv.shape[0]
    outs = (qkv.shape, (shard, D), down_one.shape, up_one.shape, (16, shard))
    return pl.pallas_call(
        final_kernel,
        out_shape=tuple(jax.ShapeDtypeStruct(shape, F32) for shape in outs),
        in_specs=[VSPEC] * 6,
        out_specs=(VSPEC,) * 5,
        compiler_params=pltpu.CompilerParams(vmem_limit_bytes=48 * 1024 * 1024),
        cost_estimate=lasting(10),
        name="final_layouts",
    )(qkv, out, mine, far, down_one, up_one)


def halves_pair(down, up):
    s = lax.axis_index("section")
    both = jnp.stack([down, up])
    both = both.reshape(2, 2, both.shape[1] // 2, D)
    keep = lax.dynamic_index_in_dim(both, s, 1, keepdims=False)
    give = lax.dynamic_index_in_dim(both, 1 - s, 1, keepdims=False)
    return (keep.astype(F32) + on_chip(give).astype(F32)).astype(BF)


def halves_settle(zero, one):
    s = lax.axis_index("section")
    mine, far = pick(s, zero, one), on_chip(pick(s, one, zero))
    return jnp.concatenate([pick(s, mine, far), pick(s, far, mine)], axis=1).astype(F32)


def reduce_plain(pieces):
    s = lax.axis_index("section")
    pair = ("fsdp", "section")
    a = jnp.stack([lax.psum_scatter(p, pair, scatter_dimension=0, tiled=True) for p in pieces])
    a = lax.psum(a, "ctx")
    far = on_chip(a)
    return jnp.concatenate([pick(s, a, far), pick(s, far, a)], axis=1)


def shift(value, steps):
    count = lax.axis_size("ctx")
    pairs = [(i, i + steps) for i in range(count) if 0 <= i + steps < count]
    return lax.ppermute(value, "ctx", pairs)


def with_halo(own, chunks):
    parts = [own]
    for _ in range(chunks):
        parts.append(shift(parts[-1], 1))
    return jnp.concatenate(parts[::-1], axis=0)


def return_halo(halo, chunks, rows):
    carried = None
    for far in range(chunks):
        mine = halo[far * rows : (far + 1) * rows]
        carried = mine if carried is None else mine + carried
        carried = shift(carried.astype(BF), -1).astype(F32)
    return carried


def pick(s, first, second):
    return jnp.where(s == 0, first, second)


def on_chip(value):
    return lax.ppermute(value, "section", SWAP)


def both_layers(own, s):
    other = on_chip(own)
    return pick(s, own, other), pick(s, other, own)


def flat(values):
    return values.reshape(-1, values.shape[-1])


def widen(values):
    return jnp.pad(values, ((0, 0), (0, WIDE - D)))


TAIL = 1024


def scores_forward(q, k, v, bias, lanes):
    outs = []
    for low in (True, False):
        one = jnp.where((lanes < HD) if low else (lanes >= HD), q, jnp.zeros_like(q))
        weight = jnp.exp(mm_nt(one, k) + bias)
        prob = weight * (1.0 / jnp.sum(weight, axis=-1, keepdims=True))
        outs.append(mm(prob.astype(BF), v))
    return jnp.where(lanes < HD, outs[0], outs[1]).astype(BF)


def scores_backward(q, k, v, grad, bias_t, lanes):
    dqs, dk, dv = [], 0.0, 0.0
    for low in (True, False):
        mine = (lanes < HD) if low else (lanes >= HD)
        one = jnp.where(mine, q, jnp.zeros_like(q))
        g = jnp.where(mine, grad, jnp.zeros_like(grad))
        weight = jnp.exp(mm_nt(k, one) + bias_t)
        prob = weight * (1.0 / jnp.sum(weight, axis=0, keepdims=True))
        d_prob = mm_nt(v, g)
        row = jnp.sum(prob * d_prob, axis=0, keepdims=True)
        d_score = (prob * (d_prob - row)).astype(BF)
        dqs.append(mm_tn(d_score, k))
        dk = dk + mm(d_score, one)
        dv = dv + mm(prob.astype(BF), g)
    dq = jnp.where(lanes < HD, dqs[0], dqs[1]) * SCALE
    return dq.astype(BF), dk.astype(BF), dv.astype(BF)


def lane_tile(i):
    return pl.ds(pl.multiple_of(i * 128, 128), 128)


def widened(row):
    return jnp.concatenate([row, jnp.zeros((row.shape[0], WIDE - D), row.dtype)], axis=1)


def block_kernel(
    wide, wq, wk, wv, wo, bias, normed, q_ref, k_ref, v_ref, att, resid, second, par, held
):
    rows = resid.shape[0]
    total = wide.shape[0]
    pick_row = (
        lax.broadcasted_iota(jnp.int32, (16, 128), 1)
        == lax.broadcasted_iota(jnp.int32, (16, 128), 0) + (D - TAIL)
    )
    par[...] = mm_nt(pick_row.astype(F32).astype(BF), wo[:, pl.ds(TAIL, 128)])

    @pl.loop(0, total // rows)
    def _(i):
        at = pl.ds(pl.multiple_of(i * rows, 16), rows)
        unit, _ = norm_parts(wide[at, :].astype(F32))
        low = (unit * par[0:1, :] + par[2:3, :]).astype(BF)
        normed[at, :] = low
        k_ref[at, :] = mm(low, wk[...]).astype(BF)
        v_ref[at, :] = (mm(low, wv[...]) + widened(par[4:5, :])).astype(BF)

    own = pl.ds(total - rows, rows)
    q_ref[...] = (mm(normed[own, :], wq[...]) + widened(par[3:4, :])).astype(BF)
    lanes = lax.broadcasted_iota(jnp.int32, (rows, 128), 1)

    @pl.loop(0, WIDE // 128)
    def _(i):
        at = lane_tile(i)
        held[:, at] = scores_forward(
            q_ref[:, at] * jnp.asarray(SCALE, BF), k_ref[:, at], v_ref[:, at], bias[...], lanes
        )

    att[...] = held[:, pl.ds(0, D)]
    res = wide[own, :].astype(F32) + mm(att[...], wo[:, pl.ds(0, D)]) + par[5:6, :]
    resid[...] = res
    unit, _ = norm_parts(res)
    second[...] = (unit * par[1:2, :] + par[6:7, :]).astype(BF)


def weight_specs(weights):
    if weights.ndim == 3:
        return [pl.BlockSpec((None, D, WIDE), lambda i, p=p: (p, 0, 0)) for p in range(4)]
    return [pl.BlockSpec((D, WIDE), lambda i, p=p: (0, p)) for p in range(4)]


def whole(shape):
    return pl.BlockSpec(shape, lambda i: (0,) * len(shape))


def block_forward(wide, weights, bias):
    total, rows = wide.shape[0], bias.shape[0]
    outs = (
        ((total, D), BF), ((rows, WIDE), BF), ((total, WIDE), BF), ((total, WIDE), BF),
        ((rows, D), BF), ((rows, D), F32), ((rows, D), BF), ((16, D), F32),
    )
    return pl.pallas_call(
        block_kernel,
        out_shape=tuple(jax.ShapeDtypeStruct(*out) for out in outs),
        grid=(1,),
        in_specs=[whole(wide.shape), *weight_specs(weights), whole(bias.shape)],
        out_specs=tuple(whole(shape) for shape, _ in outs),
        scratch_shapes=[pltpu.VMEM((rows, WIDE), BF)],
        compiler_params=pltpu.CompilerParams(vmem_limit_bytes=56 * 1024 * 1024),
        cost_estimate=lasting(22),
        name="block_forward",
    )(wide, weights, weights, weights, weights, bias)


def block_back_kernel(
    d_second, up, resid, wide, q_ref, k_ref, v_ref, att, ffb_rows, wq, wk, wv, wo, par, bias_t,
    d_resid, dq_ref, dk_ref, dv_ref, da_own, da_halo, left, right, held, sums,
):
    rows = resid.shape[0]
    total = wide.shape[0]
    own = total - rows

    def total_of(values):
        return jnp.sum(values, axis=0, keepdims=True)

    upstream = up[...].astype(F32)
    unit, inv = norm_parts(resid[...])
    grad = upstream + norm_back(d_second[...], par[1:2, :], unit, inv)
    d_resid[...] = grad
    sums[1:2, :] = total_of(d_second[...] * unit)
    sums[5:6, :] = total_of(grad)
    sums[6:7, :] = total_of(d_second[...])
    sums[7:8, :] = total_of(upstream)
    sums[8:16, :] = ffb_rows[...]
    low = grad.astype(BF)
    right[pl.ds(0, rows), :] = jnp.zeros((rows, WIDE), BF)
    right[pl.ds(0, rows), pl.ds(0, D)] = low
    right[pl.ds(rows, 16), :] = (
        lax.broadcasted_iota(jnp.int32, (16, WIDE), 1)
        == lax.broadcasted_iota(jnp.int32, (16, WIDE), 0) + D
    ).astype(F32).astype(BF)
    held[...] = jnp.zeros((rows, WIDE), BF)
    held[:, pl.ds(0, D)] = mm_nt(low, wo[:, pl.ds(0, D)]).astype(BF)
    lanes = lax.broadcasted_iota(jnp.int32, (rows, 128), 1)

    @pl.loop(0, WIDE // 128)
    def _(i):
        at = lane_tile(i)
        dq_ref[:, at], dk_ref[:, at], dv_ref[:, at] = scores_backward(
            q_ref[:, at] * jnp.asarray(SCALE, BF), k_ref[:, at], v_ref[:, at], held[:, at],
            bias_t[...], lanes,
        )

    sums[3:4, :] = total_of(dq_ref[...].astype(F32))[:, :D]
    sums[4:5, :] = total_of(dv_ref[...].astype(F32))[:, :D]
    sums[0:1, :] = jnp.zeros((1, D), F32)
    sums[2:3, :] = jnp.zeros((1, D), F32)

    def back(at):
        da = mm_nt(dk_ref[at, :], wk[...]) + mm_nt(dv_ref[at, :], wv[...])
        return da

    def count(da, at):
        unit, _ = norm_parts(wide[at, :].astype(F32))
        sums[0:1, :] += total_of(da * unit)
        sums[2:3, :] += total_of(da)

    @pl.loop(0, own // rows)
    def _(i):
        at = pl.ds(pl.multiple_of(i * rows, 16), rows)
        da = back(at)
        da_halo[at, :] = da.astype(BF)
        count(da, at)

    at = pl.ds(own, rows)
    da = back(at) + mm_nt(dq_ref[...], wq[...])
    da_own[...] = da
    count(da, at)
    left[pl.ds(0, rows), :] = att[...]
    left[pl.ds(rows, 16), :] = sums[...].astype(BF)


def block_backward(d_second, up, resid, wide, q, k, v, att, ffb_rows, weights, par, bias_t):
    total, rows = wide.shape[0], resid.shape[0]
    outs = (
        ((rows, D), F32), ((rows, WIDE), BF), ((total, WIDE), BF), ((total, WIDE), BF),
        ((rows, D), F32), ((total - rows, D), BF), ((rows + 16, D), BF), ((rows + 16, WIDE), BF),
    )
    before = (d_second, up, resid, wide, q, k, v, att, ffb_rows)
    return pl.pallas_call(
        block_back_kernel,
        out_shape=tuple(jax.ShapeDtypeStruct(*out) for out in outs),
        grid=(1,),
        in_specs=[
            *(whole(value.shape) for value in before), *weight_specs(weights),
            whole(par.shape), whole(bias_t.shape),
        ],
        out_specs=tuple(whole(shape) for shape, _ in outs),
        scratch_shapes=[pltpu.VMEM((rows, WIDE), BF), pltpu.VMEM((16, D), F32)],
        compiler_params=pltpu.CompilerParams(vmem_limit_bytes=60 * 1024 * 1024),
        cost_estimate=lasting(38),
        name="block_backward",
    )(*before, weights, weights, weights, weights, par, bias_t)


def on_device(
    inputs, segments, cotangent, qkv_weight, out_weight, up_weight, down_weight,
    norm_gains, biases, ff_bias,
):
    rows = inputs.shape[2]
    length = segments.shape[2]
    chunks = min((length // 2 - 1 + rows - 1) // rows, lax.axis_size("ctx") - 1)
    reach = chunks * rows
    s = lax.axis_index("section")
    f = lax.axis_index("fsdp")
    nf = lax.axis_size("fsdp")
    shard = D // nf
    ff_here = ff_bias.shape[1]
    per_row = ff_here // shard
    pair = ("fsdp", "section")
    fits = nf == 4 and lax.axis_size("ctx") == 4 and chunks == 2

    own_in = lax.dynamic_index_in_dim(inputs, s, 0, keepdims=False)[0]
    own_cot = lax.dynamic_index_in_dim(cotangent, s, 0, keepdims=False)[0]
    seg = lax.dynamic_index_in_dim(segments, s, 0, keepdims=False)[0]
    start = lax.axis_index("ctx") * rows
    key_seg = lax.dynamic_slice_in_dim(
        jnp.pad(seg, (reach, 0), constant_values=-1), start, reach + rows, 0
    )
    allowed = (key_seg[reach:, None] == key_seg[None, :]) & (
        jnp.arange(reach + rows, dtype=jnp.int32)[None, :] - reach
        <= jnp.arange(rows, dtype=jnp.int32)[:, None]
    )

    bias = jnp.where(allowed, 0.0, -1e30).astype(F32)
    bias_t = bias.T

    small = jnp.concatenate(
        [norm_gains[0].T, biases[0].T, ff_bias[0].reshape(per_row, shard).T], axis=1
    )
    packed = jnp.stack(
        [
            widen(qkv_weight[0][:, :D]),
            widen(qkv_weight[0][:, D : 2 * D]),
            widen(qkv_weight[0][:, 2 * D :]),
            jnp.concatenate(
                [out_weight[0], small, jnp.zeros((shard, WIDE - D - 8 - per_row), BF)], axis=1
            ),
        ]
    )
    if fits:
        zero, wide_in, up_blocks, down_w = first_weights(
            packed, own_in, up_weight[0], down_weight[0]
        )
        packed, zero = lax.optimization_barrier((packed, zero))
    else:
        up_blocks = up_weight[0].reshape(shard, nf, ff_here).transpose(1, 0, 2)
        down_w = both_layers(down_weight[0], s)
        wide_in = with_halo(own_in, chunks)
    half = shard // 2
    halves = packed.reshape(4, 2, half, WIDE)
    keep = lax.dynamic_index_in_dim(halves, s, 1, keepdims=False)
    give = lax.dynamic_index_in_dim(halves, 1 - s, 1, keepdims=False)

    def gathered(part):
        rows_first = part.transpose(1, 0, 2).reshape(half, 4 * WIDE)
        return lax.all_gather(rows_first, pair, axis=0, tiled=True)

    recv = on_chip(give)
    one = gathered(pick(s, recv, keep))
    if not fits:
        zero = gathered(pick(s, keep, recv))
    up_own = lax.all_to_all(
        up_blocks, "fsdp", split_axis=0, concat_axis=0, tiled=True
    ).reshape(D, ff_here)

    weights = (zero, one)

    kept = []
    current = own_in
    produced = []
    for layer in range(2):
        wide = with_halo(current, chunks) if layer else wide_in
        normed, q, k, v, att, resid, second, par = block_forward(wide, weights[layer], bias)
        if layer == 0:
            up_own, second = lax.optimization_barrier((up_own, second))
            up_w = both_layers(up_own, s)
        ffb = lax.dynamic_slice(par, (8, f * shard), (per_row, shard)).reshape(1, ff_here)
        current, second_all, active, slope = mlp_forward(
            second, up_w[layer], down_w[layer], ffb, resid, par
        )
        produced.append(current)
        kept.append((wide, normed, q, k, v, att, resid, second_all, slope, active, par))

    upstream = own_cot
    derived = [None, None]
    parts = [None, None]
    mlp_sums = [None, None]
    for layer in (1, 0):
        wide, normed, q, k, v, att, resid, second_all, slope, active, par = kept[layer]
        d_second, up_all, dz_b, ffb_g = mlp_backward(upstream, up_w[layer], down_w[layer], slope)
        down_g = mm_tn(flat(active), flat(up_all))
        up_g = mm_tn(flat(second_all), flat(dz_b))
        ffb_rows = lax.dynamic_update_slice(
            jnp.zeros((8, D), F32), ffb_g.reshape(per_row, shard), (0, f * shard)
        )
        d_resid, dq, dk, dv, da_own, da_halo, left, right = block_backward(
            d_second, upstream, resid, wide, q, k, v, att, ffb_rows, weights[layer], par, bias_t
        )

        def through_norm(late):
            unit, inv = norm_parts(wide[reach:].astype(F32))
            return d_resid + norm_back(da_own + late, par[0], unit, inv)

        if layer == 1 or not fits:
            derived[layer] = through_norm(return_halo(da_halo, chunks, rows))
            upstream_next = derived[layer].astype(BF)
        pieces = (
            mm_tn(normed[reach:], dq).astype(BF),
            mm_tn(normed, dk).astype(BF),
            mm_tn(normed, dv).astype(BF),
            mm_tn(left, right).astype(BF),
        )
        parts[layer] = pieces
        up_g = lax.all_to_all(
            up_g.astype(BF).reshape(nf, shard, ff_here), "fsdp",
            split_axis=0, concat_axis=0, tiled=True,
        ).reshape(nf * shard * ff_here // D, D)
        down_g = down_g.astype(BF)
        if layer == 0:
            down_g, up_g, _ = lax.optimization_barrier((down_g, up_g, dq))
        halves = halves_pair(down_g, up_g)
        if layer == 1:
            _, upstream_next = lax.optimization_barrier((halves, upstream_next))
        else:
            halves, mlp_sums[1] = lax.optimization_barrier((halves, mlp_sums[1]))
        mlp_sums[layer] = lax.psum(halves, "ctx")
        if layer == 1:
            upstream = upstream_next

    if fits:
        qkv_g, out_g, down_one, up_one, made, grads = reduce_both(
            parts[0], parts[1], mlp_sums[1], produced, derived[1], da_halo, d_resid, da_own,
            wide[reach:], par,
        )
        late_sum, qkv_g = lax.optimization_barrier((mlp_sums[0], qkv_g))
        far = lax.ppermute(late_sum, "section", [(1, 0)])
        qkv_g, out_g, grad_down, grad_up, small = final_layouts(
            qkv_g, out_g, late_sum, far, down_one, up_one
        )
        made, grads = made[None, :, None], grads[None, :, None]
    else:
        a_tot = pick(s, reduce_plain(parts[0]), reduce_plain(parts[1])).astype(F32)
        qkv_g = jnp.concatenate([a_tot[i, :, :D] for i in range(3)], axis=1)
        out_g = a_tot[3, :, :D]
        small = a_tot[3, :, D : D + 16].T
        grad_down, grad_up = split_up(halves_settle(*mlp_sums), nf, shard)
        made, grads = both_micros(produced, s), both_micros(derived, s)
    return (
        made,
        grads,
        qkv_g[None],
        out_g[None],
        grad_up[None],
        grad_down[None],
        small[None, :2],
        small[None, 2:8],
        small[8 : 8 + per_row].reshape(1, ff_here),
    )


def split_up(both, nf, shard):
    up = both[1].reshape(nf, shard, -1)
    return both[0], up.transpose(1, 0, 2).reshape(shard, -1)


def both_micros(layers, s):
    to_zero = lax.ppermute(layers[0], "section", [(1, 0)])
    to_one = lax.ppermute(layers[1], "section", [(0, 1)])
    out = jnp.stack([pick(s, layers[0], to_one), pick(s, to_zero, layers[1])])
    return out[None, :, None]


def solution(mesh):
    return jax.shard_map(
        on_device,
        mesh=mesh,
        in_specs=(
            P(None, "fsdp", "ctx", None),
            P(None, "fsdp", None),
            P(None, "fsdp", "ctx", None),
            P("section", "fsdp", None),
            P("section", "fsdp", None),
            P("section", "fsdp", None),
            P("section", "fsdp", None),
            P("section", None, "fsdp"),
            P("section", None, "fsdp"),
            P("section", "fsdp"),
        ),
        out_specs=(
            P("section", None, "fsdp", "ctx", None),
            P("section", None, "fsdp", "ctx", None),
            P("section", "fsdp", None),
            P("section", "fsdp", None),
            P("section", "fsdp", None),
            P("section", "fsdp", None),
            P("section", None, "fsdp"),
            P("section", None, "fsdp"),
            P("section", "fsdp"),
        ),
        check_vma=False,
    )
```

```python
import functools
import math

import jax
import jax.numpy as jnp
from jax import lax
from jax.experimental import pallas as pl
from jax.experimental.pallas import tpu as pltpu
from jax.sharding import PartitionSpec as P

D = 1088
HD = 64
F32 = jnp.float32
BF = jnp.bfloat16
SCALE = 1.0 / math.sqrt(HD)
WIDE = 1152
MESH = pl.DeviceIdType.MESH
SWAP = [(0, 1), (1, 0)]


def mm(a, b):
    return jnp.dot(a, b, preferred_element_type=F32)


def mm_nt(a, b):
    return lax.dot_general(a, b, (((1,), (1,)), ((), ())), preferred_element_type=F32)


def mm_tn(a, b):
    return lax.dot_general(a, b, (((0,), (0,)), ((), ())), preferred_element_type=F32)


def norm_parts(values):
    center = jnp.mean(values, axis=-1, keepdims=True)
    offset = values - center
    spread = jnp.mean(offset * offset, axis=-1, keepdims=True)
    inv = lax.rsqrt(spread + 1e-05)
    return offset * inv, inv


def norm_back(grad, gain, unit, inv):
    dn = grad * gain
    return inv * (
        dn
        - jnp.mean(dn, axis=-1, keepdims=True)
        - unit * jnp.mean(dn * unit, axis=-1, keepdims=True)
    )


def phi_parts(z):
    cdf = 0.5 * (1.0 + lax.erf(z * (1.0 / math.sqrt(2.0))))
    pdf = jnp.exp(-0.5 * z * z) * (1.0 / math.sqrt(2.0 * math.pi))
    return cdf, pdf


def plane_neighbours():
    f = lax.axis_index("fsdp")
    x = lax.rem(f, 2)
    y = f // 2
    return y * 2 + (1 - x), (1 - y) * 2 + x


def plane_barrier(xn, yn):
    barrier = pltpu.get_barrier_semaphore()
    for nb in (xn, yn):
        pl.semaphore_signal(barrier, inc=1, device_id={"fsdp": nb}, device_id_type=MESH)
    pl.semaphore_wait(barrier, 2)


def remote(src, dst, send, recv, nb):
    return pltpu.make_async_remote_copy(
        src_ref=src, dst_ref=dst, send_sem=send, recv_sem=recv,
        device_id={"fsdp": nb}, device_id_type=MESH,
    )


def exchange_rows(own_ref, all_ref, parts, compute, finish, bufs, send, recv):
    x1, y1, x2, y2, sum_x, sum_y = bufs
    xn, yn = plane_neighbours()
    half = own_ref.shape[0] // 2
    top, low = pl.ds(0, half), pl.ds(half, half)
    plane_barrier(xn, yn)

    to_x = remote(own_ref, all_ref.at[1], send.at[0], recv.at[0], xn)
    to_y = remote(own_ref, all_ref.at[2], send.at[1], recv.at[1], yn)
    far_x = remote(all_ref.at[2, top], all_ref.at[3, top], send.at[2], recv.at[2], xn)
    far_y = remote(all_ref.at[1, low], all_ref.at[3, low], send.at[3], recv.at[3], yn)
    first_x = remote(parts.at[3, top], x1, send.at[4], recv.at[4], xn)
    first_y = remote(parts.at[3, low], y1, send.at[5], recv.at[5], yn)
    own_x = remote(parts.at[1, top], x2.at[top], send.at[6], recv.at[6], xn)
    own_y = remote(parts.at[2, low], y2.at[low], send.at[7], recv.at[7], yn)
    rest_x = remote(sum_x, x2.at[low], send.at[8], recv.at[8], xn)
    rest_y = remote(sum_y, y2.at[top], send.at[9], recv.at[9], yn)

    to_x.start()
    to_y.start()
    all_ref[0] = own_ref[...]

    @pl.loop(0, 4)
    def _(i):
        @pl.when(i == 1)
        def _():
            to_x.wait_recv()
            far_y.start()
            to_y.wait_recv()
            far_x.start()

        @pl.when(i == 2)
        def _():
            own_x.start()
            far_x.wait_recv()
            far_y.wait_recv()

        @pl.when(i == 3)
        def _():
            first_x.start()
            first_y.start()

        compute(i + (i // 2) * (1 - 2 * lax.rem(i, 2)))

    own_y.start()
    first_x.wait_recv()
    sum_y[...] = (parts[2, top, :].astype(F32) + x1[...].astype(F32)).astype(BF)
    rest_y.start()
    first_y.wait_recv()
    sum_x[...] = (parts[1, low, :].astype(F32) + y1[...].astype(F32)).astype(BF)
    rest_x.start()
    own_x.wait_recv()
    rest_y.wait_recv()
    finish(top, parts[0, top, :].astype(F32) + x2[top, :].astype(F32) + y2[top, :].astype(F32))
    own_y.wait_recv()
    rest_x.wait_recv()
    finish(low, parts[0, low, :].astype(F32) + x2[low, :].astype(F32) + y2[low, :].astype(F32))
    for copy in (to_x, to_y, far_x, far_y, first_x, first_y, own_x, own_y, rest_x, rest_y):
        copy.wait_send()


def forward_kernel(
    own, up, down, bias, resid, par, out, all_ref, active, slope,
    parts, x1, y1, x2, y2, sx, sy, send, recv,
):
    def finish(at, value):
        out[at, :] = (resid[at, :] + value + par[7:8, :]).astype(BF)

    def compute(r):
        slope[r] = mm(all_ref[r], up[...]) + bias[...]

        @pl.loop(0, own.shape[0] // 64)
        def _(j):
            at = pl.ds(pl.multiple_of(j * 64, 64), 64)
            z = slope[r, at, :]
            cdf, pdf = phi_parts(z)
            active[r, at, :] = (z * cdf).astype(BF)
            slope[r, at, :] = cdf + z * pdf

        parts[r] = mm(active[r], down[...]).astype(BF)

    exchange_rows(own, all_ref, parts, compute, finish, (x1, y1, x2, y2, sx, sy), send, recv)


def backward_kernel(
    own, up, down, slope, total, all_ref, dz_all, bias_g, parts, x1, y1, x2, y2, sx, sy, send, recv
):
    bias_g[...] = jnp.zeros_like(bias_g)

    def finish(at, value):
        total[at, :] = value

    def compute(r):
        dz = mm_nt(all_ref[r], down[...]) * slope[r]
        bias_g[...] += jnp.sum(dz, axis=0, keepdims=True)
        dz_all[r] = dz.astype(BF)
        parts[r] = mm_nt(dz_all[r], up[...]).astype(BF)

    exchange_rows(own, all_ref, parts, compute, finish, (x1, y1, x2, y2, sx, sy), send, recv)


VSPEC = pl.BlockSpec(memory_space=pltpu.VMEM)


def lasting(micros):
    return pl.CostEstimate(flops=0, transcendentals=0, bytes_accessed=int(micros * 3.5e6))


def plane_call(kernel, ident, outs, rows, *operands):
    half = rows // 2
    return pl.pallas_call(
        kernel,
        out_shape=outs,
        in_specs=[VSPEC] * len(operands),
        out_specs=(VSPEC,) * len(outs),
        scratch_shapes=[
            pltpu.VMEM((4, rows, D), BF),
            pltpu.VMEM((half, D), BF),
            pltpu.VMEM((half, D), BF),
            pltpu.VMEM((rows, D), BF),
            pltpu.VMEM((rows, D), BF),
            pltpu.VMEM((half, D), BF),
            pltpu.VMEM((half, D), BF),
            pltpu.SemaphoreType.DMA((10,)),
            pltpu.SemaphoreType.DMA((10,)),
        ],
        compiler_params=pltpu.CompilerParams(
            collective_id=ident, has_side_effects=True, vmem_limit_bytes=40 * 1024 * 1024
        ),
        cost_estimate=lasting(40),
    )(*operands)


def mlp_forward(own, up, down, bias, resid, par):
    rows = own.shape[0]
    if lax.axis_size("fsdp") != 4:
        every = lax.all_gather(own, "fsdp", axis=0, tiled=True)
        z = mm(every, up) + bias
        cdf, pdf = phi_parts(z)
        active = (z * cdf).astype(BF)
        part = mm(active, down).astype(BF)
        total = lax.psum_scatter(part, "fsdp", scatter_dimension=0, tiled=True).astype(F32)
        out = (resid + total + par[7]).astype(BF)
        return out, every, active, cdf + z * pdf
    shape = (4, rows, D)
    return plane_call(
        forward_kernel, 1,
        (
            jax.ShapeDtypeStruct((rows, D), BF),
            jax.ShapeDtypeStruct(shape, BF),
            jax.ShapeDtypeStruct(shape, BF),
            jax.ShapeDtypeStruct(shape, F32),
        ),
        rows, own, up, down, bias, resid, par,
    )


def mlp_backward(own, up, down, slope):
    rows = own.shape[0]
    if lax.axis_size("fsdp") != 4:
        every = lax.all_gather(own, "fsdp", axis=0, tiled=True)
        dz = mm_nt(every, down) * slope
        dz_b = dz.astype(BF)
        part = mm_nt(dz_b, up).astype(BF)
        total = lax.psum_scatter(part, "fsdp", scatter_dimension=0, tiled=True).astype(F32)
        return total, every, dz_b, jnp.sum(dz, axis=0, keepdims=True)
    shape = (4, rows, D)
    return plane_call(
        backward_kernel, 2,
        (
            jax.ShapeDtypeStruct((rows, D), F32),
            jax.ShapeDtypeStruct(shape, BF),
            jax.ShapeDtypeStruct(shape, BF),
            jax.ShapeDtypeStruct((1, D), F32),
        ),
        rows, own, up, down, slope,
    )


def weights_kernel(
    own, rows_in, up_in, down_in, full, rows_out, up_out, down_out,
    load, core_s, core_r, p_send, p_recv, f_send, f_recv, z_send, z_recv,
):
    s = lax.axis_index("section")
    f = lax.axis_index("fsdp")
    xn, yn = plane_neighbours()
    dn = 3 - f
    shard, wide = own.shape[1], own.shape[2]
    cut = 640
    left = pl.ds(0, cut)
    right = pl.ds(cut, wide - cut)

    def to(src, dst, send, recv, **where):
        return pltpu.make_async_remote_copy(
            src_ref=src, dst_ref=dst, send_sem=send, recv_sem=recv,
            device_id=where, device_id_type=MESH,
        )

    barrier = pltpu.get_barrier_semaphore()
    z = lax.axis_index("ctx")
    above = {"ctx": lax.rem(z + 1, 4)}
    below = {"ctx": lax.rem(z + 3, 4)}
    for where in ({"section": 1 - s}, {"fsdp": xn}, {"fsdp": yn}, above, below):
        pl.semaphore_signal(barrier, inc=1, device_id=where, device_id_type=MESH)
    pl.semaphore_wait(barrier, 5)
    rows = rows_in.shape[0]
    near_rows, far_rows = pl.ds(rows, rows), pl.ds(0, rows)
    step_one = to(rows_in, rows_out.at[near_rows], z_send.at[0], z_recv.at[0], **above)
    step_two = to(
        rows_out.at[near_rows], rows_out.at[far_rows], z_send.at[1], z_recv.at[1], **above
    )

    @pl.when(z < 3)
    def _():
        step_one.start()

    rows_out[pl.ds(2 * rows, rows), :] = rows_in[...]

    @pl.when(z == 0)
    def _():
        rows_out[near_rows, :] = jnp.zeros(rows_in.shape, BF)

    @pl.when(z < 2)
    def _():
        rows_out[far_rows, :] = jnp.zeros(rows_in.shape, BF)

    def blk(owner):
        return pl.ds(pl.multiple_of(owner * shard, 16), shard)

    def give(p):
        return to(own.at[p], full.at[p, blk(f)], core_s.at[p], core_r.at[p], section=1)

    def keep(p):
        return pltpu.make_async_copy(own.at[p], full.at[p, blk(f)], load.at[p])

    @pl.when(s == 0)
    def _():
        for p in (2, 3, 0, 1):
            give(p).start()
        for p in range(4):
            keep(p).start()
        keep(0).wait()
        keep(1).wait()

    @pl.when(s == 1)
    def _():
        give(2).wait_recv()
        give(3).wait_recv()

    def same(piece, rows, send, recv, cols=slice(None), **where):
        ref = full.at[piece, rows, cols]
        return to(ref, ref, send, recv, **where)

    def hops(k):
        p = 2 * s + k
        return (
            same(p, blk(f), p_send.at[k, 0], p_recv.at[k, 0], fsdp=xn),
            same(p, blk(f), p_send.at[k, 1], p_recv.at[k, 1], fsdp=yn),
            same(p, blk(yn), p_send.at[k, 2], p_recv.at[k, 2], left, fsdp=xn),
            same(p, blk(xn), p_send.at[k, 3], p_recv.at[k, 3], right, fsdp=yn),
        )

    def here(k):
        p = 2 * s + k
        return [
            same(p, blk(owner), f_send.at[k, i], f_recv.at[k, i], section=1 - s)
            for i, owner in enumerate((xn, yn, dn))
        ]

    for k in range(2):
        copies = hops(k)
        copies[0].start()
        copies[1].start()
    down_far = to(down_in, down_out.at[s], core_s.at[4], core_r.at[4], section=1 - s)
    down_near = pltpu.make_async_copy(down_in, down_out.at[s], load.at[4])
    down_far.start()
    down_near.start()
    for j in range(4):
        up_out[j] = up_in[:, pl.ds(j * D, D)]
    for k in range(2):
        copies, across = hops(k), here(k)
        copies[0].wait_recv()
        copies[3].start()
        across[0].start()
        copies[1].wait_recv()
        copies[2].start()
        across[1].start()

    @pl.when(z > 0)
    def _():
        step_one.wait_recv()

    @pl.when((z == 1) | (z == 2))
    def _():
        step_two.start()

    for k in range(2):
        copies, across = hops(k), here(k)
        copies[2].wait_recv()
        copies[3].wait_recv()
        across[2].start()
    for k in range(2):
        for copy in here(k):
            copy.wait()
        for copy in hops(k):
            copy.wait_send()

    @pl.when(s == 0)
    def _():
        for p in range(4):
            give(p).wait_send()
        keep(2).wait()
        keep(3).wait()

    @pl.when(s == 1)
    def _():
        give(0).wait_recv()
        give(1).wait_recv()

    down_near.wait()
    down_far.wait()

    @pl.when(z < 3)
    def _():
        step_one.wait_send()

    @pl.when((z == 1) | (z == 2))
    def _():
        step_two.wait_send()

    @pl.when(z > 1)
    def _():
        step_two.wait_recv()


def first_weights(own, rows_in, up, down):
    dma = pltpu.SemaphoreType.DMA
    return pl.pallas_call(
        weights_kernel,
        out_shape=(
            jax.ShapeDtypeStruct((4, D, WIDE), BF),
            jax.ShapeDtypeStruct((3 * rows_in.shape[0], D), BF),
            jax.ShapeDtypeStruct((4, up.shape[0], D), BF),
            jax.ShapeDtypeStruct((2, D, D), BF),
        ),
        in_specs=[pl.BlockSpec(memory_space=pl.ANY), VSPEC, VSPEC, pl.BlockSpec(memory_space=pl.ANY)],
        out_specs=(VSPEC,) * 4,
        scratch_shapes=[
            dma((5,)), dma((5,)), dma((5,)), dma((2, 4)), dma((2, 4)), dma((2, 3)), dma((2, 3)),
            dma((2,)), dma((2,)),
        ],
        compiler_params=pltpu.CompilerParams(
            collective_id=4, has_side_effects=True, vmem_limit_bytes=32 * 1024 * 1024
        ),
        cost_estimate=lasting(50),
        name="first_weights",
    )(own, rows_in, up, down)


def z_partners():
    z = lax.axis_index("ctx")
    return z + 1 - 2 * lax.rem(z, 2), 3 - z, (z == 1) | (z == 2)


def add_rows(dst, one, two, rows, step):
    @pl.loop(0, rows // step)
    def _(i):
        at = pl.ds(pl.multiple_of(i * step, 16), step)
        dst[at, :] = (one[at, :].astype(F32) + two[at, :].astype(F32)).astype(dst.dtype)


CUTS = ((0, 640, 384), (640, 512, 256))


def reduce_kernel(
    q0, k0, v0, o0, q1, k1, v1, o1, mlp, made0, made1, grad1, halo, d_resid, da_own, wide, par,
    qkv_out, out_out, down_out, up_out, made_out, grad_out,
    own_in, held, up_own, up_far, sent, caught, grad0,
    x1a, y1a, x2a, y2a, sxa, sya, ta, zaa, zba,
    x1b, y1b, x2b, y2b, sxb, syb, tb, zab, zbb,
    load, core_s, core_r, p_send, p_recv, z_send, z_recv, h_send, h_recv, x_send, x_recv,
):
    s = lax.axis_index("section")
    f = lax.axis_index("fsdp")
    xn, yn = plane_neighbours()
    dn = 3 - f
    side, across, inner = z_partners()
    pieces = ((q0, k0, v0, o0), (q1, k1, v1, o1))
    sets = (
        (x1a, y1a, x2a, y2a, sxa, sya, ta, zaa, zba),
        (x1b, y1b, x2b, y2b, sxb, syb, tb, zab, zbb),
    )
    shard = out_out.shape[0]
    rows = da_own.shape[0]
    z = lax.axis_index("ctx")
    above, below = {"ctx": lax.rem(z + 1, 4)}, {"ctx": lax.rem(z + 3, 4)}

    def to(src, dst, send, recv, **where):
        return pltpu.make_async_remote_copy(
            src_ref=src, dst_ref=dst, send_sem=send, recv_sem=recv,
            device_id=where, device_id_type=MESH,
        )

    barrier = pltpu.get_barrier_semaphore()
    partners = ({"section": 1 - s}, {"fsdp": xn}, {"fsdp": yn}, above, below)
    for where in partners:
        pl.semaphore_signal(barrier, inc=1, device_id=where, device_id_type=MESH)
    pl.semaphore_wait(barrier, 5)

    def blk(owner):
        return pl.ds(pl.multiple_of(owner * shard, 16), shard)

    def by_core(act):
        for core in range(2):
            pl.when(s == core)(functools.partial(act, core))

    def far(j, src):
        return to(src, held.at[j], core_s.at[j], core_r.at[j], section=1 - s)

    def near(j, src):
        return pltpu.make_async_copy(src, own_in.at[j % 2], load.at[j])

    def bufs(c):
        return tuple(ref.at[c // 2] for ref in sets[c % 2])

    def plane(c):
        x1, y1, x2, y2, sx, sy = bufs(c)[:6]
        own = held.at[c // 2]
        at, width, cut = CUTS[c % 2]
        left, right = pl.ds(at, cut), pl.ds(at + cut, width - cut)
        to_left, to_right = pl.ds(0, cut), pl.ds(cut, width - cut)
        sems = [(p_send.at[c, i], p_recv.at[c, i]) for i in range(6)]
        return (
            to(own.at[blk(dn), left], x1, *sems[0], fsdp=xn),
            to(own.at[blk(dn), right], y1, *sems[1], fsdp=yn),
            to(own.at[blk(xn), left], x2.at[:, to_left], *sems[2], fsdp=xn),
            to(own.at[blk(yn), right], y2.at[:, to_right], *sems[3], fsdp=yn),
            to(sx, x2.at[:, to_right], *sems[4], fsdp=xn),
            to(sy, y2.at[:, to_left], *sems[5], fsdp=yn),
        )

    def along(c):
        t, za, zb = bufs(c)[6:]
        sems = [(z_send.at[c, i], z_recv.at[c, i]) for i in range(3)]
        return (
            to(t, za, *sems[0], ctx=side),
            to(za, zb, *sems[1], ctx=across),
            to(zb, zb, *sems[2], ctx=side),
        )

    def join(j):
        far(j, q0).wait_recv()
        near(j, q0).wait()
        add_rows(held.at[j], own_in.at[j % 2], held.at[j], 4 * shard, 64)
        for c in (2 * j, 2 * j + 1):
            for copy in plane(c)[:4]:
                copy.start()
        if j < 2:
            by_core(lambda core: near(j + 2, pieces[core][j + 2]).start())

    def second(c):
        copies = plane(c)
        x1, y1, _, _, sx, sy = bufs(c)[:6]
        at, width, cut = CUTS[c % 2]
        own = held.at[c // 2]
        copies[0].wait_recv()
        add_rows(sy, own.at[blk(yn), pl.ds(at, cut)], x1, shard, 16)
        copies[5].start()
        copies[1].wait_recv()
        add_rows(sx, own.at[blk(xn), pl.ds(at + cut, width - cut)], y1, shard, 16)
        copies[4].start()

    def third(c):
        copies = plane(c)
        _, _, x2, y2, _, _, t, _, _ = bufs(c)
        at, width, _ = CUTS[c % 2]
        for copy in copies[2:]:
            copy.wait_recv()
        own = held.at[c // 2, blk(f), pl.ds(at, width)]

        @pl.loop(0, shard // 16)
        def _(i):
            part = pl.ds(pl.multiple_of(i * 16, 16), 16)
            t[part, :] = (
                own[part, :].astype(F32) + x2[part, :].astype(F32) + y2[part, :].astype(F32)
            ).astype(BF)

        @pl.when(jnp.logical_not(inner))
        def _():
            along(c)[0].start()

    def inward(c):
        @pl.when(inner)
        def _():
            t, za, _ = bufs(c)[6:]
            copies = along(c)
            copies[0].wait_recv()
            add_rows(za, t, za, shard, 16)
            copies[1].start()

    def crossed(c):
        @pl.when(inner)
        def _():
            _, za, zb = bufs(c)[6:]
            copies = along(c)
            copies[1].wait_recv()
            add_rows(zb, za, zb, shard, 16)
            copies[2].start()

    def last(c):
        at, width, _ = CUTS[c % 2]
        j = c // 2

        @pl.when(jnp.logical_not(inner))
        def _():
            along(c)[2].wait_recv()

        done = bufs(c)[8]
        keep = min(width, D - at) if j < 3 else width

        @pl.loop(0, shard // 16)
        def _(i):
            part = pl.ds(pl.multiple_of(i * 16, 16), 16)
            if j < 3:
                qkv_out[part, pl.ds(j * D + at, keep)] = done[part, pl.ds(0, keep)]
            else:
                out_out[part, pl.ds(at, keep)] = done[part, :]

    half = down_out.shape[0] // 2
    mine = pl.ds(pl.multiple_of(s * half, 16), half)
    down_far = to(mlp.at[0], down_out.at[mine], core_s.at[4], core_r.at[4], section=1 - s)
    down_near = pltpu.make_async_copy(mlp.at[0], down_out.at[mine], load.at[4])
    far_up = to(mlp.at[1], up_far, core_s.at[5], core_r.at[5], section=1 - s)
    near_up = pltpu.make_async_copy(mlp.at[1], up_own, load.at[5])

    def lay_up():
        far_up.wait_recv()
        near_up.wait()

        @pl.when(s == 1)
        def _():
            for k in range(2):
                up_out[:, pl.ds(k * D, D)] = up_far[pl.ds(k * shard, shard), :]
                up_out[:, pl.ds((2 + k) * D, D)] = up_own[pl.ds(k * shard, shard), :]

    back_one = to(halo.at[pl.ds(0, rows)], caught.at[0], h_send.at[0], h_recv.at[0], **below)
    back_two = to(sent, caught.at[1], h_send.at[1], h_recv.at[1], **below)

    def back():
        @pl.when(z < 3)
        def _():
            back_one.wait_recv()

        @pl.when(z == 3)
        def _():
            caught[0] = jnp.zeros_like(caught[0])

        @pl.when(z > 0)
        def _():
            add_rows(sent, halo.at[pl.ds(rows, rows)], caught.at[0], rows, 64)
            back_two.start()

    made_far = (
        to(made1, made_out.at[0], x_send.at[0], x_recv.at[0], section=1),
        to(made0, made_out.at[1], x_send.at[0], x_recv.at[0], section=0),
    )
    grad_far = (
        to(grad1, grad_out.at[0], x_send.at[1], x_recv.at[1], section=1),
        to(grad0, grad_out.at[1], x_send.at[1], x_recv.at[1], section=0),
    )
    made_near = (
        pltpu.make_async_copy(made0, made_out.at[0], load.at[6]),
        pltpu.make_async_copy(made1, made_out.at[1], load.at[6]),
    )
    grad_near = pltpu.make_async_copy(grad1, grad_out.at[1], load.at[7])

    def back_end():
        @pl.when(z < 3)
        def _():
            back_two.wait_recv()

        @pl.when(z == 3)
        def _():
            caught[1] = jnp.zeros_like(caught[1])

        unit, inv = norm_parts(wide[...].astype(F32))
        da = da_own[...] + caught[1].astype(F32)
        grad0[...] = d_resid[...] + norm_back(da, par[0:1, :], unit, inv)

        @pl.when(s == 0)
        def _():
            grad_out[0] = grad0[...]

        @pl.when(s == 1)
        def _():
            grad_far[1].start()

    @pl.when(s == 0)
    def _():
        made_far[0].start()
        grad_far[0].start()
        made_near[0].start()

    @pl.when(s == 1)
    def _():
        made_far[1].start()
        made_near[1].start()
        grad_near.start()

    @pl.when(z > 0)
    def _():
        back_one.start()

    for j in range(4):
        by_core(lambda core: far(j, pieces[1 - core][j]).start())
        if j < 2:
            by_core(lambda core: near(j, pieces[core][j]).start())
    for copy in (down_far, down_near, far_up, near_up):
        copy.start()

    join(0)
    for c in range(12):
        if c in (1, 3, 5):
            join((c + 1) // 2)
        if c < 8:
            second(c)
        if 1 <= c <= 8:
            third(c - 1)
        if 2 <= c <= 9:
            inward(c - 2)
        if 3 <= c <= 10:
            crossed(c - 3)
        if c >= 4:
            last(c - 4)
        if c == 2:
            back()
        if c == 4:
            lay_up()
        if c == 6:
            back_end()

    down_near.wait()
    down_far.wait()
    far_up.wait_send()

    @pl.when(s == 0)
    def _():
        made_near[0].wait()
        made_far[0].wait_send()
        grad_far[0].wait_send()
        made_far[1].wait_recv()
        grad_far[1].wait_recv()

    @pl.when(s == 1)
    def _():
        made_near[1].wait()
        grad_near.wait()
        made_far[1].wait_send()
        grad_far[1].wait_send()
        made_far[0].wait_recv()
        grad_far[0].wait_recv()

    @pl.when(z > 0)
    def _():
        back_one.wait_send()
        back_two.wait_send()

    for j in range(4):
        far(j, q0).wait_send()
    for c in range(8):
        for copy in plane(c):
            copy.wait_send()

    @pl.when(inner)
    def _():
        for c in range(8):
            for copy in along(c)[1:]:
                copy.wait_send()

    @pl.when(jnp.logical_not(inner))
    def _():
        for c in range(8):
            along(c)[0].wait_send()


def reduce_both(zero, one, mlp, made, grad1, halo, d_resid, da_own, wide, par):
    shard = D // 4
    rows = da_own.shape[0]
    dma = pltpu.SemaphoreType.DMA
    any_spec = pl.BlockSpec(memory_space=pl.ANY)

    def buf(*shape):
        return pltpu.VMEM(shape, BF)

    def part(_, width, cut):
        wide_buf = buf(4, shard, width)
        return [
            buf(4, shard, cut), buf(4, shard, width - cut), wide_buf, wide_buf,
            buf(4, shard, width - cut), buf(4, shard, cut), wide_buf, wide_buf, wide_buf,
        ]

    shapes = ((shard, 3 * D), (shard, WIDE), (D, D), (shard, 4 * D), (2, rows, D))
    return pl.pallas_call(
        reduce_kernel,
        out_shape=(
            *(jax.ShapeDtypeStruct(shape, BF) for shape in shapes),
            jax.ShapeDtypeStruct((2, rows, D), F32),
        ),
        in_specs=[any_spec] * 12 + [VSPEC] * 5,
        out_specs=(VSPEC,) * 6,
        scratch_shapes=[
            buf(2, D, WIDE), buf(4, D, WIDE), buf(D // 2, D), buf(D // 2, D), buf(rows, D),
            buf(2, rows, D), pltpu.VMEM((rows, D), F32), *part(*CUTS[0]), *part(*CUTS[1]),
            dma((8,)), dma((6,)), dma((6,)), dma((8, 6)), dma((8, 6)), dma((8, 3)), dma((8, 3)),
            dma((2,)), dma((2,)), dma((2,)), dma((2,)),
        ],
        compiler_params=pltpu.CompilerParams(
            collective_id=3, has_side_effects=True, vmem_limit_bytes=60 * 1024 * 1024
        ),
        cost_estimate=lasting(120),
        name="reduce_both",
    )(*zero, *one, mlp, *made, grad1, halo, d_resid, da_own, wide, par)


def final_kernel(qkv, out, mine, far, down_one, up_one, qkv_f, out_f, down_f, up_f, small):
    s = lax.axis_index("section")
    half = mine.shape[1]
    shard = qkv.shape[0]
    pick_row = (
        lax.broadcasted_iota(jnp.int32, (16, 128), 1)
        == lax.broadcasted_iota(jnp.int32, (16, 128), 0) + (D - TAIL)
    )
    small[...] = mm_nt(pick_row.astype(F32).astype(BF), out[:, pl.ds(TAIL, 128)])

    @pl.loop(0, shard // 16)
    def _(i):
        at = pl.ds(pl.multiple_of(i * 16, 16), 16)
        qkv_f[at, :] = qkv[at, :].astype(F32)
        out_f[at, :] = out[at, pl.ds(0, D)].astype(F32)

        @pl.when(s == 0)
        def _():
            for k in range(2):
                from_k = pl.ds(pl.multiple_of(k * shard + i * 16, 16), 16)
                up_f[at, pl.ds(k * D, D)] = mine[1, from_k, :].astype(F32)
                up_f[at, pl.ds((2 + k) * D, D)] = far[1, from_k, :].astype(F32)

        @pl.when(s == 1)
        def _():
            up_f[at, :] = up_one[at, :].astype(F32)

    @pl.loop(0, half // 16)
    def _(i):
        at = pl.ds(pl.multiple_of(i * 16, 16), 16)
        after = pl.ds(pl.multiple_of(half + i * 16, 16), 16)

        @pl.when(s == 0)
        def _():
            down_f[at, :] = mine[0, at, :].astype(F32)
            down_f[after, :] = far[0, at, :].astype(F32)

        @pl.when(s == 1)
        def _():
            down_f[at, :] = down_one[at, :].astype(F32)
            down_f[after, :] = down_one[after, :].astype(F32)


def final_layouts(qkv, out, mine, far, down_one, up_one):
    shard = qkv.shape[0]
    outs = (qkv.shape, (shard, D), down_one.shape, up_one.shape, (16, shard))
    return pl.pallas_call(
        final_kernel,
        out_shape=tuple(jax.ShapeDtypeStruct(shape, F32) for shape in outs),
        in_specs=[VSPEC] * 6,
        out_specs=(VSPEC,) * 5,
        compiler_params=pltpu.CompilerParams(vmem_limit_bytes=48 * 1024 * 1024),
        cost_estimate=lasting(10),
        name="final_layouts",
    )(qkv, out, mine, far, down_one, up_one)


def halves_pair(down, up):
    s = lax.axis_index("section")
    both = jnp.stack([down, up])
    both = both.reshape(2, 2, both.shape[1] // 2, D)
    keep = lax.dynamic_index_in_dim(both, s, 1, keepdims=False)
    give = lax.dynamic_index_in_dim(both, 1 - s, 1, keepdims=False)
    return (keep.astype(F32) + on_chip(give).astype(F32)).astype(BF)


def halves_settle(zero, one):
    s = lax.axis_index("section")
    mine, far = pick(s, zero, one), on_chip(pick(s, one, zero))
    return jnp.concatenate([pick(s, mine, far), pick(s, far, mine)], axis=1).astype(F32)


def reduce_plain(pieces):
    s = lax.axis_index("section")
    pair = ("fsdp", "section")
    a = jnp.stack([lax.psum_scatter(p, pair, scatter_dimension=0, tiled=True) for p in pieces])
    a = lax.psum(a, "ctx")
    far = on_chip(a)
    return jnp.concatenate([pick(s, a, far), pick(s, far, a)], axis=1)


def shift(value, steps):
    count = lax.axis_size("ctx")
    pairs = [(i, i + steps) for i in range(count) if 0 <= i + steps < count]
    return lax.ppermute(value, "ctx", pairs)


def with_halo(own, chunks):
    parts = [own]
    for _ in range(chunks):
        parts.append(shift(parts[-1], 1))
    return jnp.concatenate(parts[::-1], axis=0)


def return_halo(halo, chunks, rows):
    carried = None
    for far in range(chunks):
        mine = halo[far * rows : (far + 1) * rows]
        carried = mine if carried is None else mine + carried
        carried = shift(carried.astype(BF), -1).astype(F32)
    return carried


def pick(s, first, second):
    return jnp.where(s == 0, first, second)


def on_chip(value):
    return lax.ppermute(value, "section", SWAP)


def both_layers(own, s):
    other = on_chip(own)
    return pick(s, own, other), pick(s, other, own)


def flat(values):
    return values.reshape(-1, values.shape[-1])


def widen(values):
    return jnp.pad(values, ((0, 0), (0, WIDE - D)))


TAIL = 1024


def scores_forward(q, k, v, bias, lanes):
    outs = []
    for low in (True, False):
        one = jnp.where((lanes < HD) if low else (lanes >= HD), q, jnp.zeros_like(q))
        weight = jnp.exp(mm_nt(one, k) + bias)
        prob = weight * (1.0 / jnp.sum(weight, axis=-1, keepdims=True))
        outs.append(mm(prob.astype(BF), v))
    return jnp.where(lanes < HD, outs[0], outs[1]).astype(BF)


def scores_backward(q, k, v, grad, bias_t, lanes):
    dqs, dk, dv = [], 0.0, 0.0
    for low in (True, False):
        mine = (lanes < HD) if low else (lanes >= HD)
        one = jnp.where(mine, q, jnp.zeros_like(q))
        g = jnp.where(mine, grad, jnp.zeros_like(grad))
        weight = jnp.exp(mm_nt(k, one) + bias_t)
        prob = weight * (1.0 / jnp.sum(weight, axis=0, keepdims=True))
        d_prob = mm_nt(v, g)
        row = jnp.sum(prob * d_prob, axis=0, keepdims=True)
        d_score = (prob * (d_prob - row)).astype(BF)
        dqs.append(mm_tn(d_score, k))
        dk = dk + mm(d_score, one)
        dv = dv + mm(prob.astype(BF), g)
    dq = jnp.where(lanes < HD, dqs[0], dqs[1]) * SCALE
    return dq.astype(BF), dk.astype(BF), dv.astype(BF)


def lane_tile(i):
    return pl.ds(pl.multiple_of(i * 128, 128), 128)


def widened(row):
    return jnp.concatenate([row, jnp.zeros((row.shape[0], WIDE - D), row.dtype)], axis=1)


def ctx_ring(rows_in, landing, send, recv):
    z = lax.axis_index("ctx")
    above = {"ctx": lax.rem(z + 1, 4)}
    below = {"ctx": lax.rem(z + 3, 4)}
    rows = rows_in.shape[0]
    near, far = pl.ds(rows, rows), pl.ds(0, rows)
    barrier = pltpu.get_barrier_semaphore()

    def on(src, dst, i):
        return pltpu.make_async_remote_copy(
            src_ref=src, dst_ref=dst, send_sem=send.at[i], recv_sem=recv.at[i],
            device_id=above, device_id_type=MESH,
        )

    one = on(rows_in, landing.at[near], 0)
    two = on(landing.at[near], landing.at[far], 1)

    def begin():
        for where in (above, below):
            pl.semaphore_signal(barrier, inc=1, device_id=where, device_id_type=MESH)
        pl.semaphore_wait(barrier, 2)

        @pl.when(z < 3)
        def _():
            one.start()

        landing[pl.ds(2 * rows, rows), :] = rows_in[...]

        @pl.when(z == 0)
        def _():
            landing[near, :] = jnp.zeros(rows_in.shape, BF)

        @pl.when(z < 2)
        def _():
            landing[far, :] = jnp.zeros(rows_in.shape, BF)

    def middle():
        @pl.when(z > 0)
        def _():
            one.wait_recv()

        @pl.when((z == 1) | (z == 2))
        def _():
            two.start()

    def end():
        @pl.when(z > 1)
        def _():
            two.wait_recv()

        @pl.when(z < 3)
        def _():
            one.wait_send()

        @pl.when((z == 1) | (z == 2))
        def _():
            two.wait_send()

    return begin, middle, end


def block_kernel(
    ring, first, wq, wk, wv, wo, bias, normed, q_ref, k_ref, v_ref, att, resid, second, par, *rest
):
    rows = resid.shape[0]
    total = normed.shape[0]
    if ring:
        wide_out, held, wide, send, recv = rest
        begin, middle, end = ctx_ring(first, wide, send, recv)
        begin()
    else:
        (held,), wide = rest, first
    pick_row = (
        lax.broadcasted_iota(jnp.int32, (16, 128), 1)
        == lax.broadcasted_iota(jnp.int32, (16, 128), 0) + (D - TAIL)
    )
    par[...] = mm_nt(pick_row.astype(F32).astype(BF), wo[:, pl.ds(TAIL, 128)])
    last = total // rows - 1

    @pl.loop(0, last + 1)
    def _(i):
        if ring:
            pl.when(i == 1)(middle)
            pl.when(i == 2)(end)
        at = pl.ds(pl.multiple_of((last - i) * rows, 16), rows)
        unit, _ = norm_parts(wide[at, :].astype(F32))
        low = (unit * par[0:1, :] + par[2:3, :]).astype(BF)
        normed[at, :] = low
        k_ref[at, :] = mm(low, wk[...]).astype(BF)
        v_ref[at, :] = (mm(low, wv[...]) + widened(par[4:5, :])).astype(BF)

        @pl.when(i == 0)
        def _():
            q_ref[...] = (mm(normed[at, :], wq[...]) + widened(par[3:4, :])).astype(BF)

    own = pl.ds(total - rows, rows)
    lanes = lax.broadcasted_iota(jnp.int32, (rows, 128), 1)

    @pl.loop(0, WIDE // 128)
    def _(i):
        at = lane_tile(i)
        held[:, at] = scores_forward(
            q_ref[:, at] * jnp.asarray(SCALE, BF), k_ref[:, at], v_ref[:, at], bias[...], lanes
        )

    att[...] = held[:, pl.ds(0, D)]
    res = wide[own, :].astype(F32) + mm(att[...], wo[:, pl.ds(0, D)]) + par[5:6, :]
    resid[...] = res
    unit, _ = norm_parts(res)
    second[...] = (unit * par[1:2, :] + par[6:7, :]).astype(BF)
    if ring:
        wide_out[...] = wide[...]


def weight_specs(weights):
    if weights.ndim == 3:
        return [pl.BlockSpec((None, D, WIDE), lambda i, p=p: (p, 0, 0)) for p in range(4)]
    return [pl.BlockSpec((D, WIDE), lambda i, p=p: (0, p)) for p in range(4)]


def whole(shape):
    return pl.BlockSpec(shape, lambda i: (0,) * len(shape))


def block_forward(first, weights, bias, ring):
    rows, total = bias.shape
    outs = (
        ((total, D), BF), ((rows, WIDE), BF), ((total, WIDE), BF), ((total, WIDE), BF),
        ((rows, D), BF), ((rows, D), F32), ((rows, D), BF), ((16, D), F32),
    )
    scratch = [pltpu.VMEM((rows, WIDE), BF)]
    params = {}
    if ring:
        outs += (((total, D), BF),)
        scratch += [pltpu.VMEM((total, D), BF)] + [pltpu.SemaphoreType.DMA((2,))] * 2
        params = {"collective_id": 5, "has_side_effects": True}
    return pl.pallas_call(
        functools.partial(block_kernel, ring),
        out_shape=tuple(jax.ShapeDtypeStruct(*out) for out in outs),
        grid=(1,),
        in_specs=[whole(first.shape), *weight_specs(weights), whole(bias.shape)],
        out_specs=tuple(whole(shape) for shape, _ in outs),
        scratch_shapes=scratch,
        compiler_params=pltpu.CompilerParams(vmem_limit_bytes=56 * 1024 * 1024, **params),
        cost_estimate=lasting(45 if ring else 22),
        name="block_forward",
    )(first, weights, weights, weights, weights, bias)


def block_back_kernel(
    ring, d_second, up, resid, wide, q_ref, k_ref, v_ref, att, ffb_rows, wq, wk, wv, wo, par, bias_t,
    *rest,
):
    if ring:
        (d_in, d_low, dq_ref, dk_ref, dv_ref, left, right,
         held, sums, d_resid, da_own, da_halo, sent, caught, send, recv) = rest
    else:
        d_resid, dq_ref, dk_ref, dv_ref, da_own, da_halo, left, right, held, sums = rest
    rows = resid.shape[0]
    total = wide.shape[0]
    own = total - rows
    z = lax.axis_index("ctx")

    def back_to(src, dst, i):
        return pltpu.make_async_remote_copy(
            src_ref=src, dst_ref=dst, send_sem=send.at[i], recv_sem=recv.at[i],
            device_id={"ctx": lax.rem(z + 3, 4)}, device_id_type=MESH,
        )

    if ring:
        one = back_to(da_halo.at[pl.ds(0, rows)], caught.at[0], 0)
        two = back_to(sent, caught.at[1], 1)
        barrier = pltpu.get_barrier_semaphore()
        for step in (1, 3):
            pl.semaphore_signal(
                barrier, inc=1, device_id={"ctx": lax.rem(z + step, 4)}, device_id_type=MESH
            )
        pl.semaphore_wait(barrier, 2)

    def total_of(values):
        return jnp.sum(values, axis=0, keepdims=True)

    upstream = up[...].astype(F32)
    unit, inv = norm_parts(resid[...])
    grad = upstream + norm_back(d_second[...], par[1:2, :], unit, inv)
    d_resid[...] = grad
    sums[1:2, :] = total_of(d_second[...] * unit)
    sums[5:6, :] = total_of(grad)
    sums[6:7, :] = total_of(d_second[...])
    sums[7:8, :] = total_of(upstream)
    sums[8:16, :] = ffb_rows[...]
    low = grad.astype(BF)
    right[pl.ds(0, rows), :] = jnp.zeros((rows, WIDE), BF)
    right[pl.ds(0, rows), pl.ds(0, D)] = low
    right[pl.ds(rows, 16), :] = (
        lax.broadcasted_iota(jnp.int32, (16, WIDE), 1)
        == lax.broadcasted_iota(jnp.int32, (16, WIDE), 0) + D
    ).astype(F32).astype(BF)
    held[...] = jnp.zeros((rows, WIDE), BF)
    held[:, pl.ds(0, D)] = mm_nt(low, wo[:, pl.ds(0, D)]).astype(BF)
    lanes = lax.broadcasted_iota(jnp.int32, (rows, 128), 1)

    @pl.loop(0, WIDE // 128)
    def _(i):
        at = lane_tile(i)
        dq_ref[:, at], dk_ref[:, at], dv_ref[:, at] = scores_backward(
            q_ref[:, at] * jnp.asarray(SCALE, BF), k_ref[:, at], v_ref[:, at], held[:, at],
            bias_t[...], lanes,
        )

    sums[3:4, :] = total_of(dq_ref[...].astype(F32))[:, :D]
    sums[4:5, :] = total_of(dv_ref[...].astype(F32))[:, :D]
    sums[0:1, :] = jnp.zeros((1, D), F32)
    sums[2:3, :] = jnp.zeros((1, D), F32)

    def back(at):
        da = mm_nt(dk_ref[at, :], wk[...]) + mm_nt(dv_ref[at, :], wv[...])
        return da

    def count(da, at):
        unit, _ = norm_parts(wide[at, :].astype(F32))
        sums[0:1, :] += total_of(da * unit)
        sums[2:3, :] += total_of(da)

    @pl.loop(0, own // rows)
    def _(i):
        at = pl.ds(pl.multiple_of(i * rows, 16), rows)
        da = back(at)
        da_halo[at, :] = da.astype(BF)
        if ring:

            @pl.when((i == 0) & (z > 0))
            def _():
                one.start()

        count(da, at)

    at = pl.ds(own, rows)
    da = back(at) + mm_nt(dq_ref[...], wq[...])
    da_own[...] = da
    count(da, at)
    if ring:

        @pl.when(z < 3)
        def _():
            one.wait_recv()

        @pl.when(z == 3)
        def _():
            caught[0] = jnp.zeros_like(caught[0])

        @pl.when(z > 0)
        def _():
            add_rows(sent, da_halo.at[pl.ds(rows, rows)], caught.at[0], rows, 64)
            two.start()

    left[pl.ds(0, rows), :] = att[...]
    left[pl.ds(rows, 16), :] = sums[...].astype(BF)
    if ring:

        @pl.when(z < 3)
        def _():
            two.wait_recv()

        @pl.when(z == 3)
        def _():
            caught[1] = jnp.zeros_like(caught[1])

        @pl.loop(0, rows // 64)
        def _(i):
            part = pl.ds(pl.multiple_of(i * 64, 64), 64)
            behind = pl.ds(pl.multiple_of(own + i * 64, 64), 64)
            unit, inv = norm_parts(wide[behind, :].astype(F32))
            da = da_own[part, :] + caught[1, part, :].astype(F32)
            grad = d_resid[part, :] + norm_back(da, par[0:1, :], unit, inv)
            d_in[part, :] = grad
            d_low[part, :] = grad.astype(BF)

        @pl.when(z > 0)
        def _():
            one.wait_send()
            two.wait_send()


def block_backward(d_second, up, resid, wide, q, k, v, att, ffb_rows, weights, par, bias_t, ring):
    total, rows = wide.shape[0], resid.shape[0]
    f32_rows, low_rows = ((rows, D), F32), ((rows, D), BF)
    heads = (((rows, WIDE), BF), ((total, WIDE), BF), ((total, WIDE), BF))
    factors = (((rows + 16, D), BF), ((rows + 16, WIDE), BF))
    halo = ((total - rows, D), BF)
    held = [pltpu.VMEM((rows, WIDE), BF), pltpu.VMEM((16, D), F32)]
    params = {}
    if ring:
        outs = (f32_rows, low_rows, *heads, *factors)
        held += [pltpu.VMEM(*f32_rows), pltpu.VMEM(*f32_rows), pltpu.VMEM(*halo), pltpu.VMEM(*low_rows)]
        held += [pltpu.VMEM((2, rows, D), BF)] + [pltpu.SemaphoreType.DMA((2,))] * 2
        params = {"collective_id": 6, "has_side_effects": True}
    else:
        outs = (f32_rows, *heads, f32_rows, halo, *factors)
    before = (d_second, up, resid, wide, q, k, v, att, ffb_rows)
    return pl.pallas_call(
        functools.partial(block_back_kernel, ring),
        out_shape=tuple(jax.ShapeDtypeStruct(*out) for out in outs),
        grid=(1,),
        in_specs=[
            *(whole(value.shape) for value in before), *weight_specs(weights),
            whole(par.shape), whole(bias_t.shape),
        ],
        out_specs=tuple(whole(shape) for shape, _ in outs),
        scratch_shapes=held,
        compiler_params=pltpu.CompilerParams(vmem_limit_bytes=60 * 1024 * 1024, **params),
        cost_estimate=lasting(58 if ring else 38),
        name="block_backward",
    )(*before, weights, weights, weights, weights, par, bias_t)


def on_device(
    inputs, segments, cotangent, qkv_weight, out_weight, up_weight, down_weight,
    norm_gains, biases, ff_bias,
):
    rows = inputs.shape[2]
    length = segments.shape[2]
    chunks = min((length // 2 - 1 + rows - 1) // rows, lax.axis_size("ctx") - 1)
    reach = chunks * rows
    s = lax.axis_index("section")
    f = lax.axis_index("fsdp")
    nf = lax.axis_size("fsdp")
    shard = D // nf
    ff_here = ff_bias.shape[1]
    per_row = ff_here // shard
    pair = ("fsdp", "section")
    fits = nf == 4 and lax.axis_size("ctx") == 4 and chunks == 2

    own_in = lax.dynamic_index_in_dim(inputs, s, 0, keepdims=False)[0]
    own_cot = lax.dynamic_index_in_dim(cotangent, s, 0, keepdims=False)[0]
    seg = lax.dynamic_index_in_dim(segments, s, 0, keepdims=False)[0]
    start = lax.axis_index("ctx") * rows
    key_seg = lax.dynamic_slice_in_dim(
        jnp.pad(seg, (reach, 0), constant_values=-1), start, reach + rows, 0
    )
    allowed = (key_seg[reach:, None] == key_seg[None, :]) & (
        jnp.arange(reach + rows, dtype=jnp.int32)[None, :] - reach
        <= jnp.arange(rows, dtype=jnp.int32)[:, None]
    )

    bias = jnp.where(allowed, 0.0, -1e30).astype(F32)
    bias_t = bias.T

    small = jnp.concatenate(
        [norm_gains[0].T, biases[0].T, ff_bias[0].reshape(per_row, shard).T], axis=1
    )
    packed = jnp.stack(
        [
            widen(qkv_weight[0][:, :D]),
            widen(qkv_weight[0][:, D : 2 * D]),
            widen(qkv_weight[0][:, 2 * D :]),
            jnp.concatenate(
                [out_weight[0], small, jnp.zeros((shard, WIDE - D - 8 - per_row), BF)], axis=1
            ),
        ]
    )
    if fits:
        zero, wide_in, up_blocks, down_w = first_weights(
            packed, own_in, up_weight[0], down_weight[0]
        )
        packed, zero = lax.optimization_barrier((packed, zero))
    else:
        up_blocks = up_weight[0].reshape(shard, nf, ff_here).transpose(1, 0, 2)
        down_w = both_layers(down_weight[0], s)
        wide_in = with_halo(own_in, chunks)
    half = shard // 2
    halves = packed.reshape(4, 2, half, WIDE)
    keep = lax.dynamic_index_in_dim(halves, s, 1, keepdims=False)
    give = lax.dynamic_index_in_dim(halves, 1 - s, 1, keepdims=False)

    def gathered(part):
        rows_first = part.transpose(1, 0, 2).reshape(half, 4 * WIDE)
        return lax.all_gather(rows_first, pair, axis=0, tiled=True)

    recv = on_chip(give)
    one = gathered(pick(s, recv, keep))
    if not fits:
        zero = gathered(pick(s, keep, recv))
    up_own = lax.all_to_all(
        up_blocks, "fsdp", split_axis=0, concat_axis=0, tiled=True
    ).reshape(D, ff_here)

    weights = (zero, one)

    kept = []
    current = own_in
    produced = []
    for layer in range(2):
        if layer == 1 and fits:
            *made, wide = block_forward(current, weights[layer], bias, True)
        else:
            wide = with_halo(current, chunks) if layer else wide_in
            made = block_forward(wide, weights[layer], bias, False)
        normed, q, k, v, att, resid, second, par = made
        if layer == 0:
            up_own, second = lax.optimization_barrier((up_own, second))
            up_w = both_layers(up_own, s)
        ffb = lax.dynamic_slice(par, (8, f * shard), (per_row, shard)).reshape(1, ff_here)
        current, second_all, active, slope = mlp_forward(
            second, up_w[layer], down_w[layer], ffb, resid, par
        )
        produced.append(current)
        kept.append((wide, normed, q, k, v, att, resid, second_all, slope, active, par))

    upstream = own_cot
    derived = [None, None]
    parts = [None, None]
    mlp_sums = [None, None]
    for layer in (1, 0):
        wide, normed, q, k, v, att, resid, second_all, slope, active, par = kept[layer]
        d_second, up_all, dz_b, ffb_g = mlp_backward(upstream, up_w[layer], down_w[layer], slope)
        down_g = mm_tn(flat(active), flat(up_all))
        up_g = mm_tn(flat(second_all), flat(dz_b))
        ffb_rows = lax.dynamic_update_slice(
            jnp.zeros((8, D), F32), ffb_g.reshape(per_row, shard), (0, f * shard)
        )
        block = (
            d_second, upstream, resid, wide, q, k, v, att, ffb_rows, weights[layer], par, bias_t
        )
        if layer == 1 and fits:
            derived[1], upstream_next, dq, dk, dv, left, right = block_backward(*block, True)
        else:
            d_resid, dq, dk, dv, da_own, da_halo, left, right = block_backward(*block, False)
        if not fits:
            unit, inv = norm_parts(wide[reach:].astype(F32))
            late = return_halo(da_halo, chunks, rows)
            derived[layer] = d_resid + norm_back(da_own + late, par[0], unit, inv)
            upstream_next = derived[layer].astype(BF)
        pieces = (
            mm_tn(normed[reach:], dq).astype(BF),
            mm_tn(normed, dk).astype(BF),
            mm_tn(normed, dv).astype(BF),
            mm_tn(left, right).astype(BF),
        )
        parts[layer] = pieces
        up_g = lax.all_to_all(
            up_g.astype(BF).reshape(nf, shard, ff_here), "fsdp",
            split_axis=0, concat_axis=0, tiled=True,
        ).reshape(nf * shard * ff_here // D, D)
        down_g = down_g.astype(BF)
        if layer == 0:
            down_g, up_g, _ = lax.optimization_barrier((down_g, up_g, dq))
        halves = halves_pair(down_g, up_g)
        if layer == 1:
            _, upstream_next = lax.optimization_barrier((halves, upstream_next))
        else:
            halves, mlp_sums[1] = lax.optimization_barrier((halves, mlp_sums[1]))
        mlp_sums[layer] = lax.psum(halves, "ctx")
        if layer == 1:
            upstream = upstream_next

    if fits:
        qkv_g, out_g, down_one, up_one, made, grads = reduce_both(
            parts[0], parts[1], mlp_sums[1], produced, derived[1], da_halo, d_resid, da_own,
            wide[reach:], par,
        )
        late_sum, qkv_g = lax.optimization_barrier((mlp_sums[0], qkv_g))
        far = lax.ppermute(late_sum, "section", [(1, 0)])
        qkv_g, out_g, grad_down, grad_up, small = final_layouts(
            qkv_g, out_g, late_sum, far, down_one, up_one
        )
        made, grads = made[None, :, None], grads[None, :, None]
    else:
        a_tot = pick(s, reduce_plain(parts[0]), reduce_plain(parts[1])).astype(F32)
        qkv_g = jnp.concatenate([a_tot[i, :, :D] for i in range(3)], axis=1)
        out_g = a_tot[3, :, :D]
        small = a_tot[3, :, D : D + 16].T
        grad_down, grad_up = split_up(halves_settle(*mlp_sums), nf, shard)
        made, grads = both_micros(produced, s), both_micros(derived, s)
    return (
        made,
        grads,
        qkv_g[None],
        out_g[None],
        grad_up[None],
        grad_down[None],
        small[None, :2],
        small[None, 2:8],
        small[8 : 8 + per_row].reshape(1, ff_here),
    )


def split_up(both, nf, shard):
    up = both[1].reshape(nf, shard, -1)
    return both[0], up.transpose(1, 0, 2).reshape(shard, -1)


def both_micros(layers, s):
    to_zero = lax.ppermute(layers[0], "section", [(1, 0)])
    to_one = lax.ppermute(layers[1], "section", [(0, 1)])
    out = jnp.stack([pick(s, layers[0], to_one), pick(s, to_zero, layers[1])])
    return out[None, :, None]


def solution(mesh):
    return jax.shard_map(
        on_device,
        mesh=mesh,
        in_specs=(
            P(None, "fsdp", "ctx", None),
            P(None, "fsdp", None),
            P(None, "fsdp", "ctx", None),
            P("section", "fsdp", None),
            P("section", "fsdp", None),
            P("section", "fsdp", None),
            P("section", "fsdp", None),
            P("section", None, "fsdp"),
            P("section", None, "fsdp"),
            P("section", "fsdp"),
        ),
        out_specs=(
            P("section", None, "fsdp", "ctx", None),
            P("section", None, "fsdp", "ctx", None),
            P("section", "fsdp", None),
            P("section", "fsdp", None),
            P("section", "fsdp", None),
            P("section", "fsdp", None),
            P("section", None, "fsdp"),
            P("section", None, "fsdp"),
            P("section", "fsdp"),
        ),
        check_vma=False,
    )
```

```python
import functools
import math

import jax
import jax.numpy as jnp
from jax import lax
from jax.experimental import pallas as pl
from jax.experimental.pallas import tpu as pltpu
from jax.sharding import PartitionSpec as P

D = 1088
HD = 64
F32 = jnp.float32
BF = jnp.bfloat16
SCALE = 1.0 / math.sqrt(HD)
WIDE = 1152
MESH = pl.DeviceIdType.MESH
SWAP = [(0, 1), (1, 0)]


def mm(a, b):
    return jnp.dot(a, b, preferred_element_type=F32)


def mm_nt(a, b):
    return lax.dot_general(a, b, (((1,), (1,)), ((), ())), preferred_element_type=F32)


def mm_tn(a, b):
    return lax.dot_general(a, b, (((0,), (0,)), ((), ())), preferred_element_type=F32)


def norm_parts(values):
    center = jnp.mean(values, axis=-1, keepdims=True)
    offset = values - center
    spread = jnp.mean(offset * offset, axis=-1, keepdims=True)
    inv = lax.rsqrt(spread + 1e-05)
    return offset * inv, inv


def norm_back(grad, gain, unit, inv):
    dn = grad * gain
    return inv * (
        dn
        - jnp.mean(dn, axis=-1, keepdims=True)
        - unit * jnp.mean(dn * unit, axis=-1, keepdims=True)
    )


def phi_parts(z):
    cdf = 0.5 * (1.0 + lax.erf(z * (1.0 / math.sqrt(2.0))))
    pdf = jnp.exp(-0.5 * z * z) * (1.0 / math.sqrt(2.0 * math.pi))
    return cdf, pdf


def plane_neighbours():
    f = lax.axis_index("fsdp")
    x = lax.rem(f, 2)
    y = f // 2
    return y * 2 + (1 - x), (1 - y) * 2 + x


def plane_barrier(xn, yn):
    barrier = pltpu.get_barrier_semaphore()
    for nb in (xn, yn):
        pl.semaphore_signal(barrier, inc=1, device_id={"fsdp": nb}, device_id_type=MESH)
    pl.semaphore_wait(barrier, 2)


def remote(src, dst, send, recv, nb):
    return pltpu.make_async_remote_copy(
        src_ref=src, dst_ref=dst, send_sem=send, recv_sem=recv,
        device_id={"fsdp": nb}, device_id_type=MESH,
    )


def load_layer(layer, sources, targets, sems):
    copies = [
        pltpu.make_async_copy(source.at[layer], target, sems.at[i])
        for i, (source, target) in enumerate(zip(sources, targets))
    ]
    for copy in copies:
        copy.start()
    return copies


def exchange_rows(own_ref, all_ref, parts, compute, finish, bufs, send, recv, loads):
    x1, y1, x2, y2, sum_x, sum_y = bufs
    xn, yn = plane_neighbours()
    half = own_ref.shape[0] // 2
    top, low = pl.ds(0, half), pl.ds(half, half)
    plane_barrier(xn, yn)

    to_x = remote(own_ref, all_ref.at[1], send.at[0], recv.at[0], xn)
    to_y = remote(own_ref, all_ref.at[2], send.at[1], recv.at[1], yn)
    far_x = remote(all_ref.at[2, top], all_ref.at[3, top], send.at[2], recv.at[2], xn)
    far_y = remote(all_ref.at[1, low], all_ref.at[3, low], send.at[3], recv.at[3], yn)
    first_x = remote(parts.at[3, top], x1, send.at[4], recv.at[4], xn)
    first_y = remote(parts.at[3, low], y1, send.at[5], recv.at[5], yn)
    own_x = remote(parts.at[1, top], x2.at[top], send.at[6], recv.at[6], xn)
    own_y = remote(parts.at[2, low], y2.at[low], send.at[7], recv.at[7], yn)
    rest_x = remote(sum_x, x2.at[low], send.at[8], recv.at[8], xn)
    rest_y = remote(sum_y, y2.at[top], send.at[9], recv.at[9], yn)

    to_x.start()
    to_y.start()
    all_ref[0] = own_ref[...]
    for copy in loads:
        copy.wait()

    @pl.loop(0, 4)
    def _(i):
        @pl.when(i == 1)
        def _():
            to_x.wait_recv()
            far_y.start()
            to_y.wait_recv()
            far_x.start()

        @pl.when(i == 2)
        def _():
            own_x.start()
            far_x.wait_recv()
            far_y.wait_recv()

        @pl.when(i == 3)
        def _():
            first_x.start()
            first_y.start()

        compute(i + (i // 2) * (1 - 2 * lax.rem(i, 2)))

    own_y.start()
    first_x.wait_recv()
    sum_y[...] = (parts[2, top, :].astype(F32) + x1[...].astype(F32)).astype(BF)
    rest_y.start()
    first_y.wait_recv()
    sum_x[...] = (parts[1, low, :].astype(F32) + y1[...].astype(F32)).astype(BF)
    rest_x.start()
    own_x.wait_recv()
    rest_y.wait_recv()
    finish(top, parts[0, top, :].astype(F32) + x2[top, :].astype(F32) + y2[top, :].astype(F32))
    own_y.wait_recv()
    rest_x.wait_recv()
    finish(low, parts[0, low, :].astype(F32) + x2[low, :].astype(F32) + y2[low, :].astype(F32))
    for copy in (to_x, to_y, far_x, far_y, first_x, first_y, own_x, own_y, rest_x, rest_y):
        copy.wait_send()


def forward_kernel(
    layer, own, up_both, down_both, bias, resid, par, out, all_ref, active, slope,
    up, down, load, parts, x1, y1, x2, y2, sx, sy, send, recv,
):
    loads = load_layer(layer, (up_both, down_both), (up, down), load)

    def finish(at, value):
        out[at, :] = (resid[at, :] + value + par[7:8, :]).astype(BF)

    def compute(r):
        slope[r] = mm(all_ref[r], up[...]) + bias[...]

        @pl.loop(0, own.shape[0] // 64)
        def _(j):
            at = pl.ds(pl.multiple_of(j * 64, 64), 64)
            z = slope[r, at, :]
            cdf, pdf = phi_parts(z)
            active[r, at, :] = (z * cdf).astype(BF)
            slope[r, at, :] = cdf + z * pdf

        parts[r] = mm(active[r], down[...]).astype(BF)

    exchange_rows(own, all_ref, parts, compute, finish, (x1, y1, x2, y2, sx, sy), send, recv, loads)


def backward_kernel(
    layer, own, up_both, down_both, slope, total, all_ref, dz_all, bias_g,
    up, down, load, parts, x1, y1, x2, y2, sx, sy, send, recv,
):
    loads = load_layer(layer, (up_both, down_both), (up, down), load)
    bias_g[...] = jnp.zeros_like(bias_g)

    def finish(at, value):
        total[at, :] = value

    def compute(r):
        dz = mm_nt(all_ref[r], down[...]) * slope[r]
        bias_g[...] += jnp.sum(dz, axis=0, keepdims=True)
        dz_all[r] = dz.astype(BF)
        parts[r] = mm_nt(dz_all[r], up[...]).astype(BF)

    exchange_rows(own, all_ref, parts, compute, finish, (x1, y1, x2, y2, sx, sy), send, recv, loads)


VSPEC = pl.BlockSpec(memory_space=pltpu.VMEM)


def lasting(micros):
    return pl.CostEstimate(flops=0, transcendentals=0, bytes_accessed=int(micros * 3.5e6))


def plane_call(kernel, ident, outs, rows, *operands):
    half = rows // 2
    any_spec = pl.BlockSpec(memory_space=pl.ANY)
    return pl.pallas_call(
        kernel,
        out_shape=outs,
        in_specs=[VSPEC, any_spec, any_spec] + [VSPEC] * (len(operands) - 3),
        out_specs=(VSPEC,) * len(outs),
        scratch_shapes=[
            pltpu.VMEM((D, D), BF),
            pltpu.VMEM((D, D), BF),
            pltpu.SemaphoreType.DMA((2,)),
            pltpu.VMEM((4, rows, D), BF),
            pltpu.VMEM((half, D), BF),
            pltpu.VMEM((half, D), BF),
            pltpu.VMEM((rows, D), BF),
            pltpu.VMEM((rows, D), BF),
            pltpu.VMEM((half, D), BF),
            pltpu.VMEM((half, D), BF),
            pltpu.SemaphoreType.DMA((10,)),
            pltpu.SemaphoreType.DMA((10,)),
        ],
        compiler_params=pltpu.CompilerParams(
            collective_id=ident, has_side_effects=True, vmem_limit_bytes=40 * 1024 * 1024
        ),
        cost_estimate=lasting(40),
    )(*operands)


def mlp_forward(own, up, down, layer, bias, resid, par):
    rows = own.shape[0]
    if lax.axis_size("fsdp") != 4:
        every = lax.all_gather(own, "fsdp", axis=0, tiled=True)
        up, down = up[layer], down[layer]
        z = mm(every, up) + bias
        cdf, pdf = phi_parts(z)
        active = (z * cdf).astype(BF)
        part = mm(active, down).astype(BF)
        total = lax.psum_scatter(part, "fsdp", scatter_dimension=0, tiled=True).astype(F32)
        out = (resid + total + par[7]).astype(BF)
        return out, every, active, cdf + z * pdf
    shape = (4, rows, D)
    return plane_call(
        functools.partial(forward_kernel, layer), 1 + 6 * layer,
        (
            jax.ShapeDtypeStruct((rows, D), BF),
            jax.ShapeDtypeStruct(shape, BF),
            jax.ShapeDtypeStruct(shape, BF),
            jax.ShapeDtypeStruct(shape, F32),
        ),
        rows, own, up, down, bias, resid, par,
    )


def mlp_backward(own, up, down, layer, slope):
    rows = own.shape[0]
    if lax.axis_size("fsdp") != 4:
        every = lax.all_gather(own, "fsdp", axis=0, tiled=True)
        up, down = up[layer], down[layer]
        dz = mm_nt(every, down) * slope
        dz_b = dz.astype(BF)
        part = mm_nt(dz_b, up).astype(BF)
        total = lax.psum_scatter(part, "fsdp", scatter_dimension=0, tiled=True).astype(F32)
        return total, every, dz_b, jnp.sum(dz, axis=0, keepdims=True)
    shape = (4, rows, D)
    return plane_call(
        functools.partial(backward_kernel, layer), 2 + 6 * layer,
        (
            jax.ShapeDtypeStruct((rows, D), F32),
            jax.ShapeDtypeStruct(shape, BF),
            jax.ShapeDtypeStruct(shape, BF),
            jax.ShapeDtypeStruct((1, D), F32),
        ),
        rows, own, up, down, slope,
    )


def weights_kernel(
    own, rows_in, up_in, down_in, full, rows_out, up_out, down_out,
    up_blocks, load, core_s, core_r, p_send, p_recv, f_send, f_recv, z_send, z_recv,
    u_send, u_recv, v_send, v_recv,
):
    s = lax.axis_index("section")
    f = lax.axis_index("fsdp")
    xn, yn = plane_neighbours()
    dn = 3 - f
    shard, wide = own.shape[1], own.shape[2]
    cut = 640
    left = pl.ds(0, cut)
    right = pl.ds(cut, wide - cut)

    def to(src, dst, send, recv, **where):
        return pltpu.make_async_remote_copy(
            src_ref=src, dst_ref=dst, send_sem=send, recv_sem=recv,
            device_id=where, device_id_type=MESH,
        )

    barrier = pltpu.get_barrier_semaphore()
    z = lax.axis_index("ctx")
    above = {"ctx": lax.rem(z + 1, 4)}
    below = {"ctx": lax.rem(z + 3, 4)}
    partners = ({"section": 1 - s}, {"fsdp": xn}, {"fsdp": yn}, {"fsdp": dn}, above, below)
    for where in partners:
        pl.semaphore_signal(barrier, inc=1, device_id=where, device_id_type=MESH)
    pl.semaphore_wait(barrier, 6)
    rows = rows_in.shape[0]
    near_rows, far_rows = pl.ds(rows, rows), pl.ds(0, rows)
    step_one = to(rows_in, rows_out.at[near_rows], z_send.at[0], z_recv.at[0], **above)
    step_two = to(
        rows_out.at[near_rows], rows_out.at[far_rows], z_send.at[1], z_recv.at[1], **above
    )

    @pl.when(z < 3)
    def _():
        step_one.start()

    rows_out[pl.ds(2 * rows, rows), :] = rows_in[...]

    @pl.when(z == 0)
    def _():
        rows_out[near_rows, :] = jnp.zeros(rows_in.shape, BF)

    @pl.when(z < 2)
    def _():
        rows_out[far_rows, :] = jnp.zeros(rows_in.shape, BF)

    def blk(owner):
        return pl.ds(pl.multiple_of(owner * shard, 16), shard)

    def give(p):
        return to(own.at[p], full.at[p, blk(f)], core_s.at[p], core_r.at[p], section=1)

    def keep(p):
        return pltpu.make_async_copy(own.at[p], full.at[p, blk(f)], load.at[p])

    @pl.when(s == 0)
    def _():
        for p in (2, 3, 0, 1):
            give(p).start()
        for p in range(4):
            keep(p).start()
        keep(0).wait()
        keep(1).wait()

    @pl.when(s == 1)
    def _():
        give(2).wait_recv()
        give(3).wait_recv()

    def same(piece, rows, send, recv, cols=slice(None), **where):
        ref = full.at[piece, rows, cols]
        return to(ref, ref, send, recv, **where)

    def hops(k):
        p = 2 * s + k
        return (
            same(p, blk(f), p_send.at[k, 0], p_recv.at[k, 0], fsdp=xn),
            same(p, blk(f), p_send.at[k, 1], p_recv.at[k, 1], fsdp=yn),
            same(p, blk(yn), p_send.at[k, 2], p_recv.at[k, 2], left, fsdp=xn),
            same(p, blk(xn), p_send.at[k, 3], p_recv.at[k, 3], right, fsdp=yn),
        )

    def here(k):
        p = 2 * s + k
        return [
            same(p, blk(owner), f_send.at[k, i], f_recv.at[k, i], section=1 - s)
            for i, owner in enumerate((xn, yn, dn))
        ]

    for k in range(2):
        copies = hops(k)
        copies[0].start()
        copies[1].start()
    down_far = to(down_in, down_out.at[s], core_s.at[4], core_r.at[4], section=1 - s)
    down_near = pltpu.make_async_copy(down_in, down_out.at[s], load.at[4])
    down_far.start()
    down_near.start()
    for j in range(4):
        up_blocks[j] = up_in[:, pl.ds(j * D, D)]

    def up_to(i, owner, where):
        return to(up_blocks.at[owner], up_out.at[s, blk(f)], u_send.at[i], u_recv.at[i], fsdp=where)

    def up_over(i, owner):
        rows_here = up_out.at[s, blk(owner)]
        return to(rows_here, rows_here, v_send.at[i], v_recv.at[i], section=1 - s)

    others = (xn, yn, dn)
    up_near = pltpu.make_async_copy(up_blocks.at[f], up_out.at[s, blk(f)], load.at[5])
    up_near.start()
    for i, owner in enumerate(others):
        up_to(i, owner, owner).start()
    up_near.wait()
    up_over(3, f).start()
    for k in range(2):
        copies, across = hops(k), here(k)
        copies[0].wait_recv()
        copies[3].start()
        across[0].start()
        copies[1].wait_recv()
        copies[2].start()
        across[1].start()

    @pl.when(z > 0)
    def _():
        step_one.wait_recv()

    @pl.when((z == 1) | (z == 2))
    def _():
        step_two.start()

    for k in range(2):
        copies, across = hops(k), here(k)
        copies[2].wait_recv()
        copies[3].wait_recv()
        across[2].start()
    for i, owner in enumerate(others):
        up_to(i, owner, owner).wait_recv()
        up_over(i, owner).start()
    for k in range(2):
        for copy in here(k):
            copy.wait()
        for copy in hops(k):
            copy.wait_send()
    for i, owner in enumerate(others):
        up_to(i, owner, owner).wait_send()
        up_over(i, owner).wait()
    up_over(3, f).wait()

    @pl.when(s == 0)
    def _():
        for p in range(4):
            give(p).wait_send()
        keep(2).wait()
        keep(3).wait()

    @pl.when(s == 1)
    def _():
        give(0).wait_recv()
        give(1).wait_recv()

    down_near.wait()
    down_far.wait()

    @pl.when(z < 3)
    def _():
        step_one.wait_send()

    @pl.when((z == 1) | (z == 2))
    def _():
        step_two.wait_send()

    @pl.when(z > 1)
    def _():
        step_two.wait_recv()


def first_weights(own, rows_in, up, down):
    dma = pltpu.SemaphoreType.DMA
    return pl.pallas_call(
        weights_kernel,
        out_shape=(
            jax.ShapeDtypeStruct((4, D, WIDE), BF),
            jax.ShapeDtypeStruct((3 * rows_in.shape[0], D), BF),
            jax.ShapeDtypeStruct((2, D, D), BF),
            jax.ShapeDtypeStruct((2, D, D), BF),
        ),
        in_specs=[pl.BlockSpec(memory_space=pl.ANY), VSPEC, VSPEC, pl.BlockSpec(memory_space=pl.ANY)],
        out_specs=(VSPEC,) * 4,
        scratch_shapes=[
            pltpu.VMEM((4, up.shape[0], D), BF),
            dma((6,)), dma((5,)), dma((5,)), dma((2, 4)), dma((2, 4)), dma((2, 3)), dma((2, 3)),
            dma((2,)), dma((2,)), dma((3,)), dma((3,)), dma((4,)), dma((4,)),
        ],
        compiler_params=pltpu.CompilerParams(
            collective_id=4, has_side_effects=True, vmem_limit_bytes=40 * 1024 * 1024
        ),
        cost_estimate=lasting(75),
        name="first_weights",
    )(own, rows_in, up, down)


def z_partners():
    z = lax.axis_index("ctx")
    return z + 1 - 2 * lax.rem(z, 2), 3 - z, (z == 1) | (z == 2)


def add_rows(dst, one, two, rows, step):
    @pl.loop(0, rows // step)
    def _(i):
        at = pl.ds(pl.multiple_of(i * step, 16), step)
        dst[at, :] = (one[at, :].astype(F32) + two[at, :].astype(F32)).astype(dst.dtype)


CUTS = ((0, 640, 384), (640, 512, 256))


def reduce_kernel(
    q0, k0, v0, o0, q1, k1, v1, o1, mlp, made0, made1, grad1, halo, d_resid, da_own, wide, par,
    qkv_out, out_out, down_out, up_out, made_out, grad_out,
    own_in, held, up_own, up_far, sent, caught, grad0,
    x1a, y1a, x2a, y2a, sxa, sya, ta, zaa, zba,
    x1b, y1b, x2b, y2b, sxb, syb, tb, zab, zbb,
    load, core_s, core_r, p_send, p_recv, z_send, z_recv, h_send, h_recv, x_send, x_recv,
):
    s = lax.axis_index("section")
    f = lax.axis_index("fsdp")
    xn, yn = plane_neighbours()
    dn = 3 - f
    side, across, inner = z_partners()
    pieces = ((q0, k0, v0, o0), (q1, k1, v1, o1))
    sets = (
        (x1a, y1a, x2a, y2a, sxa, sya, ta, zaa, zba),
        (x1b, y1b, x2b, y2b, sxb, syb, tb, zab, zbb),
    )
    shard = out_out.shape[0]
    rows = da_own.shape[0]
    z = lax.axis_index("ctx")
    above, below = {"ctx": lax.rem(z + 1, 4)}, {"ctx": lax.rem(z + 3, 4)}

    def to(src, dst, send, recv, **where):
        return pltpu.make_async_remote_copy(
            src_ref=src, dst_ref=dst, send_sem=send, recv_sem=recv,
            device_id=where, device_id_type=MESH,
        )

    barrier = pltpu.get_barrier_semaphore()
    partners = ({"section": 1 - s}, {"fsdp": xn}, {"fsdp": yn}, above, below)
    for where in partners:
        pl.semaphore_signal(barrier, inc=1, device_id=where, device_id_type=MESH)
    pl.semaphore_wait(barrier, 5)

    def blk(owner):
        return pl.ds(pl.multiple_of(owner * shard, 16), shard)

    def by_core(act):
        for core in range(2):
            pl.when(s == core)(functools.partial(act, core))

    def far(j, src):
        return to(src, held.at[j], core_s.at[j], core_r.at[j], section=1 - s)

    def near(j, src):
        return pltpu.make_async_copy(src, own_in.at[j % 2], load.at[j])

    def bufs(c):
        return tuple(ref.at[c // 2] for ref in sets[c % 2])

    def plane(c):
        x1, y1, x2, y2, sx, sy = bufs(c)[:6]
        own = held.at[c // 2]
        at, width, cut = CUTS[c % 2]
        left, right = pl.ds(at, cut), pl.ds(at + cut, width - cut)
        to_left, to_right = pl.ds(0, cut), pl.ds(cut, width - cut)
        sems = [(p_send.at[c, i], p_recv.at[c, i]) for i in range(6)]
        return (
            to(own.at[blk(dn), left], x1, *sems[0], fsdp=xn),
            to(own.at[blk(dn), right], y1, *sems[1], fsdp=yn),
            to(own.at[blk(xn), left], x2.at[:, to_left], *sems[2], fsdp=xn),
            to(own.at[blk(yn), right], y2.at[:, to_right], *sems[3], fsdp=yn),
            to(sx, x2.at[:, to_right], *sems[4], fsdp=xn),
            to(sy, y2.at[:, to_left], *sems[5], fsdp=yn),
        )

    def along(c):
        t, za, zb = bufs(c)[6:]
        sems = [(z_send.at[c, i], z_recv.at[c, i]) for i in range(3)]
        return (
            to(t, za, *sems[0], ctx=side),
            to(za, zb, *sems[1], ctx=across),
            to(zb, zb, *sems[2], ctx=side),
        )

    def join(j):
        far(j, q0).wait_recv()
        near(j, q0).wait()
        add_rows(held.at[j], own_in.at[j % 2], held.at[j], 4 * shard, 64)
        for c in (2 * j, 2 * j + 1):
            for copy in plane(c)[:4]:
                copy.start()
        if j < 2:
            by_core(lambda core: near(j + 2, pieces[core][j + 2]).start())

    def second(c):
        copies = plane(c)
        x1, y1, _, _, sx, sy = bufs(c)[:6]
        at, width, cut = CUTS[c % 2]
        own = held.at[c // 2]
        copies[0].wait_recv()
        add_rows(sy, own.at[blk(yn), pl.ds(at, cut)], x1, shard, 16)
        copies[5].start()
        copies[1].wait_recv()
        add_rows(sx, own.at[blk(xn), pl.ds(at + cut, width - cut)], y1, shard, 16)
        copies[4].start()

    def third(c):
        copies = plane(c)
        _, _, x2, y2, _, _, t, _, _ = bufs(c)
        at, width, _ = CUTS[c % 2]
        for copy in copies[2:]:
            copy.wait_recv()
        own = held.at[c // 2, blk(f), pl.ds(at, width)]

        @pl.loop(0, shard // 16)
        def _(i):
            part = pl.ds(pl.multiple_of(i * 16, 16), 16)
            t[part, :] = (
                own[part, :].astype(F32) + x2[part, :].astype(F32) + y2[part, :].astype(F32)
            ).astype(BF)

        @pl.when(jnp.logical_not(inner))
        def _():
            along(c)[0].start()

    def inward(c):
        @pl.when(inner)
        def _():
            t, za, _ = bufs(c)[6:]
            copies = along(c)
            copies[0].wait_recv()
            add_rows(za, t, za, shard, 16)
            copies[1].start()

    def crossed(c):
        @pl.when(inner)
        def _():
            _, za, zb = bufs(c)[6:]
            copies = along(c)
            copies[1].wait_recv()
            add_rows(zb, za, zb, shard, 16)
            copies[2].start()

    def last(c):
        at, width, _ = CUTS[c % 2]
        j = c // 2

        @pl.when(jnp.logical_not(inner))
        def _():
            along(c)[2].wait_recv()

        done = bufs(c)[8]
        keep = min(width, D - at) if j < 3 else width

        @pl.loop(0, shard // 16)
        def _(i):
            part = pl.ds(pl.multiple_of(i * 16, 16), 16)
            if j < 3:
                qkv_out[part, pl.ds(j * D + at, keep)] = done[part, pl.ds(0, keep)]
            else:
                out_out[part, pl.ds(at, keep)] = done[part, :]

    half = down_out.shape[0] // 2
    mine = pl.ds(pl.multiple_of(s * half, 16), half)
    down_far = to(mlp.at[0], down_out.at[mine], core_s.at[4], core_r.at[4], section=1 - s)
    down_near = pltpu.make_async_copy(mlp.at[0], down_out.at[mine], load.at[4])
    far_up = to(mlp.at[1], up_far, core_s.at[5], core_r.at[5], section=1 - s)
    near_up = pltpu.make_async_copy(mlp.at[1], up_own, load.at[5])

    def lay_up():
        far_up.wait_recv()
        near_up.wait()

        @pl.when(s == 1)
        def _():
            for k in range(2):
                up_out[:, pl.ds(k * D, D)] = up_far[pl.ds(k * shard, shard), :]
                up_out[:, pl.ds((2 + k) * D, D)] = up_own[pl.ds(k * shard, shard), :]

    back_one = to(halo.at[pl.ds(0, rows)], caught.at[0], h_send.at[0], h_recv.at[0], **below)
    back_two = to(sent, caught.at[1], h_send.at[1], h_recv.at[1], **below)

    def back():
        @pl.when(z < 3)
        def _():
            back_one.wait_recv()

        @pl.when(z == 3)
        def _():
            caught[0] = jnp.zeros_like(caught[0])

        @pl.when(z > 0)
        def _():
            add_rows(sent, halo.at[pl.ds(rows, rows)], caught.at[0], rows, 64)
            back_two.start()

    made_far = (
        to(made1, made_out.at[0], x_send.at[0], x_recv.at[0], section=1),
        to(made0, made_out.at[1], x_send.at[0], x_recv.at[0], section=0),
    )
    grad_far = (
        to(grad1, grad_out.at[0], x_send.at[1], x_recv.at[1], section=1),
        to(grad0, grad_out.at[1], x_send.at[1], x_recv.at[1], section=0),
    )
    made_near = (
        pltpu.make_async_copy(made0, made_out.at[0], load.at[6]),
        pltpu.make_async_copy(made1, made_out.at[1], load.at[6]),
    )
    grad_near = pltpu.make_async_copy(grad1, grad_out.at[1], load.at[7])

    def back_end():
        @pl.when(z < 3)
        def _():
            back_two.wait_recv()

        @pl.when(z == 3)
        def _():
            caught[1] = jnp.zeros_like(caught[1])

        unit, inv = norm_parts(wide[...].astype(F32))
        da = da_own[...] + caught[1].astype(F32)
        grad0[...] = d_resid[...] + norm_back(da, par[0:1, :], unit, inv)

        @pl.when(s == 0)
        def _():
            grad_out[0] = grad0[...]

        @pl.when(s == 1)
        def _():
            grad_far[1].start()

    @pl.when(s == 0)
    def _():
        made_far[0].start()
        grad_far[0].start()
        made_near[0].start()

    @pl.when(s == 1)
    def _():
        made_far[1].start()
        made_near[1].start()
        grad_near.start()

    @pl.when(z > 0)
    def _():
        back_one.start()

    for j in range(4):
        by_core(lambda core: far(j, pieces[1 - core][j]).start())
        if j < 2:
            by_core(lambda core: near(j, pieces[core][j]).start())
    for copy in (down_far, down_near, far_up, near_up):
        copy.start()

    join(0)
    for c in range(12):
        if c in (1, 3, 5):
            join((c + 1) // 2)
        if c < 8:
            second(c)
        if 1 <= c <= 8:
            third(c - 1)
        if 2 <= c <= 9:
            inward(c - 2)
        if 3 <= c <= 10:
            crossed(c - 3)
        if c >= 4:
            last(c - 4)
        if c == 2:
            back()
        if c == 4:
            lay_up()
        if c == 6:
            back_end()

    down_near.wait()
    down_far.wait()
    far_up.wait_send()

    @pl.when(s == 0)
    def _():
        made_near[0].wait()
        made_far[0].wait_send()
        grad_far[0].wait_send()
        made_far[1].wait_recv()
        grad_far[1].wait_recv()

    @pl.when(s == 1)
    def _():
        made_near[1].wait()
        grad_near.wait()
        made_far[1].wait_send()
        grad_far[1].wait_send()
        made_far[0].wait_recv()
        grad_far[0].wait_recv()

    @pl.when(z > 0)
    def _():
        back_one.wait_send()
        back_two.wait_send()

    for j in range(4):
        far(j, q0).wait_send()
    for c in range(8):
        for copy in plane(c):
            copy.wait_send()

    @pl.when(inner)
    def _():
        for c in range(8):
            for copy in along(c)[1:]:
                copy.wait_send()

    @pl.when(jnp.logical_not(inner))
    def _():
        for c in range(8):
            along(c)[0].wait_send()


def reduce_both(zero, one, mlp, made, grad1, halo, d_resid, da_own, wide, par):
    shard = D // 4
    rows = da_own.shape[0]
    dma = pltpu.SemaphoreType.DMA
    any_spec = pl.BlockSpec(memory_space=pl.ANY)

    def buf(*shape):
        return pltpu.VMEM(shape, BF)

    def part(_, width, cut):
        wide_buf = buf(4, shard, width)
        return [
            buf(4, shard, cut), buf(4, shard, width - cut), wide_buf, wide_buf,
            buf(4, shard, width - cut), buf(4, shard, cut), wide_buf, wide_buf, wide_buf,
        ]

    shapes = ((shard, 3 * D), (shard, WIDE), (D, D), (shard, 4 * D), (2, rows, D))
    return pl.pallas_call(
        reduce_kernel,
        out_shape=(
            *(jax.ShapeDtypeStruct(shape, BF) for shape in shapes),
            jax.ShapeDtypeStruct((2, rows, D), F32),
        ),
        in_specs=[any_spec] * 12 + [VSPEC] * 5,
        out_specs=(VSPEC,) * 6,
        scratch_shapes=[
            buf(2, D, WIDE), buf(4, D, WIDE), buf(D // 2, D), buf(D // 2, D), buf(rows, D),
            buf(2, rows, D), pltpu.VMEM((rows, D), F32), *part(*CUTS[0]), *part(*CUTS[1]),
            dma((8,)), dma((6,)), dma((6,)), dma((8, 6)), dma((8, 6)), dma((8, 3)), dma((8, 3)),
            dma((2,)), dma((2,)), dma((2,)), dma((2,)),
        ],
        compiler_params=pltpu.CompilerParams(
            collective_id=3, has_side_effects=True, vmem_limit_bytes=60 * 1024 * 1024
        ),
        cost_estimate=lasting(120),
        name="reduce_both",
    )(*zero, *one, mlp, *made, grad1, halo, d_resid, da_own, wide, par)


def final_kernel(
    qkv, out, mine, far, down_one, up_one, made, grads,
    qkv_f, out_f, down_f, up_f, small, made_out, grads_out,
):
    s = lax.axis_index("section")
    half = mine.shape[1]
    shard = qkv.shape[0]
    pick_row = (
        lax.broadcasted_iota(jnp.int32, (16, 128), 1)
        == lax.broadcasted_iota(jnp.int32, (16, 128), 0) + (D - TAIL)
    )
    small[...] = mm_nt(pick_row.astype(F32).astype(BF), out[:, pl.ds(TAIL, 128)])

    @pl.loop(0, made.shape[1] // 16)
    def _(i):
        at = pl.ds(pl.multiple_of(i * 16, 16), 16)
        for m in range(2):
            made_out[m, at, :] = made[m, at, :]
            grads_out[m, at, :] = grads[m, at, :]

    @pl.loop(0, shard // 16)
    def _(i):
        at = pl.ds(pl.multiple_of(i * 16, 16), 16)
        qkv_f[at, :] = qkv[at, :].astype(F32)
        out_f[at, :] = out[at, pl.ds(0, D)].astype(F32)

        @pl.when(s == 0)
        def _():
            for k in range(2):
                from_k = pl.ds(pl.multiple_of(k * shard + i * 16, 16), 16)
                up_f[at, pl.ds(k * D, D)] = mine[1, from_k, :].astype(F32)
                up_f[at, pl.ds((2 + k) * D, D)] = far[1, from_k, :].astype(F32)

        @pl.when(s == 1)
        def _():
            up_f[at, :] = up_one[at, :].astype(F32)

    @pl.loop(0, half // 16)
    def _(i):
        at = pl.ds(pl.multiple_of(i * 16, 16), 16)
        after = pl.ds(pl.multiple_of(half + i * 16, 16), 16)

        @pl.when(s == 0)
        def _():
            down_f[at, :] = mine[0, at, :].astype(F32)
            down_f[after, :] = far[0, at, :].astype(F32)

        @pl.when(s == 1)
        def _():
            down_f[at, :] = down_one[at, :].astype(F32)
            down_f[after, :] = down_one[after, :].astype(F32)


def final_layouts(*values):
    qkv, _, _, _, down_one, up_one, made, grads = values
    shard = qkv.shape[0]
    outs = [(shape, F32) for shape in (qkv.shape, (shard, D), down_one.shape, up_one.shape)]
    outs += [((16, shard), F32), (made.shape, BF), (grads.shape, F32)]
    return pl.pallas_call(
        final_kernel,
        out_shape=tuple(jax.ShapeDtypeStruct(*out) for out in outs),
        in_specs=[VSPEC] * 8,
        out_specs=(VSPEC,) * 7,
        compiler_params=pltpu.CompilerParams(vmem_limit_bytes=52 * 1024 * 1024),
        cost_estimate=lasting(10),
        name="final_layouts",
    )(*values)


def halves_pair(down, up):
    s = lax.axis_index("section")
    both = jnp.stack([down, up])
    both = both.reshape(2, 2, both.shape[1] // 2, D)
    keep = lax.dynamic_index_in_dim(both, s, 1, keepdims=False)
    give = lax.dynamic_index_in_dim(both, 1 - s, 1, keepdims=False)
    return (keep.astype(F32) + on_chip(give).astype(F32)).astype(BF)


def halves_settle(zero, one):
    s = lax.axis_index("section")
    mine, far = pick(s, zero, one), on_chip(pick(s, one, zero))
    return jnp.concatenate([pick(s, mine, far), pick(s, far, mine)], axis=1).astype(F32)


def reduce_plain(pieces):
    s = lax.axis_index("section")
    pair = ("fsdp", "section")
    a = jnp.stack([lax.psum_scatter(p, pair, scatter_dimension=0, tiled=True) for p in pieces])
    a = lax.psum(a, "ctx")
    far = on_chip(a)
    return jnp.concatenate([pick(s, a, far), pick(s, far, a)], axis=1)


def shift(value, steps):
    count = lax.axis_size("ctx")
    pairs = [(i, i + steps) for i in range(count) if 0 <= i + steps < count]
    return lax.ppermute(value, "ctx", pairs)


def with_halo(own, chunks):
    parts = [own]
    for _ in range(chunks):
        parts.append(shift(parts[-1], 1))
    return jnp.concatenate(parts[::-1], axis=0)


def return_halo(halo, chunks, rows):
    carried = None
    for far in range(chunks):
        mine = halo[far * rows : (far + 1) * rows]
        carried = mine if carried is None else mine + carried
        carried = shift(carried.astype(BF), -1).astype(F32)
    return carried


def pick(s, first, second):
    return jnp.where(s == 0, first, second)


def on_chip(value):
    return lax.ppermute(value, "section", SWAP)


def both_layers(own, s):
    other = on_chip(own)
    return pick(s, own, other), pick(s, other, own)


def flat(values):
    return values.reshape(-1, values.shape[-1])


def widen(values):
    return jnp.pad(values, ((0, 0), (0, WIDE - D)))


TAIL = 1024


def scores_forward(q, k, v, bias, lanes):
    outs = []
    for low in (True, False):
        one = jnp.where((lanes < HD) if low else (lanes >= HD), q, jnp.zeros_like(q))
        weight = jnp.exp(mm_nt(one, k) + bias)
        prob = weight * (1.0 / jnp.sum(weight, axis=-1, keepdims=True))
        outs.append(mm(prob.astype(BF), v))
    return jnp.where(lanes < HD, outs[0], outs[1]).astype(BF)


def scores_backward(q, k, v, grad, bias_t, lanes):
    dqs, dk, dv = [], 0.0, 0.0
    for low in (True, False):
        mine = (lanes < HD) if low else (lanes >= HD)
        one = jnp.where(mine, q, jnp.zeros_like(q))
        g = jnp.where(mine, grad, jnp.zeros_like(grad))
        weight = jnp.exp(mm_nt(k, one) + bias_t)
        prob = weight * (1.0 / jnp.sum(weight, axis=0, keepdims=True))
        d_prob = mm_nt(v, g)
        row = jnp.sum(prob * d_prob, axis=0, keepdims=True)
        d_score = (prob * (d_prob - row)).astype(BF)
        dqs.append(mm_tn(d_score, k))
        dk = dk + mm(d_score, one)
        dv = dv + mm(prob.astype(BF), g)
    dq = jnp.where(lanes < HD, dqs[0], dqs[1]) * SCALE
    return dq.astype(BF), dk.astype(BF), dv.astype(BF)


def lane_tile(i):
    return pl.ds(pl.multiple_of(i * 128, 128), 128)


def widened(row):
    return jnp.concatenate([row, jnp.zeros((row.shape[0], WIDE - D), row.dtype)], axis=1)


def ctx_ring(rows_in, landing, send, recv):
    z = lax.axis_index("ctx")
    above = {"ctx": lax.rem(z + 1, 4)}
    below = {"ctx": lax.rem(z + 3, 4)}
    rows = rows_in.shape[0]
    near, far = pl.ds(rows, rows), pl.ds(0, rows)
    barrier = pltpu.get_barrier_semaphore()

    def on(src, dst, i):
        return pltpu.make_async_remote_copy(
            src_ref=src, dst_ref=dst, send_sem=send.at[i], recv_sem=recv.at[i],
            device_id=above, device_id_type=MESH,
        )

    one = on(rows_in, landing.at[near], 0)
    two = on(landing.at[near], landing.at[far], 1)

    def begin():
        for where in (above, below):
            pl.semaphore_signal(barrier, inc=1, device_id=where, device_id_type=MESH)
        pl.semaphore_wait(barrier, 2)

        @pl.when(z < 3)
        def _():
            one.start()

        landing[pl.ds(2 * rows, rows), :] = rows_in[...]

        @pl.when(z == 0)
        def _():
            landing[near, :] = jnp.zeros(rows_in.shape, BF)

        @pl.when(z < 2)
        def _():
            landing[far, :] = jnp.zeros(rows_in.shape, BF)

    def middle():
        @pl.when(z > 0)
        def _():
            one.wait_recv()

        @pl.when((z == 1) | (z == 2))
        def _():
            two.start()

    def end():
        @pl.when(z > 1)
        def _():
            two.wait_recv()

        @pl.when(z < 3)
        def _():
            one.wait_send()

        @pl.when((z == 1) | (z == 2))
        def _():
            two.wait_send()

    return begin, middle, end


def block_kernel(
    ring, first, wq, wk, wv, wo, bias, normed, q_ref, k_ref, v_ref, att, resid, second, par, *rest
):
    rows = resid.shape[0]
    total = normed.shape[0]
    if ring:
        wide_out, held, wide, send, recv = rest
        begin, middle, end = ctx_ring(first, wide, send, recv)
        begin()
    else:
        (held,), wide = rest, first
    pick_row = (
        lax.broadcasted_iota(jnp.int32, (16, 128), 1)
        == lax.broadcasted_iota(jnp.int32, (16, 128), 0) + (D - TAIL)
    )
    par[...] = mm_nt(pick_row.astype(F32).astype(BF), wo[:, pl.ds(TAIL, 128)])
    last = total // rows - 1

    @pl.loop(0, last + 1)
    def _(i):
        if ring:
            pl.when(i == 1)(middle)
            pl.when(i == 2)(end)
        at = pl.ds(pl.multiple_of((last - i) * rows, 16), rows)
        unit, _ = norm_parts(wide[at, :].astype(F32))
        low = (unit * par[0:1, :] + par[2:3, :]).astype(BF)
        normed[at, :] = low
        k_ref[at, :] = mm(low, wk[...]).astype(BF)
        v_ref[at, :] = (mm(low, wv[...]) + widened(par[4:5, :])).astype(BF)

        @pl.when(i == 0)
        def _():
            q_ref[...] = (mm(normed[at, :], wq[...]) + widened(par[3:4, :])).astype(BF)

    own = pl.ds(total - rows, rows)
    lanes = lax.broadcasted_iota(jnp.int32, (rows, 128), 1)

    @pl.loop(0, WIDE // 128)
    def _(i):
        at = lane_tile(i)
        held[:, at] = scores_forward(
            q_ref[:, at] * jnp.asarray(SCALE, BF), k_ref[:, at], v_ref[:, at], bias[...], lanes
        )

    att[...] = held[:, pl.ds(0, D)]
    res = wide[own, :].astype(F32) + mm(att[...], wo[:, pl.ds(0, D)]) + par[5:6, :]
    resid[...] = res
    unit, _ = norm_parts(res)
    second[...] = (unit * par[1:2, :] + par[6:7, :]).astype(BF)
    if ring:
        wide_out[...] = wide[...]


def weight_specs(weights):
    if weights.ndim == 3:
        return [pl.BlockSpec((None, D, WIDE), lambda i, p=p: (p, 0, 0)) for p in range(4)]
    return [pl.BlockSpec((D, WIDE), lambda i, p=p: (0, p)) for p in range(4)]


def whole(shape):
    return pl.BlockSpec(shape, lambda i: (0,) * len(shape))


def block_forward(first, weights, bias, ring):
    rows, total = bias.shape
    outs = (
        ((total, D), BF), ((rows, WIDE), BF), ((total, WIDE), BF), ((total, WIDE), BF),
        ((rows, D), BF), ((rows, D), F32), ((rows, D), BF), ((16, D), F32),
    )
    scratch = [pltpu.VMEM((rows, WIDE), BF)]
    params = {}
    if ring:
        outs += (((total, D), BF),)
        scratch += [pltpu.VMEM((total, D), BF)] + [pltpu.SemaphoreType.DMA((2,))] * 2
        params = {"collective_id": 5, "has_side_effects": True}
    return pl.pallas_call(
        functools.partial(block_kernel, ring),
        out_shape=tuple(jax.ShapeDtypeStruct(*out) for out in outs),
        grid=(1,),
        in_specs=[whole(first.shape), *weight_specs(weights), whole(bias.shape)],
        out_specs=tuple(whole(shape) for shape, _ in outs),
        scratch_shapes=scratch,
        compiler_params=pltpu.CompilerParams(vmem_limit_bytes=56 * 1024 * 1024, **params),
        cost_estimate=lasting(45 if ring else 22),
        name="block_forward",
    )(first, weights, weights, weights, weights, bias)


def block_back_kernel(
    ring, d_second, up, resid, wide, q_ref, k_ref, v_ref, att, ffb_rows, wq, wk, wv, wo, par, bias_t,
    *rest,
):
    if ring:
        (d_in, d_low, dq_ref, dk_ref, dv_ref, left, right,
         held, sums, d_resid, da_own, da_halo, sent, caught, send, recv) = rest
    else:
        d_resid, dq_ref, dk_ref, dv_ref, da_own, da_halo, left, right, held, sums = rest
    rows = resid.shape[0]
    total = wide.shape[0]
    own = total - rows
    z = lax.axis_index("ctx")

    def back_to(src, dst, i):
        return pltpu.make_async_remote_copy(
            src_ref=src, dst_ref=dst, send_sem=send.at[i], recv_sem=recv.at[i],
            device_id={"ctx": lax.rem(z + 3, 4)}, device_id_type=MESH,
        )

    if ring:
        one = back_to(da_halo.at[pl.ds(0, rows)], caught.at[0], 0)
        two = back_to(sent, caught.at[1], 1)
        barrier = pltpu.get_barrier_semaphore()
        for step in (1, 3):
            pl.semaphore_signal(
                barrier, inc=1, device_id={"ctx": lax.rem(z + step, 4)}, device_id_type=MESH
            )
        pl.semaphore_wait(barrier, 2)

    def total_of(values):
        return jnp.sum(values, axis=0, keepdims=True)

    upstream = up[...].astype(F32)
    unit, inv = norm_parts(resid[...])
    grad = upstream + norm_back(d_second[...], par[1:2, :], unit, inv)
    d_resid[...] = grad
    sums[1:2, :] = total_of(d_second[...] * unit)
    sums[5:6, :] = total_of(grad)
    sums[6:7, :] = total_of(d_second[...])
    sums[7:8, :] = total_of(upstream)
    sums[8:16, :] = ffb_rows[...]
    low = grad.astype(BF)
    right[pl.ds(0, rows), :] = jnp.zeros((rows, WIDE), BF)
    right[pl.ds(0, rows), pl.ds(0, D)] = low
    right[pl.ds(rows, 16), :] = (
        lax.broadcasted_iota(jnp.int32, (16, WIDE), 1)
        == lax.broadcasted_iota(jnp.int32, (16, WIDE), 0) + D
    ).astype(F32).astype(BF)
    held[...] = jnp.zeros((rows, WIDE), BF)
    held[:, pl.ds(0, D)] = mm_nt(low, wo[:, pl.ds(0, D)]).astype(BF)
    lanes = lax.broadcasted_iota(jnp.int32, (rows, 128), 1)

    @pl.loop(0, WIDE // 128)
    def _(i):
        at = lane_tile(i)
        dq_ref[:, at], dk_ref[:, at], dv_ref[:, at] = scores_backward(
            q_ref[:, at] * jnp.asarray(SCALE, BF), k_ref[:, at], v_ref[:, at], held[:, at],
            bias_t[...], lanes,
        )

    sums[3:4, :] = total_of(dq_ref[...].astype(F32))[:, :D]
    sums[4:5, :] = total_of(dv_ref[...].astype(F32))[:, :D]
    sums[0:1, :] = jnp.zeros((1, D), F32)
    sums[2:3, :] = jnp.zeros((1, D), F32)

    def back(at):
        da = mm_nt(dk_ref[at, :], wk[...]) + mm_nt(dv_ref[at, :], wv[...])
        return da

    def count(da, at):
        unit, _ = norm_parts(wide[at, :].astype(F32))
        sums[0:1, :] += total_of(da * unit)
        sums[2:3, :] += total_of(da)

    @pl.loop(0, own // rows)
    def _(i):
        at = pl.ds(pl.multiple_of(i * rows, 16), rows)
        da = back(at)
        da_halo[at, :] = da.astype(BF)
        if ring:

            @pl.when((i == 0) & (z > 0))
            def _():
                one.start()

        count(da, at)

    at = pl.ds(own, rows)
    da = back(at) + mm_nt(dq_ref[...], wq[...])
    da_own[...] = da
    count(da, at)
    if ring:

        @pl.when(z < 3)
        def _():
            one.wait_recv()

        @pl.when(z == 3)
        def _():
            caught[0] = jnp.zeros_like(caught[0])

        @pl.when(z > 0)
        def _():
            add_rows(sent, da_halo.at[pl.ds(rows, rows)], caught.at[0], rows, 64)
            two.start()

    left[pl.ds(0, rows), :] = att[...]
    left[pl.ds(rows, 16), :] = sums[...].astype(BF)
    if ring:

        @pl.when(z < 3)
        def _():
            two.wait_recv()

        @pl.when(z == 3)
        def _():
            caught[1] = jnp.zeros_like(caught[1])

        @pl.loop(0, rows // 64)
        def _(i):
            part = pl.ds(pl.multiple_of(i * 64, 64), 64)
            behind = pl.ds(pl.multiple_of(own + i * 64, 64), 64)
            unit, inv = norm_parts(wide[behind, :].astype(F32))
            da = da_own[part, :] + caught[1, part, :].astype(F32)
            grad = d_resid[part, :] + norm_back(da, par[0:1, :], unit, inv)
            d_in[part, :] = grad
            d_low[part, :] = grad.astype(BF)

        @pl.when(z > 0)
        def _():
            one.wait_send()
            two.wait_send()


def block_backward(d_second, up, resid, wide, q, k, v, att, ffb_rows, weights, par, bias_t, ring):
    total, rows = wide.shape[0], resid.shape[0]
    f32_rows, low_rows = ((rows, D), F32), ((rows, D), BF)
    heads = (((rows, WIDE), BF), ((total, WIDE), BF), ((total, WIDE), BF))
    factors = (((rows + 16, D), BF), ((rows + 16, WIDE), BF))
    halo = ((total - rows, D), BF)
    held = [pltpu.VMEM((rows, WIDE), BF), pltpu.VMEM((16, D), F32)]
    params = {}
    if ring:
        outs = (f32_rows, low_rows, *heads, *factors)
        held += [pltpu.VMEM(*f32_rows), pltpu.VMEM(*f32_rows), pltpu.VMEM(*halo), pltpu.VMEM(*low_rows)]
        held += [pltpu.VMEM((2, rows, D), BF)] + [pltpu.SemaphoreType.DMA((2,))] * 2
        params = {"collective_id": 6, "has_side_effects": True}
    else:
        outs = (f32_rows, *heads, f32_rows, halo, *factors)
    before = (d_second, up, resid, wide, q, k, v, att, ffb_rows)
    return pl.pallas_call(
        functools.partial(block_back_kernel, ring),
        out_shape=tuple(jax.ShapeDtypeStruct(*out) for out in outs),
        grid=(1,),
        in_specs=[
            *(whole(value.shape) for value in before), *weight_specs(weights),
            whole(par.shape), whole(bias_t.shape),
        ],
        out_specs=tuple(whole(shape) for shape, _ in outs),
        scratch_shapes=held,
        compiler_params=pltpu.CompilerParams(vmem_limit_bytes=60 * 1024 * 1024, **params),
        cost_estimate=lasting(58 if ring else 38),
        name="block_backward",
    )(*before, weights, weights, weights, weights, par, bias_t)


def on_device(
    inputs, segments, cotangent, qkv_weight, out_weight, up_weight, down_weight,
    norm_gains, biases, ff_bias,
):
    rows = inputs.shape[2]
    length = segments.shape[2]
    chunks = min((length // 2 - 1 + rows - 1) // rows, lax.axis_size("ctx") - 1)
    reach = chunks * rows
    s = lax.axis_index("section")
    f = lax.axis_index("fsdp")
    nf = lax.axis_size("fsdp")
    shard = D // nf
    ff_here = ff_bias.shape[1]
    per_row = ff_here // shard
    pair = ("fsdp", "section")
    fits = nf == 4 and lax.axis_size("ctx") == 4 and chunks == 2

    own_in = lax.dynamic_index_in_dim(inputs, s, 0, keepdims=False)[0]
    own_cot = lax.dynamic_index_in_dim(cotangent, s, 0, keepdims=False)[0]
    seg = lax.dynamic_index_in_dim(segments, s, 0, keepdims=False)[0]
    start = lax.axis_index("ctx") * rows
    key_seg = lax.dynamic_slice_in_dim(
        jnp.pad(seg, (reach, 0), constant_values=-1), start, reach + rows, 0
    )
    allowed = (key_seg[reach:, None] == key_seg[None, :]) & (
        jnp.arange(reach + rows, dtype=jnp.int32)[None, :] - reach
        <= jnp.arange(rows, dtype=jnp.int32)[:, None]
    )

    bias = jnp.where(allowed, 0.0, -1e30).astype(F32)
    bias_t = bias.T

    small = jnp.concatenate(
        [norm_gains[0].T, biases[0].T, ff_bias[0].reshape(per_row, shard).T], axis=1
    )
    packed = jnp.stack(
        [
            widen(qkv_weight[0][:, :D]),
            widen(qkv_weight[0][:, D : 2 * D]),
            widen(qkv_weight[0][:, 2 * D :]),
            jnp.concatenate(
                [out_weight[0], small, jnp.zeros((shard, WIDE - D - 8 - per_row), BF)], axis=1
            ),
        ]
    )
    if fits:
        zero, wide_in, up_w, down_w = first_weights(
            packed, own_in, up_weight[0], down_weight[0]
        )
        packed, zero = lax.optimization_barrier((packed, zero))
    else:
        up_own = lax.all_to_all(
            up_weight[0].reshape(shard, nf, ff_here), "fsdp", split_axis=1, concat_axis=0, tiled=True
        ).reshape(D, ff_here)
        up_w = both_layers(up_own, s)
        down_w = both_layers(down_weight[0], s)
        wide_in = with_halo(own_in, chunks)
    half = shard // 2
    halves = packed.reshape(4, 2, half, WIDE)
    keep = lax.dynamic_index_in_dim(halves, s, 1, keepdims=False)
    give = lax.dynamic_index_in_dim(halves, 1 - s, 1, keepdims=False)

    def gathered(part):
        rows_first = part.transpose(1, 0, 2).reshape(half, 4 * WIDE)
        return lax.all_gather(rows_first, pair, axis=0, tiled=True)

    recv = on_chip(give)
    one = gathered(pick(s, recv, keep))
    if not fits:
        zero = gathered(pick(s, keep, recv))
    weights = (zero, one)

    kept = []
    current = own_in
    produced = []
    for layer in range(2):
        if layer == 1 and fits:
            *made, wide = block_forward(current, weights[layer], bias, True)
        else:
            wide = with_halo(current, chunks) if layer else wide_in
            made = block_forward(wide, weights[layer], bias, False)
        normed, q, k, v, att, resid, second, par = made
        ffb = lax.dynamic_slice(par, (8, f * shard), (per_row, shard)).reshape(1, ff_here)
        current, second_all, active, slope = mlp_forward(
            second, up_w, down_w, layer, ffb, resid, par
        )
        produced.append(current)
        kept.append((wide, normed, q, k, v, att, resid, second_all, slope, active, par))

    upstream = own_cot
    derived = [None, None]
    parts = [None, None]
    mlp_sums = [None, None]
    for layer in (1, 0):
        wide, normed, q, k, v, att, resid, second_all, slope, active, par = kept[layer]
        d_second, up_all, dz_b, ffb_g = mlp_backward(upstream, up_w, down_w, layer, slope)
        down_g = mm_tn(flat(active), flat(up_all))
        up_g = mm_tn(flat(second_all), flat(dz_b))
        ffb_rows = lax.dynamic_update_slice(
            jnp.zeros((8, D), F32), ffb_g.reshape(per_row, shard), (0, f * shard)
        )
        block = (
            d_second, upstream, resid, wide, q, k, v, att, ffb_rows, weights[layer], par, bias_t
        )
        if layer == 1 and fits:
            derived[1], upstream_next, dq, dk, dv, left, right = block_backward(*block, True)
        else:
            d_resid, dq, dk, dv, da_own, da_halo, left, right = block_backward(*block, False)
        if not fits:
            unit, inv = norm_parts(wide[reach:].astype(F32))
            late = return_halo(da_halo, chunks, rows)
            derived[layer] = d_resid + norm_back(da_own + late, par[0], unit, inv)
            upstream_next = derived[layer].astype(BF)
        pieces = (
            mm_tn(normed[reach:], dq).astype(BF),
            mm_tn(normed, dk).astype(BF),
            mm_tn(normed, dv).astype(BF),
            mm_tn(left, right).astype(BF),
        )
        parts[layer] = pieces
        up_g = lax.all_to_all(
            up_g.astype(BF).reshape(nf, shard, ff_here), "fsdp",
            split_axis=0, concat_axis=0, tiled=True,
        ).reshape(nf * shard * ff_here // D, D)
        down_g = down_g.astype(BF)
        down_g, up_g, _ = lax.optimization_barrier((down_g, up_g, dq))
        halves = halves_pair(down_g, up_g)
        if layer == 1:
            _, upstream_next = lax.optimization_barrier((halves, upstream_next))
        else:
            halves, mlp_sums[1] = lax.optimization_barrier((halves, mlp_sums[1]))
        mlp_sums[layer] = lax.psum(halves, "ctx")
        if layer == 1:
            upstream = upstream_next

    if fits:
        qkv_g, out_g, down_one, up_one, made, grads = reduce_both(
            parts[0], parts[1], mlp_sums[1], produced, derived[1], da_halo, d_resid, da_own,
            wide[reach:], par,
        )
        late_sum, qkv_g = lax.optimization_barrier((mlp_sums[0], qkv_g))
        far = lax.ppermute(late_sum, "section", [(1, 0)])
        qkv_g, out_g, grad_down, grad_up, small, made, grads = final_layouts(
            qkv_g, out_g, late_sum, far, down_one, up_one, made, grads
        )
        made, grads = made[None, :, None], grads[None, :, None]
    else:
        a_tot = pick(s, reduce_plain(parts[0]), reduce_plain(parts[1])).astype(F32)
        qkv_g = jnp.concatenate([a_tot[i, :, :D] for i in range(3)], axis=1)
        out_g = a_tot[3, :, :D]
        small = a_tot[3, :, D : D + 16].T
        grad_down, grad_up = split_up(halves_settle(*mlp_sums), nf, shard)
        made, grads = both_micros(produced, s), both_micros(derived, s)
    return (
        made,
        grads,
        qkv_g[None],
        out_g[None],
        grad_up[None],
        grad_down[None],
        small[None, :2],
        small[None, 2:8],
        small[8 : 8 + per_row].reshape(1, ff_here),
    )


def split_up(both, nf, shard):
    up = both[1].reshape(nf, shard, -1)
    return both[0], up.transpose(1, 0, 2).reshape(shard, -1)


def both_micros(layers, s):
    to_zero = lax.ppermute(layers[0], "section", [(1, 0)])
    to_one = lax.ppermute(layers[1], "section", [(0, 1)])
    out = jnp.stack([pick(s, layers[0], to_one), pick(s, to_zero, layers[1])])
    return out[None, :, None]


def solution(mesh):
    return jax.shard_map(
        on_device,
        mesh=mesh,
        in_specs=(
            P(None, "fsdp", "ctx", None),
            P(None, "fsdp", None),
            P(None, "fsdp", "ctx", None),
            P("section", "fsdp", None),
            P("section", "fsdp", None),
            P("section", "fsdp", None),
            P("section", "fsdp", None),
            P("section", None, "fsdp"),
            P("section", None, "fsdp"),
            P("section", "fsdp"),
        ),
        out_specs=(
            P("section", None, "fsdp", "ctx", None),
            P("section", None, "fsdp", "ctx", None),
            P("section", "fsdp", None),
            P("section", "fsdp", None),
            P("section", "fsdp", None),
            P("section", "fsdp", None),
            P("section", None, "fsdp"),
            P("section", None, "fsdp"),
            P("section", "fsdp"),
        ),
        check_vma=False,
    )
```

```python
import functools
import math

import jax
import jax.numpy as jnp
from jax import lax
from jax.experimental import pallas as pl
from jax.experimental.pallas import tpu as pltpu
from jax.sharding import PartitionSpec as P

D = 1088
HD = 64
F32 = jnp.float32
BF = jnp.bfloat16
SCALE = 1.0 / math.sqrt(HD)
WIDE = 1152
MESH = pl.DeviceIdType.MESH
SWAP = [(0, 1), (1, 0)]


def mm(a, b):
    return jnp.dot(a, b, preferred_element_type=F32)


def mm_nt(a, b):
    return lax.dot_general(a, b, (((1,), (1,)), ((), ())), preferred_element_type=F32)


def mm_tn(a, b):
    return lax.dot_general(a, b, (((0,), (0,)), ((), ())), preferred_element_type=F32)


def norm_parts(values):
    center = jnp.mean(values, axis=-1, keepdims=True)
    offset = values - center
    spread = jnp.mean(offset * offset, axis=-1, keepdims=True)
    inv = lax.rsqrt(spread + 1e-05)
    return offset * inv, inv


def norm_back(grad, gain, unit, inv):
    dn = grad * gain
    return inv * (
        dn
        - jnp.mean(dn, axis=-1, keepdims=True)
        - unit * jnp.mean(dn * unit, axis=-1, keepdims=True)
    )


def phi_parts(z):
    cdf = 0.5 * (1.0 + lax.erf(z * (1.0 / math.sqrt(2.0))))
    pdf = jnp.exp(-0.5 * z * z) * (1.0 / math.sqrt(2.0 * math.pi))
    return cdf, pdf


def plane_neighbours():
    f = lax.axis_index("fsdp")
    x = lax.rem(f, 2)
    y = f // 2
    return y * 2 + (1 - x), (1 - y) * 2 + x


def plane_barrier(xn, yn):
    barrier = pltpu.get_barrier_semaphore()
    for nb in (xn, yn):
        pl.semaphore_signal(barrier, inc=1, device_id={"fsdp": nb}, device_id_type=MESH)
    pl.semaphore_wait(barrier, 2)


def remote(src, dst, send, recv, nb):
    return pltpu.make_async_remote_copy(
        src_ref=src, dst_ref=dst, send_sem=send, recv_sem=recv,
        device_id={"fsdp": nb}, device_id_type=MESH,
    )


def load_layer(layer, sources, targets, sems):
    copies = [
        pltpu.make_async_copy(source.at[layer], target, sems.at[i])
        for i, (source, target) in enumerate(zip(sources, targets))
    ]
    for copy in copies:
        copy.start()
    return copies


def exchange_rows(own_ref, all_ref, parts, compute, finish, bufs, send, recv, loads):
    x1, y1, x2, y2, sum_x, sum_y = bufs
    xn, yn = plane_neighbours()
    half = own_ref.shape[0] // 2
    top, low = pl.ds(0, half), pl.ds(half, half)
    plane_barrier(xn, yn)

    to_x = remote(own_ref, all_ref.at[1], send.at[0], recv.at[0], xn)
    to_y = remote(own_ref, all_ref.at[2], send.at[1], recv.at[1], yn)
    far_x = remote(all_ref.at[2, top], all_ref.at[3, top], send.at[2], recv.at[2], xn)
    far_y = remote(all_ref.at[1, low], all_ref.at[3, low], send.at[3], recv.at[3], yn)
    first_x = remote(parts.at[3, top], x1, send.at[4], recv.at[4], xn)
    first_y = remote(parts.at[3, low], y1, send.at[5], recv.at[5], yn)
    own_x = remote(parts.at[1, top], x2.at[top], send.at[6], recv.at[6], xn)
    own_y = remote(parts.at[2, low], y2.at[low], send.at[7], recv.at[7], yn)
    rest_x = remote(sum_x, x2.at[low], send.at[8], recv.at[8], xn)
    rest_y = remote(sum_y, y2.at[top], send.at[9], recv.at[9], yn)

    to_x.start()
    to_y.start()
    all_ref[0] = own_ref[...]
    for copy in loads:
        copy.wait()

    @pl.loop(0, 4)
    def _(i):
        @pl.when(i == 1)
        def _():
            to_x.wait_recv()
            far_y.start()
            to_y.wait_recv()
            far_x.start()

        @pl.when(i == 2)
        def _():
            own_x.start()
            far_x.wait_recv()
            far_y.wait_recv()

        @pl.when(i == 3)
        def _():
            first_x.start()
            first_y.start()

        compute(i + (i // 2) * (1 - 2 * lax.rem(i, 2)))

    own_y.start()
    first_x.wait_recv()
    sum_y[...] = (parts[2, top, :].astype(F32) + x1[...].astype(F32)).astype(BF)
    rest_y.start()
    first_y.wait_recv()
    sum_x[...] = (parts[1, low, :].astype(F32) + y1[...].astype(F32)).astype(BF)
    rest_x.start()
    own_x.wait_recv()
    rest_y.wait_recv()
    finish(top, parts[0, top, :].astype(F32) + x2[top, :].astype(F32) + y2[top, :].astype(F32))
    own_y.wait_recv()
    rest_x.wait_recv()
    finish(low, parts[0, low, :].astype(F32) + x2[low, :].astype(F32) + y2[low, :].astype(F32))
    for copy in (to_x, to_y, far_x, far_y, first_x, first_y, own_x, own_y, rest_x, rest_y):
        copy.wait_send()


def forward_kernel(
    layer, own, up_both, down_both, bias, resid, par, out, all_ref, active, slope,
    up, down, load, parts, x1, y1, x2, y2, sx, sy, send, recv,
):
    loads = load_layer(layer, (up_both, down_both), (up, down), load)

    def finish(at, value):
        out[at, :] = (resid[at, :] + value + par[7:8, :]).astype(BF)

    def compute(r):
        slope[r] = mm(all_ref[r], up[...]) + bias[...]

        @pl.loop(0, own.shape[0] // 64)
        def _(j):
            at = pl.ds(pl.multiple_of(j * 64, 64), 64)
            z = slope[r, at, :]
            cdf, pdf = phi_parts(z)
            active[r, at, :] = (z * cdf).astype(BF)
            slope[r, at, :] = cdf + z * pdf

        parts[r] = mm(active[r], down[...]).astype(BF)

    exchange_rows(own, all_ref, parts, compute, finish, (x1, y1, x2, y2, sx, sy), send, recv, loads)


def backward_kernel(
    layer, own, up_both, down_both, slope, total, all_ref, dz_all, bias_g,
    up, down, load, parts, x1, y1, x2, y2, sx, sy, send, recv,
):
    loads = load_layer(layer, (up_both, down_both), (up, down), load)
    bias_g[...] = jnp.zeros_like(bias_g)

    def finish(at, value):
        total[at, :] = value

    def compute(r):
        dz = mm_nt(all_ref[r], down[...]) * slope[r]
        bias_g[...] += jnp.sum(dz, axis=0, keepdims=True)
        dz_all[r] = dz.astype(BF)
        parts[r] = mm_nt(dz_all[r], up[...]).astype(BF)

    exchange_rows(own, all_ref, parts, compute, finish, (x1, y1, x2, y2, sx, sy), send, recv, loads)


VSPEC = pl.BlockSpec(memory_space=pltpu.VMEM)


def lasting(micros):
    return pl.CostEstimate(flops=0, transcendentals=0, bytes_accessed=int(micros * 3.5e6))


def plane_call(kernel, ident, outs, rows, *operands):
    half = rows // 2
    any_spec = pl.BlockSpec(memory_space=pl.ANY)
    return pl.pallas_call(
        kernel,
        out_shape=outs,
        in_specs=[VSPEC, any_spec, any_spec] + [VSPEC] * (len(operands) - 3),
        out_specs=(VSPEC,) * len(outs),
        scratch_shapes=[
            pltpu.VMEM((D, D), BF),
            pltpu.VMEM((D, D), BF),
            pltpu.SemaphoreType.DMA((2,)),
            pltpu.VMEM((4, rows, D), BF),
            pltpu.VMEM((half, D), BF),
            pltpu.VMEM((half, D), BF),
            pltpu.VMEM((rows, D), BF),
            pltpu.VMEM((rows, D), BF),
            pltpu.VMEM((half, D), BF),
            pltpu.VMEM((half, D), BF),
            pltpu.SemaphoreType.DMA((10,)),
            pltpu.SemaphoreType.DMA((10,)),
        ],
        compiler_params=pltpu.CompilerParams(
            collective_id=ident, has_side_effects=True, vmem_limit_bytes=40 * 1024 * 1024
        ),
        cost_estimate=lasting(40),
    )(*operands)


def mlp_forward(own, up, down, layer, bias, resid, par):
    rows = own.shape[0]
    if lax.axis_size("fsdp") != 4:
        every = lax.all_gather(own, "fsdp", axis=0, tiled=True)
        up, down = up[layer], down[layer]
        z = mm(every, up) + bias
        cdf, pdf = phi_parts(z)
        active = (z * cdf).astype(BF)
        part = mm(active, down).astype(BF)
        total = lax.psum_scatter(part, "fsdp", scatter_dimension=0, tiled=True).astype(F32)
        out = (resid + total + par[7]).astype(BF)
        return out, every, active, cdf + z * pdf
    shape = (4, rows, D)
    return plane_call(
        functools.partial(forward_kernel, layer), 1 + 6 * layer,
        (
            jax.ShapeDtypeStruct((rows, D), BF),
            jax.ShapeDtypeStruct(shape, BF),
            jax.ShapeDtypeStruct(shape, BF),
            jax.ShapeDtypeStruct(shape, F32),
        ),
        rows, own, up, down, bias, resid, par,
    )


def mlp_backward(own, up, down, layer, slope):
    rows = own.shape[0]
    if lax.axis_size("fsdp") != 4:
        every = lax.all_gather(own, "fsdp", axis=0, tiled=True)
        up, down = up[layer], down[layer]
        dz = mm_nt(every, down) * slope
        dz_b = dz.astype(BF)
        part = mm_nt(dz_b, up).astype(BF)
        total = lax.psum_scatter(part, "fsdp", scatter_dimension=0, tiled=True).astype(F32)
        return total, every, dz_b, jnp.sum(dz, axis=0, keepdims=True)
    shape = (4, rows, D)
    return plane_call(
        functools.partial(backward_kernel, layer), 2 + 6 * layer,
        (
            jax.ShapeDtypeStruct((rows, D), F32),
            jax.ShapeDtypeStruct(shape, BF),
            jax.ShapeDtypeStruct(shape, BF),
            jax.ShapeDtypeStruct((1, D), F32),
        ),
        rows, own, up, down, slope,
    )


def weights_kernel(
    qkv_in, out_in, gains, biases, hidden, rows_in, up_in, down_in,
    full, rows_out, up_out, down_out, next_half,
    own, other_half, up_blocks, load, core_s, core_r, p_send, p_recv, f_send, f_recv, z_send, z_recv,
    u_send, u_recv, v_send, v_recv,
):
    s = lax.axis_index("section")
    f = lax.axis_index("fsdp")
    xn, yn = plane_neighbours()
    dn = 3 - f
    shard, wide = own.shape[1], own.shape[2]
    cut = 640
    left = pl.ds(0, cut)
    right = pl.ds(cut, wide - cut)

    def to(src, dst, send, recv, **where):
        return pltpu.make_async_remote_copy(
            src_ref=src, dst_ref=dst, send_sem=send, recv_sem=recv,
            device_id=where, device_id_type=MESH,
        )

    pad = jnp.zeros((shard, wide - D), BF)
    for p in range(3):
        own[p] = jnp.concatenate([qkv_in[:, pl.ds(p * D, D)], pad], axis=1)
    unit_rows = (
        lax.broadcasted_iota(jnp.int32, (16, 64), 0) == lax.broadcasted_iota(jnp.int32, (16, 64), 1)
    ).astype(F32)
    hidden_rows = [hidden[:, pl.ds(i * shard, shard)] for i in range(hidden.shape[1] // shard)]
    small = jnp.concatenate(
        [
            value.astype(F32)
            for value in (gains[...], biases[...], *hidden_rows, jnp.zeros((8 - len(hidden_rows), shard)))
        ],
        axis=0,
    )
    beside = mm_tn(small.astype(BF), unit_rows.astype(BF)).astype(BF)
    own[3] = jnp.concatenate([out_in[...], beside], axis=1)

    barrier = pltpu.get_barrier_semaphore()
    z = lax.axis_index("ctx")
    above = {"ctx": lax.rem(z + 1, 4)}
    below = {"ctx": lax.rem(z + 3, 4)}
    partners = ({"section": 1 - s}, {"fsdp": xn}, {"fsdp": yn}, {"fsdp": dn}, above, below)
    for where in partners:
        pl.semaphore_signal(barrier, inc=1, device_id=where, device_id_type=MESH)
    pl.semaphore_wait(barrier, 6)
    rows = rows_in.shape[0]
    near_rows, far_rows = pl.ds(rows, rows), pl.ds(0, rows)
    step_one = to(rows_in, rows_out.at[near_rows], z_send.at[0], z_recv.at[0], **above)
    step_two = to(
        rows_out.at[near_rows], rows_out.at[far_rows], z_send.at[1], z_recv.at[1], **above
    )

    @pl.when(z < 3)
    def _():
        step_one.start()

    rows_out[pl.ds(2 * rows, rows), :] = rows_in[...]

    @pl.when(z == 0)
    def _():
        rows_out[near_rows, :] = jnp.zeros(rows_in.shape, BF)

    @pl.when(z < 2)
    def _():
        rows_out[far_rows, :] = jnp.zeros(rows_in.shape, BF)

    def blk(owner):
        return pl.ds(pl.multiple_of(owner * shard, 16), shard)

    def give(p):
        return to(own.at[p], full.at[p, blk(f)], core_s.at[p], core_r.at[p], section=1)

    def keep(p):
        return pltpu.make_async_copy(own.at[p], full.at[p, blk(f)], load.at[p])

    @pl.when(s == 0)
    def _():
        for p in (2, 3, 0, 1):
            give(p).start()
        for p in range(4):
            keep(p).start()
        keep(0).wait()
        keep(1).wait()

    @pl.when(s == 1)
    def _():
        give(2).wait_recv()
        give(3).wait_recv()

    def same(piece, rows, send, recv, cols=slice(None), **where):
        ref = full.at[piece, rows, cols]
        return to(ref, ref, send, recv, **where)

    def hops(k):
        p = 2 * s + k
        return (
            same(p, blk(f), p_send.at[k, 0], p_recv.at[k, 0], fsdp=xn),
            same(p, blk(f), p_send.at[k, 1], p_recv.at[k, 1], fsdp=yn),
            same(p, blk(yn), p_send.at[k, 2], p_recv.at[k, 2], left, fsdp=xn),
            same(p, blk(xn), p_send.at[k, 3], p_recv.at[k, 3], right, fsdp=yn),
        )

    def here(k):
        p = 2 * s + k
        return [
            same(p, blk(owner), f_send.at[k, i], f_recv.at[k, i], section=1 - s)
            for i, owner in enumerate((xn, yn, dn))
        ]

    for k in range(2):
        copies = hops(k)
        copies[0].start()
        copies[1].start()
    down_far = to(down_in, down_out.at[s], core_s.at[4], core_r.at[4], section=1 - s)
    down_near = pltpu.make_async_copy(down_in, down_out.at[s], load.at[4])
    down_far.start()
    down_near.start()
    swap = to(other_half, next_half, core_s.at[5], core_r.at[5], section=0)

    @pl.when(s == 1)
    def _():
        for p in range(4):
            at = pl.ds(p * wide, wide)
            other_half[:, at] = own[p, pl.ds(0, shard // 2), :]
            next_half[:, at] = own[p, pl.ds(shard // 2, shard // 2), :]
        swap.start()

    for j in range(4):
        up_blocks[j] = up_in[:, pl.ds(j * D, D)]

    def up_to(i, owner, where):
        return to(up_blocks.at[owner], up_out.at[s, blk(f)], u_send.at[i], u_recv.at[i], fsdp=where)

    def up_over(i, owner):
        rows_here = up_out.at[s, blk(owner)]
        return to(rows_here, rows_here, v_send.at[i], v_recv.at[i], section=1 - s)

    others = (xn, yn, dn)
    up_near = pltpu.make_async_copy(up_blocks.at[f], up_out.at[s, blk(f)], load.at[5])
    up_near.start()
    for i, owner in enumerate(others):
        up_to(i, owner, owner).start()
    up_near.wait()
    up_over(3, f).start()
    for k in range(2):
        copies, across = hops(k), here(k)
        copies[0].wait_recv()
        copies[3].start()
        across[0].start()
        copies[1].wait_recv()
        copies[2].start()
        across[1].start()

    @pl.when(z > 0)
    def _():
        step_one.wait_recv()

    @pl.when((z == 1) | (z == 2))
    def _():
        step_two.start()

    for k in range(2):
        copies, across = hops(k), here(k)
        copies[2].wait_recv()
        copies[3].wait_recv()
        across[2].start()
    for i, owner in enumerate(others):
        up_to(i, owner, owner).wait_recv()
        up_over(i, owner).start()
    for k in range(2):
        for copy in here(k):
            copy.wait()
        for copy in hops(k):
            copy.wait_send()
    for i, owner in enumerate(others):
        up_to(i, owner, owner).wait_send()
        up_over(i, owner).wait()
    up_over(3, f).wait()

    @pl.when(s == 0)
    def _():
        for p in range(4):
            give(p).wait_send()
        keep(2).wait()
        keep(3).wait()

    @pl.when(s == 1)
    def _():
        give(0).wait_recv()
        give(1).wait_recv()

    down_near.wait()
    down_far.wait()
    pl.when(s == 0)(swap.wait_recv)
    pl.when(s == 1)(swap.wait_send)

    @pl.when(z < 3)
    def _():
        step_one.wait_send()

    @pl.when((z == 1) | (z == 2))
    def _():
        step_two.wait_send()

    @pl.when(z > 1)
    def _():
        step_two.wait_recv()


def first_weights(qkv, out, gains, biases, hidden, rows_in, up, down):
    dma = pltpu.SemaphoreType.DMA
    shard = qkv.shape[0]
    shapes = ((4, D, WIDE), (3 * rows_in.shape[0], D), (2, D, D), (2, D, D), (shard // 2, 4 * WIDE))
    return pl.pallas_call(
        weights_kernel,
        out_shape=tuple(jax.ShapeDtypeStruct(shape, BF) for shape in shapes),
        in_specs=[VSPEC] * 7 + [pl.BlockSpec(memory_space=pl.ANY)],
        out_specs=(VSPEC,) * 5,
        scratch_shapes=[
            pltpu.VMEM((4, shard, WIDE), BF),
            pltpu.VMEM((shard // 2, 4 * WIDE), BF),
            pltpu.VMEM((4, shard, D), BF),
            dma((6,)), dma((6,)), dma((6,)), dma((2, 4)), dma((2, 4)), dma((2, 3)), dma((2, 3)),
            dma((2,)), dma((2,)), dma((3,)), dma((3,)), dma((4,)), dma((4,)),
        ],
        compiler_params=pltpu.CompilerParams(
            collective_id=4, has_side_effects=True, vmem_limit_bytes=48 * 1024 * 1024
        ),
        cost_estimate=lasting(75),
        name="first_weights",
    )(qkv, out, gains, biases, hidden, rows_in, up, down)


def z_partners():
    z = lax.axis_index("ctx")
    return z + 1 - 2 * lax.rem(z, 2), 3 - z, (z == 1) | (z == 2)


def add_rows(dst, one, two, rows, step):
    @pl.loop(0, rows // step)
    def _(i):
        at = pl.ds(pl.multiple_of(i * step, 16), step)
        dst[at, :] = (one[at, :].astype(F32) + two[at, :].astype(F32)).astype(dst.dtype)


CUTS = ((0, 640, 384), (640, 512, 256))


def reduce_kernel(
    q0, k0, v0, o0, q1, k1, v1, o1, mlp, made0, made1, grad1, halo, d_resid, da_own, wide, par,
    qkv_out, out_out, down_out, up_out, made_out, grad_out,
    own_in, held, up_own, up_far, sent, caught, grad0,
    x1a, y1a, x2a, y2a, sxa, sya, ta, zaa, zba,
    x1b, y1b, x2b, y2b, sxb, syb, tb, zab, zbb,
    load, core_s, core_r, p_send, p_recv, z_send, z_recv, h_send, h_recv, x_send, x_recv,
):
    s = lax.axis_index("section")
    f = lax.axis_index("fsdp")
    xn, yn = plane_neighbours()
    dn = 3 - f
    side, across, inner = z_partners()
    pieces = ((q0, k0, v0, o0), (q1, k1, v1, o1))
    sets = (
        (x1a, y1a, x2a, y2a, sxa, sya, ta, zaa, zba),
        (x1b, y1b, x2b, y2b, sxb, syb, tb, zab, zbb),
    )
    shard = out_out.shape[0]
    rows = da_own.shape[0]
    z = lax.axis_index("ctx")
    above, below = {"ctx": lax.rem(z + 1, 4)}, {"ctx": lax.rem(z + 3, 4)}

    def to(src, dst, send, recv, **where):
        return pltpu.make_async_remote_copy(
            src_ref=src, dst_ref=dst, send_sem=send, recv_sem=recv,
            device_id=where, device_id_type=MESH,
        )

    barrier = pltpu.get_barrier_semaphore()
    partners = ({"section": 1 - s}, {"fsdp": xn}, {"fsdp": yn}, above, below)
    for where in partners:
        pl.semaphore_signal(barrier, inc=1, device_id=where, device_id_type=MESH)
    pl.semaphore_wait(barrier, 5)

    def blk(owner):
        return pl.ds(pl.multiple_of(owner * shard, 16), shard)

    def by_core(act):
        for core in range(2):
            pl.when(s == core)(functools.partial(act, core))

    def far(j, src):
        return to(src, held.at[j], core_s.at[j], core_r.at[j], section=1 - s)

    def near(j, src):
        return pltpu.make_async_copy(src, own_in.at[j % 2], load.at[j])

    def bufs(c):
        return tuple(ref.at[c // 2] for ref in sets[c % 2])

    def plane(c):
        x1, y1, x2, y2, sx, sy = bufs(c)[:6]
        own = held.at[c // 2]
        at, width, cut = CUTS[c % 2]
        left, right = pl.ds(at, cut), pl.ds(at + cut, width - cut)
        to_left, to_right = pl.ds(0, cut), pl.ds(cut, width - cut)
        sems = [(p_send.at[c, i], p_recv.at[c, i]) for i in range(6)]
        return (
            to(own.at[blk(dn), left], x1, *sems[0], fsdp=xn),
            to(own.at[blk(dn), right], y1, *sems[1], fsdp=yn),
            to(own.at[blk(xn), left], x2.at[:, to_left], *sems[2], fsdp=xn),
            to(own.at[blk(yn), right], y2.at[:, to_right], *sems[3], fsdp=yn),
            to(sx, x2.at[:, to_right], *sems[4], fsdp=xn),
            to(sy, y2.at[:, to_left], *sems[5], fsdp=yn),
        )

    def along(c):
        t, za, zb = bufs(c)[6:]
        sems = [(z_send.at[c, i], z_recv.at[c, i]) for i in range(3)]
        return (
            to(t, za, *sems[0], ctx=side),
            to(za, zb, *sems[1], ctx=across),
            to(zb, zb, *sems[2], ctx=side),
        )

    def join(j):
        far(j, q0).wait_recv()
        near(j, q0).wait()
        add_rows(held.at[j], own_in.at[j % 2], held.at[j], 4 * shard, 64)
        for c in (2 * j, 2 * j + 1):
            for copy in plane(c)[:4]:
                copy.start()
        if j < 2:
            by_core(lambda core: near(j + 2, pieces[core][j + 2]).start())

    def second(c):
        copies = plane(c)
        x1, y1, _, _, sx, sy = bufs(c)[:6]
        at, width, cut = CUTS[c % 2]
        own = held.at[c // 2]
        copies[0].wait_recv()
        add_rows(sy, own.at[blk(yn), pl.ds(at, cut)], x1, shard, 16)
        copies[5].start()
        copies[1].wait_recv()
        add_rows(sx, own.at[blk(xn), pl.ds(at + cut, width - cut)], y1, shard, 16)
        copies[4].start()

    def third(c):
        copies = plane(c)
        _, _, x2, y2, _, _, t, _, _ = bufs(c)
        at, width, _ = CUTS[c % 2]
        for copy in copies[2:]:
            copy.wait_recv()
        own = held.at[c // 2, blk(f), pl.ds(at, width)]

        @pl.loop(0, shard // 16)
        def _(i):
            part = pl.ds(pl.multiple_of(i * 16, 16), 16)
            t[part, :] = (
                own[part, :].astype(F32) + x2[part, :].astype(F32) + y2[part, :].astype(F32)
            ).astype(BF)

        @pl.when(jnp.logical_not(inner))
        def _():
            along(c)[0].start()

    def inward(c):
        @pl.when(inner)
        def _():
            t, za, _ = bufs(c)[6:]
            copies = along(c)
            copies[0].wait_recv()
            add_rows(za, t, za, shard, 16)
            copies[1].start()

    def crossed(c):
        @pl.when(inner)
        def _():
            _, za, zb = bufs(c)[6:]
            copies = along(c)
            copies[1].wait_recv()
            add_rows(zb, za, zb, shard, 16)
            copies[2].start()

    def last(c):
        at, width, _ = CUTS[c % 2]
        j = c // 2

        @pl.when(jnp.logical_not(inner))
        def _():
            along(c)[2].wait_recv()

        done = bufs(c)[8]
        keep = min(width, D - at) if j < 3 else width

        @pl.loop(0, shard // 16)
        def _(i):
            part = pl.ds(pl.multiple_of(i * 16, 16), 16)
            if j < 3:
                qkv_out[part, pl.ds(j * D + at, keep)] = done[part, pl.ds(0, keep)]
            else:
                out_out[part, pl.ds(at, keep)] = done[part, :]

    half = down_out.shape[0] // 2
    mine = pl.ds(pl.multiple_of(s * half, 16), half)
    down_far = to(mlp.at[0], down_out.at[mine], core_s.at[4], core_r.at[4], section=1 - s)
    down_near = pltpu.make_async_copy(mlp.at[0], down_out.at[mine], load.at[4])
    far_up = to(mlp.at[1], up_far, core_s.at[5], core_r.at[5], section=1 - s)
    near_up = pltpu.make_async_copy(mlp.at[1], up_own, load.at[5])

    def lay_up():
        far_up.wait_recv()
        near_up.wait()

        @pl.when(s == 1)
        def _():
            for k in range(2):
                up_out[:, pl.ds(k * D, D)] = up_far[pl.ds(k * shard, shard), :]
                up_out[:, pl.ds((2 + k) * D, D)] = up_own[pl.ds(k * shard, shard), :]

    back_one = to(halo.at[pl.ds(0, rows)], caught.at[0], h_send.at[0], h_recv.at[0], **below)
    back_two = to(sent, caught.at[1], h_send.at[1], h_recv.at[1], **below)

    def back():
        @pl.when(z < 3)
        def _():
            back_one.wait_recv()

        @pl.when(z == 3)
        def _():
            caught[0] = jnp.zeros_like(caught[0])

        @pl.when(z > 0)
        def _():
            add_rows(sent, halo.at[pl.ds(rows, rows)], caught.at[0], rows, 64)
            back_two.start()

    made_far = (
        to(made1, made_out.at[0], x_send.at[0], x_recv.at[0], section=1),
        to(made0, made_out.at[1], x_send.at[0], x_recv.at[0], section=0),
    )
    grad_far = (
        to(grad1, grad_out.at[0], x_send.at[1], x_recv.at[1], section=1),
        to(grad0, grad_out.at[1], x_send.at[1], x_recv.at[1], section=0),
    )
    made_near = (
        pltpu.make_async_copy(made0, made_out.at[0], load.at[6]),
        pltpu.make_async_copy(made1, made_out.at[1], load.at[6]),
    )
    grad_near = pltpu.make_async_copy(grad1, grad_out.at[1], load.at[7])

    def back_end():
        @pl.when(z < 3)
        def _():
            back_two.wait_recv()

        @pl.when(z == 3)
        def _():
            caught[1] = jnp.zeros_like(caught[1])

        unit, inv = norm_parts(wide[...].astype(F32))
        da = da_own[...] + caught[1].astype(F32)
        grad0[...] = d_resid[...] + norm_back(da, par[0:1, :], unit, inv)

        @pl.when(s == 0)
        def _():
            grad_out[0] = grad0[...]

        @pl.when(s == 1)
        def _():
            grad_far[1].start()

    @pl.when(s == 0)
    def _():
        made_far[0].start()
        grad_far[0].start()
        made_near[0].start()

    @pl.when(s == 1)
    def _():
        made_far[1].start()
        made_near[1].start()
        grad_near.start()

    @pl.when(z > 0)
    def _():
        back_one.start()

    for j in range(4):
        by_core(lambda core: far(j, pieces[1 - core][j]).start())
        if j < 2:
            by_core(lambda core: near(j, pieces[core][j]).start())
    for copy in (down_far, down_near, far_up, near_up):
        copy.start()

    join(0)
    for c in range(12):
        if c in (1, 3, 5):
            join((c + 1) // 2)
        if c < 8:
            second(c)
        if 1 <= c <= 8:
            third(c - 1)
        if 2 <= c <= 9:
            inward(c - 2)
        if 3 <= c <= 10:
            crossed(c - 3)
        if c >= 4:
            last(c - 4)
        if c == 2:
            back()
        if c == 4:
            lay_up()
        if c == 6:
            back_end()

    down_near.wait()
    down_far.wait()
    far_up.wait_send()

    @pl.when(s == 0)
    def _():
        made_near[0].wait()
        made_far[0].wait_send()
        grad_far[0].wait_send()
        made_far[1].wait_recv()
        grad_far[1].wait_recv()

    @pl.when(s == 1)
    def _():
        made_near[1].wait()
        grad_near.wait()
        made_far[1].wait_send()
        grad_far[1].wait_send()
        made_far[0].wait_recv()
        grad_far[0].wait_recv()

    @pl.when(z > 0)
    def _():
        back_one.wait_send()
        back_two.wait_send()

    for j in range(4):
        far(j, q0).wait_send()
    for c in range(8):
        for copy in plane(c):
            copy.wait_send()

    @pl.when(inner)
    def _():
        for c in range(8):
            for copy in along(c)[1:]:
                copy.wait_send()

    @pl.when(jnp.logical_not(inner))
    def _():
        for c in range(8):
            along(c)[0].wait_send()


def reduce_both(zero, one, mlp, made, grad1, halo, d_resid, da_own, wide, par):
    shard = D // 4
    rows = da_own.shape[0]
    dma = pltpu.SemaphoreType.DMA
    any_spec = pl.BlockSpec(memory_space=pl.ANY)

    def buf(*shape):
        return pltpu.VMEM(shape, BF)

    def part(_, width, cut):
        wide_buf = buf(4, shard, width)
        return [
            buf(4, shard, cut), buf(4, shard, width - cut), wide_buf, wide_buf,
            buf(4, shard, width - cut), buf(4, shard, cut), wide_buf, wide_buf, wide_buf,
        ]

    shapes = ((shard, 3 * D), (shard, WIDE), (D, D), (shard, 4 * D), (2, rows, D))
    return pl.pallas_call(
        reduce_kernel,
        out_shape=(
            *(jax.ShapeDtypeStruct(shape, BF) for shape in shapes),
            jax.ShapeDtypeStruct((2, rows, D), F32),
        ),
        in_specs=[any_spec] * 12 + [VSPEC] * 5,
        out_specs=(VSPEC,) * 6,
        scratch_shapes=[
            buf(2, D, WIDE), buf(4, D, WIDE), buf(D // 2, D), buf(D // 2, D), buf(rows, D),
            buf(2, rows, D), pltpu.VMEM((rows, D), F32), *part(*CUTS[0]), *part(*CUTS[1]),
            dma((8,)), dma((6,)), dma((6,)), dma((8, 6)), dma((8, 6)), dma((8, 3)), dma((8, 3)),
            dma((2,)), dma((2,)), dma((2,)), dma((2,)),
        ],
        compiler_params=pltpu.CompilerParams(
            collective_id=3, has_side_effects=True, vmem_limit_bytes=60 * 1024 * 1024
        ),
        cost_estimate=lasting(120),
        name="reduce_both",
    )(*zero, *one, mlp, *made, grad1, halo, d_resid, da_own, wide, par)


def final_kernel(
    qkv, out, mine, far, down_one, up_one, made, grads,
    qkv_f, out_f, down_f, up_f, small, made_out, grads_out,
):
    s = lax.axis_index("section")
    half = mine.shape[1]
    shard = qkv.shape[0]
    pick_row = (
        lax.broadcasted_iota(jnp.int32, (16, 128), 1)
        == lax.broadcasted_iota(jnp.int32, (16, 128), 0) + (D - TAIL)
    )
    small[...] = mm_nt(pick_row.astype(F32).astype(BF), out[:, pl.ds(TAIL, 128)])

    @pl.loop(0, made.shape[1] // 16)
    def _(i):
        at = pl.ds(pl.multiple_of(i * 16, 16), 16)
        for m in range(2):
            made_out[m, at, :] = made[m, at, :]
            grads_out[m, at, :] = grads[m, at, :]

    @pl.loop(0, shard // 16)
    def _(i):
        at = pl.ds(pl.multiple_of(i * 16, 16), 16)
        qkv_f[at, :] = qkv[at, :].astype(F32)
        out_f[at, :] = out[at, pl.ds(0, D)].astype(F32)

        @pl.when(s == 0)
        def _():
            for k in range(2):
                from_k = pl.ds(pl.multiple_of(k * shard + i * 16, 16), 16)
                up_f[at, pl.ds(k * D, D)] = mine[1, from_k, :].astype(F32)
                up_f[at, pl.ds((2 + k) * D, D)] = far[1, from_k, :].astype(F32)

        @pl.when(s == 1)
        def _():
            up_f[at, :] = up_one[at, :].astype(F32)

    @pl.loop(0, half // 16)
    def _(i):
        at = pl.ds(pl.multiple_of(i * 16, 16), 16)
        after = pl.ds(pl.multiple_of(half + i * 16, 16), 16)

        @pl.when(s == 0)
        def _():
            down_f[at, :] = mine[0, at, :].astype(F32)
            down_f[after, :] = far[0, at, :].astype(F32)

        @pl.when(s == 1)
        def _():
            down_f[at, :] = down_one[at, :].astype(F32)
            down_f[after, :] = down_one[after, :].astype(F32)


def final_layouts(*values):
    qkv, _, _, _, down_one, up_one, made, grads = values
    shard = qkv.shape[0]
    outs = [(shape, F32) for shape in (qkv.shape, (shard, D), down_one.shape, up_one.shape)]
    outs += [((16, shard), F32), (made.shape, BF), (grads.shape, F32)]
    return pl.pallas_call(
        final_kernel,
        out_shape=tuple(jax.ShapeDtypeStruct(*out) for out in outs),
        in_specs=[VSPEC] * 8,
        out_specs=(VSPEC,) * 7,
        compiler_params=pltpu.CompilerParams(vmem_limit_bytes=52 * 1024 * 1024),
        cost_estimate=lasting(10),
        name="final_layouts",
    )(*values)


def halves_pair(down, up):
    s = lax.axis_index("section")
    both = jnp.stack([down, up])
    both = both.reshape(2, 2, both.shape[1] // 2, D)
    keep = lax.dynamic_index_in_dim(both, s, 1, keepdims=False)
    give = lax.dynamic_index_in_dim(both, 1 - s, 1, keepdims=False)
    return (keep.astype(F32) + on_chip(give).astype(F32)).astype(BF)


def halves_settle(zero, one):
    s = lax.axis_index("section")
    mine, far = pick(s, zero, one), on_chip(pick(s, one, zero))
    return jnp.concatenate([pick(s, mine, far), pick(s, far, mine)], axis=1).astype(F32)


def reduce_plain(pieces):
    s = lax.axis_index("section")
    pair = ("fsdp", "section")
    a = jnp.stack([lax.psum_scatter(p, pair, scatter_dimension=0, tiled=True) for p in pieces])
    a = lax.psum(a, "ctx")
    far = on_chip(a)
    return jnp.concatenate([pick(s, a, far), pick(s, far, a)], axis=1)


def shift(value, steps):
    count = lax.axis_size("ctx")
    pairs = [(i, i + steps) for i in range(count) if 0 <= i + steps < count]
    return lax.ppermute(value, "ctx", pairs)


def with_halo(own, chunks):
    parts = [own]
    for _ in range(chunks):
        parts.append(shift(parts[-1], 1))
    return jnp.concatenate(parts[::-1], axis=0)


def return_halo(halo, chunks, rows):
    carried = None
    for far in range(chunks):
        mine = halo[far * rows : (far + 1) * rows]
        carried = mine if carried is None else mine + carried
        carried = shift(carried.astype(BF), -1).astype(F32)
    return carried


def pick(s, first, second):
    return jnp.where(s == 0, first, second)


def on_chip(value):
    return lax.ppermute(value, "section", SWAP)


def both_layers(own, s):
    other = on_chip(own)
    return pick(s, own, other), pick(s, other, own)


def flat(values):
    return values.reshape(-1, values.shape[-1])


def widen(values):
    return jnp.pad(values, ((0, 0), (0, WIDE - D)))


TAIL = 1024


def scores_forward(q, k, v, bias, lanes):
    outs = []
    for low in (True, False):
        one = jnp.where((lanes < HD) if low else (lanes >= HD), q, jnp.zeros_like(q))
        weight = jnp.exp(mm_nt(one, k) + bias)
        prob = weight * (1.0 / jnp.sum(weight, axis=-1, keepdims=True))
        outs.append(mm(prob.astype(BF), v))
    return jnp.where(lanes < HD, outs[0], outs[1]).astype(BF)


def scores_backward(q, k, v, grad, bias_t, lanes):
    dqs, dk, dv = [], 0.0, 0.0
    for low in (True, False):
        mine = (lanes < HD) if low else (lanes >= HD)
        one = jnp.where(mine, q, jnp.zeros_like(q))
        g = jnp.where(mine, grad, jnp.zeros_like(grad))
        weight = jnp.exp(mm_nt(k, one) + bias_t)
        prob = weight * (1.0 / jnp.sum(weight, axis=0, keepdims=True))
        d_prob = mm_nt(v, g)
        row = jnp.sum(prob * d_prob, axis=0, keepdims=True)
        d_score = (prob * (d_prob - row)).astype(BF)
        dqs.append(mm_tn(d_score, k))
        dk = dk + mm(d_score, one)
        dv = dv + mm(prob.astype(BF), g)
    dq = jnp.where(lanes < HD, dqs[0], dqs[1]) * SCALE
    return dq.astype(BF), dk.astype(BF), dv.astype(BF)


def lane_tile(i):
    return pl.ds(pl.multiple_of(i * 128, 128), 128)


def widened(row):
    return jnp.concatenate([row, jnp.zeros((row.shape[0], WIDE - D), row.dtype)], axis=1)


def ctx_ring(rows_in, landing, send, recv):
    z = lax.axis_index("ctx")
    above = {"ctx": lax.rem(z + 1, 4)}
    below = {"ctx": lax.rem(z + 3, 4)}
    rows = rows_in.shape[0]
    near, far = pl.ds(rows, rows), pl.ds(0, rows)
    barrier = pltpu.get_barrier_semaphore()

    def on(src, dst, i):
        return pltpu.make_async_remote_copy(
            src_ref=src, dst_ref=dst, send_sem=send.at[i], recv_sem=recv.at[i],
            device_id=above, device_id_type=MESH,
        )

    one = on(rows_in, landing.at[near], 0)
    two = on(landing.at[near], landing.at[far], 1)

    def begin():
        for where in (above, below):
            pl.semaphore_signal(barrier, inc=1, device_id=where, device_id_type=MESH)
        pl.semaphore_wait(barrier, 2)

        @pl.when(z < 3)
        def _():
            one.start()

        landing[pl.ds(2 * rows, rows), :] = rows_in[...]

        @pl.when(z == 0)
        def _():
            landing[near, :] = jnp.zeros(rows_in.shape, BF)

        @pl.when(z < 2)
        def _():
            landing[far, :] = jnp.zeros(rows_in.shape, BF)

    def middle():
        @pl.when(z > 0)
        def _():
            one.wait_recv()

        @pl.when((z == 1) | (z == 2))
        def _():
            two.start()

    def end():
        @pl.when(z > 1)
        def _():
            two.wait_recv()

        @pl.when(z < 3)
        def _():
            one.wait_send()

        @pl.when((z == 1) | (z == 2))
        def _():
            two.wait_send()

    return begin, middle, end


def block_kernel(
    ring, first, wq, wk, wv, wo, bias, normed, q_ref, k_ref, v_ref, att, resid, second, par, *rest
):
    rows = resid.shape[0]
    total = normed.shape[0]
    if ring:
        wide_out, held, wide, send, recv = rest
        begin, middle, end = ctx_ring(first, wide, send, recv)
        begin()
    else:
        (held,), wide = rest, first
    pick_row = (
        lax.broadcasted_iota(jnp.int32, (16, 128), 1)
        == lax.broadcasted_iota(jnp.int32, (16, 128), 0) + (D - TAIL)
    )
    par[...] = mm_nt(pick_row.astype(F32).astype(BF), wo[:, pl.ds(TAIL, 128)])
    last = total // rows - 1

    @pl.loop(0, last + 1)
    def _(i):
        if ring:
            pl.when(i == 1)(middle)
            pl.when(i == 2)(end)
        at = pl.ds(pl.multiple_of((last - i) * rows, 16), rows)
        unit, _ = norm_parts(wide[at, :].astype(F32))
        low = (unit * par[0:1, :] + par[2:3, :]).astype(BF)
        normed[at, :] = low
        k_ref[at, :] = mm(low, wk[...]).astype(BF)
        v_ref[at, :] = (mm(low, wv[...]) + widened(par[4:5, :])).astype(BF)

        @pl.when(i == 0)
        def _():
            q_ref[...] = (mm(normed[at, :], wq[...]) + widened(par[3:4, :])).astype(BF)

    own = pl.ds(total - rows, rows)
    lanes = lax.broadcasted_iota(jnp.int32, (rows, 128), 1)

    @pl.loop(0, WIDE // 128)
    def _(i):
        at = lane_tile(i)
        held[:, at] = scores_forward(
            q_ref[:, at] * jnp.asarray(SCALE, BF), k_ref[:, at], v_ref[:, at], bias[...], lanes
        )

    att[...] = held[:, pl.ds(0, D)]
    res = wide[own, :].astype(F32) + mm(att[...], wo[:, pl.ds(0, D)]) + par[5:6, :]
    resid[...] = res
    unit, _ = norm_parts(res)
    second[...] = (unit * par[1:2, :] + par[6:7, :]).astype(BF)
    if ring:
        wide_out[...] = wide[...]


def weight_specs(weights):
    if weights.ndim == 3:
        return [pl.BlockSpec((None, D, WIDE), lambda i, p=p: (p, 0, 0)) for p in range(4)]
    return [pl.BlockSpec((D, WIDE), lambda i, p=p: (0, p)) for p in range(4)]


def whole(shape):
    return pl.BlockSpec(shape, lambda i: (0,) * len(shape))


def block_forward(first, weights, bias, ring):
    rows, total = bias.shape
    outs = (
        ((total, D), BF), ((rows, WIDE), BF), ((total, WIDE), BF), ((total, WIDE), BF),
        ((rows, D), BF), ((rows, D), F32), ((rows, D), BF), ((16, D), F32),
    )
    scratch = [pltpu.VMEM((rows, WIDE), BF)]
    params = {}
    if ring:
        outs += (((total, D), BF),)
        scratch += [pltpu.VMEM((total, D), BF)] + [pltpu.SemaphoreType.DMA((2,))] * 2
        params = {"collective_id": 5, "has_side_effects": True}
    return pl.pallas_call(
        functools.partial(block_kernel, ring),
        out_shape=tuple(jax.ShapeDtypeStruct(*out) for out in outs),
        grid=(1,),
        in_specs=[whole(first.shape), *weight_specs(weights), whole(bias.shape)],
        out_specs=tuple(whole(shape) for shape, _ in outs),
        scratch_shapes=scratch,
        compiler_params=pltpu.CompilerParams(vmem_limit_bytes=56 * 1024 * 1024, **params),
        cost_estimate=lasting(45 if ring else 22),
        name="block_forward",
    )(first, weights, weights, weights, weights, bias)


def block_back_kernel(
    ring, d_second, up, resid, wide, q_ref, k_ref, v_ref, att, ffb_rows, wq, wk, wv, wo, par, bias_t,
    *rest,
):
    if ring:
        (d_in, d_low, dq_ref, dk_ref, dv_ref, left, right,
         held, sums, d_resid, da_own, da_halo, sent, caught, send, recv) = rest
    else:
        d_resid, dq_ref, dk_ref, dv_ref, da_own, da_halo, left, right, held, sums = rest
    rows = resid.shape[0]
    total = wide.shape[0]
    own = total - rows
    z = lax.axis_index("ctx")

    def back_to(src, dst, i):
        return pltpu.make_async_remote_copy(
            src_ref=src, dst_ref=dst, send_sem=send.at[i], recv_sem=recv.at[i],
            device_id={"ctx": lax.rem(z + 3, 4)}, device_id_type=MESH,
        )

    if ring:
        one = back_to(da_halo.at[pl.ds(0, rows)], caught.at[0], 0)
        two = back_to(sent, caught.at[1], 1)
        barrier = pltpu.get_barrier_semaphore()
        for step in (1, 3):
            pl.semaphore_signal(
                barrier, inc=1, device_id={"ctx": lax.rem(z + step, 4)}, device_id_type=MESH
            )
        pl.semaphore_wait(barrier, 2)

    def total_of(values):
        return jnp.sum(values, axis=0, keepdims=True)

    upstream = up[...].astype(F32)
    unit, inv = norm_parts(resid[...])
    grad = upstream + norm_back(d_second[...], par[1:2, :], unit, inv)
    d_resid[...] = grad
    sums[1:2, :] = total_of(d_second[...] * unit)
    sums[5:6, :] = total_of(grad)
    sums[6:7, :] = total_of(d_second[...])
    sums[7:8, :] = total_of(upstream)
    sums[8:16, :] = ffb_rows[...]
    low = grad.astype(BF)
    right[pl.ds(0, rows), :] = jnp.zeros((rows, WIDE), BF)
    right[pl.ds(0, rows), pl.ds(0, D)] = low
    right[pl.ds(rows, 16), :] = (
        lax.broadcasted_iota(jnp.int32, (16, WIDE), 1)
        == lax.broadcasted_iota(jnp.int32, (16, WIDE), 0) + D
    ).astype(F32).astype(BF)
    held[...] = jnp.zeros((rows, WIDE), BF)
    held[:, pl.ds(0, D)] = mm_nt(low, wo[:, pl.ds(0, D)]).astype(BF)
    lanes = lax.broadcasted_iota(jnp.int32, (rows, 128), 1)

    @pl.loop(0, WIDE // 128)
    def _(i):
        at = lane_tile(i)
        dq_ref[:, at], dk_ref[:, at], dv_ref[:, at] = scores_backward(
            q_ref[:, at] * jnp.asarray(SCALE, BF), k_ref[:, at], v_ref[:, at], held[:, at],
            bias_t[...], lanes,
        )

    sums[3:4, :] = total_of(dq_ref[...].astype(F32))[:, :D]
    sums[4:5, :] = total_of(dv_ref[...].astype(F32))[:, :D]
    sums[0:1, :] = jnp.zeros((1, D), F32)
    sums[2:3, :] = jnp.zeros((1, D), F32)

    def back(at):
        da = mm_nt(dk_ref[at, :], wk[...]) + mm_nt(dv_ref[at, :], wv[...])
        return da

    def count(da, at):
        unit, _ = norm_parts(wide[at, :].astype(F32))
        sums[0:1, :] += total_of(da * unit)
        sums[2:3, :] += total_of(da)

    @pl.loop(0, own // rows)
    def _(i):
        at = pl.ds(pl.multiple_of(i * rows, 16), rows)
        da = back(at)
        da_halo[at, :] = da.astype(BF)
        if ring:

            @pl.when((i == 0) & (z > 0))
            def _():
                one.start()

        count(da, at)

    at = pl.ds(own, rows)
    da = back(at) + mm_nt(dq_ref[...], wq[...])
    da_own[...] = da
    count(da, at)
    if ring:

        @pl.when(z < 3)
        def _():
            one.wait_recv()

        @pl.when(z == 3)
        def _():
            caught[0] = jnp.zeros_like(caught[0])

        @pl.when(z > 0)
        def _():
            add_rows(sent, da_halo.at[pl.ds(rows, rows)], caught.at[0], rows, 64)
            two.start()

    left[pl.ds(0, rows), :] = att[...]
    left[pl.ds(rows, 16), :] = sums[...].astype(BF)
    if ring:

        @pl.when(z < 3)
        def _():
            two.wait_recv()

        @pl.when(z == 3)
        def _():
            caught[1] = jnp.zeros_like(caught[1])

        @pl.loop(0, rows // 64)
        def _(i):
            part = pl.ds(pl.multiple_of(i * 64, 64), 64)
            behind = pl.ds(pl.multiple_of(own + i * 64, 64), 64)
            unit, inv = norm_parts(wide[behind, :].astype(F32))
            da = da_own[part, :] + caught[1, part, :].astype(F32)
            grad = d_resid[part, :] + norm_back(da, par[0:1, :], unit, inv)
            d_in[part, :] = grad
            d_low[part, :] = grad.astype(BF)

        @pl.when(z > 0)
        def _():
            one.wait_send()
            two.wait_send()


def block_backward(d_second, up, resid, wide, q, k, v, att, ffb_rows, weights, par, bias_t, ring):
    total, rows = wide.shape[0], resid.shape[0]
    f32_rows, low_rows = ((rows, D), F32), ((rows, D), BF)
    heads = (((rows, WIDE), BF), ((total, WIDE), BF), ((total, WIDE), BF))
    factors = (((rows + 16, D), BF), ((rows + 16, WIDE), BF))
    halo = ((total - rows, D), BF)
    held = [pltpu.VMEM((rows, WIDE), BF), pltpu.VMEM((16, D), F32)]
    params = {}
    if ring:
        outs = (f32_rows, low_rows, *heads, *factors)
        held += [pltpu.VMEM(*f32_rows), pltpu.VMEM(*f32_rows), pltpu.VMEM(*halo), pltpu.VMEM(*low_rows)]
        held += [pltpu.VMEM((2, rows, D), BF)] + [pltpu.SemaphoreType.DMA((2,))] * 2
        params = {"collective_id": 6, "has_side_effects": True}
    else:
        outs = (f32_rows, *heads, f32_rows, halo, *factors)
    before = (d_second, up, resid, wide, q, k, v, att, ffb_rows)
    return pl.pallas_call(
        functools.partial(block_back_kernel, ring),
        out_shape=tuple(jax.ShapeDtypeStruct(*out) for out in outs),
        grid=(1,),
        in_specs=[
            *(whole(value.shape) for value in before), *weight_specs(weights),
            whole(par.shape), whole(bias_t.shape),
        ],
        out_specs=tuple(whole(shape) for shape, _ in outs),
        scratch_shapes=held,
        compiler_params=pltpu.CompilerParams(vmem_limit_bytes=60 * 1024 * 1024, **params),
        cost_estimate=lasting(58 if ring else 38),
        name="block_backward",
    )(*before, weights, weights, weights, weights, par, bias_t)


def on_device(
    inputs, segments, cotangent, qkv_weight, out_weight, up_weight, down_weight,
    norm_gains, biases, ff_bias,
):
    rows = inputs.shape[2]
    length = segments.shape[2]
    chunks = min((length // 2 - 1 + rows - 1) // rows, lax.axis_size("ctx") - 1)
    reach = chunks * rows
    s = lax.axis_index("section")
    f = lax.axis_index("fsdp")
    nf = lax.axis_size("fsdp")
    shard = D // nf
    ff_here = ff_bias.shape[1]
    per_row = ff_here // shard
    pair = ("fsdp", "section")
    fits = nf == 4 and lax.axis_size("ctx") == 4 and chunks == 2

    own_in = lax.dynamic_index_in_dim(inputs, s, 0, keepdims=False)[0]
    own_cot = lax.dynamic_index_in_dim(cotangent, s, 0, keepdims=False)[0]
    seg = lax.dynamic_index_in_dim(segments, s, 0, keepdims=False)[0]
    start = lax.axis_index("ctx") * rows
    key_seg = lax.dynamic_slice_in_dim(
        jnp.pad(seg, (reach, 0), constant_values=-1), start, reach + rows, 0
    )
    allowed = (key_seg[reach:, None] == key_seg[None, :]) & (
        jnp.arange(reach + rows, dtype=jnp.int32)[None, :] - reach
        <= jnp.arange(rows, dtype=jnp.int32)[:, None]
    )

    bias = jnp.where(allowed, 0.0, -1e30).astype(F32)
    bias_t = bias.T

    def gathered(rows_first):
        return lax.all_gather(rows_first, pair, axis=0, tiled=True)

    if fits:
        zero, wide_in, up_w, down_w, one_half = first_weights(
            qkv_weight[0], out_weight[0], norm_gains[0], biases[0], ff_bias,
            own_in, up_weight[0], down_weight[0],
        )
        one = gathered(one_half)
    else:
        small = jnp.concatenate(
            [norm_gains[0].T, biases[0].T, ff_bias[0].reshape(per_row, shard).T], axis=1
        )
        beside = jnp.pad(small, ((0, 0), (0, WIDE - D - 8 - per_row)))
        packed = jnp.concatenate(
            [widen(qkv_weight[0][:, i * D : (i + 1) * D]) for i in range(3)]
            + [out_weight[0], beside],
            axis=1,
        )
        halves = packed.reshape(2, shard // 2, 4 * WIDE)
        keep = lax.dynamic_index_in_dim(halves, s, 0, keepdims=False)
        recv = on_chip(lax.dynamic_index_in_dim(halves, 1 - s, 0, keepdims=False))
        zero, one = gathered(pick(s, keep, recv)), gathered(pick(s, recv, keep))
        up_own = lax.all_to_all(
            up_weight[0].reshape(shard, nf, ff_here), "fsdp", split_axis=1, concat_axis=0, tiled=True
        ).reshape(D, ff_here)
        up_w = both_layers(up_own, s)
        down_w = both_layers(down_weight[0], s)
        wide_in = with_halo(own_in, chunks)

    weights = (zero, one)

    kept = []
    current = own_in
    produced = []
    for layer in range(2):
        if layer == 1 and fits:
            *made, wide = block_forward(current, weights[layer], bias, True)
        else:
            wide = with_halo(current, chunks) if layer else wide_in
            made = block_forward(wide, weights[layer], bias, False)
        normed, q, k, v, att, resid, second, par = made
        ffb = lax.dynamic_slice(par, (8, f * shard), (per_row, shard)).reshape(1, ff_here)
        current, second_all, active, slope = mlp_forward(
            second, up_w, down_w, layer, ffb, resid, par
        )
        produced.append(current)
        kept.append((wide, normed, q, k, v, att, resid, second_all, slope, active, par))

    upstream = own_cot
    derived = [None, None]
    parts = [None, None]
    mlp_sums = [None, None]
    for layer in (1, 0):
        wide, normed, q, k, v, att, resid, second_all, slope, active, par = kept[layer]
        d_second, up_all, dz_b, ffb_g = mlp_backward(upstream, up_w, down_w, layer, slope)
        down_g = mm_tn(flat(active), flat(up_all))
        up_g = mm_tn(flat(second_all), flat(dz_b))
        ffb_rows = lax.dynamic_update_slice(
            jnp.zeros((8, D), F32), ffb_g.reshape(per_row, shard), (0, f * shard)
        )
        block = (
            d_second, upstream, resid, wide, q, k, v, att, ffb_rows, weights[layer], par, bias_t
        )
        if layer == 1 and fits:
            derived[1], upstream_next, dq, dk, dv, left, right = block_backward(*block, True)
        else:
            d_resid, dq, dk, dv, da_own, da_halo, left, right = block_backward(*block, False)
        if not fits:
            unit, inv = norm_parts(wide[reach:].astype(F32))
            late = return_halo(da_halo, chunks, rows)
            derived[layer] = d_resid + norm_back(da_own + late, par[0], unit, inv)
            upstream_next = derived[layer].astype(BF)
        pieces = (
            mm_tn(normed[reach:], dq).astype(BF),
            mm_tn(normed, dk).astype(BF),
            mm_tn(normed, dv).astype(BF),
            mm_tn(left, right).astype(BF),
        )
        parts[layer] = pieces
        up_g = lax.all_to_all(
            up_g.astype(BF).reshape(nf, shard, ff_here), "fsdp",
            split_axis=0, concat_axis=0, tiled=True,
        ).reshape(nf * shard * ff_here // D, D)
        down_g = down_g.astype(BF)
        down_g, up_g, _ = lax.optimization_barrier((down_g, up_g, dq))
        halves = halves_pair(down_g, up_g)
        if layer == 1:
            _, upstream_next = lax.optimization_barrier((halves, upstream_next))
        else:
            halves, mlp_sums[1] = lax.optimization_barrier((halves, mlp_sums[1]))
        mlp_sums[layer] = lax.psum(halves, "ctx")
        if layer == 1:
            upstream = upstream_next

    if fits:
        qkv_g, out_g, down_one, up_one, made, grads = reduce_both(
            parts[0], parts[1], mlp_sums[1], produced, derived[1], da_halo, d_resid, da_own,
            wide[reach:], par,
        )
        late_sum, qkv_g = lax.optimization_barrier((mlp_sums[0], qkv_g))
        far = lax.ppermute(late_sum, "section", [(1, 0)])
        qkv_g, out_g, grad_down, grad_up, small, made, grads = final_layouts(
            qkv_g, out_g, late_sum, far, down_one, up_one, made, grads
        )
        made, grads = made[None, :, None], grads[None, :, None]
    else:
        a_tot = pick(s, reduce_plain(parts[0]), reduce_plain(parts[1])).astype(F32)
        qkv_g = jnp.concatenate([a_tot[i, :, :D] for i in range(3)], axis=1)
        out_g = a_tot[3, :, :D]
        small = a_tot[3, :, D : D + 16].T
        grad_down, grad_up = split_up(halves_settle(*mlp_sums), nf, shard)
        made, grads = both_micros(produced, s), both_micros(derived, s)
    return (
        made,
        grads,
        qkv_g[None],
        out_g[None],
        grad_up[None],
        grad_down[None],
        small[None, :2],
        small[None, 2:8],
        small[8 : 8 + per_row].reshape(1, ff_here),
    )


def split_up(both, nf, shard):
    up = both[1].reshape(nf, shard, -1)
    return both[0], up.transpose(1, 0, 2).reshape(shard, -1)


def both_micros(layers, s):
    to_zero = lax.ppermute(layers[0], "section", [(1, 0)])
    to_one = lax.ppermute(layers[1], "section", [(0, 1)])
    out = jnp.stack([pick(s, layers[0], to_one), pick(s, to_zero, layers[1])])
    return out[None, :, None]


def solution(mesh):
    return jax.shard_map(
        on_device,
        mesh=mesh,
        in_specs=(
            P(None, "fsdp", "ctx", None),
            P(None, "fsdp", None),
            P(None, "fsdp", "ctx", None),
            P("section", "fsdp", None),
            P("section", "fsdp", None),
            P("section", "fsdp", None),
            P("section", "fsdp", None),
            P("section", None, "fsdp"),
            P("section", None, "fsdp"),
            P("section", "fsdp"),
        ),
        out_specs=(
            P("section", None, "fsdp", "ctx", None),
            P("section", None, "fsdp", "ctx", None),
            P("section", "fsdp", None),
            P("section", "fsdp", None),
            P("section", "fsdp", None),
            P("section", "fsdp", None),
            P("section", None, "fsdp"),
            P("section", None, "fsdp"),
            P("section", "fsdp"),
        ),
        check_vma=False,
    )
```

```python
import functools
import math

import jax
import jax.numpy as jnp
from jax import lax
from jax.experimental import pallas as pl
from jax.experimental.pallas import tpu as pltpu
from jax.sharding import PartitionSpec as P

D = 1088
HD = 64
F32 = jnp.float32
BF = jnp.bfloat16
SCALE = 1.0 / math.sqrt(HD)
WIDE = 1152
MESH = pl.DeviceIdType.MESH
SWAP = [(0, 1), (1, 0)]


def mm(a, b):
    return jnp.dot(a, b, preferred_element_type=F32)


def mm_nt(a, b):
    return lax.dot_general(a, b, (((1,), (1,)), ((), ())), preferred_element_type=F32)


def mm_tn(a, b):
    return lax.dot_general(a, b, (((0,), (0,)), ((), ())), preferred_element_type=F32)


def norm_parts(values):
    center = jnp.mean(values, axis=-1, keepdims=True)
    offset = values - center
    spread = jnp.mean(offset * offset, axis=-1, keepdims=True)
    inv = lax.rsqrt(spread + 1e-05)
    return offset * inv, inv


def norm_back(grad, gain, unit, inv):
    dn = grad * gain
    return inv * (
        dn
        - jnp.mean(dn, axis=-1, keepdims=True)
        - unit * jnp.mean(dn * unit, axis=-1, keepdims=True)
    )


def phi_parts(z):
    cdf = 0.5 * (1.0 + lax.erf(z * (1.0 / math.sqrt(2.0))))
    pdf = jnp.exp(-0.5 * z * z) * (1.0 / math.sqrt(2.0 * math.pi))
    return cdf, pdf


def plane_neighbours():
    f = lax.axis_index("fsdp")
    x = lax.rem(f, 2)
    y = f // 2
    return y * 2 + (1 - x), (1 - y) * 2 + x


def plane_barrier(xn, yn):
    barrier = pltpu.get_barrier_semaphore()
    for nb in (xn, yn):
        pl.semaphore_signal(barrier, inc=1, device_id={"fsdp": nb}, device_id_type=MESH)
    pl.semaphore_wait(barrier, 2)


def remote(src, dst, send, recv, nb):
    return pltpu.make_async_remote_copy(
        src_ref=src, dst_ref=dst, send_sem=send, recv_sem=recv,
        device_id={"fsdp": nb}, device_id_type=MESH,
    )


def load_layer(layer, sources, targets, sems):
    copies = [
        pltpu.make_async_copy(source.at[layer], target, sems.at[i])
        for i, (source, target) in enumerate(zip(sources, targets))
    ]
    for copy in copies:
        copy.start()
    return copies


def exchange_rows(own_ref, all_ref, parts, compute, finish, bufs, send, recv, loads):
    x1, y1, x2, y2, sum_x, sum_y = bufs
    xn, yn = plane_neighbours()
    half = own_ref.shape[0] // 2
    top, low = pl.ds(0, half), pl.ds(half, half)
    plane_barrier(xn, yn)

    to_x = remote(own_ref, all_ref.at[1], send.at[0], recv.at[0], xn)
    to_y = remote(own_ref, all_ref.at[2], send.at[1], recv.at[1], yn)
    far_x = remote(all_ref.at[2, top], all_ref.at[3, top], send.at[2], recv.at[2], xn)
    far_y = remote(all_ref.at[1, low], all_ref.at[3, low], send.at[3], recv.at[3], yn)
    first_x = remote(parts.at[3, top], x1, send.at[4], recv.at[4], xn)
    first_y = remote(parts.at[3, low], y1, send.at[5], recv.at[5], yn)
    own_x = remote(parts.at[1, top], x2.at[top], send.at[6], recv.at[6], xn)
    own_y = remote(parts.at[2, low], y2.at[low], send.at[7], recv.at[7], yn)
    rest_x = remote(sum_x, x2.at[low], send.at[8], recv.at[8], xn)
    rest_y = remote(sum_y, y2.at[top], send.at[9], recv.at[9], yn)

    to_x.start()
    to_y.start()
    all_ref[0] = own_ref[...]
    for copy in loads:
        copy.wait()

    @pl.loop(0, 4)
    def _(i):
        @pl.when(i == 1)
        def _():
            to_x.wait_recv()
            far_y.start()
            to_y.wait_recv()
            far_x.start()

        @pl.when(i == 2)
        def _():
            own_x.start()
            far_x.wait_recv()
            far_y.wait_recv()

        @pl.when(i == 3)
        def _():
            first_x.start()
            first_y.start()

        compute(i + (i // 2) * (1 - 2 * lax.rem(i, 2)))

    own_y.start()
    first_x.wait_recv()
    sum_y[...] = (parts[2, top, :].astype(F32) + x1[...].astype(F32)).astype(BF)
    rest_y.start()
    first_y.wait_recv()
    sum_x[...] = (parts[1, low, :].astype(F32) + y1[...].astype(F32)).astype(BF)
    rest_x.start()
    own_x.wait_recv()
    rest_y.wait_recv()
    finish(top, parts[0, top, :].astype(F32) + x2[top, :].astype(F32) + y2[top, :].astype(F32))
    own_y.wait_recv()
    rest_x.wait_recv()
    finish(low, parts[0, low, :].astype(F32) + x2[low, :].astype(F32) + y2[low, :].astype(F32))
    for copy in (to_x, to_y, far_x, far_y, first_x, first_y, own_x, own_y, rest_x, rest_y):
        copy.wait_send()


def forward_kernel(
    layer, own, up_both, down_both, bias, resid, par, out, all_ref, active, slope,
    up, down, load, parts, x1, y1, x2, y2, sx, sy, send, recv,
):
    loads = load_layer(layer, (up_both, down_both), (up, down), load)

    def finish(at, value):
        out[at, :] = (resid[at, :] + value + par[7:8, :]).astype(BF)

    def compute(r):
        slope[r] = mm(all_ref[r], up[...]) + bias[...]

        @pl.loop(0, own.shape[0] // 64)
        def _(j):
            at = pl.ds(pl.multiple_of(j * 64, 64), 64)
            z = slope[r, at, :]
            cdf, pdf = phi_parts(z)
            active[r, at, :] = (z * cdf).astype(BF)
            slope[r, at, :] = cdf + z * pdf

        parts[r] = mm(active[r], down[...]).astype(BF)

    exchange_rows(own, all_ref, parts, compute, finish, (x1, y1, x2, y2, sx, sy), send, recv, loads)


def backward_kernel(
    layer, own, up_both, down_both, slope, total, all_ref, dz_all, bias_g,
    up, down, load, parts, x1, y1, x2, y2, sx, sy, send, recv,
):
    loads = load_layer(layer, (up_both, down_both), (up, down), load)
    bias_g[...] = jnp.zeros_like(bias_g)

    def finish(at, value):
        total[at, :] = value

    def compute(r):
        dz = mm_nt(all_ref[r], down[...]) * slope[r]
        bias_g[...] += jnp.sum(dz, axis=0, keepdims=True)
        dz_all[r] = dz.astype(BF)
        parts[r] = mm_nt(dz_all[r], up[...]).astype(BF)

    exchange_rows(own, all_ref, parts, compute, finish, (x1, y1, x2, y2, sx, sy), send, recv, loads)


VSPEC = pl.BlockSpec(memory_space=pltpu.VMEM)


def lasting(micros):
    return pl.CostEstimate(flops=0, transcendentals=0, bytes_accessed=int(micros * 3.5e6))


def plane_call(kernel, ident, outs, rows, *operands):
    half = rows // 2
    any_spec = pl.BlockSpec(memory_space=pl.ANY)
    return pl.pallas_call(
        kernel,
        out_shape=outs,
        in_specs=[VSPEC, any_spec, any_spec] + [VSPEC] * (len(operands) - 3),
        out_specs=(VSPEC,) * len(outs),
        scratch_shapes=[
            pltpu.VMEM((D, D), BF),
            pltpu.VMEM((D, D), BF),
            pltpu.SemaphoreType.DMA((2,)),
            pltpu.VMEM((4, rows, D), BF),
            pltpu.VMEM((half, D), BF),
            pltpu.VMEM((half, D), BF),
            pltpu.VMEM((rows, D), BF),
            pltpu.VMEM((rows, D), BF),
            pltpu.VMEM((half, D), BF),
            pltpu.VMEM((half, D), BF),
            pltpu.SemaphoreType.DMA((10,)),
            pltpu.SemaphoreType.DMA((10,)),
        ],
        compiler_params=pltpu.CompilerParams(
            collective_id=ident, has_side_effects=True, vmem_limit_bytes=40 * 1024 * 1024
        ),
        cost_estimate=lasting(40),
    )(*operands)


def mlp_forward(own, up, down, layer, bias, resid, par):
    rows = own.shape[0]
    if lax.axis_size("fsdp") != 4:
        every = lax.all_gather(own, "fsdp", axis=0, tiled=True)
        up, down = up[layer], down[layer]
        z = mm(every, up) + bias
        cdf, pdf = phi_parts(z)
        active = (z * cdf).astype(BF)
        part = mm(active, down).astype(BF)
        total = lax.psum_scatter(part, "fsdp", scatter_dimension=0, tiled=True).astype(F32)
        out = (resid + total + par[7]).astype(BF)
        return out, every, active, cdf + z * pdf
    shape = (4, rows, D)
    return plane_call(
        functools.partial(forward_kernel, layer), 1 + 6 * layer,
        (
            jax.ShapeDtypeStruct((rows, D), BF),
            jax.ShapeDtypeStruct(shape, BF),
            jax.ShapeDtypeStruct(shape, BF),
            jax.ShapeDtypeStruct(shape, F32),
        ),
        rows, own, up, down, bias, resid, par,
    )


def mlp_backward(own, up, down, layer, slope):
    rows = own.shape[0]
    if lax.axis_size("fsdp") != 4:
        every = lax.all_gather(own, "fsdp", axis=0, tiled=True)
        up, down = up[layer], down[layer]
        dz = mm_nt(every, down) * slope
        dz_b = dz.astype(BF)
        part = mm_nt(dz_b, up).astype(BF)
        total = lax.psum_scatter(part, "fsdp", scatter_dimension=0, tiled=True).astype(F32)
        return total, every, dz_b, jnp.sum(dz, axis=0, keepdims=True)
    shape = (4, rows, D)
    return plane_call(
        functools.partial(backward_kernel, layer), 2 + 6 * layer,
        (
            jax.ShapeDtypeStruct((rows, D), F32),
            jax.ShapeDtypeStruct(shape, BF),
            jax.ShapeDtypeStruct(shape, BF),
            jax.ShapeDtypeStruct((1, D), F32),
        ),
        rows, own, up, down, slope,
    )


def weights_kernel(
    qkv_in, out_in, gains, biases, hidden, rows_in, up_in, down_in,
    full, rows_out, up_out, down_out, next_half,
    own, other_half, up_blocks, load, core_s, core_r, p_send, p_recv, f_send, f_recv, z_send, z_recv,
    u_send, u_recv, v_send, v_recv,
):
    s = lax.axis_index("section")
    f = lax.axis_index("fsdp")
    xn, yn = plane_neighbours()
    dn = 3 - f
    shard, wide = own.shape[1], own.shape[2]
    cut = 640
    left = pl.ds(0, cut)
    right = pl.ds(cut, wide - cut)

    def to(src, dst, send, recv, **where):
        return pltpu.make_async_remote_copy(
            src_ref=src, dst_ref=dst, send_sem=send, recv_sem=recv,
            device_id=where, device_id_type=MESH,
        )

    pad = jnp.zeros((shard, wide - D), BF)
    for p in range(3):
        own[p] = jnp.concatenate([qkv_in[:, pl.ds(p * D, D)], pad], axis=1)
    unit_rows = (
        lax.broadcasted_iota(jnp.int32, (16, 64), 0) == lax.broadcasted_iota(jnp.int32, (16, 64), 1)
    ).astype(F32)
    hidden_rows = [hidden[:, pl.ds(i * shard, shard)] for i in range(hidden.shape[1] // shard)]
    small = jnp.concatenate(
        [
            value.astype(F32)
            for value in (gains[...], biases[...], *hidden_rows, jnp.zeros((8 - len(hidden_rows), shard)))
        ],
        axis=0,
    )
    beside = mm_tn(small.astype(BF), unit_rows.astype(BF)).astype(BF)
    own[3] = jnp.concatenate([out_in[...], beside], axis=1)

    barrier = pltpu.get_barrier_semaphore()
    z = lax.axis_index("ctx")
    above = {"ctx": lax.rem(z + 1, 4)}
    below = {"ctx": lax.rem(z + 3, 4)}
    partners = ({"section": 1 - s}, {"fsdp": xn}, {"fsdp": yn}, {"fsdp": dn}, above, below)
    for where in partners:
        pl.semaphore_signal(barrier, inc=1, device_id=where, device_id_type=MESH)
    pl.semaphore_wait(barrier, 6)
    rows = rows_in.shape[0]
    near_rows, far_rows = pl.ds(rows, rows), pl.ds(0, rows)
    step_one = to(rows_in, rows_out.at[near_rows], z_send.at[0], z_recv.at[0], **above)
    step_two = to(
        rows_out.at[near_rows], rows_out.at[far_rows], z_send.at[1], z_recv.at[1], **above
    )

    @pl.when(z < 3)
    def _():
        step_one.start()

    rows_out[pl.ds(2 * rows, rows), :] = rows_in[...]

    @pl.when(z == 0)
    def _():
        rows_out[near_rows, :] = jnp.zeros(rows_in.shape, BF)

    @pl.when(z < 2)
    def _():
        rows_out[far_rows, :] = jnp.zeros(rows_in.shape, BF)

    def blk(owner):
        return pl.ds(pl.multiple_of(owner * shard, 16), shard)

    def give(p):
        return to(own.at[p], full.at[p, blk(f)], core_s.at[p], core_r.at[p], section=1)

    def keep(p):
        return pltpu.make_async_copy(own.at[p], full.at[p, blk(f)], load.at[p])

    @pl.when(s == 0)
    def _():
        for p in (2, 3, 0, 1):
            give(p).start()
        for p in range(4):
            keep(p).start()
        keep(0).wait()
        keep(1).wait()

    @pl.when(s == 1)
    def _():
        give(2).wait_recv()
        give(3).wait_recv()

    def same(piece, rows, send, recv, cols=slice(None), **where):
        ref = full.at[piece, rows, cols]
        return to(ref, ref, send, recv, **where)

    def hops(k):
        p = 2 * s + k
        return (
            same(p, blk(f), p_send.at[k, 0], p_recv.at[k, 0], fsdp=xn),
            same(p, blk(f), p_send.at[k, 1], p_recv.at[k, 1], fsdp=yn),
            same(p, blk(yn), p_send.at[k, 2], p_recv.at[k, 2], left, fsdp=xn),
            same(p, blk(xn), p_send.at[k, 3], p_recv.at[k, 3], right, fsdp=yn),
        )

    def here(k):
        p = 2 * s + k
        return [
            same(p, blk(owner), f_send.at[k, i], f_recv.at[k, i], section=1 - s)
            for i, owner in enumerate((xn, yn, dn))
        ]

    for k in range(2):
        copies = hops(k)
        copies[0].start()
        copies[1].start()
    down_far = to(down_in, down_out.at[s], core_s.at[4], core_r.at[4], section=1 - s)
    down_near = pltpu.make_async_copy(down_in, down_out.at[s], load.at[4])
    down_far.start()
    down_near.start()
    swap = to(other_half, next_half, core_s.at[5], core_r.at[5], section=0)

    @pl.when(s == 1)
    def _():
        for p in range(4):
            at = pl.ds(p * wide, wide)
            other_half[:, at] = own[p, pl.ds(0, shard // 2), :]
            next_half[:, at] = own[p, pl.ds(shard // 2, shard // 2), :]
        swap.start()

    for j in range(4):
        up_blocks[j] = up_in[:, pl.ds(j * D, D)]

    def up_to(i, owner, where):
        return to(up_blocks.at[owner], up_out.at[s, blk(f)], u_send.at[i], u_recv.at[i], fsdp=where)

    def up_over(i, owner):
        rows_here = up_out.at[s, blk(owner)]
        return to(rows_here, rows_here, v_send.at[i], v_recv.at[i], section=1 - s)

    others = (xn, yn, dn)
    up_near = pltpu.make_async_copy(up_blocks.at[f], up_out.at[s, blk(f)], load.at[5])
    up_near.start()
    for i, owner in enumerate(others):
        up_to(i, owner, owner).start()
    up_near.wait()
    up_over(3, f).start()
    for k in range(2):
        copies, across = hops(k), here(k)
        copies[0].wait_recv()
        copies[3].start()
        across[0].start()
        copies[1].wait_recv()
        copies[2].start()
        across[1].start()

    @pl.when(z > 0)
    def _():
        step_one.wait_recv()

    @pl.when((z == 1) | (z == 2))
    def _():
        step_two.start()

    for k in range(2):
        copies, across = hops(k), here(k)
        copies[2].wait_recv()
        copies[3].wait_recv()
        across[2].start()
    for i, owner in enumerate(others):
        up_to(i, owner, owner).wait_recv()
        up_over(i, owner).start()
    for k in range(2):
        for copy in here(k):
            copy.wait()
        for copy in hops(k):
            copy.wait_send()
    for i, owner in enumerate(others):
        up_to(i, owner, owner).wait_send()
        up_over(i, owner).wait()
    up_over(3, f).wait()

    @pl.when(s == 0)
    def _():
        for p in range(4):
            give(p).wait_send()
        keep(2).wait()
        keep(3).wait()

    @pl.when(s == 1)
    def _():
        give(0).wait_recv()
        give(1).wait_recv()

    down_near.wait()
    down_far.wait()
    pl.when(s == 0)(swap.wait_recv)
    pl.when(s == 1)(swap.wait_send)

    @pl.when(z < 3)
    def _():
        step_one.wait_send()

    @pl.when((z == 1) | (z == 2))
    def _():
        step_two.wait_send()

    @pl.when(z > 1)
    def _():
        step_two.wait_recv()


def first_weights(qkv, out, gains, biases, hidden, rows_in, up, down):
    dma = pltpu.SemaphoreType.DMA
    shard = qkv.shape[0]
    shapes = ((4, D, WIDE), (3 * rows_in.shape[0], D), (2, D, D), (2, D, D), (shard // 2, 4 * WIDE))
    return pl.pallas_call(
        weights_kernel,
        out_shape=tuple(jax.ShapeDtypeStruct(shape, BF) for shape in shapes),
        in_specs=[VSPEC] * 7 + [pl.BlockSpec(memory_space=pl.ANY)],
        out_specs=(VSPEC,) * 5,
        scratch_shapes=[
            pltpu.VMEM((4, shard, WIDE), BF),
            pltpu.VMEM((shard // 2, 4 * WIDE), BF),
            pltpu.VMEM((4, shard, D), BF),
            dma((6,)), dma((6,)), dma((6,)), dma((2, 4)), dma((2, 4)), dma((2, 3)), dma((2, 3)),
            dma((2,)), dma((2,)), dma((3,)), dma((3,)), dma((4,)), dma((4,)),
        ],
        compiler_params=pltpu.CompilerParams(
            collective_id=4, has_side_effects=True, vmem_limit_bytes=48 * 1024 * 1024
        ),
        cost_estimate=lasting(75),
        name="first_weights",
    )(qkv, out, gains, biases, hidden, rows_in, up, down)


def z_partners():
    z = lax.axis_index("ctx")
    return z + 1 - 2 * lax.rem(z, 2), 3 - z, (z == 1) | (z == 2)


def add_rows(dst, one, two, rows, step):
    @pl.loop(0, rows // step)
    def _(i):
        at = pl.ds(pl.multiple_of(i * step, 16), step)
        dst[at, :] = (one[at, :].astype(F32) + two[at, :].astype(F32)).astype(dst.dtype)


CUTS = ((0, 640, 384), (640, 512, 256))


def reduce_kernel(
    q0, k0, v0, o0, q1, k1, v1, o1, mlp, made0, made1, grad1, halo, d_resid, da_own, wide, par,
    qkv_out, out_out, down_out, up_out, made_out, grad_out,
    own_in, held, up_own, up_far, sent, caught, grad0,
    x1a, y1a, x2a, y2a, sxa, sya, ta, zaa, zba,
    x1b, y1b, x2b, y2b, sxb, syb, tb, zab, zbb,
    load, core_s, core_r, p_send, p_recv, z_send, z_recv, h_send, h_recv, x_send, x_recv,
):
    s = lax.axis_index("section")
    f = lax.axis_index("fsdp")
    xn, yn = plane_neighbours()
    dn = 3 - f
    side, across, inner = z_partners()
    pieces = ((q0, k0, v0, o0), (q1, k1, v1, o1))
    sets = (
        (x1a, y1a, x2a, y2a, sxa, sya, ta, zaa, zba),
        (x1b, y1b, x2b, y2b, sxb, syb, tb, zab, zbb),
    )
    shard = out_out.shape[0]
    rows = da_own.shape[0]
    z = lax.axis_index("ctx")
    above, below = {"ctx": lax.rem(z + 1, 4)}, {"ctx": lax.rem(z + 3, 4)}

    def to(src, dst, send, recv, **where):
        return pltpu.make_async_remote_copy(
            src_ref=src, dst_ref=dst, send_sem=send, recv_sem=recv,
            device_id=where, device_id_type=MESH,
        )

    barrier = pltpu.get_barrier_semaphore()
    partners = ({"section": 1 - s}, {"fsdp": xn}, {"fsdp": yn}, above, below)
    for where in partners:
        pl.semaphore_signal(barrier, inc=1, device_id=where, device_id_type=MESH)
    pl.semaphore_wait(barrier, 5)

    def blk(owner):
        return pl.ds(pl.multiple_of(owner * shard, 16), shard)

    def by_core(act):
        for core in range(2):
            pl.when(s == core)(functools.partial(act, core))

    def far(j, src):
        return to(src, held.at[j], core_s.at[j], core_r.at[j], section=1 - s)

    def near(j, src):
        return pltpu.make_async_copy(src, own_in.at[j % 2], load.at[j])

    def bufs(c):
        return tuple(ref.at[c // 2] for ref in sets[c % 2])

    def plane(c):
        x1, y1, x2, y2, sx, sy = bufs(c)[:6]
        own = held.at[c // 2]
        at, width, cut = CUTS[c % 2]
        left, right = pl.ds(at, cut), pl.ds(at + cut, width - cut)
        to_left, to_right = pl.ds(0, cut), pl.ds(cut, width - cut)
        sems = [(p_send.at[c, i], p_recv.at[c, i]) for i in range(6)]
        return (
            to(own.at[blk(dn), left], x1, *sems[0], fsdp=xn),
            to(own.at[blk(dn), right], y1, *sems[1], fsdp=yn),
            to(own.at[blk(xn), left], x2.at[:, to_left], *sems[2], fsdp=xn),
            to(own.at[blk(yn), right], y2.at[:, to_right], *sems[3], fsdp=yn),
            to(sx, x2.at[:, to_right], *sems[4], fsdp=xn),
            to(sy, y2.at[:, to_left], *sems[5], fsdp=yn),
        )

    def along(c):
        t, za, zb = bufs(c)[6:]
        sems = [(z_send.at[c, i], z_recv.at[c, i]) for i in range(3)]
        return (
            to(t, za, *sems[0], ctx=side),
            to(za, zb, *sems[1], ctx=across),
            to(zb, zb, *sems[2], ctx=side),
        )

    def join(j):
        far(j, q0).wait_recv()
        near(j, q0).wait()
        add_rows(held.at[j], own_in.at[j % 2], held.at[j], 4 * shard, 64)
        for c in (2 * j, 2 * j + 1):
            for copy in plane(c)[:4]:
                copy.start()
        if j < 2:
            by_core(lambda core: near(j + 2, pieces[core][j + 2]).start())

    def second(c):
        copies = plane(c)
        x1, y1, _, _, sx, sy = bufs(c)[:6]
        at, width, cut = CUTS[c % 2]
        own = held.at[c // 2]
        copies[0].wait_recv()
        add_rows(sy, own.at[blk(yn), pl.ds(at, cut)], x1, shard, 16)
        copies[5].start()
        copies[1].wait_recv()
        add_rows(sx, own.at[blk(xn), pl.ds(at + cut, width - cut)], y1, shard, 16)
        copies[4].start()

    def third(c):
        copies = plane(c)
        _, _, x2, y2, _, _, t, _, _ = bufs(c)
        at, width, _ = CUTS[c % 2]
        for copy in copies[2:]:
            copy.wait_recv()
        own = held.at[c // 2, blk(f), pl.ds(at, width)]

        @pl.loop(0, shard // 16)
        def _(i):
            part = pl.ds(pl.multiple_of(i * 16, 16), 16)
            t[part, :] = (
                own[part, :].astype(F32) + x2[part, :].astype(F32) + y2[part, :].astype(F32)
            ).astype(BF)

        @pl.when(jnp.logical_not(inner))
        def _():
            along(c)[0].start()

    def inward(c):
        @pl.when(inner)
        def _():
            t, za, _ = bufs(c)[6:]
            copies = along(c)
            copies[0].wait_recv()
            add_rows(za, t, za, shard, 16)
            copies[1].start()

    def crossed(c):
        @pl.when(inner)
        def _():
            _, za, zb = bufs(c)[6:]
            copies = along(c)
            copies[1].wait_recv()
            add_rows(zb, za, zb, shard, 16)
            copies[2].start()

    def last(c):
        at, width, _ = CUTS[c % 2]
        j = c // 2

        @pl.when(jnp.logical_not(inner))
        def _():
            along(c)[2].wait_recv()

        done = bufs(c)[8]
        keep = min(width, D - at) if j < 3 else width

        @pl.loop(0, shard // 16)
        def _(i):
            part = pl.ds(pl.multiple_of(i * 16, 16), 16)
            if j < 3:
                qkv_out[part, pl.ds(j * D + at, keep)] = done[part, pl.ds(0, keep)]
            else:
                out_out[part, pl.ds(at, keep)] = done[part, :]

    half = down_out.shape[0] // 2
    mine = pl.ds(pl.multiple_of(s * half, 16), half)
    down_far = to(mlp.at[0], down_out.at[mine], core_s.at[4], core_r.at[4], section=1 - s)
    down_near = pltpu.make_async_copy(mlp.at[0], down_out.at[mine], load.at[4])
    far_up = to(mlp.at[1], up_far, core_s.at[5], core_r.at[5], section=1 - s)
    near_up = pltpu.make_async_copy(mlp.at[1], up_own, load.at[5])

    def lay_up():
        far_up.wait_recv()
        near_up.wait()

        @pl.when(s == 1)
        def _():
            for k in range(4):
                at = pl.ds(k * (shard // 2), shard // 2)
                up_out[:, pl.ds(k * D, D)] = jnp.concatenate([up_far[at, :], up_own[at, :]], axis=0)

    back_one = to(halo.at[pl.ds(0, rows)], caught.at[0], h_send.at[0], h_recv.at[0], **below)
    back_two = to(sent, caught.at[1], h_send.at[1], h_recv.at[1], **below)

    def back():
        @pl.when(z < 3)
        def _():
            back_one.wait_recv()

        @pl.when(z == 3)
        def _():
            caught[0] = jnp.zeros_like(caught[0])

        @pl.when(z > 0)
        def _():
            add_rows(sent, halo.at[pl.ds(rows, rows)], caught.at[0], rows, 64)
            back_two.start()

    made_far = (
        to(made1, made_out.at[0], x_send.at[0], x_recv.at[0], section=1),
        to(made0, made_out.at[1], x_send.at[0], x_recv.at[0], section=0),
    )
    grad_far = (
        to(grad1, grad_out.at[0], x_send.at[1], x_recv.at[1], section=1),
        to(grad0, grad_out.at[1], x_send.at[1], x_recv.at[1], section=0),
    )
    made_near = (
        pltpu.make_async_copy(made0, made_out.at[0], load.at[6]),
        pltpu.make_async_copy(made1, made_out.at[1], load.at[6]),
    )
    grad_near = pltpu.make_async_copy(grad1, grad_out.at[1], load.at[7])

    def back_end():
        @pl.when(z < 3)
        def _():
            back_two.wait_recv()

        @pl.when(z == 3)
        def _():
            caught[1] = jnp.zeros_like(caught[1])

        unit, inv = norm_parts(wide[...].astype(F32))
        da = da_own[...] + caught[1].astype(F32)
        grad0[...] = d_resid[...] + norm_back(da, par[0:1, :], unit, inv)

        @pl.when(s == 0)
        def _():
            grad_out[0] = grad0[...]

        @pl.when(s == 1)
        def _():
            grad_far[1].start()

    @pl.when(s == 0)
    def _():
        made_far[0].start()
        grad_far[0].start()
        made_near[0].start()

    @pl.when(s == 1)
    def _():
        made_far[1].start()
        made_near[1].start()
        grad_near.start()

    @pl.when(z > 0)
    def _():
        back_one.start()

    for j in range(4):
        by_core(lambda core: far(j, pieces[1 - core][j]).start())
        if j < 2:
            by_core(lambda core: near(j, pieces[core][j]).start())
    for copy in (down_far, down_near, far_up, near_up):
        copy.start()

    join(0)
    for c in range(12):
        if c in (1, 3, 5):
            join((c + 1) // 2)
        if c < 8:
            second(c)
        if 1 <= c <= 8:
            third(c - 1)
        if 2 <= c <= 9:
            inward(c - 2)
        if 3 <= c <= 10:
            crossed(c - 3)
        if c >= 4:
            last(c - 4)
        if c == 2:
            back()
        if c == 4:
            lay_up()
        if c == 6:
            back_end()

    down_near.wait()
    down_far.wait()
    far_up.wait_send()

    @pl.when(s == 0)
    def _():
        made_near[0].wait()
        made_far[0].wait_send()
        grad_far[0].wait_send()
        made_far[1].wait_recv()
        grad_far[1].wait_recv()

    @pl.when(s == 1)
    def _():
        made_near[1].wait()
        grad_near.wait()
        made_far[1].wait_send()
        grad_far[1].wait_send()
        made_far[0].wait_recv()
        grad_far[0].wait_recv()

    @pl.when(z > 0)
    def _():
        back_one.wait_send()
        back_two.wait_send()

    for j in range(4):
        far(j, q0).wait_send()
    for c in range(8):
        for copy in plane(c):
            copy.wait_send()

    @pl.when(inner)
    def _():
        for c in range(8):
            for copy in along(c)[1:]:
                copy.wait_send()

    @pl.when(jnp.logical_not(inner))
    def _():
        for c in range(8):
            along(c)[0].wait_send()


def reduce_both(zero, one, mlp, made, grad1, halo, d_resid, da_own, wide, par):
    shard = D // 4
    rows = da_own.shape[0]
    dma = pltpu.SemaphoreType.DMA
    any_spec = pl.BlockSpec(memory_space=pl.ANY)

    def buf(*shape):
        return pltpu.VMEM(shape, BF)

    def part(_, width, cut):
        wide_buf = buf(4, shard, width)
        return [
            buf(4, shard, cut), buf(4, shard, width - cut), wide_buf, wide_buf,
            buf(4, shard, width - cut), buf(4, shard, cut), wide_buf, wide_buf, wide_buf,
        ]

    shapes = ((shard, 3 * D), (shard, WIDE), (D, D), (shard, 4 * D), (2, rows, D))
    return pl.pallas_call(
        reduce_kernel,
        out_shape=(
            *(jax.ShapeDtypeStruct(shape, BF) for shape in shapes),
            jax.ShapeDtypeStruct((2, rows, D), F32),
        ),
        in_specs=[any_spec] * 12 + [VSPEC] * 5,
        out_specs=(VSPEC,) * 6,
        scratch_shapes=[
            buf(2, D, WIDE), buf(4, D, WIDE), buf(D // 2, D), buf(D // 2, D), buf(rows, D),
            buf(2, rows, D), pltpu.VMEM((rows, D), F32), *part(*CUTS[0]), *part(*CUTS[1]),
            dma((8,)), dma((6,)), dma((6,)), dma((8, 6)), dma((8, 6)), dma((8, 3)), dma((8, 3)),
            dma((2,)), dma((2,)), dma((2,)), dma((2,)),
        ],
        compiler_params=pltpu.CompilerParams(
            collective_id=3, has_side_effects=True, vmem_limit_bytes=60 * 1024 * 1024
        ),
        cost_estimate=lasting(120),
        name="reduce_both",
    )(*zero, *one, mlp, *made, grad1, halo, d_resid, da_own, wide, par)


def final_kernel(
    qkv, out, mine, far, down_one, up_one, made, grads,
    qkv_f, out_f, down_f, up_f, small, made_out, grads_out,
):
    s = lax.axis_index("section")
    half = mine.shape[1]
    shard = qkv.shape[0]
    pick_row = (
        lax.broadcasted_iota(jnp.int32, (16, 128), 1)
        == lax.broadcasted_iota(jnp.int32, (16, 128), 0) + (D - TAIL)
    )
    small[...] = mm_nt(pick_row.astype(F32).astype(BF), out[:, pl.ds(TAIL, 128)])

    @pl.loop(0, made.shape[1] // 16)
    def _(i):
        at = pl.ds(pl.multiple_of(i * 16, 16), 16)
        for m in range(2):
            made_out[m, at, :] = made[m, at, :]
            grads_out[m, at, :] = grads[m, at, :]

    @pl.loop(0, shard // 16)
    def _(i):
        at = pl.ds(pl.multiple_of(i * 16, 16), 16)
        qkv_f[at, :] = qkv[at, :].astype(F32)
        out_f[at, :] = out[at, pl.ds(0, D)].astype(F32)

        @pl.when(s == 1)
        def _():
            up_f[at, :] = up_one[at, :].astype(F32)

    @pl.when(s == 0)
    def _():
        for k in range(4):
            at = pl.ds(k * (shard // 2), shard // 2)
            rows_k = jnp.concatenate([mine[1, at, :], far[1, at, :]], axis=0)
            up_f[:, pl.ds(k * D, D)] = rows_k.astype(F32)

    @pl.loop(0, half // 16)
    def _(i):
        at = pl.ds(pl.multiple_of(i * 16, 16), 16)
        after = pl.ds(pl.multiple_of(half + i * 16, 16), 16)

        @pl.when(s == 0)
        def _():
            down_f[at, :] = mine[0, at, :].astype(F32)
            down_f[after, :] = far[0, at, :].astype(F32)

        @pl.when(s == 1)
        def _():
            down_f[at, :] = down_one[at, :].astype(F32)
            down_f[after, :] = down_one[after, :].astype(F32)


def final_layouts(*values):
    qkv, _, _, _, down_one, up_one, made, grads = values
    shard = qkv.shape[0]
    outs = [(shape, F32) for shape in (qkv.shape, (shard, D), down_one.shape, up_one.shape)]
    outs += [((16, shard), F32), (made.shape, BF), (grads.shape, F32)]
    return pl.pallas_call(
        final_kernel,
        out_shape=tuple(jax.ShapeDtypeStruct(*out) for out in outs),
        in_specs=[VSPEC] * 8,
        out_specs=(VSPEC,) * 7,
        compiler_params=pltpu.CompilerParams(vmem_limit_bytes=52 * 1024 * 1024),
        cost_estimate=lasting(10),
        name="final_layouts",
    )(*values)


def core_half(values, axis):
    s = lax.axis_index("section")
    keep = lax.dynamic_index_in_dim(values, s, axis, keepdims=False)
    give = lax.dynamic_index_in_dim(values, 1 - s, axis, keepdims=False)
    return (keep.astype(F32) + on_chip(give).astype(F32)).astype(BF)


def halves_settle(zero, one, nf, shard):
    s = lax.axis_index("section")
    mine, far = pick(s, zero, one), on_chip(pick(s, one, zero))
    first, second = pick(s, mine, far).astype(F32), pick(s, far, mine).astype(F32)
    down = jnp.concatenate([first[0], second[0]], axis=0)
    up = jnp.concatenate([half[1].reshape(nf, shard // 2, -1) for half in (first, second)], axis=1)
    return down, up.transpose(1, 0, 2).reshape(shard, -1)


def reduce_plain(pieces):
    s = lax.axis_index("section")
    pair = ("fsdp", "section")
    a = jnp.stack([lax.psum_scatter(p, pair, scatter_dimension=0, tiled=True) for p in pieces])
    a = lax.psum(a, "ctx")
    far = on_chip(a)
    return jnp.concatenate([pick(s, a, far), pick(s, far, a)], axis=1)


def shift(value, steps):
    count = lax.axis_size("ctx")
    pairs = [(i, i + steps) for i in range(count) if 0 <= i + steps < count]
    return lax.ppermute(value, "ctx", pairs)


def with_halo(own, chunks):
    parts = [own]
    for _ in range(chunks):
        parts.append(shift(parts[-1], 1))
    return jnp.concatenate(parts[::-1], axis=0)


def return_halo(halo, chunks, rows):
    carried = None
    for far in range(chunks):
        mine = halo[far * rows : (far + 1) * rows]
        carried = mine if carried is None else mine + carried
        carried = shift(carried.astype(BF), -1).astype(F32)
    return carried


def pick(s, first, second):
    return jnp.where(s == 0, first, second)


def on_chip(value):
    return lax.ppermute(value, "section", SWAP)


def both_layers(own, s):
    other = on_chip(own)
    return pick(s, own, other), pick(s, other, own)


def flat(values):
    return values.reshape(-1, values.shape[-1])


def widen(values):
    return jnp.pad(values, ((0, 0), (0, WIDE - D)))


TAIL = 1024


def scores_forward(q, k, v, bias, lanes):
    outs = []
    for low in (True, False):
        one = jnp.where((lanes < HD) if low else (lanes >= HD), q, jnp.zeros_like(q))
        weight = jnp.exp(mm_nt(one, k) + bias)
        prob = weight * (1.0 / jnp.sum(weight, axis=-1, keepdims=True))
        outs.append(mm(prob.astype(BF), v))
    return jnp.where(lanes < HD, outs[0], outs[1]).astype(BF)


def scores_backward(q, k, v, grad, bias_t, lanes):
    dqs, dk, dv = [], 0.0, 0.0
    for low in (True, False):
        mine = (lanes < HD) if low else (lanes >= HD)
        one = jnp.where(mine, q, jnp.zeros_like(q))
        g = jnp.where(mine, grad, jnp.zeros_like(grad))
        weight = jnp.exp(mm_nt(k, one) + bias_t)
        prob = weight * (1.0 / jnp.sum(weight, axis=0, keepdims=True))
        d_prob = mm_nt(v, g)
        row = jnp.sum(prob * d_prob, axis=0, keepdims=True)
        d_score = (prob * (d_prob - row)).astype(BF)
        dqs.append(mm_tn(d_score, k))
        dk = dk + mm(d_score, one)
        dv = dv + mm(prob.astype(BF), g)
    dq = jnp.where(lanes < HD, dqs[0], dqs[1]) * SCALE
    return dq.astype(BF), dk.astype(BF), dv.astype(BF)


def lane_tile(i):
    return pl.ds(pl.multiple_of(i * 128, 128), 128)


def widened(row):
    return jnp.concatenate([row, jnp.zeros((row.shape[0], WIDE - D), row.dtype)], axis=1)


def ctx_ring(rows_in, landing, send, recv):
    z = lax.axis_index("ctx")
    above = {"ctx": lax.rem(z + 1, 4)}
    below = {"ctx": lax.rem(z + 3, 4)}
    rows = rows_in.shape[0]
    near, far = pl.ds(rows, rows), pl.ds(0, rows)
    barrier = pltpu.get_barrier_semaphore()

    def on(src, dst, i):
        return pltpu.make_async_remote_copy(
            src_ref=src, dst_ref=dst, send_sem=send.at[i], recv_sem=recv.at[i],
            device_id=above, device_id_type=MESH,
        )

    one = on(rows_in, landing.at[near], 0)
    two = on(landing.at[near], landing.at[far], 1)

    def begin():
        for where in (above, below):
            pl.semaphore_signal(barrier, inc=1, device_id=where, device_id_type=MESH)
        pl.semaphore_wait(barrier, 2)

        @pl.when(z < 3)
        def _():
            one.start()

        landing[pl.ds(2 * rows, rows), :] = rows_in[...]

        @pl.when(z == 0)
        def _():
            landing[near, :] = jnp.zeros(rows_in.shape, BF)

        @pl.when(z < 2)
        def _():
            landing[far, :] = jnp.zeros(rows_in.shape, BF)

    def middle():
        @pl.when(z > 0)
        def _():
            one.wait_recv()

        @pl.when((z == 1) | (z == 2))
        def _():
            two.start()

    def end():
        @pl.when(z > 1)
        def _():
            two.wait_recv()

        @pl.when(z < 3)
        def _():
            one.wait_send()

        @pl.when((z == 1) | (z == 2))
        def _():
            two.wait_send()

    return begin, middle, end


def block_kernel(
    ring, first, wq, wk, wv, wo, bias, normed, q_ref, k_ref, v_ref, att, resid, second, par, *rest
):
    rows = resid.shape[0]
    total = normed.shape[0]
    if ring:
        wide_out, held, wide, send, recv = rest
        begin, middle, end = ctx_ring(first, wide, send, recv)
        begin()
    else:
        (held,), wide = rest, first
    pick_row = (
        lax.broadcasted_iota(jnp.int32, (16, 128), 1)
        == lax.broadcasted_iota(jnp.int32, (16, 128), 0) + (D - TAIL)
    )
    par[...] = mm_nt(pick_row.astype(F32).astype(BF), wo[:, pl.ds(TAIL, 128)])
    last = total // rows - 1

    @pl.loop(0, last + 1)
    def _(i):
        if ring:
            pl.when(i == 1)(middle)
            pl.when(i == 2)(end)
        at = pl.ds(pl.multiple_of((last - i) * rows, 16), rows)
        unit, _ = norm_parts(wide[at, :].astype(F32))
        low = (unit * par[0:1, :] + par[2:3, :]).astype(BF)
        normed[at, :] = low
        k_ref[at, :] = mm(low, wk[...]).astype(BF)
        v_ref[at, :] = (mm(low, wv[...]) + widened(par[4:5, :])).astype(BF)

        @pl.when(i == 0)
        def _():
            q_ref[...] = (mm(normed[at, :], wq[...]) + widened(par[3:4, :])).astype(BF)

    own = pl.ds(total - rows, rows)
    lanes = lax.broadcasted_iota(jnp.int32, (rows, 128), 1)

    @pl.loop(0, WIDE // 128)
    def _(i):
        at = lane_tile(i)
        held[:, at] = scores_forward(
            q_ref[:, at] * jnp.asarray(SCALE, BF), k_ref[:, at], v_ref[:, at], bias[...], lanes
        )

    att[...] = held[:, pl.ds(0, D)]
    res = wide[own, :].astype(F32) + mm(att[...], wo[:, pl.ds(0, D)]) + par[5:6, :]
    resid[...] = res
    unit, _ = norm_parts(res)
    second[...] = (unit * par[1:2, :] + par[6:7, :]).astype(BF)
    if ring:
        wide_out[...] = wide[...]


def weight_specs(weights):
    if weights.ndim == 3:
        return [pl.BlockSpec((None, D, WIDE), lambda i, p=p: (p, 0, 0)) for p in range(4)]
    return [pl.BlockSpec((D, WIDE), lambda i, p=p: (0, p)) for p in range(4)]


def whole(shape):
    return pl.BlockSpec(shape, lambda i: (0,) * len(shape))


def block_forward(first, weights, bias, ring):
    rows, total = bias.shape
    outs = (
        ((total, D), BF), ((rows, WIDE), BF), ((total, WIDE), BF), ((total, WIDE), BF),
        ((rows, D), BF), ((rows, D), F32), ((rows, D), BF), ((16, D), F32),
    )
    scratch = [pltpu.VMEM((rows, WIDE), BF)]
    params = {}
    if ring:
        outs += (((total, D), BF),)
        scratch += [pltpu.VMEM((total, D), BF)] + [pltpu.SemaphoreType.DMA((2,))] * 2
        params = {"collective_id": 5, "has_side_effects": True}
    return pl.pallas_call(
        functools.partial(block_kernel, ring),
        out_shape=tuple(jax.ShapeDtypeStruct(*out) for out in outs),
        grid=(1,),
        in_specs=[whole(first.shape), *weight_specs(weights), whole(bias.shape)],
        out_specs=tuple(whole(shape) for shape, _ in outs),
        scratch_shapes=scratch,
        compiler_params=pltpu.CompilerParams(vmem_limit_bytes=56 * 1024 * 1024, **params),
        cost_estimate=lasting(45 if ring else 22),
        name="block_forward",
    )(first, weights, weights, weights, weights, bias)


def block_back_kernel(
    ring, d_second, up, resid, wide, q_ref, k_ref, v_ref, att, ffb_rows, wq, wk, wv, wo, par, bias_t,
    *rest,
):
    if ring:
        (d_in, d_low, dq_ref, dk_ref, dv_ref, left, right,
         held, sums, d_resid, da_own, da_halo, sent, caught, send, recv) = rest
    else:
        d_resid, dq_ref, dk_ref, dv_ref, da_own, da_halo, left, right, held, sums = rest
    rows = resid.shape[0]
    total = wide.shape[0]
    own = total - rows
    z = lax.axis_index("ctx")

    def back_to(src, dst, i):
        return pltpu.make_async_remote_copy(
            src_ref=src, dst_ref=dst, send_sem=send.at[i], recv_sem=recv.at[i],
            device_id={"ctx": lax.rem(z + 3, 4)}, device_id_type=MESH,
        )

    if ring:
        one = back_to(da_halo.at[pl.ds(0, rows)], caught.at[0], 0)
        two = back_to(sent, caught.at[1], 1)
        barrier = pltpu.get_barrier_semaphore()
        for step in (1, 3):
            pl.semaphore_signal(
                barrier, inc=1, device_id={"ctx": lax.rem(z + step, 4)}, device_id_type=MESH
            )
        pl.semaphore_wait(barrier, 2)

    def total_of(values):
        return jnp.sum(values, axis=0, keepdims=True)

    upstream = up[...].astype(F32)
    unit, inv = norm_parts(resid[...])
    grad = upstream + norm_back(d_second[...], par[1:2, :], unit, inv)
    d_resid[...] = grad
    sums[1:2, :] = total_of(d_second[...] * unit)
    sums[5:6, :] = total_of(grad)
    sums[6:7, :] = total_of(d_second[...])
    sums[7:8, :] = total_of(upstream)
    sums[8:16, :] = ffb_rows[...]
    low = grad.astype(BF)
    right[pl.ds(0, rows), :] = jnp.zeros((rows, WIDE), BF)
    right[pl.ds(0, rows), pl.ds(0, D)] = low
    right[pl.ds(rows, 16), :] = (
        lax.broadcasted_iota(jnp.int32, (16, WIDE), 1)
        == lax.broadcasted_iota(jnp.int32, (16, WIDE), 0) + D
    ).astype(F32).astype(BF)
    held[...] = jnp.zeros((rows, WIDE), BF)
    held[:, pl.ds(0, D)] = mm_nt(low, wo[:, pl.ds(0, D)]).astype(BF)
    lanes = lax.broadcasted_iota(jnp.int32, (rows, 128), 1)

    @pl.loop(0, WIDE // 128)
    def _(i):
        at = lane_tile(i)
        dq_ref[:, at], dk_ref[:, at], dv_ref[:, at] = scores_backward(
            q_ref[:, at] * jnp.asarray(SCALE, BF), k_ref[:, at], v_ref[:, at], held[:, at],
            bias_t[...], lanes,
        )

    sums[3:4, :] = total_of(dq_ref[...].astype(F32))[:, :D]
    sums[4:5, :] = total_of(dv_ref[...].astype(F32))[:, :D]
    sums[0:1, :] = jnp.zeros((1, D), F32)
    sums[2:3, :] = jnp.zeros((1, D), F32)

    def back(at):
        da = mm_nt(dk_ref[at, :], wk[...]) + mm_nt(dv_ref[at, :], wv[...])
        return da

    def count(da, at):
        unit, _ = norm_parts(wide[at, :].astype(F32))
        sums[0:1, :] += total_of(da * unit)
        sums[2:3, :] += total_of(da)

    @pl.loop(0, own // rows)
    def _(i):
        at = pl.ds(pl.multiple_of(i * rows, 16), rows)
        da = back(at)
        da_halo[at, :] = da.astype(BF)
        if ring:

            @pl.when((i == 0) & (z > 0))
            def _():
                one.start()

        count(da, at)

    at = pl.ds(own, rows)
    da = back(at) + mm_nt(dq_ref[...], wq[...])
    da_own[...] = da
    count(da, at)
    if ring:

        @pl.when(z < 3)
        def _():
            one.wait_recv()

        @pl.when(z == 3)
        def _():
            caught[0] = jnp.zeros_like(caught[0])

        @pl.when(z > 0)
        def _():
            add_rows(sent, da_halo.at[pl.ds(rows, rows)], caught.at[0], rows, 64)
            two.start()

    left[pl.ds(0, rows), :] = att[...]
    left[pl.ds(rows, 16), :] = sums[...].astype(BF)
    if ring:

        @pl.when(z < 3)
        def _():
            two.wait_recv()

        @pl.when(z == 3)
        def _():
            caught[1] = jnp.zeros_like(caught[1])

        @pl.loop(0, rows // 64)
        def _(i):
            part = pl.ds(pl.multiple_of(i * 64, 64), 64)
            behind = pl.ds(pl.multiple_of(own + i * 64, 64), 64)
            unit, inv = norm_parts(wide[behind, :].astype(F32))
            da = da_own[part, :] + caught[1, part, :].astype(F32)
            grad = d_resid[part, :] + norm_back(da, par[0:1, :], unit, inv)
            d_in[part, :] = grad
            d_low[part, :] = grad.astype(BF)

        @pl.when(z > 0)
        def _():
            one.wait_send()
            two.wait_send()


def block_backward(d_second, up, resid, wide, q, k, v, att, ffb_rows, weights, par, bias_t, ring):
    total, rows = wide.shape[0], resid.shape[0]
    f32_rows, low_rows = ((rows, D), F32), ((rows, D), BF)
    heads = (((rows, WIDE), BF), ((total, WIDE), BF), ((total, WIDE), BF))
    factors = (((rows + 16, D), BF), ((rows + 16, WIDE), BF))
    halo = ((total - rows, D), BF)
    held = [pltpu.VMEM((rows, WIDE), BF), pltpu.VMEM((16, D), F32)]
    params = {}
    if ring:
        outs = (f32_rows, low_rows, *heads, *factors)
        held += [pltpu.VMEM(*f32_rows), pltpu.VMEM(*f32_rows), pltpu.VMEM(*halo), pltpu.VMEM(*low_rows)]
        held += [pltpu.VMEM((2, rows, D), BF)] + [pltpu.SemaphoreType.DMA((2,))] * 2
        params = {"collective_id": 6, "has_side_effects": True}
    else:
        outs = (f32_rows, *heads, f32_rows, halo, *factors)
    before = (d_second, up, resid, wide, q, k, v, att, ffb_rows)
    return pl.pallas_call(
        functools.partial(block_back_kernel, ring),
        out_shape=tuple(jax.ShapeDtypeStruct(*out) for out in outs),
        grid=(1,),
        in_specs=[
            *(whole(value.shape) for value in before), *weight_specs(weights),
            whole(par.shape), whole(bias_t.shape),
        ],
        out_specs=tuple(whole(shape) for shape, _ in outs),
        scratch_shapes=held,
        compiler_params=pltpu.CompilerParams(vmem_limit_bytes=60 * 1024 * 1024, **params),
        cost_estimate=lasting(58 if ring else 38),
        name="block_backward",
    )(*before, weights, weights, weights, weights, par, bias_t)


def on_device(
    inputs, segments, cotangent, qkv_weight, out_weight, up_weight, down_weight,
    norm_gains, biases, ff_bias,
):
    rows = inputs.shape[2]
    length = segments.shape[2]
    chunks = min((length // 2 - 1 + rows - 1) // rows, lax.axis_size("ctx") - 1)
    reach = chunks * rows
    s = lax.axis_index("section")
    f = lax.axis_index("fsdp")
    nf = lax.axis_size("fsdp")
    shard = D // nf
    ff_here = ff_bias.shape[1]
    per_row = ff_here // shard
    pair = ("fsdp", "section")
    fits = nf == 4 and lax.axis_size("ctx") == 4 and chunks == 2

    own_in = lax.dynamic_index_in_dim(inputs, s, 0, keepdims=False)[0]
    own_cot = lax.dynamic_index_in_dim(cotangent, s, 0, keepdims=False)[0]
    seg = lax.dynamic_index_in_dim(segments, s, 0, keepdims=False)[0]
    start = lax.axis_index("ctx") * rows
    key_seg = lax.dynamic_slice_in_dim(
        jnp.pad(seg, (reach, 0), constant_values=-1), start, reach + rows, 0
    )
    allowed = (key_seg[reach:, None] == key_seg[None, :]) & (
        jnp.arange(reach + rows, dtype=jnp.int32)[None, :] - reach
        <= jnp.arange(rows, dtype=jnp.int32)[:, None]
    )

    bias = jnp.where(allowed, 0.0, -1e30).astype(F32)
    bias_t = bias.T

    def gathered(rows_first):
        return lax.all_gather(rows_first, pair, axis=0, tiled=True)

    if fits:
        zero, wide_in, up_w, down_w, one_half = first_weights(
            qkv_weight[0], out_weight[0], norm_gains[0], biases[0], ff_bias,
            own_in, up_weight[0], down_weight[0],
        )
        one = gathered(one_half)
    else:
        small = jnp.concatenate(
            [norm_gains[0].T, biases[0].T, ff_bias[0].reshape(per_row, shard).T], axis=1
        )
        beside = jnp.pad(small, ((0, 0), (0, WIDE - D - 8 - per_row)))
        packed = jnp.concatenate(
            [widen(qkv_weight[0][:, i * D : (i + 1) * D]) for i in range(3)]
            + [out_weight[0], beside],
            axis=1,
        )
        halves = packed.reshape(2, shard // 2, 4 * WIDE)
        keep = lax.dynamic_index_in_dim(halves, s, 0, keepdims=False)
        recv = on_chip(lax.dynamic_index_in_dim(halves, 1 - s, 0, keepdims=False))
        zero, one = gathered(pick(s, keep, recv)), gathered(pick(s, recv, keep))
        up_own = lax.all_to_all(
            up_weight[0].reshape(shard, nf, ff_here), "fsdp", split_axis=1, concat_axis=0, tiled=True
        ).reshape(D, ff_here)
        up_w = both_layers(up_own, s)
        down_w = both_layers(down_weight[0], s)
        wide_in = with_halo(own_in, chunks)

    weights = (zero, one)

    kept = []
    current = own_in
    produced = []
    for layer in range(2):
        if layer == 1 and fits:
            *made, wide = block_forward(current, weights[layer], bias, True)
        else:
            wide = with_halo(current, chunks) if layer else wide_in
            made = block_forward(wide, weights[layer], bias, False)
        normed, q, k, v, att, resid, second, par = made
        ffb = lax.dynamic_slice(par, (8, f * shard), (per_row, shard)).reshape(1, ff_here)
        current, second_all, active, slope = mlp_forward(
            second, up_w, down_w, layer, ffb, resid, par
        )
        produced.append(current)
        kept.append((wide, normed, q, k, v, att, resid, second_all, slope, active, par))

    upstream = own_cot
    derived = [None, None]
    parts = [None, None]
    mlp_sums = [None, None]
    for layer in (1, 0):
        wide, normed, q, k, v, att, resid, second_all, slope, active, par = kept[layer]
        d_second, up_all, dz_b, ffb_g = mlp_backward(upstream, up_w, down_w, layer, slope)
        up_g = mm_tn(flat(second_all), flat(dz_b)).astype(BF)
        up_half = core_half(up_g.reshape(nf, 2, shard // 2, ff_here), 1)
        down_g = mm_tn(flat(active), flat(up_all)).astype(BF)
        down_half = core_half(down_g.reshape(2, ff_here // 2, D), 0)
        d_second, up_half, down_half = lax.optimization_barrier((d_second, up_half, down_half))
        up_half = lax.all_to_all(up_half, "fsdp", split_axis=0, concat_axis=0, tiled=True)
        ffb_rows = lax.dynamic_update_slice(
            jnp.zeros((8, D), F32), ffb_g.reshape(per_row, shard), (0, f * shard)
        )
        block = (
            d_second, upstream, resid, wide, q, k, v, att, ffb_rows, weights[layer], par, bias_t
        )
        if layer == 1 and fits:
            derived[1], upstream_next, dq, dk, dv, left, right = block_backward(*block, True)
        else:
            d_resid, dq, dk, dv, da_own, da_halo, left, right = block_backward(*block, False)
        if not fits:
            unit, inv = norm_parts(wide[reach:].astype(F32))
            late = return_halo(da_halo, chunks, rows)
            derived[layer] = d_resid + norm_back(da_own + late, par[0], unit, inv)
            upstream_next = derived[layer].astype(BF)
        pieces = (
            mm_tn(normed[reach:], dq).astype(BF),
            mm_tn(normed, dk).astype(BF),
            mm_tn(normed, dv).astype(BF),
            mm_tn(left, right).astype(BF),
        )
        parts[layer] = pieces
        up_half, down_half, _ = lax.optimization_barrier((up_half, down_half, dq))
        halves = jnp.stack([down_half, up_half.reshape(ff_here // 2, D)])
        if layer == 1:
            _, upstream_next = lax.optimization_barrier((halves, upstream_next))
        else:
            halves, mlp_sums[1] = lax.optimization_barrier((halves, mlp_sums[1]))
        mlp_sums[layer] = lax.psum(halves, "ctx")
        if layer == 1:
            upstream = upstream_next

    if fits:
        qkv_g, out_g, down_one, up_one, made, grads = reduce_both(
            parts[0], parts[1], mlp_sums[1], produced, derived[1], da_halo, d_resid, da_own,
            wide[reach:], par,
        )
        late_sum, qkv_g = lax.optimization_barrier((mlp_sums[0], qkv_g))
        far = lax.ppermute(late_sum, "section", [(1, 0)])
        qkv_g, out_g, grad_down, grad_up, small, made, grads = final_layouts(
            qkv_g, out_g, late_sum, far, down_one, up_one, made, grads
        )
        made, grads = made[None, :, None], grads[None, :, None]
    else:
        a_tot = pick(s, reduce_plain(parts[0]), reduce_plain(parts[1])).astype(F32)
        qkv_g = jnp.concatenate([a_tot[i, :, :D] for i in range(3)], axis=1)
        out_g = a_tot[3, :, :D]
        small = a_tot[3, :, D : D + 16].T
        grad_down, grad_up = halves_settle(*mlp_sums, nf, shard)
        made, grads = both_micros(produced, s), both_micros(derived, s)
    return (
        made,
        grads,
        qkv_g[None],
        out_g[None],
        grad_up[None],
        grad_down[None],
        small[None, :2],
        small[None, 2:8],
        small[8 : 8 + per_row].reshape(1, ff_here),
    )


def both_micros(layers, s):
    to_zero = lax.ppermute(layers[0], "section", [(1, 0)])
    to_one = lax.ppermute(layers[1], "section", [(0, 1)])
    out = jnp.stack([pick(s, layers[0], to_one), pick(s, to_zero, layers[1])])
    return out[None, :, None]


def solution(mesh):
    return jax.shard_map(
        on_device,
        mesh=mesh,
        in_specs=(
            P(None, "fsdp", "ctx", None),
            P(None, "fsdp", None),
            P(None, "fsdp", "ctx", None),
            P("section", "fsdp", None),
            P("section", "fsdp", None),
            P("section", "fsdp", None),
            P("section", "fsdp", None),
            P("section", None, "fsdp"),
            P("section", None, "fsdp"),
            P("section", "fsdp"),
        ),
        out_specs=(
            P("section", None, "fsdp", "ctx", None),
            P("section", None, "fsdp", "ctx", None),
            P("section", "fsdp", None),
            P("section", "fsdp", None),
            P("section", "fsdp", None),
            P("section", "fsdp", None),
            P("section", None, "fsdp"),
            P("section", None, "fsdp"),
            P("section", "fsdp"),
        ),
        check_vma=False,
    )
```

```python
import functools
import math

import jax
import jax.numpy as jnp
from jax import lax
from jax.experimental import pallas as pl
from jax.experimental.pallas import tpu as pltpu
from jax.sharding import PartitionSpec as P

D = 1088
HD = 64
F32 = jnp.float32
BF = jnp.bfloat16
SCALE = 1.0 / math.sqrt(HD)
WIDE = 1152
MESH = pl.DeviceIdType.MESH
SWAP = [(0, 1), (1, 0)]


def mm(a, b):
    return jnp.dot(a, b, preferred_element_type=F32)


def mm_nt(a, b):
    return lax.dot_general(a, b, (((1,), (1,)), ((), ())), preferred_element_type=F32)


def mm_tn(a, b):
    return lax.dot_general(a, b, (((0,), (0,)), ((), ())), preferred_element_type=F32)


def norm_parts(values):
    center = jnp.mean(values, axis=-1, keepdims=True)
    offset = values - center
    spread = jnp.mean(offset * offset, axis=-1, keepdims=True)
    inv = lax.rsqrt(spread + 1e-05)
    return offset * inv, inv


def norm_back(grad, gain, unit, inv):
    dn = grad * gain
    return inv * (
        dn
        - jnp.mean(dn, axis=-1, keepdims=True)
        - unit * jnp.mean(dn * unit, axis=-1, keepdims=True)
    )


def phi_parts(z):
    cdf = 0.5 * (1.0 + lax.erf(z * (1.0 / math.sqrt(2.0))))
    pdf = jnp.exp(-0.5 * z * z) * (1.0 / math.sqrt(2.0 * math.pi))
    return cdf, pdf


def plane_neighbours():
    f = lax.axis_index("fsdp")
    x = lax.rem(f, 2)
    y = f // 2
    return y * 2 + (1 - x), (1 - y) * 2 + x


def plane_barrier(xn, yn):
    barrier = pltpu.get_barrier_semaphore()
    for nb in (xn, yn):
        pl.semaphore_signal(barrier, inc=1, device_id={"fsdp": nb}, device_id_type=MESH)
    pl.semaphore_wait(barrier, 2)


def remote(src, dst, send, recv, nb):
    return pltpu.make_async_remote_copy(
        src_ref=src, dst_ref=dst, send_sem=send, recv_sem=recv,
        device_id={"fsdp": nb}, device_id_type=MESH,
    )


def load_layer(sources, targets, sems):
    copies = [
        pltpu.make_async_copy(source, target, sems.at[i])
        for i, (source, target) in enumerate(zip(sources, targets))
    ]
    for copy in copies:
        copy.start()
    return copies


def exchange_rows(own_ref, all_ref, parts, compute, finish, bufs, send, recv, loads):
    x1, y1, x2, y2, sum_x, sum_y = bufs
    xn, yn = plane_neighbours()
    half = own_ref.shape[0] // 2
    top, low = pl.ds(0, half), pl.ds(half, half)
    plane_barrier(xn, yn)

    to_x = remote(own_ref, all_ref.at[1], send.at[0], recv.at[0], xn)
    to_y = remote(own_ref, all_ref.at[2], send.at[1], recv.at[1], yn)
    far_x = remote(all_ref.at[2, top], all_ref.at[3, top], send.at[2], recv.at[2], xn)
    far_y = remote(all_ref.at[1, low], all_ref.at[3, low], send.at[3], recv.at[3], yn)
    first_x = remote(parts.at[3, top], x1, send.at[4], recv.at[4], xn)
    first_y = remote(parts.at[3, low], y1, send.at[5], recv.at[5], yn)
    own_x = remote(parts.at[1, top], x2.at[top], send.at[6], recv.at[6], xn)
    own_y = remote(parts.at[2, low], y2.at[low], send.at[7], recv.at[7], yn)
    rest_x = remote(sum_x, x2.at[low], send.at[8], recv.at[8], xn)
    rest_y = remote(sum_y, y2.at[top], send.at[9], recv.at[9], yn)

    to_x.start()
    to_y.start()
    all_ref[0] = own_ref[...]
    for copy in loads:
        copy.wait()

    @pl.loop(0, 4)
    def _(i):
        @pl.when(i == 1)
        def _():
            to_x.wait_recv()
            far_y.start()
            to_y.wait_recv()
            far_x.start()

        @pl.when(i == 2)
        def _():
            own_x.start()
            far_x.wait_recv()
            far_y.wait_recv()

        @pl.when(i == 3)
        def _():
            first_x.start()
            first_y.start()

        compute(i + (i // 2) * (1 - 2 * lax.rem(i, 2)))

    own_y.start()
    first_x.wait_recv()
    sum_y[...] = (parts[2, top, :].astype(F32) + x1[...].astype(F32)).astype(BF)
    rest_y.start()
    first_y.wait_recv()
    sum_x[...] = (parts[1, low, :].astype(F32) + y1[...].astype(F32)).astype(BF)
    rest_x.start()
    own_x.wait_recv()
    rest_y.wait_recv()
    finish(top, parts[0, top, :].astype(F32) + x2[top, :].astype(F32) + y2[top, :].astype(F32))
    own_y.wait_recv()
    rest_x.wait_recv()
    finish(low, parts[0, low, :].astype(F32) + x2[low, :].astype(F32) + y2[low, :].astype(F32))
    for copy in (to_x, to_y, far_x, far_y, first_x, first_y, own_x, own_y, rest_x, rest_y):
        copy.wait_send()


def forward_kernel(
    layer, own, up_here, down_both, bias, resid, par, out, all_ref, active, slope,
    up, down, load, parts, x1, y1, x2, y2, sx, sy, send, recv,
):
    loads = load_layer((up_here, down_both.at[layer]), (up, down), load)

    def finish(at, value):
        out[at, :] = (resid[at, :] + value + par[7:8, :]).astype(BF)

    def compute(r):
        slope[r] = mm(all_ref[r], up[...]) + bias[...]

        @pl.loop(0, own.shape[0] // 64)
        def _(j):
            at = pl.ds(pl.multiple_of(j * 64, 64), 64)
            z = slope[r, at, :]
            cdf, pdf = phi_parts(z)
            active[r, at, :] = (z * cdf).astype(BF)
            slope[r, at, :] = cdf + z * pdf

        parts[r] = mm(active[r], down[...]).astype(BF)

    exchange_rows(own, all_ref, parts, compute, finish, (x1, y1, x2, y2, sx, sy), send, recv, loads)


def backward_kernel(
    layer, own, up_here, down_both, slope, total, all_ref, dz_all, bias_g,
    up, down, load, parts, x1, y1, x2, y2, sx, sy, send, recv,
):
    loads = load_layer((up_here, down_both.at[layer]), (up, down), load)
    bias_g[...] = jnp.zeros_like(bias_g)

    def finish(at, value):
        total[at, :] = value

    def compute(r):
        dz = mm_nt(all_ref[r], down[...]) * slope[r]
        bias_g[...] += jnp.sum(dz, axis=0, keepdims=True)
        dz_all[r] = dz.astype(BF)
        parts[r] = mm_nt(dz_all[r], up[...]).astype(BF)

    exchange_rows(own, all_ref, parts, compute, finish, (x1, y1, x2, y2, sx, sy), send, recv, loads)


VSPEC = pl.BlockSpec(memory_space=pltpu.VMEM)


def lasting(micros):
    return pl.CostEstimate(flops=0, transcendentals=0, bytes_accessed=int(micros * 3.5e6))


def plane_call(kernel, ident, outs, rows, *operands):
    half = rows // 2
    any_spec = pl.BlockSpec(memory_space=pl.ANY)
    return pl.pallas_call(
        kernel,
        out_shape=outs,
        in_specs=[VSPEC, any_spec, any_spec] + [VSPEC] * (len(operands) - 3),
        out_specs=(VSPEC,) * len(outs),
        scratch_shapes=[
            pltpu.VMEM((D, D), BF),
            pltpu.VMEM((D, D), BF),
            pltpu.SemaphoreType.DMA((2,)),
            pltpu.VMEM((4, rows, D), BF),
            pltpu.VMEM((half, D), BF),
            pltpu.VMEM((half, D), BF),
            pltpu.VMEM((rows, D), BF),
            pltpu.VMEM((rows, D), BF),
            pltpu.VMEM((half, D), BF),
            pltpu.VMEM((half, D), BF),
            pltpu.SemaphoreType.DMA((10,)),
            pltpu.SemaphoreType.DMA((10,)),
        ],
        compiler_params=pltpu.CompilerParams(
            collective_id=ident, has_side_effects=True, vmem_limit_bytes=40 * 1024 * 1024
        ),
        cost_estimate=lasting(40),
    )(*operands)


def mlp_forward(own, up, down, layer, bias, resid, par):
    rows = own.shape[0]
    if lax.axis_size("fsdp") != 4:
        every = lax.all_gather(own, "fsdp", axis=0, tiled=True)
        down = down[layer]
        z = mm(every, up) + bias
        cdf, pdf = phi_parts(z)
        active = (z * cdf).astype(BF)
        part = mm(active, down).astype(BF)
        total = lax.psum_scatter(part, "fsdp", scatter_dimension=0, tiled=True).astype(F32)
        out = (resid + total + par[7]).astype(BF)
        return out, every, active, cdf + z * pdf
    shape = (4, rows, D)
    return plane_call(
        functools.partial(forward_kernel, layer), 1 + 6 * layer,
        (
            jax.ShapeDtypeStruct((rows, D), BF),
            jax.ShapeDtypeStruct(shape, BF),
            jax.ShapeDtypeStruct(shape, BF),
            jax.ShapeDtypeStruct(shape, F32),
        ),
        rows, own, up, down, bias, resid, par,
    )


def mlp_backward(own, up, down, layer, slope):
    rows = own.shape[0]
    if lax.axis_size("fsdp") != 4:
        every = lax.all_gather(own, "fsdp", axis=0, tiled=True)
        down = down[layer]
        dz = mm_nt(every, down) * slope
        dz_b = dz.astype(BF)
        part = mm_nt(dz_b, up).astype(BF)
        total = lax.psum_scatter(part, "fsdp", scatter_dimension=0, tiled=True).astype(F32)
        return total, every, dz_b, jnp.sum(dz, axis=0, keepdims=True)
    shape = (4, rows, D)
    return plane_call(
        functools.partial(backward_kernel, layer), 2 + 6 * layer,
        (
            jax.ShapeDtypeStruct((rows, D), F32),
            jax.ShapeDtypeStruct(shape, BF),
            jax.ShapeDtypeStruct(shape, BF),
            jax.ShapeDtypeStruct((1, D), F32),
        ),
        rows, own, up, down, slope,
    )


def spread_up(core, blocks, full, load, u_send, u_recv, v_send, v_recv):
    s = lax.axis_index("section")
    f = lax.axis_index("fsdp")
    xn, yn = plane_neighbours()
    others = (xn, yn, 3 - f)
    shard = blocks.shape[1]

    def rows_of(owner):
        return full.at[pl.ds(pl.multiple_of(owner * shard, 16), shard)]

    def to(src, dst, send, recv, **where):
        return pltpu.make_async_remote_copy(
            src_ref=src, dst_ref=dst, send_sem=send, recv_sem=recv,
            device_id=where, device_id_type=MESH,
        )

    def chip(i):
        return to(blocks.at[others[i]], rows_of(f), u_send.at[i], u_recv.at[i], fsdp=others[i])

    def over(i):
        rows = rows_of((*others, f)[i])
        return to(rows, rows, v_send.at[i], v_recv.at[i], section=1 - core)

    near = pltpu.make_async_copy(blocks.at[f], rows_of(f), load)

    def first():
        @pl.when(s == core)
        def _():
            near.start()
            for i in range(3):
                chip(i).start()
            near.wait()
            over(3).start()

    def then():
        @pl.when(s == core)
        def _():
            for i in range(3):
                chip(i).wait_recv()
                over(i).start()

    def last():
        @pl.when(s == core)
        def _():
            for i in range(3):
                chip(i).wait_send()
            for i in range(4):
                over(i).wait_send()

        @pl.when(s == 1 - core)
        def _():
            for i in range(4):
                over(i).wait_recv()

    return first, then, last


def spread_sems():
    return [pltpu.SemaphoreType.DMA((n,)) for n in (3, 3, 4, 4)]


def weights_kernel(
    qkv_in, out_in, gains, biases, hidden, rows_in, up_in, down_in,
    full, rows_out, up_out, up_blocks, down_out, next_half,
    own, other_half, load, core_s, core_r, p_send, p_recv, f_send, f_recv, z_send, z_recv,
    u_send, u_recv, v_send, v_recv,
):
    s = lax.axis_index("section")
    f = lax.axis_index("fsdp")
    xn, yn = plane_neighbours()
    dn = 3 - f
    shard, wide = own.shape[1], own.shape[2]
    cut = 640
    left = pl.ds(0, cut)
    right = pl.ds(cut, wide - cut)

    def to(src, dst, send, recv, **where):
        return pltpu.make_async_remote_copy(
            src_ref=src, dst_ref=dst, send_sem=send, recv_sem=recv,
            device_id=where, device_id_type=MESH,
        )

    pad = jnp.zeros((shard, wide - D), BF)
    for p in range(3):
        own[p] = jnp.concatenate([qkv_in[:, pl.ds(p * D, D)], pad], axis=1)
    unit_rows = (
        lax.broadcasted_iota(jnp.int32, (16, 64), 0) == lax.broadcasted_iota(jnp.int32, (16, 64), 1)
    ).astype(F32)
    hidden_rows = [hidden[:, pl.ds(i * shard, shard)] for i in range(hidden.shape[1] // shard)]
    small = jnp.concatenate(
        [
            value.astype(F32)
            for value in (gains[...], biases[...], *hidden_rows, jnp.zeros((8 - len(hidden_rows), shard)))
        ],
        axis=0,
    )
    beside = mm_tn(small.astype(BF), unit_rows.astype(BF)).astype(BF)
    own[3] = jnp.concatenate([out_in[...], beside], axis=1)

    barrier = pltpu.get_barrier_semaphore()
    z = lax.axis_index("ctx")
    above = {"ctx": lax.rem(z + 1, 4)}
    below = {"ctx": lax.rem(z + 3, 4)}
    partners = ({"section": 1 - s}, {"fsdp": xn}, {"fsdp": yn}, {"fsdp": dn}, above, below)
    for where in partners:
        pl.semaphore_signal(barrier, inc=1, device_id=where, device_id_type=MESH)
    pl.semaphore_wait(barrier, 6)
    rows = rows_in.shape[0]
    near_rows, far_rows = pl.ds(rows, rows), pl.ds(0, rows)
    step_one = to(rows_in, rows_out.at[near_rows], z_send.at[0], z_recv.at[0], **above)
    step_two = to(
        rows_out.at[near_rows], rows_out.at[far_rows], z_send.at[1], z_recv.at[1], **above
    )

    @pl.when(z < 3)
    def _():
        step_one.start()

    rows_out[pl.ds(2 * rows, rows), :] = rows_in[...]

    @pl.when(z == 0)
    def _():
        rows_out[near_rows, :] = jnp.zeros(rows_in.shape, BF)

    @pl.when(z < 2)
    def _():
        rows_out[far_rows, :] = jnp.zeros(rows_in.shape, BF)

    def blk(owner):
        return pl.ds(pl.multiple_of(owner * shard, 16), shard)

    def give(p):
        return to(own.at[p], full.at[p, blk(f)], core_s.at[p], core_r.at[p], section=1)

    def keep(p):
        return pltpu.make_async_copy(own.at[p], full.at[p, blk(f)], load.at[p])

    @pl.when(s == 0)
    def _():
        for p in (2, 3, 0, 1):
            give(p).start()
        for p in range(4):
            keep(p).start()
        keep(0).wait()
        keep(1).wait()

    @pl.when(s == 1)
    def _():
        give(2).wait_recv()
        give(3).wait_recv()

    def same(piece, rows, send, recv, cols=slice(None), **where):
        ref = full.at[piece, rows, cols]
        return to(ref, ref, send, recv, **where)

    def hops(k):
        p = 2 * s + k
        return (
            same(p, blk(f), p_send.at[k, 0], p_recv.at[k, 0], fsdp=xn),
            same(p, blk(f), p_send.at[k, 1], p_recv.at[k, 1], fsdp=yn),
            same(p, blk(yn), p_send.at[k, 2], p_recv.at[k, 2], left, fsdp=xn),
            same(p, blk(xn), p_send.at[k, 3], p_recv.at[k, 3], right, fsdp=yn),
        )

    def here(k):
        p = 2 * s + k
        return [
            same(p, blk(owner), f_send.at[k, i], f_recv.at[k, i], section=1 - s)
            for i, owner in enumerate((xn, yn, dn))
        ]

    for k in range(2):
        copies = hops(k)
        copies[0].start()
        copies[1].start()
    down_far = to(down_in, down_out.at[s], core_s.at[4], core_r.at[4], section=1 - s)
    down_near = pltpu.make_async_copy(down_in, down_out.at[s], load.at[4])
    down_far.start()
    down_near.start()
    swap = to(other_half, next_half, core_s.at[5], core_r.at[5], section=0)

    @pl.when(s == 1)
    def _():
        for p in range(4):
            at = pl.ds(p * wide, wide)
            other_half[:, at] = own[p, pl.ds(0, shard // 2), :]
            next_half[:, at] = own[p, pl.ds(shard // 2, shard // 2), :]
        swap.start()

    for j in range(4):
        up_blocks[j] = up_in[:, pl.ds(j * D, D)]

    up_first, up_then, up_last = spread_up(
        0, up_blocks, up_out, load.at[5], u_send, u_recv, v_send, v_recv
    )
    up_first()
    for k in range(2):
        copies, across = hops(k), here(k)
        copies[0].wait_recv()
        copies[3].start()
        across[0].start()
        copies[1].wait_recv()
        copies[2].start()
        across[1].start()

    @pl.when(z > 0)
    def _():
        step_one.wait_recv()

    @pl.when((z == 1) | (z == 2))
    def _():
        step_two.start()

    for k in range(2):
        copies, across = hops(k), here(k)
        copies[2].wait_recv()
        copies[3].wait_recv()
        across[2].start()
    up_then()
    for k in range(2):
        for copy in here(k):
            copy.wait()
        for copy in hops(k):
            copy.wait_send()
    up_last()

    @pl.when(s == 0)
    def _():
        for p in range(4):
            give(p).wait_send()
        keep(2).wait()
        keep(3).wait()

    @pl.when(s == 1)
    def _():
        give(0).wait_recv()
        give(1).wait_recv()

    down_near.wait()
    down_far.wait()
    pl.when(s == 0)(swap.wait_recv)
    pl.when(s == 1)(swap.wait_send)

    @pl.when(z < 3)
    def _():
        step_one.wait_send()

    @pl.when((z == 1) | (z == 2))
    def _():
        step_two.wait_send()

    @pl.when(z > 1)
    def _():
        step_two.wait_recv()


def first_weights(qkv, out, gains, biases, hidden, rows_in, up, down):
    dma = pltpu.SemaphoreType.DMA
    shard = qkv.shape[0]
    shapes = (
        (4, D, WIDE), (3 * rows_in.shape[0], D), (D, D), (4, shard, D), (2, D, D), (shard // 2, 4 * WIDE)
    )
    return pl.pallas_call(
        weights_kernel,
        out_shape=tuple(jax.ShapeDtypeStruct(shape, BF) for shape in shapes),
        in_specs=[VSPEC] * 7 + [pl.BlockSpec(memory_space=pl.ANY)],
        out_specs=(VSPEC,) * 6,
        scratch_shapes=[
            pltpu.VMEM((4, shard, WIDE), BF),
            pltpu.VMEM((shard // 2, 4 * WIDE), BF),
            dma((6,)), dma((6,)), dma((6,)), dma((2, 4)), dma((2, 4)), dma((2, 3)), dma((2, 3)),
            dma((2,)), dma((2,)), *spread_sems(),
        ],
        compiler_params=pltpu.CompilerParams(
            collective_id=4, has_side_effects=True, vmem_limit_bytes=48 * 1024 * 1024
        ),
        cost_estimate=lasting(75),
        name="first_weights",
    )(qkv, out, gains, biases, hidden, rows_in, up, down)


def z_partners():
    z = lax.axis_index("ctx")
    return z + 1 - 2 * lax.rem(z, 2), 3 - z, (z == 1) | (z == 2)


def add_rows(dst, one, two, rows, step):
    @pl.loop(0, rows // step)
    def _(i):
        at = pl.ds(pl.multiple_of(i * step, 16), step)
        dst[at, :] = (one[at, :].astype(F32) + two[at, :].astype(F32)).astype(dst.dtype)


CUTS = ((0, 640, 384), (640, 512, 256))


def reduce_kernel(
    q0, k0, v0, o0, q1, k1, v1, o1, mlp, made0, made1, grad1, halo, d_resid, da_own, wide, par,
    qkv_out, out_out, down_out, up_out, made_out, grad_out,
    own_in, held, up_own, up_far, sent, caught, grad0,
    x1a, y1a, x2a, y2a, sxa, sya, ta, zaa, zba,
    x1b, y1b, x2b, y2b, sxb, syb, tb, zab, zbb,
    load, core_s, core_r, p_send, p_recv, z_send, z_recv, h_send, h_recv, x_send, x_recv,
):
    s = lax.axis_index("section")
    f = lax.axis_index("fsdp")
    xn, yn = plane_neighbours()
    dn = 3 - f
    side, across, inner = z_partners()
    pieces = ((q0, k0, v0, o0), (q1, k1, v1, o1))
    sets = (
        (x1a, y1a, x2a, y2a, sxa, sya, ta, zaa, zba),
        (x1b, y1b, x2b, y2b, sxb, syb, tb, zab, zbb),
    )
    shard = out_out.shape[0]
    rows = da_own.shape[0]
    z = lax.axis_index("ctx")
    above, below = {"ctx": lax.rem(z + 1, 4)}, {"ctx": lax.rem(z + 3, 4)}

    def to(src, dst, send, recv, **where):
        return pltpu.make_async_remote_copy(
            src_ref=src, dst_ref=dst, send_sem=send, recv_sem=recv,
            device_id=where, device_id_type=MESH,
        )

    barrier = pltpu.get_barrier_semaphore()
    partners = ({"section": 1 - s}, {"fsdp": xn}, {"fsdp": yn}, above, below)
    for where in partners:
        pl.semaphore_signal(barrier, inc=1, device_id=where, device_id_type=MESH)
    pl.semaphore_wait(barrier, 5)

    def blk(owner):
        return pl.ds(pl.multiple_of(owner * shard, 16), shard)

    def by_core(act):
        for core in range(2):
            pl.when(s == core)(functools.partial(act, core))

    def far(j, src):
        return to(src, held.at[j], core_s.at[j], core_r.at[j], section=1 - s)

    def near(j, src):
        return pltpu.make_async_copy(src, own_in.at[j % 2], load.at[j])

    def bufs(c):
        return tuple(ref.at[c // 2] for ref in sets[c % 2])

    def plane(c):
        x1, y1, x2, y2, sx, sy = bufs(c)[:6]
        own = held.at[c // 2]
        at, width, cut = CUTS[c % 2]
        left, right = pl.ds(at, cut), pl.ds(at + cut, width - cut)
        to_left, to_right = pl.ds(0, cut), pl.ds(cut, width - cut)
        sems = [(p_send.at[c, i], p_recv.at[c, i]) for i in range(6)]
        return (
            to(own.at[blk(dn), left], x1, *sems[0], fsdp=xn),
            to(own.at[blk(dn), right], y1, *sems[1], fsdp=yn),
            to(own.at[blk(xn), left], x2.at[:, to_left], *sems[2], fsdp=xn),
            to(own.at[blk(yn), right], y2.at[:, to_right], *sems[3], fsdp=yn),
            to(sx, x2.at[:, to_right], *sems[4], fsdp=xn),
            to(sy, y2.at[:, to_left], *sems[5], fsdp=yn),
        )

    def along(c):
        t, za, zb = bufs(c)[6:]
        sems = [(z_send.at[c, i], z_recv.at[c, i]) for i in range(3)]
        return (
            to(t, za, *sems[0], ctx=side),
            to(za, zb, *sems[1], ctx=across),
            to(zb, zb, *sems[2], ctx=side),
        )

    def join(j):
        far(j, q0).wait_recv()
        near(j, q0).wait()
        add_rows(held.at[j], own_in.at[j % 2], held.at[j], 4 * shard, 64)
        for c in (2 * j, 2 * j + 1):
            for copy in plane(c)[:4]:
                copy.start()
        if j < 2:
            by_core(lambda core: near(j + 2, pieces[core][j + 2]).start())

    def second(c):
        copies = plane(c)
        x1, y1, _, _, sx, sy = bufs(c)[:6]
        at, width, cut = CUTS[c % 2]
        own = held.at[c // 2]
        copies[0].wait_recv()
        add_rows(sy, own.at[blk(yn), pl.ds(at, cut)], x1, shard, 16)
        copies[5].start()
        copies[1].wait_recv()
        add_rows(sx, own.at[blk(xn), pl.ds(at + cut, width - cut)], y1, shard, 16)
        copies[4].start()

    def third(c):
        copies = plane(c)
        _, _, x2, y2, _, _, t, _, _ = bufs(c)
        at, width, _ = CUTS[c % 2]
        for copy in copies[2:]:
            copy.wait_recv()
        own = held.at[c // 2, blk(f), pl.ds(at, width)]

        @pl.loop(0, shard // 16)
        def _(i):
            part = pl.ds(pl.multiple_of(i * 16, 16), 16)
            t[part, :] = (
                own[part, :].astype(F32) + x2[part, :].astype(F32) + y2[part, :].astype(F32)
            ).astype(BF)

        @pl.when(jnp.logical_not(inner))
        def _():
            along(c)[0].start()

    def inward(c):
        @pl.when(inner)
        def _():
            t, za, _ = bufs(c)[6:]
            copies = along(c)
            copies[0].wait_recv()
            add_rows(za, t, za, shard, 16)
            copies[1].start()

    def crossed(c):
        @pl.when(inner)
        def _():
            _, za, zb = bufs(c)[6:]
            copies = along(c)
            copies[1].wait_recv()
            add_rows(zb, za, zb, shard, 16)
            copies[2].start()

    def last(c):
        at, width, _ = CUTS[c % 2]
        j = c // 2

        @pl.when(jnp.logical_not(inner))
        def _():
            along(c)[2].wait_recv()

        done = bufs(c)[8]
        keep = min(width, D - at) if j < 3 else width

        @pl.loop(0, shard // 16)
        def _(i):
            part = pl.ds(pl.multiple_of(i * 16, 16), 16)
            if j < 3:
                qkv_out[part, pl.ds(j * D + at, keep)] = done[part, pl.ds(0, keep)]
            else:
                out_out[part, pl.ds(at, keep)] = done[part, :]

    half = down_out.shape[0] // 2
    mine = pl.ds(pl.multiple_of(s * half, 16), half)
    down_far = to(mlp.at[0], down_out.at[mine], core_s.at[4], core_r.at[4], section=1 - s)
    down_near = pltpu.make_async_copy(mlp.at[0], down_out.at[mine], load.at[4])
    far_up = to(mlp.at[1], up_far, core_s.at[5], core_r.at[5], section=1 - s)
    near_up = pltpu.make_async_copy(mlp.at[1], up_own, load.at[5])

    def lay_up():
        far_up.wait_recv()
        near_up.wait()

        @pl.when(s == 1)
        def _():
            for k in range(4):
                at = pl.ds(k * (shard // 2), shard // 2)
                up_out[:, pl.ds(k * D, D)] = jnp.concatenate([up_far[at, :], up_own[at, :]], axis=0)

    back_one = to(halo.at[pl.ds(0, rows)], caught.at[0], h_send.at[0], h_recv.at[0], **below)
    back_two = to(sent, caught.at[1], h_send.at[1], h_recv.at[1], **below)

    def back():
        @pl.when(z < 3)
        def _():
            back_one.wait_recv()

        @pl.when(z == 3)
        def _():
            caught[0] = jnp.zeros_like(caught[0])

        @pl.when(z > 0)
        def _():
            add_rows(sent, halo.at[pl.ds(rows, rows)], caught.at[0], rows, 64)
            back_two.start()

    made_far = (
        to(made1, made_out.at[0], x_send.at[0], x_recv.at[0], section=1),
        to(made0, made_out.at[1], x_send.at[0], x_recv.at[0], section=0),
    )
    grad_far = (
        to(grad1, grad_out.at[0], x_send.at[1], x_recv.at[1], section=1),
        to(grad0, grad_out.at[1], x_send.at[1], x_recv.at[1], section=0),
    )
    made_near = (
        pltpu.make_async_copy(made0, made_out.at[0], load.at[6]),
        pltpu.make_async_copy(made1, made_out.at[1], load.at[6]),
    )
    grad_near = pltpu.make_async_copy(grad1, grad_out.at[1], load.at[7])

    def back_end():
        @pl.when(z < 3)
        def _():
            back_two.wait_recv()

        @pl.when(z == 3)
        def _():
            caught[1] = jnp.zeros_like(caught[1])

        unit, inv = norm_parts(wide[...].astype(F32))
        da = da_own[...] + caught[1].astype(F32)
        grad0[...] = d_resid[...] + norm_back(da, par[0:1, :], unit, inv)

        @pl.when(s == 0)
        def _():
            grad_out[0] = grad0[...]

        @pl.when(s == 1)
        def _():
            grad_far[1].start()

    @pl.when(s == 0)
    def _():
        made_far[0].start()
        grad_far[0].start()
        made_near[0].start()

    @pl.when(s == 1)
    def _():
        made_far[1].start()
        made_near[1].start()
        grad_near.start()

    @pl.when(z > 0)
    def _():
        back_one.start()

    for j in range(4):
        by_core(lambda core: far(j, pieces[1 - core][j]).start())
        if j < 2:
            by_core(lambda core: near(j, pieces[core][j]).start())
    for copy in (down_far, down_near, far_up, near_up):
        copy.start()

    join(0)
    for c in range(12):
        if c in (1, 3, 5):
            join((c + 1) // 2)
        if c < 8:
            second(c)
        if 1 <= c <= 8:
            third(c - 1)
        if 2 <= c <= 9:
            inward(c - 2)
        if 3 <= c <= 10:
            crossed(c - 3)
        if c >= 4:
            last(c - 4)
        if c == 2:
            back()
        if c == 4:
            lay_up()
        if c == 6:
            back_end()

    down_near.wait()
    down_far.wait()
    far_up.wait_send()

    @pl.when(s == 0)
    def _():
        made_near[0].wait()
        made_far[0].wait_send()
        grad_far[0].wait_send()
        made_far[1].wait_recv()
        grad_far[1].wait_recv()

    @pl.when(s == 1)
    def _():
        made_near[1].wait()
        grad_near.wait()
        made_far[1].wait_send()
        grad_far[1].wait_send()
        made_far[0].wait_recv()
        grad_far[0].wait_recv()

    @pl.when(z > 0)
    def _():
        back_one.wait_send()
        back_two.wait_send()

    for j in range(4):
        far(j, q0).wait_send()
    for c in range(8):
        for copy in plane(c):
            copy.wait_send()

    @pl.when(inner)
    def _():
        for c in range(8):
            for copy in along(c)[1:]:
                copy.wait_send()

    @pl.when(jnp.logical_not(inner))
    def _():
        for c in range(8):
            along(c)[0].wait_send()


def reduce_both(zero, one, mlp, made, grad1, halo, d_resid, da_own, wide, par):
    shard = D // 4
    rows = da_own.shape[0]
    dma = pltpu.SemaphoreType.DMA
    any_spec = pl.BlockSpec(memory_space=pl.ANY)

    def buf(*shape):
        return pltpu.VMEM(shape, BF)

    def part(_, width, cut):
        wide_buf = buf(4, shard, width)
        return [
            buf(4, shard, cut), buf(4, shard, width - cut), wide_buf, wide_buf,
            buf(4, shard, width - cut), buf(4, shard, cut), wide_buf, wide_buf, wide_buf,
        ]

    shapes = ((shard, 3 * D), (shard, WIDE), (D, D), (shard, 4 * D), (2, rows, D))
    return pl.pallas_call(
        reduce_kernel,
        out_shape=(
            *(jax.ShapeDtypeStruct(shape, BF) for shape in shapes),
            jax.ShapeDtypeStruct((2, rows, D), F32),
        ),
        in_specs=[any_spec] * 12 + [VSPEC] * 5,
        out_specs=(VSPEC,) * 6,
        scratch_shapes=[
            buf(2, D, WIDE), buf(4, D, WIDE), buf(D // 2, D), buf(D // 2, D), buf(rows, D),
            buf(2, rows, D), pltpu.VMEM((rows, D), F32), *part(*CUTS[0]), *part(*CUTS[1]),
            dma((8,)), dma((6,)), dma((6,)), dma((8, 6)), dma((8, 6)), dma((8, 3)), dma((8, 3)),
            dma((2,)), dma((2,)), dma((2,)), dma((2,)),
        ],
        compiler_params=pltpu.CompilerParams(
            collective_id=3, has_side_effects=True, vmem_limit_bytes=60 * 1024 * 1024
        ),
        cost_estimate=lasting(120),
        name="reduce_both",
    )(*zero, *one, mlp, *made, grad1, halo, d_resid, da_own, wide, par)


def final_kernel(
    qkv, out, mine, far, down_one, up_one, made, grads,
    qkv_f, out_f, down_f, up_f, small, made_out, grads_out,
):
    s = lax.axis_index("section")
    half = mine.shape[1]
    shard = qkv.shape[0]
    pick_row = (
        lax.broadcasted_iota(jnp.int32, (16, 128), 1)
        == lax.broadcasted_iota(jnp.int32, (16, 128), 0) + (D - TAIL)
    )
    small[...] = mm_nt(pick_row.astype(F32).astype(BF), out[:, pl.ds(TAIL, 128)])

    @pl.loop(0, made.shape[1] // 16)
    def _(i):
        at = pl.ds(pl.multiple_of(i * 16, 16), 16)
        for m in range(2):
            made_out[m, at, :] = made[m, at, :]
            grads_out[m, at, :] = grads[m, at, :]

    @pl.loop(0, shard // 16)
    def _(i):
        at = pl.ds(pl.multiple_of(i * 16, 16), 16)
        qkv_f[at, :] = qkv[at, :].astype(F32)
        out_f[at, :] = out[at, pl.ds(0, D)].astype(F32)

        @pl.when(s == 1)
        def _():
            up_f[at, :] = up_one[at, :].astype(F32)

    @pl.when(s == 0)
    def _():
        for k in range(4):
            at = pl.ds(k * (shard // 2), shard // 2)
            rows_k = jnp.concatenate([mine[1, at, :], far[1, at, :]], axis=0)
            up_f[:, pl.ds(k * D, D)] = rows_k.astype(F32)

    @pl.loop(0, half // 16)
    def _(i):
        at = pl.ds(pl.multiple_of(i * 16, 16), 16)
        after = pl.ds(pl.multiple_of(half + i * 16, 16), 16)

        @pl.when(s == 0)
        def _():
            down_f[at, :] = mine[0, at, :].astype(F32)
            down_f[after, :] = far[0, at, :].astype(F32)

        @pl.when(s == 1)
        def _():
            down_f[at, :] = down_one[at, :].astype(F32)
            down_f[after, :] = down_one[after, :].astype(F32)


def final_layouts(*values):
    qkv, _, _, _, down_one, up_one, made, grads = values
    shard = qkv.shape[0]
    outs = [(shape, F32) for shape in (qkv.shape, (shard, D), down_one.shape, up_one.shape)]
    outs += [((16, shard), F32), (made.shape, BF), (grads.shape, F32)]
    return pl.pallas_call(
        final_kernel,
        out_shape=tuple(jax.ShapeDtypeStruct(*out) for out in outs),
        in_specs=[VSPEC] * 8,
        out_specs=(VSPEC,) * 7,
        compiler_params=pltpu.CompilerParams(vmem_limit_bytes=52 * 1024 * 1024),
        cost_estimate=lasting(10),
        name="final_layouts",
    )(*values)


def core_half(values, axis):
    s = lax.axis_index("section")
    keep = lax.dynamic_index_in_dim(values, s, axis, keepdims=False)
    give = lax.dynamic_index_in_dim(values, 1 - s, axis, keepdims=False)
    return (keep.astype(F32) + on_chip(give).astype(F32)).astype(BF)


def halves_settle(zero, one, nf, shard):
    s = lax.axis_index("section")
    mine, far = pick(s, zero, one), on_chip(pick(s, one, zero))
    first, second = pick(s, mine, far).astype(F32), pick(s, far, mine).astype(F32)
    down = jnp.concatenate([first[0], second[0]], axis=0)
    up = jnp.concatenate([half[1].reshape(nf, shard // 2, -1) for half in (first, second)], axis=1)
    return down, up.transpose(1, 0, 2).reshape(shard, -1)


def reduce_plain(pieces):
    s = lax.axis_index("section")
    pair = ("fsdp", "section")
    a = jnp.stack([lax.psum_scatter(p, pair, scatter_dimension=0, tiled=True) for p in pieces])
    a = lax.psum(a, "ctx")
    far = on_chip(a)
    return jnp.concatenate([pick(s, a, far), pick(s, far, a)], axis=1)


def shift(value, steps):
    count = lax.axis_size("ctx")
    pairs = [(i, i + steps) for i in range(count) if 0 <= i + steps < count]
    return lax.ppermute(value, "ctx", pairs)


def with_halo(own, chunks):
    parts = [own]
    for _ in range(chunks):
        parts.append(shift(parts[-1], 1))
    return jnp.concatenate(parts[::-1], axis=0)


def return_halo(halo, chunks, rows):
    carried = None
    for far in range(chunks):
        mine = halo[far * rows : (far + 1) * rows]
        carried = mine if carried is None else mine + carried
        carried = shift(carried.astype(BF), -1).astype(F32)
    return carried


def pick(s, first, second):
    return jnp.where(s == 0, first, second)


def on_chip(value):
    return lax.ppermute(value, "section", SWAP)


def both_layers(own, s):
    other = on_chip(own)
    return pick(s, own, other), pick(s, other, own)


def flat(values):
    return values.reshape(-1, values.shape[-1])


def widen(values):
    return jnp.pad(values, ((0, 0), (0, WIDE - D)))


TAIL = 1024


def scores_forward(q, k, v, bias, lanes):
    outs = []
    for low in (True, False):
        one = jnp.where((lanes < HD) if low else (lanes >= HD), q, jnp.zeros_like(q))
        weight = jnp.exp(mm_nt(one, k) + bias)
        prob = weight * (1.0 / jnp.sum(weight, axis=-1, keepdims=True))
        outs.append(mm(prob.astype(BF), v))
    return jnp.where(lanes < HD, outs[0], outs[1]).astype(BF)


def scores_backward(q, k, v, grad, bias_t, lanes):
    dqs, dk, dv = [], 0.0, 0.0
    for low in (True, False):
        mine = (lanes < HD) if low else (lanes >= HD)
        one = jnp.where(mine, q, jnp.zeros_like(q))
        g = jnp.where(mine, grad, jnp.zeros_like(grad))
        weight = jnp.exp(mm_nt(k, one) + bias_t)
        prob = weight * (1.0 / jnp.sum(weight, axis=0, keepdims=True))
        d_prob = mm_nt(v, g)
        row = jnp.sum(prob * d_prob, axis=0, keepdims=True)
        d_score = (prob * (d_prob - row)).astype(BF)
        dqs.append(mm_tn(d_score, k))
        dk = dk + mm(d_score, one)
        dv = dv + mm(prob.astype(BF), g)
    dq = jnp.where(lanes < HD, dqs[0], dqs[1]) * SCALE
    return dq.astype(BF), dk.astype(BF), dv.astype(BF)


def lane_tile(i):
    return pl.ds(pl.multiple_of(i * 128, 128), 128)


def widened(row):
    return jnp.concatenate([row, jnp.zeros((row.shape[0], WIDE - D), row.dtype)], axis=1)


def ctx_ring(rows_in, landing, send, recv, partners=()):
    z = lax.axis_index("ctx")
    above = {"ctx": lax.rem(z + 1, 4)}
    below = {"ctx": lax.rem(z + 3, 4)}
    rows = rows_in.shape[0]
    near, far = pl.ds(rows, rows), pl.ds(0, rows)
    barrier = pltpu.get_barrier_semaphore()

    def on(src, dst, i):
        return pltpu.make_async_remote_copy(
            src_ref=src, dst_ref=dst, send_sem=send.at[i], recv_sem=recv.at[i],
            device_id=above, device_id_type=MESH,
        )

    one = on(rows_in, landing.at[near], 0)
    two = on(landing.at[near], landing.at[far], 1)

    def begin():
        for where in (above, below, *partners):
            pl.semaphore_signal(barrier, inc=1, device_id=where, device_id_type=MESH)
        pl.semaphore_wait(barrier, 2 + len(partners))

        @pl.when(z < 3)
        def _():
            one.start()

        landing[pl.ds(2 * rows, rows), :] = rows_in[...]

        @pl.when(z == 0)
        def _():
            landing[near, :] = jnp.zeros(rows_in.shape, BF)

        @pl.when(z < 2)
        def _():
            landing[far, :] = jnp.zeros(rows_in.shape, BF)

    def middle():
        @pl.when(z > 0)
        def _():
            one.wait_recv()

        @pl.when((z == 1) | (z == 2))
        def _():
            two.start()

    def end():
        @pl.when(z > 1)
        def _():
            two.wait_recv()

        @pl.when(z < 3)
        def _():
            one.wait_send()

        @pl.when((z == 1) | (z == 2))
        def _():
            two.wait_send()

    return begin, middle, end


def block_kernel(ring, first, wq, wk, wv, wo, bias, *rest):
    if ring:
        up_blocks, *rest = rest
    normed, q_ref, k_ref, v_ref, att, resid, second, par, *rest = rest
    rows = resid.shape[0]
    total = normed.shape[0]
    if ring:
        wide_out, up_out, held, wide, up_full, send, recv, load, *sems = rest
        s = lax.axis_index("section")
        f = lax.axis_index("fsdp")
        xn, yn = plane_neighbours()
        partners = ({"section": 1 - s}, {"fsdp": xn}, {"fsdp": yn}, {"fsdp": 3 - f})
        begin, middle, end = ctx_ring(first, wide, send, recv, partners)
        up_first, up_then, up_last = spread_up(1, up_blocks, up_full, load.at[0], *sems)
        begin()
        up_first()
    else:
        (held,), wide = rest, first
    pick_row = (
        lax.broadcasted_iota(jnp.int32, (16, 128), 1)
        == lax.broadcasted_iota(jnp.int32, (16, 128), 0) + (D - TAIL)
    )
    par[...] = mm_nt(pick_row.astype(F32).astype(BF), wo[:, pl.ds(TAIL, 128)])
    last = total // rows - 1

    @pl.loop(0, last + 1)
    def _(i):
        if ring:
            pl.when(i == 1)(middle)
            pl.when(i == 2)(up_then)
            pl.when(i == 2)(end)
        at = pl.ds(pl.multiple_of((last - i) * rows, 16), rows)
        unit, _ = norm_parts(wide[at, :].astype(F32))
        low = (unit * par[0:1, :] + par[2:3, :]).astype(BF)
        normed[at, :] = low
        k_ref[at, :] = mm(low, wk[...]).astype(BF)
        v_ref[at, :] = (mm(low, wv[...]) + widened(par[4:5, :])).astype(BF)

        @pl.when(i == 0)
        def _():
            q_ref[...] = (mm(normed[at, :], wq[...]) + widened(par[3:4, :])).astype(BF)

    own = pl.ds(total - rows, rows)
    lanes = lax.broadcasted_iota(jnp.int32, (rows, 128), 1)

    @pl.loop(0, WIDE // 128)
    def _(i):
        at = lane_tile(i)
        held[:, at] = scores_forward(
            q_ref[:, at] * jnp.asarray(SCALE, BF), k_ref[:, at], v_ref[:, at], bias[...], lanes
        )

    att[...] = held[:, pl.ds(0, D)]
    res = wide[own, :].astype(F32) + mm(att[...], wo[:, pl.ds(0, D)]) + par[5:6, :]
    resid[...] = res
    unit, _ = norm_parts(res)
    second[...] = (unit * par[1:2, :] + par[6:7, :]).astype(BF)
    if ring:
        wide_out[...] = wide[...]
        up_last()
        up_out[...] = up_full[...]


def weight_specs(weights):
    if weights.ndim == 3:
        return [pl.BlockSpec((None, D, WIDE), lambda i, p=p: (p, 0, 0)) for p in range(4)]
    return [pl.BlockSpec((D, WIDE), lambda i, p=p: (0, p)) for p in range(4)]


def whole(shape):
    return pl.BlockSpec(shape, lambda i: (0,) * len(shape))


def block_forward(first, weights, bias, up_blocks=None):
    rows, total = bias.shape
    outs = (
        ((total, D), BF), ((rows, WIDE), BF), ((total, WIDE), BF), ((total, WIDE), BF),
        ((rows, D), BF), ((rows, D), F32), ((rows, D), BF), ((16, D), F32),
    )
    scratch = [pltpu.VMEM((rows, WIDE), BF)]
    params, more = {}, ()
    if up_blocks is not None:
        outs += (((total, D), BF), ((D, D), BF))
        scratch += [pltpu.VMEM((total, D), BF), pltpu.VMEM((D, D), BF)]
        scratch += [pltpu.SemaphoreType.DMA((n,)) for n in (2, 2, 1)] + spread_sems()
        params, more = {"collective_id": 5, "has_side_effects": True}, (up_blocks,)
    return pl.pallas_call(
        functools.partial(block_kernel, bool(more)),
        out_shape=tuple(jax.ShapeDtypeStruct(*out) for out in outs),
        grid=(1,),
        in_specs=[
            whole(first.shape), *weight_specs(weights), whole(bias.shape),
            *(whole(value.shape) for value in more),
        ],
        out_specs=tuple(whole(shape) for shape, _ in outs),
        scratch_shapes=scratch,
        compiler_params=pltpu.CompilerParams(vmem_limit_bytes=60 * 1024 * 1024, **params),
        cost_estimate=lasting(45 if more else 22),
        name="block_forward",
    )(first, weights, weights, weights, weights, bias, *more)


def block_back_kernel(
    ring, d_second, up, resid, wide, q_ref, k_ref, v_ref, att, ffb_rows, wq, wk, wv, wo, par, bias_t,
    *rest,
):
    if ring:
        (d_in, d_low, dq_ref, dk_ref, dv_ref, left, right,
         held, sums, d_resid, da_own, da_halo, sent, caught, send, recv) = rest
    else:
        d_resid, dq_ref, dk_ref, dv_ref, da_own, da_halo, left, right, held, sums = rest
    rows = resid.shape[0]
    total = wide.shape[0]
    own = total - rows
    z = lax.axis_index("ctx")

    def back_to(src, dst, i):
        return pltpu.make_async_remote_copy(
            src_ref=src, dst_ref=dst, send_sem=send.at[i], recv_sem=recv.at[i],
            device_id={"ctx": lax.rem(z + 3, 4)}, device_id_type=MESH,
        )

    if ring:
        one = back_to(da_halo.at[pl.ds(0, rows)], caught.at[0], 0)
        two = back_to(sent, caught.at[1], 1)
        barrier = pltpu.get_barrier_semaphore()
        for step in (1, 3):
            pl.semaphore_signal(
                barrier, inc=1, device_id={"ctx": lax.rem(z + step, 4)}, device_id_type=MESH
            )
        pl.semaphore_wait(barrier, 2)

    def total_of(values):
        return jnp.sum(values, axis=0, keepdims=True)

    upstream = up[...].astype(F32)
    unit, inv = norm_parts(resid[...])
    grad = upstream + norm_back(d_second[...], par[1:2, :], unit, inv)
    d_resid[...] = grad
    sums[1:2, :] = total_of(d_second[...] * unit)
    sums[5:6, :] = total_of(grad)
    sums[6:7, :] = total_of(d_second[...])
    sums[7:8, :] = total_of(upstream)
    sums[8:16, :] = ffb_rows[...]
    low = grad.astype(BF)
    right[pl.ds(0, rows), :] = jnp.zeros((rows, WIDE), BF)
    right[pl.ds(0, rows), pl.ds(0, D)] = low
    right[pl.ds(rows, 16), :] = (
        lax.broadcasted_iota(jnp.int32, (16, WIDE), 1)
        == lax.broadcasted_iota(jnp.int32, (16, WIDE), 0) + D
    ).astype(F32).astype(BF)
    held[...] = jnp.zeros((rows, WIDE), BF)
    held[:, pl.ds(0, D)] = mm_nt(low, wo[:, pl.ds(0, D)]).astype(BF)
    lanes = lax.broadcasted_iota(jnp.int32, (rows, 128), 1)

    @pl.loop(0, WIDE // 128)
    def _(i):
        at = lane_tile(i)
        dq_ref[:, at], dk_ref[:, at], dv_ref[:, at] = scores_backward(
            q_ref[:, at] * jnp.asarray(SCALE, BF), k_ref[:, at], v_ref[:, at], held[:, at],
            bias_t[...], lanes,
        )

    sums[3:4, :] = total_of(dq_ref[...].astype(F32))[:, :D]
    sums[4:5, :] = total_of(dv_ref[...].astype(F32))[:, :D]
    sums[0:1, :] = jnp.zeros((1, D), F32)
    sums[2:3, :] = jnp.zeros((1, D), F32)

    def back(at):
        da = mm_nt(dk_ref[at, :], wk[...]) + mm_nt(dv_ref[at, :], wv[...])
        return da

    def count(da, at):
        unit, _ = norm_parts(wide[at, :].astype(F32))
        sums[0:1, :] += total_of(da * unit)
        sums[2:3, :] += total_of(da)

    @pl.loop(0, own // rows)
    def _(i):
        at = pl.ds(pl.multiple_of(i * rows, 16), rows)
        da = back(at)
        da_halo[at, :] = da.astype(BF)
        if ring:

            @pl.when((i == 0) & (z > 0))
            def _():
                one.start()

        count(da, at)

    at = pl.ds(own, rows)
    da = back(at) + mm_nt(dq_ref[...], wq[...])
    da_own[...] = da
    count(da, at)
    if ring:

        @pl.when(z < 3)
        def _():
            one.wait_recv()

        @pl.when(z == 3)
        def _():
            caught[0] = jnp.zeros_like(caught[0])

        @pl.when(z > 0)
        def _():
            add_rows(sent, da_halo.at[pl.ds(rows, rows)], caught.at[0], rows, 64)
            two.start()

    left[pl.ds(0, rows), :] = att[...]
    left[pl.ds(rows, 16), :] = sums[...].astype(BF)
    if ring:

        @pl.when(z < 3)
        def _():
            two.wait_recv()

        @pl.when(z == 3)
        def _():
            caught[1] = jnp.zeros_like(caught[1])

        @pl.loop(0, rows // 64)
        def _(i):
            part = pl.ds(pl.multiple_of(i * 64, 64), 64)
            behind = pl.ds(pl.multiple_of(own + i * 64, 64), 64)
            unit, inv = norm_parts(wide[behind, :].astype(F32))
            da = da_own[part, :] + caught[1, part, :].astype(F32)
            grad = d_resid[part, :] + norm_back(da, par[0:1, :], unit, inv)
            d_in[part, :] = grad
            d_low[part, :] = grad.astype(BF)

        @pl.when(z > 0)
        def _():
            one.wait_send()
            two.wait_send()


def block_backward(d_second, up, resid, wide, q, k, v, att, ffb_rows, weights, par, bias_t, ring):
    total, rows = wide.shape[0], resid.shape[0]
    f32_rows, low_rows = ((rows, D), F32), ((rows, D), BF)
    heads = (((rows, WIDE), BF), ((total, WIDE), BF), ((total, WIDE), BF))
    factors = (((rows + 16, D), BF), ((rows + 16, WIDE), BF))
    halo = ((total - rows, D), BF)
    held = [pltpu.VMEM((rows, WIDE), BF), pltpu.VMEM((16, D), F32)]
    params = {}
    if ring:
        outs = (f32_rows, low_rows, *heads, *factors)
        held += [pltpu.VMEM(*f32_rows), pltpu.VMEM(*f32_rows), pltpu.VMEM(*halo), pltpu.VMEM(*low_rows)]
        held += [pltpu.VMEM((2, rows, D), BF)] + [pltpu.SemaphoreType.DMA((2,))] * 2
        params = {"collective_id": 6, "has_side_effects": True}
    else:
        outs = (f32_rows, *heads, f32_rows, halo, *factors)
    before = (d_second, up, resid, wide, q, k, v, att, ffb_rows)
    return pl.pallas_call(
        functools.partial(block_back_kernel, ring),
        out_shape=tuple(jax.ShapeDtypeStruct(*out) for out in outs),
        grid=(1,),
        in_specs=[
            *(whole(value.shape) for value in before), *weight_specs(weights),
            whole(par.shape), whole(bias_t.shape),
        ],
        out_specs=tuple(whole(shape) for shape, _ in outs),
        scratch_shapes=held,
        compiler_params=pltpu.CompilerParams(vmem_limit_bytes=60 * 1024 * 1024, **params),
        cost_estimate=lasting(58 if ring else 38),
        name="block_backward",
    )(*before, weights, weights, weights, weights, par, bias_t)


def on_device(
    inputs, segments, cotangent, qkv_weight, out_weight, up_weight, down_weight,
    norm_gains, biases, ff_bias,
):
    rows = inputs.shape[2]
    length = segments.shape[2]
    chunks = min((length // 2 - 1 + rows - 1) // rows, lax.axis_size("ctx") - 1)
    reach = chunks * rows
    s = lax.axis_index("section")
    f = lax.axis_index("fsdp")
    nf = lax.axis_size("fsdp")
    shard = D // nf
    ff_here = ff_bias.shape[1]
    per_row = ff_here // shard
    pair = ("fsdp", "section")
    fits = nf == 4 and lax.axis_size("ctx") == 4 and chunks == 2

    own_in = lax.dynamic_index_in_dim(inputs, s, 0, keepdims=False)[0]
    own_cot = lax.dynamic_index_in_dim(cotangent, s, 0, keepdims=False)[0]
    seg = lax.dynamic_index_in_dim(segments, s, 0, keepdims=False)[0]
    start = lax.axis_index("ctx") * rows
    key_seg = lax.dynamic_slice_in_dim(
        jnp.pad(seg, (reach, 0), constant_values=-1), start, reach + rows, 0
    )
    allowed = (key_seg[reach:, None] == key_seg[None, :]) & (
        jnp.arange(reach + rows, dtype=jnp.int32)[None, :] - reach
        <= jnp.arange(rows, dtype=jnp.int32)[:, None]
    )

    bias = jnp.where(allowed, 0.0, -1e30).astype(F32)
    bias_t = bias.T

    def gathered(rows_first):
        return lax.all_gather(rows_first, pair, axis=0, tiled=True)

    if fits:
        zero, wide_in, up_zero, up_blocks, down_w, one_half = first_weights(
            qkv_weight[0], out_weight[0], norm_gains[0], biases[0], ff_bias,
            own_in, up_weight[0], down_weight[0],
        )
        one = gathered(one_half)
        up_w = (up_zero, None)
    else:
        small = jnp.concatenate(
            [norm_gains[0].T, biases[0].T, ff_bias[0].reshape(per_row, shard).T], axis=1
        )
        beside = jnp.pad(small, ((0, 0), (0, WIDE - D - 8 - per_row)))
        packed = jnp.concatenate(
            [widen(qkv_weight[0][:, i * D : (i + 1) * D]) for i in range(3)]
            + [out_weight[0], beside],
            axis=1,
        )
        halves = packed.reshape(2, shard // 2, 4 * WIDE)
        keep = lax.dynamic_index_in_dim(halves, s, 0, keepdims=False)
        recv = on_chip(lax.dynamic_index_in_dim(halves, 1 - s, 0, keepdims=False))
        zero, one = gathered(pick(s, keep, recv)), gathered(pick(s, recv, keep))
        up_own = lax.all_to_all(
            up_weight[0].reshape(shard, nf, ff_here), "fsdp", split_axis=1, concat_axis=0, tiled=True
        ).reshape(D, ff_here)
        up_w = both_layers(up_own, s)
        down_w = both_layers(down_weight[0], s)
        wide_in = with_halo(own_in, chunks)

    weights = (zero, one)

    kept = []
    current = own_in
    produced = []
    for layer in range(2):
        if layer == 1 and fits:
            *made, wide, up_one = block_forward(current, weights[layer], bias, up_blocks)
            up_w = (up_w[0], up_one)
        else:
            wide = with_halo(current, chunks) if layer else wide_in
            made = block_forward(wide, weights[layer], bias)
        normed, q, k, v, att, resid, second, par = made
        ffb = lax.dynamic_slice(par, (8, f * shard), (per_row, shard)).reshape(1, ff_here)
        current, second_all, active, slope = mlp_forward(
            second, up_w[layer], down_w, layer, ffb, resid, par
        )
        produced.append(current)
        kept.append((wide, normed, q, k, v, att, resid, second_all, slope, active, par))

    upstream = own_cot
    derived = [None, None]
    parts = [None, None]
    mlp_sums = [None, None]
    for layer in (1, 0):
        wide, normed, q, k, v, att, resid, second_all, slope, active, par = kept[layer]
        d_second, up_all, dz_b, ffb_g = mlp_backward(upstream, up_w[layer], down_w, layer, slope)
        up_g = mm_tn(flat(second_all), flat(dz_b)).astype(BF)
        up_half = core_half(up_g.reshape(nf, 2, shard // 2, ff_here), 1)
        down_g = mm_tn(flat(active), flat(up_all)).astype(BF)
        down_half = core_half(down_g.reshape(2, ff_here // 2, D), 0)
        d_second, up_half, down_half = lax.optimization_barrier((d_second, up_half, down_half))
        up_half = lax.all_to_all(up_half, "fsdp", split_axis=0, concat_axis=0, tiled=True)
        ffb_rows = lax.dynamic_update_slice(
            jnp.zeros((8, D), F32), ffb_g.reshape(per_row, shard), (0, f * shard)
        )
        block = (
            d_second, upstream, resid, wide, q, k, v, att, ffb_rows, weights[layer], par, bias_t
        )
        if layer == 1 and fits:
            derived[1], upstream_next, dq, dk, dv, left, right = block_backward(*block, True)
        else:
            d_resid, dq, dk, dv, da_own, da_halo, left, right = block_backward(*block, False)
        if not fits:
            unit, inv = norm_parts(wide[reach:].astype(F32))
            late = return_halo(da_halo, chunks, rows)
            derived[layer] = d_resid + norm_back(da_own + late, par[0], unit, inv)
            upstream_next = derived[layer].astype(BF)
        pieces = (
            mm_tn(normed[reach:], dq).astype(BF),
            mm_tn(normed, dk).astype(BF),
            mm_tn(normed, dv).astype(BF),
            mm_tn(left, right).astype(BF),
        )
        parts[layer] = pieces
        up_half, down_half, _ = lax.optimization_barrier((up_half, down_half, dq))
        halves = jnp.stack([down_half, up_half.reshape(ff_here // 2, D)])
        if layer == 1:
            _, upstream_next = lax.optimization_barrier((halves, upstream_next))
        else:
            halves, mlp_sums[1] = lax.optimization_barrier((halves, mlp_sums[1]))
        mlp_sums[layer] = lax.psum(halves, "ctx")
        if layer == 1:
            upstream = upstream_next

    if fits:
        qkv_g, out_g, down_one, up_one, made, grads = reduce_both(
            parts[0], parts[1], mlp_sums[1], produced, derived[1], da_halo, d_resid, da_own,
            wide[reach:], par,
        )
        late_sum, qkv_g = lax.optimization_barrier((mlp_sums[0], qkv_g))
        far = lax.ppermute(late_sum, "section", [(1, 0)])
        qkv_g, out_g, grad_down, grad_up, small, made, grads = final_layouts(
            qkv_g, out_g, late_sum, far, down_one, up_one, made, grads
        )
        made, grads = made[None, :, None], grads[None, :, None]
    else:
        a_tot = pick(s, reduce_plain(parts[0]), reduce_plain(parts[1])).astype(F32)
        qkv_g = jnp.concatenate([a_tot[i, :, :D] for i in range(3)], axis=1)
        out_g = a_tot[3, :, :D]
        small = a_tot[3, :, D : D + 16].T
        grad_down, grad_up = halves_settle(*mlp_sums, nf, shard)
        made, grads = both_micros(produced, s), both_micros(derived, s)
    return (
        made,
        grads,
        qkv_g[None],
        out_g[None],
        grad_up[None],
        grad_down[None],
        small[None, :2],
        small[None, 2:8],
        small[8 : 8 + per_row].reshape(1, ff_here),
    )


def both_micros(layers, s):
    to_zero = lax.ppermute(layers[0], "section", [(1, 0)])
    to_one = lax.ppermute(layers[1], "section", [(0, 1)])
    out = jnp.stack([pick(s, layers[0], to_one), pick(s, to_zero, layers[1])])
    return out[None, :, None]


def solution(mesh):
    return jax.shard_map(
        on_device,
        mesh=mesh,
        in_specs=(
            P(None, "fsdp", "ctx", None),
            P(None, "fsdp", None),
            P(None, "fsdp", "ctx", None),
            P("section", "fsdp", None),
            P("section", "fsdp", None),
            P("section", "fsdp", None),
            P("section", "fsdp", None),
            P("section", None, "fsdp"),
            P("section", None, "fsdp"),
            P("section", "fsdp"),
        ),
        out_specs=(
            P("section", None, "fsdp", "ctx", None),
            P("section", None, "fsdp", "ctx", None),
            P("section", "fsdp", None),
            P("section", "fsdp", None),
            P("section", "fsdp", None),
            P("section", "fsdp", None),
            P("section", None, "fsdp"),
            P("section", None, "fsdp"),
            P("section", "fsdp"),
        ),
        check_vma=False,
    )
```

```python
import functools
import math

import jax
import jax.numpy as jnp
from jax import lax
from jax.experimental import pallas as pl
from jax.experimental.pallas import tpu as pltpu
from jax.sharding import PartitionSpec as P

D = 1088
HD = 64
F32 = jnp.float32
BF = jnp.bfloat16
SCALE = 1.0 / math.sqrt(HD)
WIDE = 1152
MESH = pl.DeviceIdType.MESH
SWAP = [(0, 1), (1, 0)]


def mm(a, b):
    return jnp.dot(a, b, preferred_element_type=F32)


def mm_nt(a, b):
    return lax.dot_general(a, b, (((1,), (1,)), ((), ())), preferred_element_type=F32)


def mm_tn(a, b):
    return lax.dot_general(a, b, (((0,), (0,)), ((), ())), preferred_element_type=F32)


def norm_parts(values):
    center = jnp.mean(values, axis=-1, keepdims=True)
    offset = values - center
    spread = jnp.mean(offset * offset, axis=-1, keepdims=True)
    inv = lax.rsqrt(spread + 1e-05)
    return offset * inv, inv


def norm_back(grad, gain, unit, inv):
    dn = grad * gain
    return inv * (
        dn
        - jnp.mean(dn, axis=-1, keepdims=True)
        - unit * jnp.mean(dn * unit, axis=-1, keepdims=True)
    )


def phi_parts(z):
    cdf = 0.5 * (1.0 + lax.erf(z * (1.0 / math.sqrt(2.0))))
    pdf = jnp.exp(-0.5 * z * z) * (1.0 / math.sqrt(2.0 * math.pi))
    return cdf, pdf


def plane_neighbours():
    f = lax.axis_index("fsdp")
    x = lax.rem(f, 2)
    y = f // 2
    return y * 2 + (1 - x), (1 - y) * 2 + x


def plane_barrier(xn, yn):
    barrier = pltpu.get_barrier_semaphore()
    for nb in (xn, yn):
        pl.semaphore_signal(barrier, inc=1, device_id={"fsdp": nb}, device_id_type=MESH)
    pl.semaphore_wait(barrier, 2)


def remote(src, dst, send, recv, nb):
    return pltpu.make_async_remote_copy(
        src_ref=src, dst_ref=dst, send_sem=send, recv_sem=recv,
        device_id={"fsdp": nb}, device_id_type=MESH,
    )


def load_layer(sources, targets, sems):
    copies = [
        pltpu.make_async_copy(source, target, sems.at[i])
        for i, (source, target) in enumerate(zip(sources, targets))
    ]
    for copy in copies:
        copy.start()
    return copies


def exchange_rows(own_ref, all_ref, parts, compute, finish, bufs, send, recv, loads):
    x1, y1, x2, y2, sum_x, sum_y = bufs
    xn, yn = plane_neighbours()
    half = own_ref.shape[0] // 2
    top, low = pl.ds(0, half), pl.ds(half, half)
    plane_barrier(xn, yn)

    to_x = remote(own_ref, all_ref.at[1], send.at[0], recv.at[0], xn)
    to_y = remote(own_ref, all_ref.at[2], send.at[1], recv.at[1], yn)
    far_x = remote(all_ref.at[2, top], all_ref.at[3, top], send.at[2], recv.at[2], xn)
    far_y = remote(all_ref.at[1, low], all_ref.at[3, low], send.at[3], recv.at[3], yn)
    first_x = remote(parts.at[3, top], x1, send.at[4], recv.at[4], xn)
    first_y = remote(parts.at[3, low], y1, send.at[5], recv.at[5], yn)
    own_x = remote(parts.at[1, top], x2.at[top], send.at[6], recv.at[6], xn)
    own_y = remote(parts.at[2, low], y2.at[low], send.at[7], recv.at[7], yn)
    rest_x = remote(sum_x, x2.at[low], send.at[8], recv.at[8], xn)
    rest_y = remote(sum_y, y2.at[top], send.at[9], recv.at[9], yn)

    to_x.start()
    to_y.start()
    all_ref[0] = own_ref[...]
    for copy in loads:
        copy.wait()

    @pl.loop(0, 4)
    def _(i):
        @pl.when(i == 1)
        def _():
            to_x.wait_recv()
            far_y.start()
            to_y.wait_recv()
            far_x.start()

        @pl.when(i == 2)
        def _():
            own_x.start()
            far_x.wait_recv()
            far_y.wait_recv()

        @pl.when(i == 3)
        def _():
            first_x.start()
            first_y.start()

        compute(i + (i // 2) * (1 - 2 * lax.rem(i, 2)))

    own_y.start()
    first_x.wait_recv()
    sum_y[...] = (parts[2, top, :].astype(F32) + x1[...].astype(F32)).astype(BF)
    rest_y.start()
    first_y.wait_recv()
    sum_x[...] = (parts[1, low, :].astype(F32) + y1[...].astype(F32)).astype(BF)
    rest_x.start()
    own_x.wait_recv()
    rest_y.wait_recv()
    finish(top, parts[0, top, :].astype(F32) + x2[top, :].astype(F32) + y2[top, :].astype(F32))
    own_y.wait_recv()
    rest_x.wait_recv()
    finish(low, parts[0, low, :].astype(F32) + x2[low, :].astype(F32) + y2[low, :].astype(F32))
    for copy in (to_x, to_y, far_x, far_y, first_x, first_y, own_x, own_y, rest_x, rest_y):
        copy.wait_send()


def forward_kernel(
    layer, own, up_here, down_both, bias, resid, par, out, all_ref, active, slope,
    up, down, load, parts, x1, y1, x2, y2, sx, sy, send, recv,
):
    loads = load_layer((up_here, down_both.at[layer]), (up, down), load)

    def finish(at, value):
        out[at, :] = (resid[at, :] + value + par[7:8, :]).astype(BF)

    def compute(r):
        slope[r] = mm(all_ref[r], up[...]) + bias[...]

        @pl.loop(0, own.shape[0] // 64)
        def _(j):
            at = pl.ds(pl.multiple_of(j * 64, 64), 64)
            z = slope[r, at, :]
            cdf, pdf = phi_parts(z)
            active[r, at, :] = (z * cdf).astype(BF)
            slope[r, at, :] = cdf + z * pdf

        parts[r] = mm(active[r], down[...]).astype(BF)

    exchange_rows(own, all_ref, parts, compute, finish, (x1, y1, x2, y2, sx, sy), send, recv, loads)


def backward_kernel(
    layer, own, up_here, down_both, slope, total, all_ref, dz_all, bias_g,
    up, down, load, parts, x1, y1, x2, y2, sx, sy, send, recv,
):
    loads = load_layer((up_here, down_both.at[layer]), (up, down), load)
    bias_g[...] = jnp.zeros_like(bias_g)

    def finish(at, value):
        total[at, :] = value

    def compute(r):
        dz = mm_nt(all_ref[r], down[...]) * slope[r]
        bias_g[...] += jnp.sum(dz, axis=0, keepdims=True)
        dz_all[r] = dz.astype(BF)
        parts[r] = mm_nt(dz_all[r], up[...]).astype(BF)

    exchange_rows(own, all_ref, parts, compute, finish, (x1, y1, x2, y2, sx, sy), send, recv, loads)


VSPEC = pl.BlockSpec(memory_space=pltpu.VMEM)


def lasting(micros):
    return pl.CostEstimate(flops=0, transcendentals=0, bytes_accessed=int(micros * 3.5e6))


def plane_call(kernel, ident, outs, rows, *operands):
    half = rows // 2
    any_spec = pl.BlockSpec(memory_space=pl.ANY)
    return pl.pallas_call(
        kernel,
        out_shape=outs,
        in_specs=[VSPEC, any_spec, any_spec] + [VSPEC] * (len(operands) - 3),
        out_specs=(VSPEC,) * len(outs),
        scratch_shapes=[
            pltpu.VMEM((D, D), BF),
            pltpu.VMEM((D, D), BF),
            pltpu.SemaphoreType.DMA((2,)),
            pltpu.VMEM((4, rows, D), BF),
            pltpu.VMEM((half, D), BF),
            pltpu.VMEM((half, D), BF),
            pltpu.VMEM((rows, D), BF),
            pltpu.VMEM((rows, D), BF),
            pltpu.VMEM((half, D), BF),
            pltpu.VMEM((half, D), BF),
            pltpu.SemaphoreType.DMA((10,)),
            pltpu.SemaphoreType.DMA((10,)),
        ],
        compiler_params=pltpu.CompilerParams(
            collective_id=ident, has_side_effects=True, vmem_limit_bytes=56 * 1024 * 1024
        ),
        cost_estimate=lasting(40),
    )(*operands)


def mlp_forward(own, up, down, layer, bias, resid, par):
    rows = own.shape[0]
    if lax.axis_size("fsdp") != 4:
        every = lax.all_gather(own, "fsdp", axis=0, tiled=True)
        down = down[layer]
        z = mm(every, up) + bias
        cdf, pdf = phi_parts(z)
        active = (z * cdf).astype(BF)
        part = mm(active, down).astype(BF)
        total = lax.psum_scatter(part, "fsdp", scatter_dimension=0, tiled=True).astype(F32)
        out = (resid + total + par[7]).astype(BF)
        return out, every, active, cdf + z * pdf
    shape = (4, rows, D)
    return plane_call(
        functools.partial(forward_kernel, layer), 1 + 6 * layer,
        (
            jax.ShapeDtypeStruct((rows, D), BF),
            jax.ShapeDtypeStruct(shape, BF),
            jax.ShapeDtypeStruct(shape, BF),
            jax.ShapeDtypeStruct(shape, F32),
        ),
        rows, own, up, down, bias, resid, par,
    )


def mlp_backward(own, up, down, layer, slope):
    rows = own.shape[0]
    if lax.axis_size("fsdp") != 4:
        every = lax.all_gather(own, "fsdp", axis=0, tiled=True)
        down = down[layer]
        dz = mm_nt(every, down) * slope
        dz_b = dz.astype(BF)
        part = mm_nt(dz_b, up).astype(BF)
        total = lax.psum_scatter(part, "fsdp", scatter_dimension=0, tiled=True).astype(F32)
        return total, every, dz_b, jnp.sum(dz, axis=0, keepdims=True)
    shape = (4, rows, D)
    return plane_call(
        functools.partial(backward_kernel, layer), 2 + 6 * layer,
        (
            jax.ShapeDtypeStruct((rows, D), F32),
            jax.ShapeDtypeStruct(shape, BF),
            jax.ShapeDtypeStruct(shape, BF),
            jax.ShapeDtypeStruct((1, D), F32),
        ),
        rows, own, up, down, slope,
    )


def spread_up(core, blocks, full, load, u_send, u_recv, v_send, v_recv):
    s = lax.axis_index("section")
    f = lax.axis_index("fsdp")
    xn, yn = plane_neighbours()
    others = (xn, yn, 3 - f)
    shard = blocks.shape[1]

    def rows_of(owner):
        return full.at[pl.ds(pl.multiple_of(owner * shard, 16), shard)]

    def to(src, dst, send, recv, **where):
        return pltpu.make_async_remote_copy(
            src_ref=src, dst_ref=dst, send_sem=send, recv_sem=recv,
            device_id=where, device_id_type=MESH,
        )

    def chip(i):
        return to(blocks.at[others[i]], rows_of(f), u_send.at[i], u_recv.at[i], fsdp=others[i])

    def over(i):
        rows = rows_of((*others, f)[i])
        return to(rows, rows, v_send.at[i], v_recv.at[i], section=1 - core)

    near = pltpu.make_async_copy(blocks.at[f], rows_of(f), load)

    def first():
        @pl.when(s == core)
        def _():
            near.start()
            for i in range(3):
                chip(i).start()
            near.wait()
            over(3).start()

    def then():
        @pl.when(s == core)
        def _():
            for i in range(3):
                chip(i).wait_recv()
                over(i).start()

    def last():
        @pl.when(s == core)
        def _():
            for i in range(3):
                chip(i).wait_send()
            for i in range(4):
                over(i).wait_send()

        @pl.when(s == 1 - core)
        def _():
            for i in range(4):
                over(i).wait_recv()

    return first, then, last


def spread_sems():
    return [pltpu.SemaphoreType.DMA((n,)) for n in (3, 3, 4, 4)]


def weights_kernel(
    qkv_in, out_in, gains, biases, hidden, rows_in, up_in, down_in,
    full, rows_out, up_out, up_blocks, down_out, next_half,
    own, other_half, load, core_s, core_r, p_send, p_recv, f_send, f_recv, z_send, z_recv,
    u_send, u_recv, v_send, v_recv,
):
    s = lax.axis_index("section")
    f = lax.axis_index("fsdp")
    xn, yn = plane_neighbours()
    dn = 3 - f
    shard, wide = own.shape[1], own.shape[2]
    cut = 640
    left = pl.ds(0, cut)
    right = pl.ds(cut, wide - cut)

    def to(src, dst, send, recv, **where):
        return pltpu.make_async_remote_copy(
            src_ref=src, dst_ref=dst, send_sem=send, recv_sem=recv,
            device_id=where, device_id_type=MESH,
        )

    pad = jnp.zeros((shard, wide - D), BF)
    for p in range(3):
        own[p] = jnp.concatenate([qkv_in[:, pl.ds(p * D, D)], pad], axis=1)
    unit_rows = (
        lax.broadcasted_iota(jnp.int32, (16, 64), 0) == lax.broadcasted_iota(jnp.int32, (16, 64), 1)
    ).astype(F32)
    hidden_rows = [hidden[:, pl.ds(i * shard, shard)] for i in range(hidden.shape[1] // shard)]
    small = jnp.concatenate(
        [
            value.astype(F32)
            for value in (gains[...], biases[...], *hidden_rows, jnp.zeros((8 - len(hidden_rows), shard)))
        ],
        axis=0,
    )
    beside = mm_tn(small.astype(BF), unit_rows.astype(BF)).astype(BF)
    own[3] = jnp.concatenate([out_in[...], beside], axis=1)

    barrier = pltpu.get_barrier_semaphore()
    z = lax.axis_index("ctx")
    above = {"ctx": lax.rem(z + 1, 4)}
    below = {"ctx": lax.rem(z + 3, 4)}
    partners = ({"section": 1 - s}, {"fsdp": xn}, {"fsdp": yn}, {"fsdp": dn}, above, below)
    for where in partners:
        pl.semaphore_signal(barrier, inc=1, device_id=where, device_id_type=MESH)
    pl.semaphore_wait(barrier, 6)
    rows = rows_in.shape[0]
    near_rows, far_rows = pl.ds(rows, rows), pl.ds(0, rows)
    step_one = to(rows_in, rows_out.at[near_rows], z_send.at[0], z_recv.at[0], **above)
    step_two = to(
        rows_out.at[near_rows], rows_out.at[far_rows], z_send.at[1], z_recv.at[1], **above
    )

    @pl.when(z < 3)
    def _():
        step_one.start()

    rows_out[pl.ds(2 * rows, rows), :] = rows_in[...]

    @pl.when(z == 0)
    def _():
        rows_out[near_rows, :] = jnp.zeros(rows_in.shape, BF)

    @pl.when(z < 2)
    def _():
        rows_out[far_rows, :] = jnp.zeros(rows_in.shape, BF)

    def blk(owner):
        return pl.ds(pl.multiple_of(owner * shard, 16), shard)

    def give(p):
        return to(own.at[p], full.at[p, blk(f)], core_s.at[p], core_r.at[p], section=1)

    def keep(p):
        return pltpu.make_async_copy(own.at[p], full.at[p, blk(f)], load.at[p])

    @pl.when(s == 0)
    def _():
        for p in (2, 3, 0, 1):
            give(p).start()
        for p in range(4):
            keep(p).start()
        keep(0).wait()
        keep(1).wait()

    @pl.when(s == 1)
    def _():
        give(2).wait_recv()
        give(3).wait_recv()

    def same(piece, rows, send, recv, cols=slice(None), **where):
        ref = full.at[piece, rows, cols]
        return to(ref, ref, send, recv, **where)

    def hops(k):
        p = 2 * s + k
        return (
            same(p, blk(f), p_send.at[k, 0], p_recv.at[k, 0], fsdp=xn),
            same(p, blk(f), p_send.at[k, 1], p_recv.at[k, 1], fsdp=yn),
            same(p, blk(yn), p_send.at[k, 2], p_recv.at[k, 2], left, fsdp=xn),
            same(p, blk(xn), p_send.at[k, 3], p_recv.at[k, 3], right, fsdp=yn),
        )

    def here(k):
        p = 2 * s + k
        return [
            same(p, blk(owner), f_send.at[k, i], f_recv.at[k, i], section=1 - s)
            for i, owner in enumerate((xn, yn, dn))
        ]

    for k in range(2):
        copies = hops(k)
        copies[0].start()
        copies[1].start()
    down_far = to(down_in, down_out.at[s], core_s.at[4], core_r.at[4], section=1 - s)
    down_near = pltpu.make_async_copy(down_in, down_out.at[s], load.at[4])
    down_far.start()
    down_near.start()
    swap = to(other_half, next_half, core_s.at[5], core_r.at[5], section=0)

    @pl.when(s == 1)
    def _():
        for p in range(4):
            at = pl.ds(p * wide, wide)
            other_half[:, at] = own[p, pl.ds(0, shard // 2), :]
            next_half[:, at] = own[p, pl.ds(shard // 2, shard // 2), :]
        swap.start()

    for j in range(4):
        up_blocks[j] = up_in[:, pl.ds(j * D, D)]

    up_first, up_then, up_last = spread_up(
        0, up_blocks, up_out, load.at[5], u_send, u_recv, v_send, v_recv
    )
    up_first()
    for k in range(2):
        copies, across = hops(k), here(k)
        copies[0].wait_recv()
        copies[3].start()
        across[0].start()
        copies[1].wait_recv()
        copies[2].start()
        across[1].start()

    @pl.when(z > 0)
    def _():
        step_one.wait_recv()

    @pl.when((z == 1) | (z == 2))
    def _():
        step_two.start()

    for k in range(2):
        copies, across = hops(k), here(k)
        copies[2].wait_recv()
        copies[3].wait_recv()
        across[2].start()
    up_then()
    for k in range(2):
        for copy in here(k):
            copy.wait()
        for copy in hops(k):
            copy.wait_send()
    up_last()

    @pl.when(s == 0)
    def _():
        for p in range(4):
            give(p).wait_send()
        keep(2).wait()
        keep(3).wait()

    @pl.when(s == 1)
    def _():
        give(0).wait_recv()
        give(1).wait_recv()

    down_near.wait()
    down_far.wait()
    pl.when(s == 0)(swap.wait_recv)
    pl.when(s == 1)(swap.wait_send)

    @pl.when(z < 3)
    def _():
        step_one.wait_send()

    @pl.when((z == 1) | (z == 2))
    def _():
        step_two.wait_send()

    @pl.when(z > 1)
    def _():
        step_two.wait_recv()


def first_weights(qkv, out, gains, biases, hidden, rows_in, up, down):
    dma = pltpu.SemaphoreType.DMA
    shard = qkv.shape[0]
    shapes = (
        (4, D, WIDE), (3 * rows_in.shape[0], D), (D, D), (4, shard, D), (2, D, D), (shard // 2, 4 * WIDE)
    )
    return pl.pallas_call(
        weights_kernel,
        out_shape=tuple(jax.ShapeDtypeStruct(shape, BF) for shape in shapes),
        in_specs=[VSPEC] * 7 + [pl.BlockSpec(memory_space=pl.ANY)],
        out_specs=(VSPEC,) * 6,
        scratch_shapes=[
            pltpu.VMEM((4, shard, WIDE), BF),
            pltpu.VMEM((shard // 2, 4 * WIDE), BF),
            dma((6,)), dma((6,)), dma((6,)), dma((2, 4)), dma((2, 4)), dma((2, 3)), dma((2, 3)),
            dma((2,)), dma((2,)), *spread_sems(),
        ],
        compiler_params=pltpu.CompilerParams(
            collective_id=4, has_side_effects=True, vmem_limit_bytes=58 * 1024 * 1024
        ),
        cost_estimate=lasting(75),
        name="first_weights",
    )(qkv, out, gains, biases, hidden, rows_in, up, down)


def z_partners():
    z = lax.axis_index("ctx")
    return z + 1 - 2 * lax.rem(z, 2), 3 - z, (z == 1) | (z == 2)


def add_rows(dst, one, two, rows, step):
    @pl.loop(0, rows // step)
    def _(i):
        at = pl.ds(pl.multiple_of(i * step, 16), step)
        dst[at, :] = (one[at, :].astype(F32) + two[at, :].astype(F32)).astype(dst.dtype)


CUTS = ((0, 640, 384), (640, 512, 256))


def reduce_kernel(
    q0, k0, v0, o0, q1, k1, v1, o1, mlp, made0, made1, grad1, halo, d_resid, da_own, wide, par,
    qkv_out, out_out, down_out, up_out, made_out, grad_out,
    own_in, held, up_own, up_far, sent, caught, grad0,
    x1a, y1a, x2a, y2a, sxa, sya, ta, zaa, zba,
    x1b, y1b, x2b, y2b, sxb, syb, tb, zab, zbb,
    load, core_s, core_r, p_send, p_recv, z_send, z_recv, h_send, h_recv, x_send, x_recv,
):
    s = lax.axis_index("section")
    f = lax.axis_index("fsdp")
    xn, yn = plane_neighbours()
    dn = 3 - f
    side, across, inner = z_partners()
    pieces = ((q0, k0, v0, o0), (q1, k1, v1, o1))
    sets = (
        (x1a, y1a, x2a, y2a, sxa, sya, ta, zaa, zba),
        (x1b, y1b, x2b, y2b, sxb, syb, tb, zab, zbb),
    )
    shard = out_out.shape[0]
    rows = da_own.shape[0]
    z = lax.axis_index("ctx")
    above, below = {"ctx": lax.rem(z + 1, 4)}, {"ctx": lax.rem(z + 3, 4)}

    def to(src, dst, send, recv, **where):
        return pltpu.make_async_remote_copy(
            src_ref=src, dst_ref=dst, send_sem=send, recv_sem=recv,
            device_id=where, device_id_type=MESH,
        )

    barrier = pltpu.get_barrier_semaphore()
    partners = ({"section": 1 - s}, {"fsdp": xn}, {"fsdp": yn}, above, below)
    for where in partners:
        pl.semaphore_signal(barrier, inc=1, device_id=where, device_id_type=MESH)
    pl.semaphore_wait(barrier, 5)

    def blk(owner):
        return pl.ds(pl.multiple_of(owner * shard, 16), shard)

    def by_core(act):
        for core in range(2):
            pl.when(s == core)(functools.partial(act, core))

    def far(j, src):
        return to(src, held.at[j], core_s.at[j], core_r.at[j], section=1 - s)

    def near(j, src):
        return pltpu.make_async_copy(src, own_in.at[j % 2], load.at[j])

    def bufs(c):
        return tuple(ref.at[c // 2] for ref in sets[c % 2])

    def plane(c):
        x1, y1, x2, y2, sx, sy = bufs(c)[:6]
        own = held.at[c // 2]
        at, width, cut = CUTS[c % 2]
        left, right = pl.ds(at, cut), pl.ds(at + cut, width - cut)
        to_left, to_right = pl.ds(0, cut), pl.ds(cut, width - cut)
        sems = [(p_send.at[c, i], p_recv.at[c, i]) for i in range(6)]
        return (
            to(own.at[blk(dn), left], x1, *sems[0], fsdp=xn),
            to(own.at[blk(dn), right], y1, *sems[1], fsdp=yn),
            to(own.at[blk(xn), left], x2.at[:, to_left], *sems[2], fsdp=xn),
            to(own.at[blk(yn), right], y2.at[:, to_right], *sems[3], fsdp=yn),
            to(sx, x2.at[:, to_right], *sems[4], fsdp=xn),
            to(sy, y2.at[:, to_left], *sems[5], fsdp=yn),
        )

    def along(c):
        t, za, zb = bufs(c)[6:]
        sems = [(z_send.at[c, i], z_recv.at[c, i]) for i in range(3)]
        return (
            to(t, za, *sems[0], ctx=side),
            to(za, zb, *sems[1], ctx=across),
            to(zb, zb, *sems[2], ctx=side),
        )

    def join(j):
        far(j, q0).wait_recv()
        near(j, q0).wait()
        add_rows(held.at[j], own_in.at[j % 2], held.at[j], 4 * shard, 64)
        for c in (2 * j, 2 * j + 1):
            for copy in plane(c)[:4]:
                copy.start()
        if j < 2:
            by_core(lambda core: near(j + 2, pieces[core][j + 2]).start())

    def second(c):
        copies = plane(c)
        x1, y1, _, _, sx, sy = bufs(c)[:6]
        at, width, cut = CUTS[c % 2]
        own = held.at[c // 2]
        copies[0].wait_recv()
        add_rows(sy, own.at[blk(yn), pl.ds(at, cut)], x1, shard, 16)
        copies[5].start()
        copies[1].wait_recv()
        add_rows(sx, own.at[blk(xn), pl.ds(at + cut, width - cut)], y1, shard, 16)
        copies[4].start()

    def third(c):
        copies = plane(c)
        _, _, x2, y2, _, _, t, _, _ = bufs(c)
        at, width, _ = CUTS[c % 2]
        for copy in copies[2:]:
            copy.wait_recv()
        own = held.at[c // 2, blk(f), pl.ds(at, width)]

        @pl.loop(0, shard // 16)
        def _(i):
            part = pl.ds(pl.multiple_of(i * 16, 16), 16)
            t[part, :] = (
                own[part, :].astype(F32) + x2[part, :].astype(F32) + y2[part, :].astype(F32)
            ).astype(BF)

        @pl.when(jnp.logical_not(inner))
        def _():
            along(c)[0].start()

    def inward(c):
        @pl.when(inner)
        def _():
            t, za, _ = bufs(c)[6:]
            copies = along(c)
            copies[0].wait_recv()
            add_rows(za, t, za, shard, 16)
            copies[1].start()

    def crossed(c):
        @pl.when(inner)
        def _():
            _, za, zb = bufs(c)[6:]
            copies = along(c)
            copies[1].wait_recv()
            add_rows(zb, za, zb, shard, 16)
            copies[2].start()

    def last(c):
        at, width, _ = CUTS[c % 2]
        j = c // 2

        @pl.when(jnp.logical_not(inner))
        def _():
            along(c)[2].wait_recv()

        done = bufs(c)[8]
        keep = min(width, D - at) if j < 3 else width

        @pl.loop(0, shard // 16)
        def _(i):
            part = pl.ds(pl.multiple_of(i * 16, 16), 16)
            if j < 3:
                qkv_out[part, pl.ds(j * D + at, keep)] = done[part, pl.ds(0, keep)]
            else:
                out_out[part, pl.ds(at, keep)] = done[part, :]

    half = down_out.shape[0] // 2
    mine = pl.ds(pl.multiple_of(s * half, 16), half)
    down_far = to(mlp.at[0], down_out.at[mine], core_s.at[4], core_r.at[4], section=1 - s)
    down_near = pltpu.make_async_copy(mlp.at[0], down_out.at[mine], load.at[4])
    far_up = to(mlp.at[1], up_far, core_s.at[5], core_r.at[5], section=1 - s)
    near_up = pltpu.make_async_copy(mlp.at[1], up_own, load.at[5])

    def lay_up():
        far_up.wait_recv()
        near_up.wait()

        @pl.when(s == 1)
        def _():
            for k in range(4):
                at = pl.ds(k * (shard // 2), shard // 2)
                up_out[:, pl.ds(k * D, D)] = jnp.concatenate([up_far[at, :], up_own[at, :]], axis=0)

    back_one = to(halo.at[pl.ds(0, rows)], caught.at[0], h_send.at[0], h_recv.at[0], **below)
    back_two = to(sent, caught.at[1], h_send.at[1], h_recv.at[1], **below)

    def back():
        @pl.when(z < 3)
        def _():
            back_one.wait_recv()

        @pl.when(z == 3)
        def _():
            caught[0] = jnp.zeros_like(caught[0])

        @pl.when(z > 0)
        def _():
            add_rows(sent, halo.at[pl.ds(rows, rows)], caught.at[0], rows, 64)
            back_two.start()

    made_far = (
        to(made1, made_out.at[0], x_send.at[0], x_recv.at[0], section=1),
        to(made0, made_out.at[1], x_send.at[0], x_recv.at[0], section=0),
    )
    grad_far = (
        to(grad1, grad_out.at[0], x_send.at[1], x_recv.at[1], section=1),
        to(grad0, grad_out.at[1], x_send.at[1], x_recv.at[1], section=0),
    )
    made_near = (
        pltpu.make_async_copy(made0, made_out.at[0], load.at[6]),
        pltpu.make_async_copy(made1, made_out.at[1], load.at[6]),
    )
    grad_near = pltpu.make_async_copy(grad1, grad_out.at[1], load.at[7])

    def back_end():
        @pl.when(z < 3)
        def _():
            back_two.wait_recv()

        @pl.when(z == 3)
        def _():
            caught[1] = jnp.zeros_like(caught[1])

        unit, inv = norm_parts(wide[...].astype(F32))
        da = da_own[...] + caught[1].astype(F32)
        grad0[...] = d_resid[...] + norm_back(da, par[0:1, :], unit, inv)

        @pl.when(s == 0)
        def _():
            grad_out[0] = grad0[...]

        @pl.when(s == 1)
        def _():
            grad_far[1].start()

    @pl.when(s == 0)
    def _():
        made_far[0].start()
        grad_far[0].start()
        made_near[0].start()

    @pl.when(s == 1)
    def _():
        made_far[1].start()
        made_near[1].start()
        grad_near.start()

    @pl.when(z > 0)
    def _():
        back_one.start()

    for j in range(4):
        by_core(lambda core: far(j, pieces[1 - core][j]).start())
        if j < 2:
            by_core(lambda core: near(j, pieces[core][j]).start())
    for copy in (down_far, down_near, far_up, near_up):
        copy.start()

    join(0)
    for c in range(12):
        if c in (1, 3, 5):
            join((c + 1) // 2)
        if c < 8:
            second(c)
        if 1 <= c <= 8:
            third(c - 1)
        if 2 <= c <= 9:
            inward(c - 2)
        if 3 <= c <= 10:
            crossed(c - 3)
        if c >= 4:
            last(c - 4)
        if c == 2:
            back()
        if c == 4:
            lay_up()
        if c == 6:
            back_end()

    down_near.wait()
    down_far.wait()
    far_up.wait_send()

    @pl.when(s == 0)
    def _():
        made_near[0].wait()
        made_far[0].wait_send()
        grad_far[0].wait_send()
        made_far[1].wait_recv()
        grad_far[1].wait_recv()

    @pl.when(s == 1)
    def _():
        made_near[1].wait()
        grad_near.wait()
        made_far[1].wait_send()
        grad_far[1].wait_send()
        made_far[0].wait_recv()
        grad_far[0].wait_recv()

    @pl.when(z > 0)
    def _():
        back_one.wait_send()
        back_two.wait_send()

    for j in range(4):
        far(j, q0).wait_send()
    for c in range(8):
        for copy in plane(c):
            copy.wait_send()

    @pl.when(inner)
    def _():
        for c in range(8):
            for copy in along(c)[1:]:
                copy.wait_send()

    @pl.when(jnp.logical_not(inner))
    def _():
        for c in range(8):
            along(c)[0].wait_send()


def reduce_both(zero, one, mlp, made, grad1, halo, d_resid, da_own, wide, par):
    shard = D // 4
    rows = da_own.shape[0]
    dma = pltpu.SemaphoreType.DMA
    any_spec = pl.BlockSpec(memory_space=pl.ANY)

    def buf(*shape):
        return pltpu.VMEM(shape, BF)

    def part(_, width, cut):
        wide_buf = buf(4, shard, width)
        return [
            buf(4, shard, cut), buf(4, shard, width - cut), wide_buf, wide_buf,
            buf(4, shard, width - cut), buf(4, shard, cut), wide_buf, wide_buf, wide_buf,
        ]

    shapes = ((shard, 3 * D), (shard, WIDE), (D, D), (shard, 4 * D), (2, rows, D))
    return pl.pallas_call(
        reduce_kernel,
        out_shape=(
            *(jax.ShapeDtypeStruct(shape, BF) for shape in shapes),
            jax.ShapeDtypeStruct((2, rows, D), F32),
        ),
        in_specs=[any_spec] * 12 + [VSPEC] * 5,
        out_specs=(VSPEC,) * 6,
        scratch_shapes=[
            buf(2, D, WIDE), buf(4, D, WIDE), buf(D // 2, D), buf(D // 2, D), buf(rows, D),
            buf(2, rows, D), pltpu.VMEM((rows, D), F32), *part(*CUTS[0]), *part(*CUTS[1]),
            dma((8,)), dma((6,)), dma((6,)), dma((8, 6)), dma((8, 6)), dma((8, 3)), dma((8, 3)),
            dma((2,)), dma((2,)), dma((2,)), dma((2,)),
        ],
        compiler_params=pltpu.CompilerParams(
            collective_id=3, has_side_effects=True, vmem_limit_bytes=60 * 1024 * 1024
        ),
        cost_estimate=lasting(120),
        name="reduce_both",
    )(*zero, *one, mlp, *made, grad1, halo, d_resid, da_own, wide, par)


def final_kernel(
    qkv, out, mine, far, down_one, up_one, made, grads,
    qkv_f, out_f, down_f, up_f, small, made_out, grads_out,
):
    s = lax.axis_index("section")
    half = mine.shape[1]
    shard = qkv.shape[0]
    pick_row = (
        lax.broadcasted_iota(jnp.int32, (16, 128), 1)
        == lax.broadcasted_iota(jnp.int32, (16, 128), 0) + (D - TAIL)
    )
    small[...] = mm_nt(pick_row.astype(F32).astype(BF), out[:, pl.ds(TAIL, 128)])

    @pl.loop(0, made.shape[1] // 16)
    def _(i):
        at = pl.ds(pl.multiple_of(i * 16, 16), 16)
        for m in range(2):
            made_out[m, at, :] = made[m, at, :]
            grads_out[m, at, :] = grads[m, at, :]

    @pl.loop(0, shard // 16)
    def _(i):
        at = pl.ds(pl.multiple_of(i * 16, 16), 16)
        qkv_f[at, :] = qkv[at, :].astype(F32)
        out_f[at, :] = out[at, pl.ds(0, D)].astype(F32)

        @pl.when(s == 1)
        def _():
            up_f[at, :] = up_one[at, :].astype(F32)

    @pl.when(s == 0)
    def _():
        for k in range(4):
            at = pl.ds(k * (shard // 2), shard // 2)
            rows_k = jnp.concatenate([mine[1, at, :], far[1, at, :]], axis=0)
            up_f[:, pl.ds(k * D, D)] = rows_k.astype(F32)

    @pl.loop(0, half // 16)
    def _(i):
        at = pl.ds(pl.multiple_of(i * 16, 16), 16)
        after = pl.ds(pl.multiple_of(half + i * 16, 16), 16)

        @pl.when(s == 0)
        def _():
            down_f[at, :] = mine[0, at, :].astype(F32)
            down_f[after, :] = far[0, at, :].astype(F32)

        @pl.when(s == 1)
        def _():
            down_f[at, :] = down_one[at, :].astype(F32)
            down_f[after, :] = down_one[after, :].astype(F32)


def final_layouts(*values):
    qkv, _, _, _, down_one, up_one, made, grads = values
    shard = qkv.shape[0]
    outs = [(shape, F32) for shape in (qkv.shape, (shard, D), down_one.shape, up_one.shape)]
    outs += [((16, shard), F32), (made.shape, BF), (grads.shape, F32)]
    return pl.pallas_call(
        final_kernel,
        out_shape=tuple(jax.ShapeDtypeStruct(*out) for out in outs),
        in_specs=[VSPEC] * 8,
        out_specs=(VSPEC,) * 7,
        compiler_params=pltpu.CompilerParams(vmem_limit_bytes=58 * 1024 * 1024),
        cost_estimate=lasting(10),
        name="final_layouts",
    )(*values)


def core_half(values, axis):
    s = lax.axis_index("section")
    keep = lax.dynamic_index_in_dim(values, s, axis, keepdims=False)
    give = lax.dynamic_index_in_dim(values, 1 - s, axis, keepdims=False)
    return (keep.astype(F32) + on_chip(give).astype(F32)).astype(BF)


def halves_settle(zero, one, nf, shard):
    s = lax.axis_index("section")
    mine, far = pick(s, zero, one), on_chip(pick(s, one, zero))
    first, second = pick(s, mine, far).astype(F32), pick(s, far, mine).astype(F32)
    down = jnp.concatenate([first[0], second[0]], axis=0)
    up = jnp.concatenate([half[1].reshape(nf, shard // 2, -1) for half in (first, second)], axis=1)
    return down, up.transpose(1, 0, 2).reshape(shard, -1)


def reduce_plain(pieces):
    s = lax.axis_index("section")
    pair = ("fsdp", "section")
    a = jnp.stack([lax.psum_scatter(p, pair, scatter_dimension=0, tiled=True) for p in pieces])
    a = lax.psum(a, "ctx")
    far = on_chip(a)
    return jnp.concatenate([pick(s, a, far), pick(s, far, a)], axis=1)


def shift(value, steps):
    count = lax.axis_size("ctx")
    pairs = [(i, i + steps) for i in range(count) if 0 <= i + steps < count]
    return lax.ppermute(value, "ctx", pairs)


def with_halo(own, chunks):
    parts = [own]
    for _ in range(chunks):
        parts.append(shift(parts[-1], 1))
    return jnp.concatenate(parts[::-1], axis=0)


def return_halo(halo, chunks, rows):
    carried = None
    for far in range(chunks):
        mine = halo[far * rows : (far + 1) * rows]
        carried = mine if carried is None else mine + carried
        carried = shift(carried.astype(BF), -1).astype(F32)
    return carried


def pick(s, first, second):
    return jnp.where(s == 0, first, second)


def on_chip(value):
    return lax.ppermute(value, "section", SWAP)


def both_layers(own, s):
    other = on_chip(own)
    return pick(s, own, other), pick(s, other, own)


def flat(values):
    return values.reshape(-1, values.shape[-1])


def widen(values):
    return jnp.pad(values, ((0, 0), (0, WIDE - D)))


TAIL = 1024


def scores_forward(q, k, v, bias, lanes):
    outs = []
    for low in (True, False):
        one = jnp.where((lanes < HD) if low else (lanes >= HD), q, jnp.zeros_like(q))
        weight = jnp.exp(mm_nt(one, k) + bias)
        prob = weight * (1.0 / jnp.sum(weight, axis=-1, keepdims=True))
        outs.append(mm(prob.astype(BF), v))
    return jnp.where(lanes < HD, outs[0], outs[1]).astype(BF)


def scores_backward(q, k, v, grad, bias_t, lanes):
    dqs, dk, dv = [], 0.0, 0.0
    for low in (True, False):
        mine = (lanes < HD) if low else (lanes >= HD)
        one = jnp.where(mine, q, jnp.zeros_like(q))
        g = jnp.where(mine, grad, jnp.zeros_like(grad))
        weight = jnp.exp(mm_nt(k, one) + bias_t)
        prob = weight * (1.0 / jnp.sum(weight, axis=0, keepdims=True))
        d_prob = mm_nt(v, g)
        row = jnp.sum(prob * d_prob, axis=0, keepdims=True)
        d_score = (prob * (d_prob - row)).astype(BF)
        dqs.append(mm_tn(d_score, k))
        dk = dk + mm(d_score, one)
        dv = dv + mm(prob.astype(BF), g)
    dq = jnp.where(lanes < HD, dqs[0], dqs[1]) * SCALE
    return dq.astype(BF), dk.astype(BF), dv.astype(BF)


def lane_tile(i):
    return pl.ds(pl.multiple_of(i * 128, 128), 128)


def widened(row):
    return jnp.concatenate([row, jnp.zeros((row.shape[0], WIDE - D), row.dtype)], axis=1)


def ctx_ring(rows_in, landing, send, recv, partners=()):
    z = lax.axis_index("ctx")
    above = {"ctx": lax.rem(z + 1, 4)}
    below = {"ctx": lax.rem(z + 3, 4)}
    rows = rows_in.shape[0]
    near, far = pl.ds(rows, rows), pl.ds(0, rows)
    barrier = pltpu.get_barrier_semaphore()

    def on(src, dst, i):
        return pltpu.make_async_remote_copy(
            src_ref=src, dst_ref=dst, send_sem=send.at[i], recv_sem=recv.at[i],
            device_id=above, device_id_type=MESH,
        )

    one = on(rows_in, landing.at[near], 0)
    two = on(landing.at[near], landing.at[far], 1)

    def begin():
        for where in (above, below, *partners):
            pl.semaphore_signal(barrier, inc=1, device_id=where, device_id_type=MESH)
        pl.semaphore_wait(barrier, 2 + len(partners))

        @pl.when(z < 3)
        def _():
            one.start()

        landing[pl.ds(2 * rows, rows), :] = rows_in[...]

        @pl.when(z == 0)
        def _():
            landing[near, :] = jnp.zeros(rows_in.shape, BF)

        @pl.when(z < 2)
        def _():
            landing[far, :] = jnp.zeros(rows_in.shape, BF)

    def middle():
        @pl.when(z > 0)
        def _():
            one.wait_recv()

        @pl.when((z == 1) | (z == 2))
        def _():
            two.start()

    def end():
        @pl.when(z > 1)
        def _():
            two.wait_recv()

        @pl.when(z < 3)
        def _():
            one.wait_send()

        @pl.when((z == 1) | (z == 2))
        def _():
            two.wait_send()

    return begin, middle, end


def block_kernel(ring, first, wq, wk, wv, wo, bias, *rest):
    if ring:
        up_blocks, *rest = rest
    normed, q_ref, k_ref, v_ref, att, resid, second, par, *rest = rest
    rows = resid.shape[0]
    total = normed.shape[0]
    if ring:
        wide_out, up_out, held, wide, up_full, send, recv, load, *sems = rest
        s = lax.axis_index("section")
        f = lax.axis_index("fsdp")
        xn, yn = plane_neighbours()
        partners = ({"section": 1 - s}, {"fsdp": xn}, {"fsdp": yn}, {"fsdp": 3 - f})
        begin, middle, end = ctx_ring(first, wide, send, recv, partners)
        up_first, up_then, up_last = spread_up(1, up_blocks, up_full, load.at[0], *sems)
        begin()
        up_first()
    else:
        (held,), wide = rest, first
    pick_row = (
        lax.broadcasted_iota(jnp.int32, (16, 128), 1)
        == lax.broadcasted_iota(jnp.int32, (16, 128), 0) + (D - TAIL)
    )
    par[...] = mm_nt(pick_row.astype(F32).astype(BF), wo[:, pl.ds(TAIL, 128)])
    last = total // rows - 1

    @pl.loop(0, last + 1)
    def _(i):
        if ring:
            pl.when(i == 1)(middle)
            pl.when(i == 2)(up_then)
            pl.when(i == 2)(end)
        at = pl.ds(pl.multiple_of((last - i) * rows, 16), rows)
        unit, _ = norm_parts(wide[at, :].astype(F32))
        low = (unit * par[0:1, :] + par[2:3, :]).astype(BF)
        normed[at, :] = low
        k_ref[at, :] = mm(low, wk[...]).astype(BF)
        v_ref[at, :] = (mm(low, wv[...]) + widened(par[4:5, :])).astype(BF)

        @pl.when(i == 0)
        def _():
            q_ref[...] = (mm(normed[at, :], wq[...]) + widened(par[3:4, :])).astype(BF)

    own = pl.ds(total - rows, rows)
    lanes = lax.broadcasted_iota(jnp.int32, (rows, 128), 1)

    @pl.loop(0, WIDE // 128)
    def _(i):
        at = lane_tile(i)
        held[:, at] = scores_forward(
            q_ref[:, at] * jnp.asarray(SCALE, BF), k_ref[:, at], v_ref[:, at], bias[...], lanes
        )

    att[...] = held[:, pl.ds(0, D)]
    res = wide[own, :].astype(F32) + mm(att[...], wo[:, pl.ds(0, D)]) + par[5:6, :]
    resid[...] = res
    unit, _ = norm_parts(res)
    second[...] = (unit * par[1:2, :] + par[6:7, :]).astype(BF)
    if ring:
        wide_out[...] = wide[...]
        up_last()
        up_out[...] = up_full[...]


def weight_specs(weights):
    if weights.ndim == 3:
        return [pl.BlockSpec((None, D, WIDE), lambda i, p=p: (p, 0, 0)) for p in range(4)]
    return [pl.BlockSpec((D, WIDE), lambda i, p=p: (0, p)) for p in range(4)]


def whole(shape):
    return pl.BlockSpec(shape, lambda i: (0,) * len(shape))


def block_forward(first, weights, bias, up_blocks=None):
    rows, total = bias.shape
    outs = (
        ((total, D), BF), ((rows, WIDE), BF), ((total, WIDE), BF), ((total, WIDE), BF),
        ((rows, D), BF), ((rows, D), F32), ((rows, D), BF), ((16, D), F32),
    )
    scratch = [pltpu.VMEM((rows, WIDE), BF)]
    params, more = {}, ()
    if up_blocks is not None:
        outs += (((total, D), BF), ((D, D), BF))
        scratch += [pltpu.VMEM((total, D), BF), pltpu.VMEM((D, D), BF)]
        scratch += [pltpu.SemaphoreType.DMA((n,)) for n in (2, 2, 1)] + spread_sems()
        params, more = {"collective_id": 5, "has_side_effects": True}, (up_blocks,)
    return pl.pallas_call(
        functools.partial(block_kernel, bool(more)),
        out_shape=tuple(jax.ShapeDtypeStruct(*out) for out in outs),
        grid=(1,),
        in_specs=[
            whole(first.shape), *weight_specs(weights), whole(bias.shape),
            *(whole(value.shape) for value in more),
        ],
        out_specs=tuple(whole(shape) for shape, _ in outs),
        scratch_shapes=scratch,
        compiler_params=pltpu.CompilerParams(vmem_limit_bytes=62 * 1024 * 1024, **params),
        cost_estimate=lasting(45 if more else 22),
        name="block_forward",
    )(first, weights, weights, weights, weights, bias, *more)


def block_back_kernel(
    ring, d_second, up, resid, wide, q_ref, k_ref, v_ref, att, ffb_rows, wq, wk, wv, wo, par, bias_t,
    *rest,
):
    if ring:
        (d_in, d_low, dq_ref, dk_ref, dv_ref, left, right,
         held, sums, d_resid, da_own, da_halo, sent, caught, send, recv) = rest
    else:
        d_resid, dq_ref, dk_ref, dv_ref, da_own, da_halo, left, right, held, sums = rest
    rows = resid.shape[0]
    total = wide.shape[0]
    own = total - rows
    z = lax.axis_index("ctx")

    def back_to(src, dst, i):
        return pltpu.make_async_remote_copy(
            src_ref=src, dst_ref=dst, send_sem=send.at[i], recv_sem=recv.at[i],
            device_id={"ctx": lax.rem(z + 3, 4)}, device_id_type=MESH,
        )

    if ring:
        one = back_to(da_halo.at[pl.ds(0, rows)], caught.at[0], 0)
        two = back_to(sent, caught.at[1], 1)
        barrier = pltpu.get_barrier_semaphore()
        for step in (1, 3):
            pl.semaphore_signal(
                barrier, inc=1, device_id={"ctx": lax.rem(z + step, 4)}, device_id_type=MESH
            )
        pl.semaphore_wait(barrier, 2)

    def total_of(values):
        return jnp.sum(values, axis=0, keepdims=True)

    upstream = up[...].astype(F32)
    unit, inv = norm_parts(resid[...])
    grad = upstream + norm_back(d_second[...], par[1:2, :], unit, inv)
    d_resid[...] = grad
    sums[1:2, :] = total_of(d_second[...] * unit)
    sums[5:6, :] = total_of(grad)
    sums[6:7, :] = total_of(d_second[...])
    sums[7:8, :] = total_of(upstream)
    sums[8:16, :] = ffb_rows[...]
    low = grad.astype(BF)
    right[pl.ds(0, rows), :] = jnp.zeros((rows, WIDE), BF)
    right[pl.ds(0, rows), pl.ds(0, D)] = low
    right[pl.ds(rows, 16), :] = (
        lax.broadcasted_iota(jnp.int32, (16, WIDE), 1)
        == lax.broadcasted_iota(jnp.int32, (16, WIDE), 0) + D
    ).astype(F32).astype(BF)
    held[...] = jnp.zeros((rows, WIDE), BF)
    held[:, pl.ds(0, D)] = mm_nt(low, wo[:, pl.ds(0, D)]).astype(BF)
    lanes = lax.broadcasted_iota(jnp.int32, (rows, 128), 1)

    @pl.loop(0, WIDE // 128)
    def _(i):
        at = lane_tile(i)
        dq_ref[:, at], dk_ref[:, at], dv_ref[:, at] = scores_backward(
            q_ref[:, at] * jnp.asarray(SCALE, BF), k_ref[:, at], v_ref[:, at], held[:, at],
            bias_t[...], lanes,
        )

    sums[3:4, :] = total_of(dq_ref[...].astype(F32))[:, :D]
    sums[4:5, :] = total_of(dv_ref[...].astype(F32))[:, :D]
    sums[0:1, :] = jnp.zeros((1, D), F32)
    sums[2:3, :] = jnp.zeros((1, D), F32)

    def back(at):
        da = mm_nt(dk_ref[at, :], wk[...]) + mm_nt(dv_ref[at, :], wv[...])
        return da

    def count(da, at):
        unit, _ = norm_parts(wide[at, :].astype(F32))
        sums[0:1, :] += total_of(da * unit)
        sums[2:3, :] += total_of(da)

    @pl.loop(0, own // rows)
    def _(i):
        at = pl.ds(pl.multiple_of(i * rows, 16), rows)
        da = back(at)
        da_halo[at, :] = da.astype(BF)
        if ring:

            @pl.when((i == 0) & (z > 0))
            def _():
                one.start()

        count(da, at)

    at = pl.ds(own, rows)
    da = back(at) + mm_nt(dq_ref[...], wq[...])
    da_own[...] = da
    count(da, at)
    if ring:

        @pl.when(z < 3)
        def _():
            one.wait_recv()

        @pl.when(z == 3)
        def _():
            caught[0] = jnp.zeros_like(caught[0])

        @pl.when(z > 0)
        def _():
            add_rows(sent, da_halo.at[pl.ds(rows, rows)], caught.at[0], rows, 64)
            two.start()

    left[pl.ds(0, rows), :] = att[...]
    left[pl.ds(rows, 16), :] = sums[...].astype(BF)
    if ring:

        @pl.when(z < 3)
        def _():
            two.wait_recv()

        @pl.when(z == 3)
        def _():
            caught[1] = jnp.zeros_like(caught[1])

        @pl.loop(0, rows // 64)
        def _(i):
            part = pl.ds(pl.multiple_of(i * 64, 64), 64)
            behind = pl.ds(pl.multiple_of(own + i * 64, 64), 64)
            unit, inv = norm_parts(wide[behind, :].astype(F32))
            da = da_own[part, :] + caught[1, part, :].astype(F32)
            grad = d_resid[part, :] + norm_back(da, par[0:1, :], unit, inv)
            d_in[part, :] = grad
            d_low[part, :] = grad.astype(BF)

        @pl.when(z > 0)
        def _():
            one.wait_send()
            two.wait_send()


def block_backward(d_second, up, resid, wide, q, k, v, att, ffb_rows, weights, par, bias_t, ring):
    total, rows = wide.shape[0], resid.shape[0]
    f32_rows, low_rows = ((rows, D), F32), ((rows, D), BF)
    heads = (((rows, WIDE), BF), ((total, WIDE), BF), ((total, WIDE), BF))
    factors = (((rows + 16, D), BF), ((rows + 16, WIDE), BF))
    halo = ((total - rows, D), BF)
    held = [pltpu.VMEM((rows, WIDE), BF), pltpu.VMEM((16, D), F32)]
    params = {}
    if ring:
        outs = (f32_rows, low_rows, *heads, *factors)
        held += [pltpu.VMEM(*f32_rows), pltpu.VMEM(*f32_rows), pltpu.VMEM(*halo), pltpu.VMEM(*low_rows)]
        held += [pltpu.VMEM((2, rows, D), BF)] + [pltpu.SemaphoreType.DMA((2,))] * 2
        params = {"collective_id": 6, "has_side_effects": True}
    else:
        outs = (f32_rows, *heads, f32_rows, halo, *factors)
    before = (d_second, up, resid, wide, q, k, v, att, ffb_rows)
    return pl.pallas_call(
        functools.partial(block_back_kernel, ring),
        out_shape=tuple(jax.ShapeDtypeStruct(*out) for out in outs),
        grid=(1,),
        in_specs=[
            *(whole(value.shape) for value in before), *weight_specs(weights),
            whole(par.shape), whole(bias_t.shape),
        ],
        out_specs=tuple(whole(shape) for shape, _ in outs),
        scratch_shapes=held,
        compiler_params=pltpu.CompilerParams(vmem_limit_bytes=62 * 1024 * 1024, **params),
        cost_estimate=lasting(58 if ring else 38),
        name="block_backward",
    )(*before, weights, weights, weights, weights, par, bias_t)


def on_device(
    inputs, segments, cotangent, qkv_weight, out_weight, up_weight, down_weight,
    norm_gains, biases, ff_bias,
):
    rows = inputs.shape[2]
    length = segments.shape[2]
    chunks = min((length // 2 - 1 + rows - 1) // rows, lax.axis_size("ctx") - 1)
    reach = chunks * rows
    s = lax.axis_index("section")
    f = lax.axis_index("fsdp")
    nf = lax.axis_size("fsdp")
    shard = D // nf
    ff_here = ff_bias.shape[1]
    per_row = ff_here // shard
    pair = ("fsdp", "section")
    fits = nf == 4 and lax.axis_size("ctx") == 4 and chunks == 2

    own_in = lax.dynamic_index_in_dim(inputs, s, 0, keepdims=False)[0]
    own_cot = lax.dynamic_index_in_dim(cotangent, s, 0, keepdims=False)[0]
    seg = lax.dynamic_index_in_dim(segments, s, 0, keepdims=False)[0]
    start = lax.axis_index("ctx") * rows
    key_seg = lax.dynamic_slice_in_dim(
        jnp.pad(seg, (reach, 0), constant_values=-1), start, reach + rows, 0
    )
    allowed = (key_seg[reach:, None] == key_seg[None, :]) & (
        jnp.arange(reach + rows, dtype=jnp.int32)[None, :] - reach
        <= jnp.arange(rows, dtype=jnp.int32)[:, None]
    )

    bias = jnp.where(allowed, 0.0, -1e30).astype(F32)
    bias_t = bias.T

    def gathered(rows_first):
        return lax.all_gather(rows_first, pair, axis=0, tiled=True)

    if fits:
        zero, wide_in, up_zero, up_blocks, down_w, one_half = first_weights(
            qkv_weight[0], out_weight[0], norm_gains[0], biases[0], ff_bias,
            own_in, up_weight[0], down_weight[0],
        )
        one = gathered(one_half)
        up_w = (up_zero, None)
    else:
        small = jnp.concatenate(
            [norm_gains[0].T, biases[0].T, ff_bias[0].reshape(per_row, shard).T], axis=1
        )
        beside = jnp.pad(small, ((0, 0), (0, WIDE - D - 8 - per_row)))
        packed = jnp.concatenate(
            [widen(qkv_weight[0][:, i * D : (i + 1) * D]) for i in range(3)]
            + [out_weight[0], beside],
            axis=1,
        )
        halves = packed.reshape(2, shard // 2, 4 * WIDE)
        keep = lax.dynamic_index_in_dim(halves, s, 0, keepdims=False)
        recv = on_chip(lax.dynamic_index_in_dim(halves, 1 - s, 0, keepdims=False))
        zero, one = gathered(pick(s, keep, recv)), gathered(pick(s, recv, keep))
        up_own = lax.all_to_all(
            up_weight[0].reshape(shard, nf, ff_here), "fsdp", split_axis=1, concat_axis=0, tiled=True
        ).reshape(D, ff_here)
        up_w = both_layers(up_own, s)
        down_w = both_layers(down_weight[0], s)
        wide_in = with_halo(own_in, chunks)

    weights = (zero, one)

    kept = []
    current = own_in
    produced = []
    for layer in range(2):
        if layer == 1 and fits:
            *made, wide, up_one = block_forward(current, weights[layer], bias, up_blocks)
            up_w = (up_w[0], up_one)
        else:
            wide = with_halo(current, chunks) if layer else wide_in
            made = block_forward(wide, weights[layer], bias)
        normed, q, k, v, att, resid, second, par = made
        ffb = lax.dynamic_slice(par, (8, f * shard), (per_row, shard)).reshape(1, ff_here)
        current, second_all, active, slope = mlp_forward(
            second, up_w[layer], down_w, layer, ffb, resid, par
        )
        produced.append(current)
        kept.append((wide, normed, q, k, v, att, resid, second_all, slope, active, par))

    upstream = own_cot
    derived = [None, None]
    parts = [None, None]
    mlp_sums = [None, None]
    for layer in (1, 0):
        wide, normed, q, k, v, att, resid, second_all, slope, active, par = kept[layer]
        d_second, up_all, dz_b, ffb_g = mlp_backward(upstream, up_w[layer], down_w, layer, slope)
        up_g = mm_tn(flat(second_all), flat(dz_b)).astype(BF)
        up_half = core_half(up_g.reshape(nf, 2, shard // 2, ff_here), 1)
        down_g = mm_tn(flat(active), flat(up_all)).astype(BF)
        down_half = core_half(down_g.reshape(2, ff_here // 2, D), 0)
        d_second, up_half, down_half = lax.optimization_barrier((d_second, up_half, down_half))
        up_half = lax.all_to_all(up_half, "fsdp", split_axis=0, concat_axis=0, tiled=True)
        ffb_rows = lax.dynamic_update_slice(
            jnp.zeros((8, D), F32), ffb_g.reshape(per_row, shard), (0, f * shard)
        )
        block = (
            d_second, upstream, resid, wide, q, k, v, att, ffb_rows, weights[layer], par, bias_t
        )
        if layer == 1 and fits:
            derived[1], upstream_next, dq, dk, dv, left, right = block_backward(*block, True)
        else:
            d_resid, dq, dk, dv, da_own, da_halo, left, right = block_backward(*block, False)
        if not fits:
            unit, inv = norm_parts(wide[reach:].astype(F32))
            late = return_halo(da_halo, chunks, rows)
            derived[layer] = d_resid + norm_back(da_own + late, par[0], unit, inv)
            upstream_next = derived[layer].astype(BF)
        pieces = (
            mm_tn(normed[reach:], dq).astype(BF),
            mm_tn(normed, dk).astype(BF),
            mm_tn(normed, dv).astype(BF),
            mm_tn(left, right).astype(BF),
        )
        parts[layer] = pieces
        up_half, down_half, _ = lax.optimization_barrier((up_half, down_half, dq))
        halves = jnp.stack([down_half, up_half.reshape(ff_here // 2, D)])
        if layer == 1:
            _, upstream_next = lax.optimization_barrier((halves, upstream_next))
        else:
            halves, mlp_sums[1] = lax.optimization_barrier((halves, mlp_sums[1]))
        mlp_sums[layer] = lax.psum(halves, "ctx")
        if layer == 1:
            upstream = upstream_next

    if fits:
        qkv_g, out_g, down_one, up_one, made, grads = reduce_both(
            parts[0], parts[1], mlp_sums[1], produced, derived[1], da_halo, d_resid, da_own,
            wide[reach:], par,
        )
        late_sum, qkv_g = lax.optimization_barrier((mlp_sums[0], qkv_g))
        far = lax.ppermute(late_sum, "section", [(1, 0)])
        qkv_g, out_g, grad_down, grad_up, small, made, grads = final_layouts(
            qkv_g, out_g, late_sum, far, down_one, up_one, made, grads
        )
        made, grads = made[None, :, None], grads[None, :, None]
    else:
        a_tot = pick(s, reduce_plain(parts[0]), reduce_plain(parts[1])).astype(F32)
        qkv_g = jnp.concatenate([a_tot[i, :, :D] for i in range(3)], axis=1)
        out_g = a_tot[3, :, :D]
        small = a_tot[3, :, D : D + 16].T
        grad_down, grad_up = halves_settle(*mlp_sums, nf, shard)
        made, grads = both_micros(produced, s), both_micros(derived, s)
    return (
        made,
        grads,
        qkv_g[None],
        out_g[None],
        grad_up[None],
        grad_down[None],
        small[None, :2],
        small[None, 2:8],
        small[8 : 8 + per_row].reshape(1, ff_here),
    )


def both_micros(layers, s):
    to_zero = lax.ppermute(layers[0], "section", [(1, 0)])
    to_one = lax.ppermute(layers[1], "section", [(0, 1)])
    out = jnp.stack([pick(s, layers[0], to_one), pick(s, to_zero, layers[1])])
    return out[None, :, None]


def solution(mesh):
    return jax.shard_map(
        on_device,
        mesh=mesh,
        in_specs=(
            P(None, "fsdp", "ctx", None),
            P(None, "fsdp", None),
            P(None, "fsdp", "ctx", None),
            P("section", "fsdp", None),
            P("section", "fsdp", None),
            P("section", "fsdp", None),
            P("section", "fsdp", None),
            P("section", None, "fsdp"),
            P("section", None, "fsdp"),
            P("section", "fsdp"),
        ),
        out_specs=(
            P("section", None, "fsdp", "ctx", None),
            P("section", None, "fsdp", "ctx", None),
            P("section", "fsdp", None),
            P("section", "fsdp", None),
            P("section", "fsdp", None),
            P("section", "fsdp", None),
            P("section", None, "fsdp"),
            P("section", None, "fsdp"),
            P("section", "fsdp"),
        ),
        check_vma=False,
    )
```

```python
import functools
import math

import jax
import jax.numpy as jnp
from jax import lax
from jax.experimental import pallas as pl
from jax.experimental.pallas import tpu as pltpu
from jax.sharding import PartitionSpec as P

D = 1088
HD = 64
F32 = jnp.float32
BF = jnp.bfloat16
SCALE = 1.0 / math.sqrt(HD)
WIDE = 1152
MESH = pl.DeviceIdType.MESH
SWAP = [(0, 1), (1, 0)]


def mm(a, b):
    return jnp.dot(a, b, preferred_element_type=F32)


def mm_nt(a, b):
    return lax.dot_general(a, b, (((1,), (1,)), ((), ())), preferred_element_type=F32)


def mm_tn(a, b):
    return lax.dot_general(a, b, (((0,), (0,)), ((), ())), preferred_element_type=F32)


def norm_parts(values):
    center = jnp.mean(values, axis=-1, keepdims=True)
    offset = values - center
    spread = jnp.mean(offset * offset, axis=-1, keepdims=True)
    inv = lax.rsqrt(spread + 1e-05)
    return offset * inv, inv


def norm_back(grad, gain, unit, inv):
    dn = grad * gain
    return inv * (
        dn
        - jnp.mean(dn, axis=-1, keepdims=True)
        - unit * jnp.mean(dn * unit, axis=-1, keepdims=True)
    )


def phi_parts(z):
    cdf = 0.5 * (1.0 + lax.erf(z * (1.0 / math.sqrt(2.0))))
    pdf = jnp.exp(-0.5 * z * z) * (1.0 / math.sqrt(2.0 * math.pi))
    return cdf, pdf


def plane_neighbours():
    f = lax.axis_index("fsdp")
    x = lax.rem(f, 2)
    y = f // 2
    return y * 2 + (1 - x), (1 - y) * 2 + x


def plane_barrier(xn, yn):
    barrier = pltpu.get_barrier_semaphore()
    for nb in (xn, yn):
        pl.semaphore_signal(barrier, inc=1, device_id={"fsdp": nb}, device_id_type=MESH)
    pl.semaphore_wait(barrier, 2)


def remote(src, dst, send, recv, nb):
    return pltpu.make_async_remote_copy(
        src_ref=src, dst_ref=dst, send_sem=send, recv_sem=recv,
        device_id={"fsdp": nb}, device_id_type=MESH,
    )


def load_layer(sources, targets, sems):
    copies = [
        pltpu.make_async_copy(source, target, sems.at[i])
        for i, (source, target) in enumerate(zip(sources, targets))
    ]
    for copy in copies:
        copy.start()
    return copies


def exchange_rows(own_ref, all_ref, parts, compute, finish, bufs, send, recv, loads):
    x1, y1, x2, y2, sum_x, sum_y = bufs
    xn, yn = plane_neighbours()
    half = own_ref.shape[0] // 2
    top, low = pl.ds(0, half), pl.ds(half, half)
    plane_barrier(xn, yn)

    to_x = remote(own_ref, all_ref.at[1], send.at[0], recv.at[0], xn)
    to_y = remote(own_ref, all_ref.at[2], send.at[1], recv.at[1], yn)
    far_x = remote(all_ref.at[2, top], all_ref.at[3, top], send.at[2], recv.at[2], xn)
    far_y = remote(all_ref.at[1, low], all_ref.at[3, low], send.at[3], recv.at[3], yn)
    first_x = remote(parts.at[3, top], x1, send.at[4], recv.at[4], xn)
    first_y = remote(parts.at[3, low], y1, send.at[5], recv.at[5], yn)
    own_x = remote(parts.at[1, top], x2.at[top], send.at[6], recv.at[6], xn)
    own_y = remote(parts.at[2, low], y2.at[low], send.at[7], recv.at[7], yn)
    rest_x = remote(sum_x, x2.at[low], send.at[8], recv.at[8], xn)
    rest_y = remote(sum_y, y2.at[top], send.at[9], recv.at[9], yn)

    to_x.start()
    to_y.start()
    all_ref[0] = own_ref[...]
    for copy in loads:
        copy.wait()

    @pl.loop(0, 4)
    def _(i):
        @pl.when(i == 1)
        def _():
            to_x.wait_recv()
            far_y.start()
            to_y.wait_recv()
            far_x.start()

        @pl.when(i == 2)
        def _():
            own_x.start()
            far_x.wait_recv()
            far_y.wait_recv()

        @pl.when(i == 3)
        def _():
            first_x.start()
            first_y.start()

        compute(i + (i // 2) * (1 - 2 * lax.rem(i, 2)))

    own_y.start()
    first_x.wait_recv()
    sum_y[...] = (parts[2, top, :].astype(F32) + x1[...].astype(F32)).astype(BF)
    rest_y.start()
    first_y.wait_recv()
    sum_x[...] = (parts[1, low, :].astype(F32) + y1[...].astype(F32)).astype(BF)
    rest_x.start()
    own_x.wait_recv()
    rest_y.wait_recv()
    finish(top, parts[0, top, :].astype(F32) + x2[top, :].astype(F32) + y2[top, :].astype(F32))
    own_y.wait_recv()
    rest_x.wait_recv()
    finish(low, parts[0, low, :].astype(F32) + x2[low, :].astype(F32) + y2[low, :].astype(F32))
    for copy in (to_x, to_y, far_x, far_y, first_x, first_y, own_x, own_y, rest_x, rest_y):
        copy.wait_send()


def forward_kernel(
    layer, own, up_here, down_both, bias, resid, par, out, all_ref, active, slope,
    up, down, load, parts, x1, y1, x2, y2, sx, sy, send, recv,
):
    loads = load_layer((up_here, down_both.at[layer]), (up, down), load)

    def finish(at, value):
        out[at, :] = (resid[at, :] + value + par[7:8, :]).astype(BF)

    def compute(r):
        slope[r] = mm(all_ref[r], up[...]) + bias[...]

        @pl.loop(0, own.shape[0] // 64)
        def _(j):
            at = pl.ds(pl.multiple_of(j * 64, 64), 64)
            z = slope[r, at, :]
            cdf, pdf = phi_parts(z)
            active[r, at, :] = (z * cdf).astype(BF)
            slope[r, at, :] = cdf + z * pdf

        parts[r] = mm(active[r], down[...]).astype(BF)

    exchange_rows(own, all_ref, parts, compute, finish, (x1, y1, x2, y2, sx, sy), send, recv, loads)


def backward_kernel(
    layer, own, up_here, down_both, slope, total, all_ref, dz_all, bias_g,
    up, down, load, parts, x1, y1, x2, y2, sx, sy, send, recv,
):
    loads = load_layer((up_here, down_both.at[layer]), (up, down), load)
    bias_g[...] = jnp.zeros_like(bias_g)

    def finish(at, value):
        total[at, :] = value

    def compute(r):
        dz = mm_nt(all_ref[r], down[...]) * slope[r]
        bias_g[...] += jnp.sum(dz, axis=0, keepdims=True)
        dz_all[r] = dz.astype(BF)
        parts[r] = mm_nt(dz_all[r], up[...]).astype(BF)

    exchange_rows(own, all_ref, parts, compute, finish, (x1, y1, x2, y2, sx, sy), send, recv, loads)


VSPEC = pl.BlockSpec(memory_space=pltpu.VMEM)


def lasting(micros):
    return pl.CostEstimate(flops=0, transcendentals=0, bytes_accessed=int(micros * 3.5e6))


def plane_call(kernel, ident, outs, rows, *operands):
    half = rows // 2
    any_spec = pl.BlockSpec(memory_space=pl.ANY)
    return pl.pallas_call(
        kernel,
        out_shape=outs,
        in_specs=[VSPEC, any_spec, any_spec] + [VSPEC] * (len(operands) - 3),
        out_specs=(VSPEC,) * len(outs),
        scratch_shapes=[
            pltpu.VMEM((D, D), BF),
            pltpu.VMEM((D, D), BF),
            pltpu.SemaphoreType.DMA((2,)),
            pltpu.VMEM((4, rows, D), BF),
            pltpu.VMEM((half, D), BF),
            pltpu.VMEM((half, D), BF),
            pltpu.VMEM((rows, D), BF),
            pltpu.VMEM((rows, D), BF),
            pltpu.VMEM((half, D), BF),
            pltpu.VMEM((half, D), BF),
            pltpu.SemaphoreType.DMA((10,)),
            pltpu.SemaphoreType.DMA((10,)),
        ],
        compiler_params=pltpu.CompilerParams(
            collective_id=ident, has_side_effects=True, vmem_limit_bytes=56 * 1024 * 1024
        ),
        cost_estimate=lasting(40),
    )(*operands)


def mlp_forward(own, up, down, layer, bias, resid, par):
    rows = own.shape[0]
    if lax.axis_size("fsdp") != 4:
        every = lax.all_gather(own, "fsdp", axis=0, tiled=True)
        down = down[layer]
        z = mm(every, up) + bias
        cdf, pdf = phi_parts(z)
        active = (z * cdf).astype(BF)
        part = mm(active, down).astype(BF)
        total = lax.psum_scatter(part, "fsdp", scatter_dimension=0, tiled=True).astype(F32)
        out = (resid + total + par[7]).astype(BF)
        return out, every, active, cdf + z * pdf
    shape = (4, rows, D)
    return plane_call(
        functools.partial(forward_kernel, layer), 1 + 6 * layer,
        (
            jax.ShapeDtypeStruct((rows, D), BF),
            jax.ShapeDtypeStruct(shape, BF),
            jax.ShapeDtypeStruct(shape, BF),
            jax.ShapeDtypeStruct(shape, F32),
        ),
        rows, own, up, down, bias, resid, par,
    )


def mlp_backward(own, up, down, layer, slope):
    rows = own.shape[0]
    if lax.axis_size("fsdp") != 4:
        every = lax.all_gather(own, "fsdp", axis=0, tiled=True)
        down = down[layer]
        dz = mm_nt(every, down) * slope
        dz_b = dz.astype(BF)
        part = mm_nt(dz_b, up).astype(BF)
        total = lax.psum_scatter(part, "fsdp", scatter_dimension=0, tiled=True).astype(F32)
        return total, every, dz_b, jnp.sum(dz, axis=0, keepdims=True)
    shape = (4, rows, D)
    return plane_call(
        functools.partial(backward_kernel, layer), 2 + 6 * layer,
        (
            jax.ShapeDtypeStruct((rows, D), F32),
            jax.ShapeDtypeStruct(shape, BF),
            jax.ShapeDtypeStruct(shape, BF),
            jax.ShapeDtypeStruct((1, D), F32),
        ),
        rows, own, up, down, slope,
    )


def spread_up(core, blocks, full, load, u_send, u_recv, v_send, v_recv):
    s = lax.axis_index("section")
    f = lax.axis_index("fsdp")
    xn, yn = plane_neighbours()
    others = (xn, yn, 3 - f)
    shard = blocks.shape[1]

    def rows_of(owner):
        return full.at[pl.ds(pl.multiple_of(owner * shard, 16), shard)]

    def to(src, dst, send, recv, **where):
        return pltpu.make_async_remote_copy(
            src_ref=src, dst_ref=dst, send_sem=send, recv_sem=recv,
            device_id=where, device_id_type=MESH,
        )

    def chip(i):
        return to(blocks.at[others[i]], rows_of(f), u_send.at[i], u_recv.at[i], fsdp=others[i])

    def over(i):
        rows = rows_of((*others, f)[i])
        return to(rows, rows, v_send.at[i], v_recv.at[i], section=1 - core)

    near = pltpu.make_async_copy(blocks.at[f], rows_of(f), load)

    def first():
        @pl.when(s == core)
        def _():
            near.start()
            for i in range(3):
                chip(i).start()
            near.wait()
            over(3).start()

    def then():
        @pl.when(s == core)
        def _():
            for i in range(3):
                chip(i).wait_recv()
                over(i).start()

    def last():
        @pl.when(s == core)
        def _():
            for i in range(3):
                chip(i).wait_send()
            for i in range(4):
                over(i).wait_send()

        @pl.when(s == 1 - core)
        def _():
            for i in range(4):
                over(i).wait_recv()

    return first, then, last


def spread_sems():
    return [pltpu.SemaphoreType.DMA((n,)) for n in (3, 3, 4, 4)]


def weights_kernel(
    qkv_in, out_in, gains, biases, hidden, rows_in, up_in, down_in,
    full, rows_out, up_out, up_blocks, down_out, next_half,
    own, other_half, load, core_s, core_r, p_send, p_recv, f_send, f_recv, z_send, z_recv,
    u_send, u_recv, v_send, v_recv,
):
    s = lax.axis_index("section")
    f = lax.axis_index("fsdp")
    xn, yn = plane_neighbours()
    dn = 3 - f
    shard, wide = own.shape[1], own.shape[2]
    cut = 640
    left = pl.ds(0, cut)
    right = pl.ds(cut, wide - cut)

    def to(src, dst, send, recv, **where):
        return pltpu.make_async_remote_copy(
            src_ref=src, dst_ref=dst, send_sem=send, recv_sem=recv,
            device_id=where, device_id_type=MESH,
        )

    pad = jnp.zeros((shard, wide - D), BF)
    for p in range(3):
        own[p] = jnp.concatenate([qkv_in[:, pl.ds(p * D, D)], pad], axis=1)
    unit_rows = (
        lax.broadcasted_iota(jnp.int32, (16, 64), 0) == lax.broadcasted_iota(jnp.int32, (16, 64), 1)
    ).astype(F32)
    hidden_rows = [hidden[:, pl.ds(i * shard, shard)] for i in range(hidden.shape[1] // shard)]
    small = jnp.concatenate(
        [
            value.astype(F32)
            for value in (gains[...], biases[...], *hidden_rows, jnp.zeros((8 - len(hidden_rows), shard)))
        ],
        axis=0,
    )
    beside = mm_tn(small.astype(BF), unit_rows.astype(BF)).astype(BF)
    own[3] = jnp.concatenate([out_in[...], beside], axis=1)

    barrier = pltpu.get_barrier_semaphore()
    z = lax.axis_index("ctx")
    above = {"ctx": lax.rem(z + 1, 4)}
    below = {"ctx": lax.rem(z + 3, 4)}
    partners = ({"section": 1 - s}, {"fsdp": xn}, {"fsdp": yn}, {"fsdp": dn}, above, below)
    for where in partners:
        pl.semaphore_signal(barrier, inc=1, device_id=where, device_id_type=MESH)
    pl.semaphore_wait(barrier, 6)
    rows = rows_in.shape[0]
    near_rows, far_rows = pl.ds(rows, rows), pl.ds(0, rows)
    step_one = to(rows_in, rows_out.at[near_rows], z_send.at[0], z_recv.at[0], **above)
    step_two = to(
        rows_out.at[near_rows], rows_out.at[far_rows], z_send.at[1], z_recv.at[1], **above
    )

    @pl.when(z < 3)
    def _():
        step_one.start()

    rows_out[pl.ds(2 * rows, rows), :] = rows_in[...]

    @pl.when(z == 0)
    def _():
        rows_out[near_rows, :] = jnp.zeros(rows_in.shape, BF)

    @pl.when(z < 2)
    def _():
        rows_out[far_rows, :] = jnp.zeros(rows_in.shape, BF)

    def blk(owner):
        return pl.ds(pl.multiple_of(owner * shard, 16), shard)

    def give(p):
        return to(own.at[p], full.at[p, blk(f)], core_s.at[p], core_r.at[p], section=1)

    def keep(p):
        return pltpu.make_async_copy(own.at[p], full.at[p, blk(f)], load.at[p])

    @pl.when(s == 0)
    def _():
        for p in (2, 3, 0, 1):
            give(p).start()
        for p in range(4):
            keep(p).start()
        keep(0).wait()
        keep(1).wait()

    @pl.when(s == 1)
    def _():
        give(2).wait_recv()
        give(3).wait_recv()

    def same(piece, rows, send, recv, cols=slice(None), **where):
        ref = full.at[piece, rows, cols]
        return to(ref, ref, send, recv, **where)

    def hops(k):
        p = 2 * s + k
        return (
            same(p, blk(f), p_send.at[k, 0], p_recv.at[k, 0], fsdp=xn),
            same(p, blk(f), p_send.at[k, 1], p_recv.at[k, 1], fsdp=yn),
            same(p, blk(yn), p_send.at[k, 2], p_recv.at[k, 2], left, fsdp=xn),
            same(p, blk(xn), p_send.at[k, 3], p_recv.at[k, 3], right, fsdp=yn),
        )

    def here(k):
        p = 2 * s + k
        return [
            same(p, blk(owner), f_send.at[k, i], f_recv.at[k, i], section=1 - s)
            for i, owner in enumerate((xn, yn, dn))
        ]

    for k in range(2):
        copies = hops(k)
        copies[0].start()
        copies[1].start()
    down_far = to(down_in, down_out.at[s], core_s.at[4], core_r.at[4], section=1 - s)
    down_near = pltpu.make_async_copy(down_in, down_out.at[s], load.at[4])
    down_far.start()
    down_near.start()
    swap = to(other_half, next_half, core_s.at[5], core_r.at[5], section=0)

    @pl.when(s == 1)
    def _():
        for p in range(4):
            at = pl.ds(p * wide, wide)
            other_half[:, at] = own[p, pl.ds(0, shard // 2), :]
            next_half[:, at] = own[p, pl.ds(shard // 2, shard // 2), :]
        swap.start()

    for j in range(4):
        up_blocks[j] = up_in[:, pl.ds(j * D, D)]

    up_first, up_then, up_last = spread_up(
        0, up_blocks, up_out, load.at[5], u_send, u_recv, v_send, v_recv
    )
    up_first()
    for k in range(2):
        copies, across = hops(k), here(k)
        copies[0].wait_recv()
        copies[3].start()
        across[0].start()
        copies[1].wait_recv()
        copies[2].start()
        across[1].start()

    @pl.when(z > 0)
    def _():
        step_one.wait_recv()

    @pl.when((z == 1) | (z == 2))
    def _():
        step_two.start()

    for k in range(2):
        copies, across = hops(k), here(k)
        copies[2].wait_recv()
        copies[3].wait_recv()
        across[2].start()
    up_then()
    for k in range(2):
        for copy in here(k):
            copy.wait()
        for copy in hops(k):
            copy.wait_send()
    up_last()

    @pl.when(s == 0)
    def _():
        for p in range(4):
            give(p).wait_send()
        keep(2).wait()
        keep(3).wait()

    @pl.when(s == 1)
    def _():
        give(0).wait_recv()
        give(1).wait_recv()

    down_near.wait()
    down_far.wait()
    pl.when(s == 0)(swap.wait_recv)
    pl.when(s == 1)(swap.wait_send)

    @pl.when(z < 3)
    def _():
        step_one.wait_send()

    @pl.when((z == 1) | (z == 2))
    def _():
        step_two.wait_send()

    @pl.when(z > 1)
    def _():
        step_two.wait_recv()


def first_weights(qkv, out, gains, biases, hidden, rows_in, up, down):
    dma = pltpu.SemaphoreType.DMA
    shard = qkv.shape[0]
    shapes = (
        (4, D, WIDE), (3 * rows_in.shape[0], D), (D, D), (4, shard, D), (2, D, D), (shard // 2, 4 * WIDE)
    )
    return pl.pallas_call(
        weights_kernel,
        out_shape=tuple(jax.ShapeDtypeStruct(shape, BF) for shape in shapes),
        in_specs=[VSPEC] * 7 + [pl.BlockSpec(memory_space=pl.ANY)],
        out_specs=(VSPEC,) * 6,
        scratch_shapes=[
            pltpu.VMEM((4, shard, WIDE), BF),
            pltpu.VMEM((shard // 2, 4 * WIDE), BF),
            dma((6,)), dma((6,)), dma((6,)), dma((2, 4)), dma((2, 4)), dma((2, 3)), dma((2, 3)),
            dma((2,)), dma((2,)), *spread_sems(),
        ],
        compiler_params=pltpu.CompilerParams(
            collective_id=4, has_side_effects=True, vmem_limit_bytes=58 * 1024 * 1024
        ),
        cost_estimate=lasting(75),
        name="first_weights",
    )(qkv, out, gains, biases, hidden, rows_in, up, down)


def z_partners():
    z = lax.axis_index("ctx")
    return z + 1 - 2 * lax.rem(z, 2), 3 - z, (z == 1) | (z == 2)


def add_rows(dst, one, two, rows, step):
    @pl.loop(0, rows // step)
    def _(i):
        at = pl.ds(pl.multiple_of(i * step, 16), step)
        dst[at, :] = (one[at, :].astype(F32) + two[at, :].astype(F32)).astype(dst.dtype)


CUTS = ((0, 640, 384), (640, 512, 256))


def reduce_kernel(
    q0, k0, v0, o0, q1, k1, v1, o1, mlp_down, mlp_up, made0, made1, grad1, halo, d_resid, da_own, wide, par,
    qkv_out, out_out, down_out, up_out, made_out, grad_out,
    own_in, held, up_own, up_far, sent, caught, grad0,
    x1a, y1a, x2a, y2a, sxa, sya, ta, zaa, zba,
    x1b, y1b, x2b, y2b, sxb, syb, tb, zab, zbb,
    load, core_s, core_r, p_send, p_recv, z_send, z_recv, h_send, h_recv, x_send, x_recv,
):
    s = lax.axis_index("section")
    f = lax.axis_index("fsdp")
    xn, yn = plane_neighbours()
    dn = 3 - f
    side, across, inner = z_partners()
    pieces = ((q0, k0, v0, o0), (q1, k1, v1, o1))
    sets = (
        (x1a, y1a, x2a, y2a, sxa, sya, ta, zaa, zba),
        (x1b, y1b, x2b, y2b, sxb, syb, tb, zab, zbb),
    )
    shard = out_out.shape[0]
    rows = da_own.shape[0]
    z = lax.axis_index("ctx")
    above, below = {"ctx": lax.rem(z + 1, 4)}, {"ctx": lax.rem(z + 3, 4)}

    def to(src, dst, send, recv, **where):
        return pltpu.make_async_remote_copy(
            src_ref=src, dst_ref=dst, send_sem=send, recv_sem=recv,
            device_id=where, device_id_type=MESH,
        )

    barrier = pltpu.get_barrier_semaphore()
    partners = ({"section": 1 - s}, {"fsdp": xn}, {"fsdp": yn}, above, below)
    for where in partners:
        pl.semaphore_signal(barrier, inc=1, device_id=where, device_id_type=MESH)
    pl.semaphore_wait(barrier, 5)

    def blk(owner):
        return pl.ds(pl.multiple_of(owner * shard, 16), shard)

    def by_core(act):
        for core in range(2):
            pl.when(s == core)(functools.partial(act, core))

    def far(j, src):
        return to(src, held.at[j], core_s.at[j], core_r.at[j], section=1 - s)

    def near(j, src):
        return pltpu.make_async_copy(src, own_in.at[j % 2], load.at[j])

    def bufs(c):
        return tuple(ref.at[c // 2] for ref in sets[c % 2])

    def plane(c):
        x1, y1, x2, y2, sx, sy = bufs(c)[:6]
        own = held.at[c // 2]
        at, width, cut = CUTS[c % 2]
        left, right = pl.ds(at, cut), pl.ds(at + cut, width - cut)
        to_left, to_right = pl.ds(0, cut), pl.ds(cut, width - cut)
        sems = [(p_send.at[c, i], p_recv.at[c, i]) for i in range(6)]
        return (
            to(own.at[blk(dn), left], x1, *sems[0], fsdp=xn),
            to(own.at[blk(dn), right], y1, *sems[1], fsdp=yn),
            to(own.at[blk(xn), left], x2.at[:, to_left], *sems[2], fsdp=xn),
            to(own.at[blk(yn), right], y2.at[:, to_right], *sems[3], fsdp=yn),
            to(sx, x2.at[:, to_right], *sems[4], fsdp=xn),
            to(sy, y2.at[:, to_left], *sems[5], fsdp=yn),
        )

    def along(c):
        t, za, zb = bufs(c)[6:]
        sems = [(z_send.at[c, i], z_recv.at[c, i]) for i in range(3)]
        return (
            to(t, za, *sems[0], ctx=side),
            to(za, zb, *sems[1], ctx=across),
            to(zb, zb, *sems[2], ctx=side),
        )

    def join(j):
        far(j, q0).wait_recv()
        near(j, q0).wait()
        add_rows(held.at[j], own_in.at[j % 2], held.at[j], 4 * shard, 64)
        for c in (2 * j, 2 * j + 1):
            for copy in plane(c)[:4]:
                copy.start()
        if j < 2:
            by_core(lambda core: near(j + 2, pieces[core][j + 2]).start())

    def second(c):
        copies = plane(c)
        x1, y1, _, _, sx, sy = bufs(c)[:6]
        at, width, cut = CUTS[c % 2]
        own = held.at[c // 2]
        copies[0].wait_recv()
        add_rows(sy, own.at[blk(yn), pl.ds(at, cut)], x1, shard, 16)
        copies[5].start()
        copies[1].wait_recv()
        add_rows(sx, own.at[blk(xn), pl.ds(at + cut, width - cut)], y1, shard, 16)
        copies[4].start()

    def third(c):
        copies = plane(c)
        _, _, x2, y2, _, _, t, _, _ = bufs(c)
        at, width, _ = CUTS[c % 2]
        for copy in copies[2:]:
            copy.wait_recv()
        own = held.at[c // 2, blk(f), pl.ds(at, width)]

        @pl.loop(0, shard // 16)
        def _(i):
            part = pl.ds(pl.multiple_of(i * 16, 16), 16)
            t[part, :] = (
                own[part, :].astype(F32) + x2[part, :].astype(F32) + y2[part, :].astype(F32)
            ).astype(BF)

        @pl.when(jnp.logical_not(inner))
        def _():
            along(c)[0].start()

    def inward(c):
        @pl.when(inner)
        def _():
            t, za, _ = bufs(c)[6:]
            copies = along(c)
            copies[0].wait_recv()
            add_rows(za, t, za, shard, 16)
            copies[1].start()

    def crossed(c):
        @pl.when(inner)
        def _():
            _, za, zb = bufs(c)[6:]
            copies = along(c)
            copies[1].wait_recv()
            add_rows(zb, za, zb, shard, 16)
            copies[2].start()

    def last(c):
        at, width, _ = CUTS[c % 2]
        j = c // 2

        @pl.when(jnp.logical_not(inner))
        def _():
            along(c)[2].wait_recv()

        done = bufs(c)[8]
        keep = min(width, D - at) if j < 3 else width

        @pl.loop(0, shard // 16)
        def _(i):
            part = pl.ds(pl.multiple_of(i * 16, 16), 16)
            if j < 3:
                qkv_out[part, pl.ds(j * D + at, keep)] = done[part, pl.ds(0, keep)]
            else:
                out_out[part, pl.ds(at, keep)] = done[part, :]

    half = down_out.shape[0] // 2
    mine = pl.ds(pl.multiple_of(s * half, 16), half)
    down_far = to(mlp_down, down_out.at[mine], core_s.at[4], core_r.at[4], section=1 - s)
    down_near = pltpu.make_async_copy(mlp_down, down_out.at[mine], load.at[4])
    far_up = to(mlp_up, up_far, core_s.at[5], core_r.at[5], section=1 - s)
    near_up = pltpu.make_async_copy(mlp_up, up_own, load.at[5])

    def lay_up():
        far_up.wait_recv()
        near_up.wait()

        @pl.when(s == 1)
        def _():
            for k in range(4):
                at = pl.ds(k * (shard // 2), shard // 2)
                up_out[:, pl.ds(k * D, D)] = jnp.concatenate([up_far[at, :], up_own[at, :]], axis=0)

    back_one = to(halo.at[pl.ds(0, rows)], caught.at[0], h_send.at[0], h_recv.at[0], **below)
    back_two = to(sent, caught.at[1], h_send.at[1], h_recv.at[1], **below)

    def back():
        @pl.when(z < 3)
        def _():
            back_one.wait_recv()

        @pl.when(z == 3)
        def _():
            caught[0] = jnp.zeros_like(caught[0])

        @pl.when(z > 0)
        def _():
            add_rows(sent, halo.at[pl.ds(rows, rows)], caught.at[0], rows, 64)
            back_two.start()

    made_far = (
        to(made1, made_out.at[0], x_send.at[0], x_recv.at[0], section=1),
        to(made0, made_out.at[1], x_send.at[0], x_recv.at[0], section=0),
    )
    grad_far = (
        to(grad1, grad_out.at[0], x_send.at[1], x_recv.at[1], section=1),
        to(grad0, grad_out.at[1], x_send.at[1], x_recv.at[1], section=0),
    )
    made_near = (
        pltpu.make_async_copy(made0, made_out.at[0], load.at[6]),
        pltpu.make_async_copy(made1, made_out.at[1], load.at[6]),
    )
    grad_near = pltpu.make_async_copy(grad1, grad_out.at[1], load.at[7])

    def back_end():
        @pl.when(z < 3)
        def _():
            back_two.wait_recv()

        @pl.when(z == 3)
        def _():
            caught[1] = jnp.zeros_like(caught[1])

        unit, inv = norm_parts(wide[...].astype(F32))
        da = da_own[...] + caught[1].astype(F32)
        grad0[...] = d_resid[...] + norm_back(da, par[0:1, :], unit, inv)

        @pl.when(s == 0)
        def _():
            grad_out[0] = grad0[...]

        @pl.when(s == 1)
        def _():
            grad_far[1].start()

    @pl.when(s == 0)
    def _():
        made_far[0].start()
        grad_far[0].start()
        made_near[0].start()

    @pl.when(s == 1)
    def _():
        made_far[1].start()
        made_near[1].start()
        grad_near.start()

    @pl.when(z > 0)
    def _():
        back_one.start()

    for j in range(4):
        by_core(lambda core: far(j, pieces[1 - core][j]).start())
        if j < 2:
            by_core(lambda core: near(j, pieces[core][j]).start())
    for copy in (down_far, down_near, far_up, near_up):
        copy.start()

    join(0)
    for c in range(12):
        if c in (1, 3, 5):
            join((c + 1) // 2)
        if c < 8:
            second(c)
        if 1 <= c <= 8:
            third(c - 1)
        if 2 <= c <= 9:
            inward(c - 2)
        if 3 <= c <= 10:
            crossed(c - 3)
        if c >= 4:
            last(c - 4)
        if c == 2:
            back()
        if c == 4:
            lay_up()
        if c == 6:
            back_end()

    down_near.wait()
    down_far.wait()
    far_up.wait_send()

    @pl.when(s == 0)
    def _():
        made_near[0].wait()
        made_far[0].wait_send()
        grad_far[0].wait_send()
        made_far[1].wait_recv()
        grad_far[1].wait_recv()

    @pl.when(s == 1)
    def _():
        made_near[1].wait()
        grad_near.wait()
        made_far[1].wait_send()
        grad_far[1].wait_send()
        made_far[0].wait_recv()
        grad_far[0].wait_recv()

    @pl.when(z > 0)
    def _():
        back_one.wait_send()
        back_two.wait_send()

    for j in range(4):
        far(j, q0).wait_send()
    for c in range(8):
        for copy in plane(c):
            copy.wait_send()

    @pl.when(inner)
    def _():
        for c in range(8):
            for copy in along(c)[1:]:
                copy.wait_send()

    @pl.when(jnp.logical_not(inner))
    def _():
        for c in range(8):
            along(c)[0].wait_send()


def reduce_both(zero, one, mlp, made, grad1, halo, d_resid, da_own, wide, par):
    shard = D // 4
    rows = da_own.shape[0]
    dma = pltpu.SemaphoreType.DMA
    any_spec = pl.BlockSpec(memory_space=pl.ANY)

    def buf(*shape):
        return pltpu.VMEM(shape, BF)

    def part(_, width, cut):
        wide_buf = buf(4, shard, width)
        return [
            buf(4, shard, cut), buf(4, shard, width - cut), wide_buf, wide_buf,
            buf(4, shard, width - cut), buf(4, shard, cut), wide_buf, wide_buf, wide_buf,
        ]

    shapes = ((shard, 3 * D), (shard, WIDE), (D, D), (shard, 4 * D), (2, rows, D))
    return pl.pallas_call(
        reduce_kernel,
        out_shape=(
            *(jax.ShapeDtypeStruct(shape, BF) for shape in shapes),
            jax.ShapeDtypeStruct((2, rows, D), F32),
        ),
        in_specs=[any_spec] * 13 + [VSPEC] * 5,
        out_specs=(VSPEC,) * 6,
        scratch_shapes=[
            buf(2, D, WIDE), buf(4, D, WIDE), buf(D // 2, D), buf(D // 2, D), buf(rows, D),
            buf(2, rows, D), pltpu.VMEM((rows, D), F32), *part(*CUTS[0]), *part(*CUTS[1]),
            dma((8,)), dma((6,)), dma((6,)), dma((8, 6)), dma((8, 6)), dma((8, 3)), dma((8, 3)),
            dma((2,)), dma((2,)), dma((2,)), dma((2,)),
        ],
        compiler_params=pltpu.CompilerParams(
            collective_id=3, has_side_effects=True, vmem_limit_bytes=60 * 1024 * 1024
        ),
        cost_estimate=lasting(120),
        name="reduce_both",
    )(*zero, *one, *mlp, *made, grad1, halo, d_resid, da_own, wide, par)


def final_kernel(
    qkv, out, down_mine, up_mine, down_far, up_far, down_one, up_one, made, grads,
    qkv_f, out_f, down_f, up_f, small, made_out, grads_out,
):
    s = lax.axis_index("section")
    half = down_mine.shape[0]
    shard = qkv.shape[0]
    pick_row = (
        lax.broadcasted_iota(jnp.int32, (16, 128), 1)
        == lax.broadcasted_iota(jnp.int32, (16, 128), 0) + (D - TAIL)
    )
    small[...] = mm_nt(pick_row.astype(F32).astype(BF), out[:, pl.ds(TAIL, 128)])

    @pl.loop(0, made.shape[1] // 16)
    def _(i):
        at = pl.ds(pl.multiple_of(i * 16, 16), 16)
        for m in range(2):
            made_out[m, at, :] = made[m, at, :]
            grads_out[m, at, :] = grads[m, at, :]

    @pl.loop(0, shard // 16)
    def _(i):
        at = pl.ds(pl.multiple_of(i * 16, 16), 16)
        qkv_f[at, :] = qkv[at, :].astype(F32)
        out_f[at, :] = out[at, pl.ds(0, D)].astype(F32)

        @pl.when(s == 1)
        def _():
            up_f[at, :] = up_one[at, :].astype(F32)

    @pl.when(s == 0)
    def _():
        for k in range(4):
            at = pl.ds(k * (shard // 2), shard // 2)
            rows_k = jnp.concatenate([up_mine[at, :], up_far[at, :]], axis=0)
            up_f[:, pl.ds(k * D, D)] = rows_k.astype(F32)

    @pl.loop(0, half // 16)
    def _(i):
        at = pl.ds(pl.multiple_of(i * 16, 16), 16)
        after = pl.ds(pl.multiple_of(half + i * 16, 16), 16)

        @pl.when(s == 0)
        def _():
            down_f[at, :] = down_mine[at, :].astype(F32)
            down_f[after, :] = down_far[at, :].astype(F32)

        @pl.when(s == 1)
        def _():
            down_f[at, :] = down_one[at, :].astype(F32)
            down_f[after, :] = down_one[after, :].astype(F32)


def final_layouts(*values):
    qkv, *_, down_one, up_one, made, grads = values
    shard = qkv.shape[0]
    outs = [(shape, F32) for shape in (qkv.shape, (shard, D), down_one.shape, up_one.shape)]
    outs += [((16, shard), F32), (made.shape, BF), (grads.shape, F32)]
    return pl.pallas_call(
        final_kernel,
        out_shape=tuple(jax.ShapeDtypeStruct(*out) for out in outs),
        in_specs=[VSPEC] * 10,
        out_specs=(VSPEC,) * 7,
        compiler_params=pltpu.CompilerParams(vmem_limit_bytes=58 * 1024 * 1024),
        cost_estimate=lasting(10),
        name="final_layouts",
    )(*values)


def core_half(values, axis):
    s = lax.axis_index("section")
    keep = lax.dynamic_index_in_dim(values, s, axis, keepdims=False)
    give = lax.dynamic_index_in_dim(values, 1 - s, axis, keepdims=False)
    return (keep.astype(F32) + on_chip(give).astype(F32)).astype(BF)


def halves_settle(zero, one, nf, shard):
    s = lax.axis_index("section")
    zero, one = jnp.stack(zero), jnp.stack(one)
    mine, far = pick(s, zero, one), on_chip(pick(s, one, zero))
    first, second = pick(s, mine, far).astype(F32), pick(s, far, mine).astype(F32)
    down = jnp.concatenate([first[0], second[0]], axis=0)
    up = jnp.concatenate([half[1].reshape(nf, shard // 2, -1) for half in (first, second)], axis=1)
    return down, up.transpose(1, 0, 2).reshape(shard, -1)


def reduce_plain(pieces):
    s = lax.axis_index("section")
    pair = ("fsdp", "section")
    a = jnp.stack([lax.psum_scatter(p, pair, scatter_dimension=0, tiled=True) for p in pieces])
    a = lax.psum(a, "ctx")
    far = on_chip(a)
    return jnp.concatenate([pick(s, a, far), pick(s, far, a)], axis=1)


def shift(value, steps):
    count = lax.axis_size("ctx")
    pairs = [(i, i + steps) for i in range(count) if 0 <= i + steps < count]
    return lax.ppermute(value, "ctx", pairs)


def with_halo(own, chunks):
    parts = [own]
    for _ in range(chunks):
        parts.append(shift(parts[-1], 1))
    return jnp.concatenate(parts[::-1], axis=0)


def return_halo(halo, chunks, rows):
    carried = None
    for far in range(chunks):
        mine = halo[far * rows : (far + 1) * rows]
        carried = mine if carried is None else mine + carried
        carried = shift(carried.astype(BF), -1).astype(F32)
    return carried


def pick(s, first, second):
    return jnp.where(s == 0, first, second)


def on_chip(value):
    return lax.ppermute(value, "section", SWAP)


def both_layers(own, s):
    other = on_chip(own)
    return pick(s, own, other), pick(s, other, own)


def flat(values):
    return values.reshape(-1, values.shape[-1])


def widen(values):
    return jnp.pad(values, ((0, 0), (0, WIDE - D)))


TAIL = 1024


def scores_forward(q, k, v, bias, lanes):
    outs = []
    for low in (True, False):
        one = jnp.where((lanes < HD) if low else (lanes >= HD), q, jnp.zeros_like(q))
        weight = jnp.exp(mm_nt(one, k) + bias)
        prob = weight * (1.0 / jnp.sum(weight, axis=-1, keepdims=True))
        outs.append(mm(prob.astype(BF), v))
    return jnp.where(lanes < HD, outs[0], outs[1]).astype(BF)


def scores_backward(q, k, v, grad, bias_t, lanes):
    dqs, dk, dv = [], 0.0, 0.0
    for low in (True, False):
        mine = (lanes < HD) if low else (lanes >= HD)
        one = jnp.where(mine, q, jnp.zeros_like(q))
        g = jnp.where(mine, grad, jnp.zeros_like(grad))
        weight = jnp.exp(mm_nt(k, one) + bias_t)
        prob = weight * (1.0 / jnp.sum(weight, axis=0, keepdims=True))
        d_prob = mm_nt(v, g)
        row = jnp.sum(prob * d_prob, axis=0, keepdims=True)
        d_score = (prob * (d_prob - row)).astype(BF)
        dqs.append(mm_tn(d_score, k))
        dk = dk + mm(d_score, one)
        dv = dv + mm(prob.astype(BF), g)
    dq = jnp.where(lanes < HD, dqs[0], dqs[1]) * SCALE
    return dq.astype(BF), dk.astype(BF), dv.astype(BF)


def lane_tile(i):
    return pl.ds(pl.multiple_of(i * 128, 128), 128)


def widened(row):
    return jnp.concatenate([row, jnp.zeros((row.shape[0], WIDE - D), row.dtype)], axis=1)


def ctx_ring(rows_in, landing, send, recv, partners=()):
    z = lax.axis_index("ctx")
    above = {"ctx": lax.rem(z + 1, 4)}
    below = {"ctx": lax.rem(z + 3, 4)}
    rows = rows_in.shape[0]
    near, far = pl.ds(rows, rows), pl.ds(0, rows)
    barrier = pltpu.get_barrier_semaphore()

    def on(src, dst, i):
        return pltpu.make_async_remote_copy(
            src_ref=src, dst_ref=dst, send_sem=send.at[i], recv_sem=recv.at[i],
            device_id=above, device_id_type=MESH,
        )

    one = on(rows_in, landing.at[near], 0)
    two = on(landing.at[near], landing.at[far], 1)

    def begin():
        for where in (above, below, *partners):
            pl.semaphore_signal(barrier, inc=1, device_id=where, device_id_type=MESH)
        pl.semaphore_wait(barrier, 2 + len(partners))

        @pl.when(z < 3)
        def _():
            one.start()

        landing[pl.ds(2 * rows, rows), :] = rows_in[...]

        @pl.when(z == 0)
        def _():
            landing[near, :] = jnp.zeros(rows_in.shape, BF)

        @pl.when(z < 2)
        def _():
            landing[far, :] = jnp.zeros(rows_in.shape, BF)

    def middle():
        @pl.when(z > 0)
        def _():
            one.wait_recv()

        @pl.when((z == 1) | (z == 2))
        def _():
            two.start()

    def end():
        @pl.when(z > 1)
        def _():
            two.wait_recv()

        @pl.when(z < 3)
        def _():
            one.wait_send()

        @pl.when((z == 1) | (z == 2))
        def _():
            two.wait_send()

    return begin, middle, end


def block_kernel(ring, first, wq, wk, wv, wo, bias, *rest):
    if ring:
        up_blocks, *rest = rest
    normed, q_ref, k_ref, v_ref, att, resid, second, par, *rest = rest
    rows = resid.shape[0]
    total = normed.shape[0]
    if ring:
        wide_out, up_out, held, wide, up_full, send, recv, load, *sems = rest
        s = lax.axis_index("section")
        f = lax.axis_index("fsdp")
        xn, yn = plane_neighbours()
        partners = ({"section": 1 - s}, {"fsdp": xn}, {"fsdp": yn}, {"fsdp": 3 - f})
        begin, middle, end = ctx_ring(first, wide, send, recv, partners)
        up_first, up_then, up_last = spread_up(1, up_blocks, up_full, load.at[0], *sems)
        begin()
        up_first()
    else:
        (held,), wide = rest, first
    pick_row = (
        lax.broadcasted_iota(jnp.int32, (16, 128), 1)
        == lax.broadcasted_iota(jnp.int32, (16, 128), 0) + (D - TAIL)
    )
    par[...] = mm_nt(pick_row.astype(F32).astype(BF), wo[:, pl.ds(TAIL, 128)])
    last = total // rows - 1

    @pl.loop(0, last + 1)
    def _(i):
        if ring:
            pl.when(i == 1)(middle)
            pl.when(i == 2)(up_then)
            pl.when(i == 2)(end)
        at = pl.ds(pl.multiple_of((last - i) * rows, 16), rows)
        unit, _ = norm_parts(wide[at, :].astype(F32))
        low = (unit * par[0:1, :] + par[2:3, :]).astype(BF)
        normed[at, :] = low
        k_ref[at, :] = mm(low, wk[...]).astype(BF)
        v_ref[at, :] = (mm(low, wv[...]) + widened(par[4:5, :])).astype(BF)

        @pl.when(i == 0)
        def _():
            q_ref[...] = (mm(normed[at, :], wq[...]) + widened(par[3:4, :])).astype(BF)

    own = pl.ds(total - rows, rows)
    lanes = lax.broadcasted_iota(jnp.int32, (rows, 128), 1)

    @pl.loop(0, WIDE // 128)
    def _(i):
        at = lane_tile(i)
        held[:, at] = scores_forward(
            q_ref[:, at] * jnp.asarray(SCALE, BF), k_ref[:, at], v_ref[:, at], bias[...], lanes
        )

    att[...] = held[:, pl.ds(0, D)]
    res = wide[own, :].astype(F32) + mm(att[...], wo[:, pl.ds(0, D)]) + par[5:6, :]
    resid[...] = res
    unit, _ = norm_parts(res)
    second[...] = (unit * par[1:2, :] + par[6:7, :]).astype(BF)
    if ring:
        wide_out[...] = wide[...]
        up_last()
        up_out[...] = up_full[...]


def weight_specs(weights):
    if weights.ndim == 3:
        return [pl.BlockSpec((None, D, WIDE), lambda i, p=p: (p, 0, 0)) for p in range(4)]
    return [pl.BlockSpec((D, WIDE), lambda i, p=p: (0, p)) for p in range(4)]


def whole(shape):
    return pl.BlockSpec(shape, lambda i: (0,) * len(shape))


def block_forward(first, weights, bias, up_blocks=None):
    rows, total = bias.shape
    outs = (
        ((total, D), BF), ((rows, WIDE), BF), ((total, WIDE), BF), ((total, WIDE), BF),
        ((rows, D), BF), ((rows, D), F32), ((rows, D), BF), ((16, D), F32),
    )
    scratch = [pltpu.VMEM((rows, WIDE), BF)]
    params, more = {}, ()
    if up_blocks is not None:
        outs += (((total, D), BF), ((D, D), BF))
        scratch += [pltpu.VMEM((total, D), BF), pltpu.VMEM((D, D), BF)]
        scratch += [pltpu.SemaphoreType.DMA((n,)) for n in (2, 2, 1)] + spread_sems()
        params, more = {"collective_id": 5, "has_side_effects": True}, (up_blocks,)
    return pl.pallas_call(
        functools.partial(block_kernel, bool(more)),
        out_shape=tuple(jax.ShapeDtypeStruct(*out) for out in outs),
        grid=(1,),
        in_specs=[
            whole(first.shape), *weight_specs(weights), whole(bias.shape),
            *(whole(value.shape) for value in more),
        ],
        out_specs=tuple(whole(shape) for shape, _ in outs),
        scratch_shapes=scratch,
        compiler_params=pltpu.CompilerParams(vmem_limit_bytes=62 * 1024 * 1024, **params),
        cost_estimate=lasting(45 if more else 22),
        name="block_forward",
    )(first, weights, weights, weights, weights, bias, *more)


def block_back_kernel(
    ring, d_second, up, resid, wide, q_ref, k_ref, v_ref, att, ffb_rows, wq, wk, wv, wo, par, bias_t,
    *rest,
):
    if ring:
        (d_in, d_low, dq_ref, dk_ref, dv_ref, left, right,
         held, sums, d_resid, da_own, da_halo, sent, caught, send, recv) = rest
    else:
        d_resid, dq_ref, dk_ref, dv_ref, da_own, da_halo, left, right, held, sums = rest
    rows = resid.shape[0]
    total = wide.shape[0]
    own = total - rows
    z = lax.axis_index("ctx")

    def back_to(src, dst, i):
        return pltpu.make_async_remote_copy(
            src_ref=src, dst_ref=dst, send_sem=send.at[i], recv_sem=recv.at[i],
            device_id={"ctx": lax.rem(z + 3, 4)}, device_id_type=MESH,
        )

    if ring:
        one = back_to(da_halo.at[pl.ds(0, rows)], caught.at[0], 0)
        two = back_to(sent, caught.at[1], 1)
        barrier = pltpu.get_barrier_semaphore()
        for step in (1, 3):
            pl.semaphore_signal(
                barrier, inc=1, device_id={"ctx": lax.rem(z + step, 4)}, device_id_type=MESH
            )
        pl.semaphore_wait(barrier, 2)

    def total_of(values):
        return jnp.sum(values, axis=0, keepdims=True)

    upstream = up[...].astype(F32)
    unit, inv = norm_parts(resid[...])
    grad = upstream + norm_back(d_second[...], par[1:2, :], unit, inv)
    d_resid[...] = grad
    sums[1:2, :] = total_of(d_second[...] * unit)
    sums[5:6, :] = total_of(grad)
    sums[6:7, :] = total_of(d_second[...])
    sums[7:8, :] = total_of(upstream)
    sums[8:16, :] = ffb_rows[...]
    low = grad.astype(BF)
    right[pl.ds(0, rows), :] = jnp.zeros((rows, WIDE), BF)
    right[pl.ds(0, rows), pl.ds(0, D)] = low
    right[pl.ds(rows, 16), :] = (
        lax.broadcasted_iota(jnp.int32, (16, WIDE), 1)
        == lax.broadcasted_iota(jnp.int32, (16, WIDE), 0) + D
    ).astype(F32).astype(BF)
    held[...] = jnp.zeros((rows, WIDE), BF)
    held[:, pl.ds(0, D)] = mm_nt(low, wo[:, pl.ds(0, D)]).astype(BF)
    lanes = lax.broadcasted_iota(jnp.int32, (rows, 128), 1)

    @pl.loop(0, WIDE // 128)
    def _(i):
        at = lane_tile(i)
        dq_ref[:, at], dk_ref[:, at], dv_ref[:, at] = scores_backward(
            q_ref[:, at] * jnp.asarray(SCALE, BF), k_ref[:, at], v_ref[:, at], held[:, at],
            bias_t[...], lanes,
        )

    sums[3:4, :] = total_of(dq_ref[...].astype(F32))[:, :D]
    sums[4:5, :] = total_of(dv_ref[...].astype(F32))[:, :D]
    sums[0:1, :] = jnp.zeros((1, D), F32)
    sums[2:3, :] = jnp.zeros((1, D), F32)

    def back(at):
        da = mm_nt(dk_ref[at, :], wk[...]) + mm_nt(dv_ref[at, :], wv[...])
        return da

    def count(da, at):
        unit, _ = norm_parts(wide[at, :].astype(F32))
        sums[0:1, :] += total_of(da * unit)
        sums[2:3, :] += total_of(da)

    @pl.loop(0, own // rows)
    def _(i):
        at = pl.ds(pl.multiple_of(i * rows, 16), rows)
        da = back(at)
        da_halo[at, :] = da.astype(BF)
        if ring:

            @pl.when((i == 0) & (z > 0))
            def _():
                one.start()

        count(da, at)

    at = pl.ds(own, rows)
    da = back(at) + mm_nt(dq_ref[...], wq[...])
    da_own[...] = da
    count(da, at)
    if ring:

        @pl.when(z < 3)
        def _():
            one.wait_recv()

        @pl.when(z == 3)
        def _():
            caught[0] = jnp.zeros_like(caught[0])

        @pl.when(z > 0)
        def _():
            add_rows(sent, da_halo.at[pl.ds(rows, rows)], caught.at[0], rows, 64)
            two.start()

    left[pl.ds(0, rows), :] = att[...]
    left[pl.ds(rows, 16), :] = sums[...].astype(BF)
    if ring:

        @pl.when(z < 3)
        def _():
            two.wait_recv()

        @pl.when(z == 3)
        def _():
            caught[1] = jnp.zeros_like(caught[1])

        @pl.loop(0, rows // 64)
        def _(i):
            part = pl.ds(pl.multiple_of(i * 64, 64), 64)
            behind = pl.ds(pl.multiple_of(own + i * 64, 64), 64)
            unit, inv = norm_parts(wide[behind, :].astype(F32))
            da = da_own[part, :] + caught[1, part, :].astype(F32)
            grad = d_resid[part, :] + norm_back(da, par[0:1, :], unit, inv)
            d_in[part, :] = grad
            d_low[part, :] = grad.astype(BF)

        @pl.when(z > 0)
        def _():
            one.wait_send()
            two.wait_send()


def block_backward(d_second, up, resid, wide, q, k, v, att, ffb_rows, weights, par, bias_t, ring):
    total, rows = wide.shape[0], resid.shape[0]
    f32_rows, low_rows = ((rows, D), F32), ((rows, D), BF)
    heads = (((rows, WIDE), BF), ((total, WIDE), BF), ((total, WIDE), BF))
    factors = (((rows + 16, D), BF), ((rows + 16, WIDE), BF))
    halo = ((total - rows, D), BF)
    held = [pltpu.VMEM((rows, WIDE), BF), pltpu.VMEM((16, D), F32)]
    params = {}
    if ring:
        outs = (f32_rows, low_rows, *heads, *factors)
        held += [pltpu.VMEM(*f32_rows), pltpu.VMEM(*f32_rows), pltpu.VMEM(*halo), pltpu.VMEM(*low_rows)]
        held += [pltpu.VMEM((2, rows, D), BF)] + [pltpu.SemaphoreType.DMA((2,))] * 2
        params = {"collective_id": 6, "has_side_effects": True}
    else:
        outs = (f32_rows, *heads, f32_rows, halo, *factors)
    before = (d_second, up, resid, wide, q, k, v, att, ffb_rows)
    return pl.pallas_call(
        functools.partial(block_back_kernel, ring),
        out_shape=tuple(jax.ShapeDtypeStruct(*out) for out in outs),
        grid=(1,),
        in_specs=[
            *(whole(value.shape) for value in before), *weight_specs(weights),
            whole(par.shape), whole(bias_t.shape),
        ],
        out_specs=tuple(whole(shape) for shape, _ in outs),
        scratch_shapes=held,
        compiler_params=pltpu.CompilerParams(vmem_limit_bytes=62 * 1024 * 1024, **params),
        cost_estimate=lasting(58 if ring else 38),
        name="block_backward",
    )(*before, weights, weights, weights, weights, par, bias_t)


def on_device(
    inputs, segments, cotangent, qkv_weight, out_weight, up_weight, down_weight,
    norm_gains, biases, ff_bias,
):
    rows = inputs.shape[2]
    length = segments.shape[2]
    chunks = min((length // 2 - 1 + rows - 1) // rows, lax.axis_size("ctx") - 1)
    reach = chunks * rows
    s = lax.axis_index("section")
    f = lax.axis_index("fsdp")
    nf = lax.axis_size("fsdp")
    shard = D // nf
    ff_here = ff_bias.shape[1]
    per_row = ff_here // shard
    pair = ("fsdp", "section")
    fits = nf == 4 and lax.axis_size("ctx") == 4 and chunks == 2

    own_in = lax.dynamic_index_in_dim(inputs, s, 0, keepdims=False)[0]
    own_cot = lax.dynamic_index_in_dim(cotangent, s, 0, keepdims=False)[0]
    seg = lax.dynamic_index_in_dim(segments, s, 0, keepdims=False)[0]
    start = lax.axis_index("ctx") * rows
    key_seg = lax.dynamic_slice_in_dim(
        jnp.pad(seg, (reach, 0), constant_values=-1), start, reach + rows, 0
    )
    allowed = (key_seg[reach:, None] == key_seg[None, :]) & (
        jnp.arange(reach + rows, dtype=jnp.int32)[None, :] - reach
        <= jnp.arange(rows, dtype=jnp.int32)[:, None]
    )

    bias = jnp.where(allowed, 0.0, -1e30).astype(F32)
    bias_t = bias.T

    def gathered(rows_first):
        return lax.all_gather(rows_first, pair, axis=0, tiled=True)

    if fits:
        zero, wide_in, up_zero, up_blocks, down_w, one_half = first_weights(
            qkv_weight[0], out_weight[0], norm_gains[0], biases[0], ff_bias,
            own_in, up_weight[0], down_weight[0],
        )
        one = gathered(one_half)
        up_w = (up_zero, None)
    else:
        small = jnp.concatenate(
            [norm_gains[0].T, biases[0].T, ff_bias[0].reshape(per_row, shard).T], axis=1
        )
        beside = jnp.pad(small, ((0, 0), (0, WIDE - D - 8 - per_row)))
        packed = jnp.concatenate(
            [widen(qkv_weight[0][:, i * D : (i + 1) * D]) for i in range(3)]
            + [out_weight[0], beside],
            axis=1,
        )
        halves = packed.reshape(2, shard // 2, 4 * WIDE)
        keep = lax.dynamic_index_in_dim(halves, s, 0, keepdims=False)
        recv = on_chip(lax.dynamic_index_in_dim(halves, 1 - s, 0, keepdims=False))
        zero, one = gathered(pick(s, keep, recv)), gathered(pick(s, recv, keep))
        up_own = lax.all_to_all(
            up_weight[0].reshape(shard, nf, ff_here), "fsdp", split_axis=1, concat_axis=0, tiled=True
        ).reshape(D, ff_here)
        up_w = both_layers(up_own, s)
        down_w = both_layers(down_weight[0], s)
        wide_in = with_halo(own_in, chunks)

    weights = (zero, one)

    kept = []
    current = own_in
    produced = []
    for layer in range(2):
        if layer == 1 and fits:
            *made, wide, up_one = block_forward(current, weights[layer], bias, up_blocks)
            up_w = (up_w[0], up_one)
        else:
            wide = with_halo(current, chunks) if layer else wide_in
            made = block_forward(wide, weights[layer], bias)
        normed, q, k, v, att, resid, second, par = made
        ffb = lax.dynamic_slice(par, (8, f * shard), (per_row, shard)).reshape(1, ff_here)
        current, second_all, active, slope = mlp_forward(
            second, up_w[layer], down_w, layer, ffb, resid, par
        )
        produced.append(current)
        kept.append((wide, normed, q, k, v, att, resid, second_all, slope, active, par))

    upstream = own_cot
    derived = [None, None]
    parts = [None, None]
    mlp_sums = [None, None]
    for layer in (1, 0):
        wide, normed, q, k, v, att, resid, second_all, slope, active, par = kept[layer]
        d_second, up_all, dz_b, ffb_g = mlp_backward(upstream, up_w[layer], down_w, layer, slope)
        up_g = mm_tn(flat(second_all), flat(dz_b)).astype(BF)
        up_half = core_half(up_g.reshape(nf, 2, shard // 2, ff_here), 1)
        down_g = mm_tn(flat(active), flat(up_all)).astype(BF)
        down_half = core_half(down_g.reshape(2, ff_here // 2, D), 0)
        d_second, up_half, down_half = lax.optimization_barrier((d_second, up_half, down_half))
        up_half = lax.all_to_all(up_half, "fsdp", split_axis=0, concat_axis=0, tiled=True)
        ffb_rows = lax.dynamic_update_slice(
            jnp.zeros((8, D), F32), ffb_g.reshape(per_row, shard), (0, f * shard)
        )
        block = (
            d_second, upstream, resid, wide, q, k, v, att, ffb_rows, weights[layer], par, bias_t
        )
        if layer == 1 and fits:
            derived[1], upstream_next, dq, dk, dv, left, right = block_backward(*block, True)
        else:
            d_resid, dq, dk, dv, da_own, da_halo, left, right = block_backward(*block, False)
        if not fits:
            unit, inv = norm_parts(wide[reach:].astype(F32))
            late = return_halo(da_halo, chunks, rows)
            derived[layer] = d_resid + norm_back(da_own + late, par[0], unit, inv)
            upstream_next = derived[layer].astype(BF)
        pieces = (
            mm_tn(normed[reach:], dq).astype(BF),
            mm_tn(normed, dk).astype(BF),
            mm_tn(normed, dv).astype(BF),
            mm_tn(left, right).astype(BF),
        )
        parts[layer] = pieces
        up_half, down_half, _ = lax.optimization_barrier((up_half, down_half, dq))
        halves = (down_half, up_half.reshape(ff_here // 2, D))
        if layer == 1:
            _, upstream_next = lax.optimization_barrier((halves, upstream_next))
        else:
            halves, mlp_sums[1] = lax.optimization_barrier((halves, mlp_sums[1]))
        mlp_sums[layer] = lax.psum(halves, "ctx")
        if layer == 1:
            upstream = upstream_next

    if fits:
        qkv_g, out_g, down_one, up_one, made, grads = reduce_both(
            parts[0], parts[1], mlp_sums[1], produced, derived[1], da_halo, d_resid, da_own,
            wide[reach:], par,
        )
        late_sum, qkv_g = lax.optimization_barrier((mlp_sums[0], qkv_g))
        far = [lax.ppermute(half, "section", [(1, 0)]) for half in late_sum]
        qkv_g, out_g, grad_down, grad_up, small, made, grads = final_layouts(
            qkv_g, out_g, *late_sum, *far, down_one, up_one, made, grads
        )
        made, grads = made[None, :, None], grads[None, :, None]
    else:
        a_tot = pick(s, reduce_plain(parts[0]), reduce_plain(parts[1])).astype(F32)
        qkv_g = jnp.concatenate([a_tot[i, :, :D] for i in range(3)], axis=1)
        out_g = a_tot[3, :, :D]
        small = a_tot[3, :, D : D + 16].T
        grad_down, grad_up = halves_settle(*mlp_sums, nf, shard)
        made, grads = both_micros(produced, s), both_micros(derived, s)
    return (
        made,
        grads,
        qkv_g[None],
        out_g[None],
        grad_up[None],
        grad_down[None],
        small[None, :2],
        small[None, 2:8],
        small[8 : 8 + per_row].reshape(1, ff_here),
    )


def both_micros(layers, s):
    to_zero = lax.ppermute(layers[0], "section", [(1, 0)])
    to_one = lax.ppermute(layers[1], "section", [(0, 1)])
    out = jnp.stack([pick(s, layers[0], to_one), pick(s, to_zero, layers[1])])
    return out[None, :, None]


def solution(mesh):
    return jax.shard_map(
        on_device,
        mesh=mesh,
        in_specs=(
            P(None, "fsdp", "ctx", None),
            P(None, "fsdp", None),
            P(None, "fsdp", "ctx", None),
            P("section", "fsdp", None),
            P("section", "fsdp", None),
            P("section", "fsdp", None),
            P("section", "fsdp", None),
            P("section", None, "fsdp"),
            P("section", None, "fsdp"),
            P("section", "fsdp"),
        ),
        out_specs=(
            P("section", None, "fsdp", "ctx", None),
            P("section", None, "fsdp", "ctx", None),
            P("section", "fsdp", None),
            P("section", "fsdp", None),
            P("section", "fsdp", None),
            P("section", "fsdp", None),
            P("section", None, "fsdp"),
            P("section", None, "fsdp"),
            P("section", "fsdp"),
        ),
        check_vma=False,
    )
```
